32 devices in a mesh: ctx: 16 (over z, x, core), fsdp: 2 (over y).
Axes of the slice: x: 2, y: 2, z: 4, core: 2. Of those that a mesh axis runs over, the one named last changes fastest.
Arguments:
- tokens: bfloat16 [2, 4096, 768], P('fsdp', 'ctx'), may hold values from -6 to 6
- cotangent: bfloat16 [2, 4096, 768], P('fsdp', 'ctx'), may hold values from -6 to 6
- lengths: int32 [2, 3], P('fsdp'), may hold values from 1 to 2048, 4096 in all within a row
- deal: int32 [2, 32], P('fsdp'), may hold values from 0 to 31, each once within a row
- joint_projection: bfloat16 [768, 2304], P('fsdp'), may hold values from -0.21875 to 0.21875
- output_projection: bfloat16 [768, 768], P('fsdp'), may hold values from -3 to 3
- expand_weight: bfloat16 [768, 2304], P('fsdp'), may hold values from -0.21875 to 0.21875
- contract_weight: bfloat16 [1152, 768], P('fsdp'), may hold values from -0.1875 to 0.1875
- gain_first: bfloat16 [768], P('fsdp'), may hold values from 0.099609375 to 1.8984375
- gain_second: bfloat16 [768], P('fsdp'), may hold values from 0.099609375 to 1.8984375
Outputs:
- output: bfloat16 [2, 4096, 768], P('fsdp', 'ctx')
- input_grad: bfloat16 [2, 4096, 768], P('fsdp', 'ctx')
- joint_grad: float32 [768, 2304], P('ctx')
- output_grad: float32 [768, 768], P('ctx')
- expand_grad: float32 [768, 2304], P('ctx')
- contract_grad: float32 [1152, 768], P('ctx')
- gain_first_grad: float32 [768], P('ctx')
- gain_second_grad: float32 [768], P('ctx')
The draws below stay inside these ranges and needn't reach their ends.
Inputs may be any that keep to these rules, and one draw needn't show every extreme that they name: Each row of 3 lengths sums to 4096, and its longest is exactly 2048. Each row deal[g, :] is a permutation of the 32 blocks of a group.
All inputs are finite; a program needn't handle non-finite values.
Results may differ from the reference program's by a relative error of at most 0.029.
Values may be sent and summed in bfloat16 or wider, within the bound.
A program may use at most 192 MiB of HBM per device.

```python
import math
import jax
import jax.numpy as jnp
import numpy as np
from jax import lax

D = 768
FF = 1152
HEADS = 12
HEAD_DIM = 64
BLOCK = 128
SEQS = 3
GROUPS = 2
NBLOCKS = 32
GROUP_TOKENS = 4096


def steps_of(key, shape, shards, least, largest):
    loudness = 1.0
    for position, parts in shards:
        draws = jax.random.uniform(jax.random.fold_in(jax.random.fold_in(key, 6), position), (parts,), jnp.float32, least / len(shards), largest / len(shards))
        loudness = loudness * jnp.repeat(jnp.exp(draws), shape[position] // parts).reshape((-1,) + (1,) * (len(shape) - 1 - position))
    return loudness


def length_profile(count, total, limit, lean):
    portions = [(1 << 20) // math.isqrt(grade ** lean) + 1 for grade in range(2, count + 1)]
    spare, counts = total - limit - (count - 1), [1] * (count - 1)
    while spare > 0:
        free = [i for i in range(count - 1) if counts[i] < limit]
        whole, remaining = sum([portions[i] for i in free]), spare
        for i in free:
            addition = min(limit - counts[i], max(1, remaining * portions[i] // whole), spare)
            counts[i] = counts[i] + addition
            spare = spare - addition
    return np.array([limit] + counts)


def uneven(rng, count, total, reach, slope):
    if count == 2:
        one = jax.random.randint(rng, (), max(1, total - reach), min(reach, total - 1) + 1)
        return jnp.stack([one, total - one])
    sizes = jnp.asarray(length_profile(count, total, reach, slope), jnp.int32)
    twos = (count - 1) // 2
    donor, taker = sizes[1:1 + 2 * twos:2], sizes[2:2 + 2 * twos:2]
    margin = jnp.minimum(donor - 1, reach - taker)
    moved = jax.random.randint(jax.random.fold_in(rng, 1), (twos,), 0, 1 << 20) % (margin + 1)
    sizes = sizes.at[1:1 + 2 * twos:2].set(donor - moved).at[2:2 + 2 * twos:2].set(taker + moved)
    return sizes[jax.random.permutation(jax.random.fold_in(rng, 2), count)]


def noise(key, shape, deviation, most, cuts=(), kind=jnp.bfloat16):
    drawn = jax.random.normal(key, shape, jnp.float32) * deviation
    if len(cuts) > 0:
        drawn = steps_of(key, shape, cuts, -0.22, 0.18) * drawn
    return jnp.clip(drawn, min=-most, max=most).astype(kind)


def setup_inputs(seed: int = 0) -> dict:
    arg_keys = jax.random.split(jax.random.key(seed), 11)
    return {
        "tokens": noise(arg_keys[0], (GROUPS, GROUP_TOKENS, D), 1.0, 6.0, ((0, 2), (1, 16))),
        "cotangent": noise(arg_keys[1], (GROUPS, GROUP_TOKENS, D), 1.0, 6.0, ((0, 2), (1, 16))),
        "lengths": jax.vmap(lambda own: uneven(own, SEQS, GROUP_TOKENS, GROUP_TOKENS // 2, 2))(jax.random.split(arg_keys[2], GROUPS)).reshape((GROUPS, SEQS)).astype(jnp.int32),
        "deal": jax.vmap(lambda own: jax.random.permutation(own, NBLOCKS))(jax.random.split(arg_keys[3], GROUPS)).reshape((GROUPS, NBLOCKS)).astype(jnp.int32),
        "joint_projection": noise(arg_keys[4], (D, 3 * D), D ** -0.5, 0.21875, ((0, 2),)),
        "output_projection": noise(arg_keys[5], (D, D), 4 ** -0.5, 3.0, ((0, 2),)),
        "expand_weight": noise(arg_keys[6], (D, 2 * FF), D ** -0.5, 0.21875, ((0, 2),)),
        "contract_weight": noise(arg_keys[7], (FF, D), FF ** -0.5, 0.1875, ((0, 2),)),
        "gain_first": jnp.clip(1.0 + 0.18 * jax.random.normal(arg_keys[8], (D,), jnp.float32), 0.099609375, 1.8984375).astype(jnp.bfloat16),
        "gain_second": jnp.clip(1.0 + 0.18 * jax.random.normal(arg_keys[9], (D,), jnp.float32), 0.099609375, 1.8984375).astype(jnp.bfloat16),
    }


rope_base = 160000.0
norm_eps = 1e-05
highest = lax.Precision.HIGHEST

@jax.custom_vjp
def low(v):
    return lax.optimization_barrier(v.astype(jnp.bfloat16)).astype(jnp.float32)

@jax.custom_vjp
def low_back(v):
    return v

def low_keep(v):
    return (low(v), None)

def low_pass(kept, grad):
    return (grad,)

def back_keep(v):
    return (v, None)

def back_low(kept, grad):
    return (low(grad),)
low.defvjp(low_keep, low_pass)
low_back.defvjp(back_keep, back_low)

def layer_norm(values, weights):
    centred = values - lax.optimization_barrier(jnp.mean(values, axis=-1, keepdims=True))
    spread = lax.optimization_barrier(jnp.mean(centred * centred, axis=-1, keepdims=True))
    return centred * lax.rsqrt(spread + norm_eps) * weights

def rotary(values, angles_cos, angles_sin):
    half_width = values.shape[-1] // 2
    turned = jnp.concatenate([-values[..., half_width:], values[..., :half_width]], axis=-1)
    return values * angles_cos + turned * angles_sin

def rotary_tables(positions):
    frequencies = rope_base ** (-jnp.arange(0, HEAD_DIM, 2).astype(jnp.float32) / HEAD_DIM)
    angles = positions.astype(jnp.float32)[:, None] * frequencies[None, :]
    angles = jnp.concatenate([angles, angles], axis=-1)
    return (jnp.cos(angles)[:, None, :], jnp.sin(angles)[:, None, :])

def group_layout(lengths_row, deal_row):
    seq_ends = jnp.cumsum(lengths_row).astype(jnp.int32)
    starts = (seq_ends - lengths_row).astype(jnp.int32)
    natural = jnp.arange(GROUP_TOKENS, dtype=jnp.int32)
    segment = lax.optimization_barrier(jnp.sum((natural[:, None] >= seq_ends[None, :]).astype(jnp.int32), axis=1))
    chosen = (segment[:, None] == jnp.arange(SEQS, dtype=jnp.int32)[None, :]).astype(jnp.int32)
    positions = natural - lax.optimization_barrier(jnp.sum(chosen * starts[None, :], axis=1))
    within = jnp.arange(BLOCK, dtype=jnp.int32)
    dealt_index = deal_row.astype(jnp.int32)[:, None] * BLOCK + within[None, :]
    return (segment, positions, dealt_index.reshape(-1).astype(jnp.int32))

def attention(query_rows, key_rows, value_rows, segment):
    row_count = query_rows.shape[0]
    block_rows = math.gcd(row_count, 512)
    query_blocks = query_rows.reshape(row_count // block_rows, block_rows, HEADS, HEAD_DIM)
    segment_blocks = segment.reshape(row_count // block_rows, block_rows)
    score_scale = HEAD_DIM ** (-0.5)

    def one_block(operands):
        query_part, segment_part = operands
        scores = jnp.einsum('qhd,khd->hqk', query_part, key_rows, precision=highest) * score_scale
        scores = low_back(scores)
        allowed = (segment_part[:, None] == segment[None, :])[None]
        scores = jnp.where(allowed, scores, -1e+30)
        probabilities = low(jax.nn.softmax(scores, axis=-1))
        return jnp.einsum('hqk,khd->qhd', probabilities, value_rows, precision=highest)
    attended = lax.map(jax.checkpoint(one_block), (query_blocks, segment_blocks))
    return attended.reshape(row_count, HEADS, HEAD_DIM)

def layer_forward(inputs, joint, out_proj, expand, contract, gain_one, gain_two, segment, angles_cos, angles_sin):
    first = low(layer_norm(inputs, gain_one))
    mixed = low_back(jnp.dot(first, joint, precision=highest)).reshape(-1, 3, HEADS, HEAD_DIM)
    queries = low(rotary(mixed[:, 0], angles_cos, angles_sin))
    keys_rot = low(rotary(mixed[:, 1], angles_cos, angles_sin))
    values = low(mixed[:, 2])
    attended = attention(queries, keys_rot, values, segment).reshape(-1, D)
    attended = low(low_back(attended))
    hidden = inputs + low_back(jnp.dot(attended, out_proj, precision=highest))
    second = low(layer_norm(hidden, gain_two))
    expanded = low_back(jnp.dot(second, expand, precision=highest))
    activated = low(jax.nn.gelu(expanded[:, :FF], approximate=False) * expanded[:, FF:])
    return hidden + low_back(jnp.dot(activated, contract, precision=highest))

def reference(tokens, cotangent, lengths, deal, joint_projection, output_projection, expand_weight, contract_weight, gain_first, gain_second):
    params = tuple((weight.astype(jnp.float32) for weight in (joint_projection, output_projection, expand_weight, contract_weight, gain_first, gain_second)))
    outputs = []
    input_grads = []
    totals = [jnp.zeros(weight.shape, jnp.float32) for weight in params]
    for group_index in range(GROUPS):
        segment, positions, dealt_index = group_layout(lengths[group_index], deal[group_index])
        angles_cos, angles_sin = rotary_tables(positions)

        def forward(inputs, joint, out_proj, expand, contract, gain_one, gain_two):
            return layer_forward(inputs, joint, out_proj, expand, contract, gain_one, gain_two, segment, angles_cos, angles_sin)
        result, pullback = jax.vjp(forward, tokens[group_index].astype(jnp.float32), *params)
        gradients = pullback(cotangent[group_index].astype(jnp.float32))
        outputs.append(result.astype(jnp.bfloat16))
        input_grads.append(jnp.take(gradients[0], dealt_index, axis=0).astype(jnp.bfloat16))
        totals = [total + grad_part for total, grad_part in zip(totals, gradients[1:])]
    return (jnp.stack(outputs), jnp.stack(input_grads), totals[0], totals[1], totals[2], totals[3], totals[4], totals[5])
```

```python
import functools

import jax
import jax.numpy as jnp
from jax import lax
from jax.experimental import pallas as pl
from jax.experimental.pallas import tpu as pltpu
from jax.sharding import PartitionSpec as P

FF = 1152
HEADS = 12
HEAD_DIM = 64
BLOCK = 128
PLANES = 4
HD = HEAD_DIM
HALF = HEAD_DIM // 2
HP = HEADS // PLANES
QW = HP * HEAD_DIM
rope_base = 160000.0
norm_eps = 1e-05
MASKED = -1e30


def head_rows(x, head, pad_to=None):
    rows=lax.broadcasted_iota(jnp.int32,x.shape,0)
    return jnp.where((rows>=head*HD)&(rows<(head+1)*HD),x,jnp.zeros_like(x))

def fwd_kernel(bounds_ref, table_ref, span_ref, qt_ref, kvt_ref, ot_ref, lowt_ref, lse_ref, keys, acc):
    units, _, T = kvt_ref.shape
    def flip(u,_):
        keys[u]=kvt_ref[u,:QW,:].T
        return 0
    lax.fori_loop(0,units,flip,0)
    def one_query_block(b,_):
        qt=qt_ref[b]
        qheads=[head_rows(qt,h) for h in range(HP)]
        q_start=span_ref[b,0:1,:]; q_end=span_ref[b,1:2,:]
        acc[...]=jnp.zeros_like(acc)
        def one_unit(u,carry):
            m,l=carry
            pos=table_ref[u]
            k=keys[pos]
            at=u*T+lax.broadcasted_iota(jnp.int32,(T,T),0)
            allowed=(at>=q_start)&(at<q_end)
            ms=[];ls=[]
            for h in range(HP):
                st=jnp.dot(k,qheads[h],preferred_element_type=jnp.float32)
                st=jnp.where(allowed,st,MASKED)
                mn=jnp.maximum(m[h],jnp.max(st,axis=0,keepdims=True))
                p=jnp.exp(st-mn)
                a=jnp.exp(m[h]-mn)
                ls.append(l[h]*a+jnp.sum(p,axis=0,keepdims=True))
                ms.append(mn)
                rows=pl.ds(h*HD,HD)
                acc[rows,:]=acc[rows,:]*a+jnp.dot(kvt_ref[pos,pl.ds(QW+h*HD,HD),:],p.astype(jnp.bfloat16),preferred_element_type=jnp.float32)
            return tuple(ms),tuple(ls)
        init=(tuple(jnp.full((1,T),MASKED,jnp.float32) for _ in range(HP)),tuple(jnp.zeros((1,T),jnp.float32) for _ in range(HP)))
        m,l=lax.fori_loop(bounds_ref[b,0],bounds_ref[b,1],one_unit,init)
        for h in range(HP):
            rows=pl.ds(h*HD,HD)
            o=acc[rows,:]/l[h]
            ot_ref[b,rows,:]=o
            lowt_ref[b,rows,:]=o.astype(jnp.bfloat16)
            lse_ref[b,h:h+1,:]=m[h]+jnp.log(l[h])
        return 0
    lax.fori_loop(0,qt_ref.shape[0],one_query_block,0)

def attn_fwd(bounds,table,span,qt,kvt):
    B,_,T=qt.shape; U=kvt.shape[0]
    sm=pl.BlockSpec(memory_space=pltpu.SMEM); vm=pl.BlockSpec(memory_space=pltpu.VMEM)
    return pl.pallas_call(fwd_kernel,
        out_shape=(jax.ShapeDtypeStruct((B,QW,T),jnp.float32),jax.ShapeDtypeStruct((B,QW,T),jnp.bfloat16),jax.ShapeDtypeStruct((B,8,T),jnp.float32)),
        in_specs=[sm,sm,vm,vm,vm],out_specs=(vm,vm,vm),
        scratch_shapes=[pltpu.VMEM((U,T,QW),jnp.bfloat16),pltpu.VMEM((QW,T),jnp.float32)],
        compiler_params=pltpu.CompilerParams(vmem_limit_bytes=50<<20))(bounds,table,span,qt,kvt)

def bwd_kernel(bounds_ref, table_ref, span_ref, qt_ref, kvt_ref, ot_ref, lse_ref, gt_ref, dqt_ref, dkvt_ref, kv, dk, dv, dq):
    units, _, T = kvt_ref.shape
    def flip(u,_):
        kv[u]=kvt_ref[u].T
        dk[u]=jnp.zeros_like(dk[u]); dv[u]=jnp.zeros_like(dv[u])
        return 0
    lax.fori_loop(0,units,flip,0)
    def one_query_block(b,_):
        qt=qt_ref[b]; gt=gt_ref[b]
        zero=jnp.zeros((HD,T),jnp.bfloat16)
        qheads=[head_rows(qt,h) for h in range(HP)]
        gheads=[head_rows(gt,h) for h in range(HP)]
        q=[x.T for x in qheads]; g=[x.T for x in gheads]
        q_start=span_ref[b,0:1,:]; q_end=span_ref[b,1:2,:]
        prod=gt.astype(jnp.float32)*ot_ref[b]
        delta=[jnp.sum(prod[h*HD:(h+1)*HD],axis=0,keepdims=True) for h in range(HP)]
        lse=[lse_ref[b,h:h+1,:] for h in range(HP)]
        dq[...]=jnp.zeros_like(dq)
        gpad=[jnp.concatenate([zero,x],axis=0) for x in gheads]
        def one_unit(u,_):
            pos=table_ref[u]
            k=kv[pos,:,:QW]; v=kv[pos,:,128:]
            at=u*T+lax.broadcasted_iota(jnp.int32,(T,T),0)
            allowed=(at>=q_start)&(at<q_end)
            dkt=None
            for h in range(HP):
                st=jnp.dot(k,qheads[h],preferred_element_type=jnp.float32)
                p=jnp.exp(jnp.where(allowed,st-lse[h],MASKED))
                dp=jnp.dot(v,gpad[h],preferred_element_type=jnp.float32)
                ds=(p*(dp-delta[h])).astype(jnp.bfloat16)
                pv=jnp.dot(p.astype(jnp.bfloat16),g[h],preferred_element_type=jnp.float32)
                pk=jnp.dot(ds,q[h],preferred_element_type=jnp.float32)
                dvt=pv if h==0 else dvt+pv
                dkt=pk if h==0 else dkt+pk
                rows=pl.ds(h*HD,HD)
                dq[rows,:]+=jnp.dot(kvt_ref[pos,rows,:],ds,preferred_element_type=jnp.float32)
            dk[pos]+=dkt; dv[pos]+=dvt
            return 0
        lax.fori_loop(bounds_ref[b,0],bounds_ref[b,1],one_unit,0)
        dqt_ref[b]=dq[...]*(HD**-0.5)
        return 0
    lax.fori_loop(0,qt_ref.shape[0],one_query_block,0)
    def out(u,_):
        dkvt_ref[u,:QW,:]=dk[u].T.astype(jnp.bfloat16)
        dkvt_ref[u,QW:,:]=dv[u].T.astype(jnp.bfloat16)
        return 0
    lax.fori_loop(0,units,out,0)

def attn_bwd(bounds,table,span,qt,kvt,ot,lse,gt):
    B,_,T=qt.shape; U=kvt.shape[0]
    sm=pl.BlockSpec(memory_space=pltpu.SMEM); vm=pl.BlockSpec(memory_space=pltpu.VMEM)
    return pl.pallas_call(bwd_kernel,
        out_shape=(jax.ShapeDtypeStruct((B,QW,T),jnp.float32),jax.ShapeDtypeStruct((U,2*QW,T),jnp.bfloat16)),
        in_specs=[sm,sm]+[vm]*6,out_specs=(vm,vm),
        scratch_shapes=[pltpu.VMEM((U,T,2*QW),jnp.bfloat16),pltpu.VMEM((U,T,QW),jnp.float32),pltpu.VMEM((U,T,QW),jnp.float32),pltpu.VMEM((QW,T),jnp.float32)],
        compiler_params=pltpu.CompilerParams(vmem_limit_bytes=60<<20))(bounds,table,span,qt,kvt,ot,lse,gt)


def layer_norm(values, weights):
    centred = values - jnp.mean(values, axis=-1, keepdims=True)
    spread = jnp.mean(centred * centred, axis=-1, keepdims=True)
    return centred * lax.rsqrt(spread + norm_eps) * weights


def rotate_rows(values, cos, sin):
    upper, lower = values[..., :HALF, :], values[..., HALF:, :]
    return jnp.concatenate([upper * cos - lower * sin, lower * cos + upper * sin], axis=-2)


def on_device(
    n,
    groups,
    tokens,
    cotangent,
    lengths,
    deal,
    joint_projection,
    output_projection,
    expand_weight,
    contract_weight,
    gain_first,
    gain_second,
):
    bf, f32 = jnp.bfloat16, jnp.float32
    T, D = tokens.shape[1:]
    S = n // PLANES
    S2 = S // 2
    units = n
    me, gy = lax.axis_index("ctx"), lax.axis_index("fsdp")
    plane, side = me // S, me % S
    s2, core = side // 2, side % 2

    def over_planes(x, k):
        return lax.ppermute(x, "ctx", [(h * S + s, (h + k) % PLANES * S + s) for h in range(PLANES) for s in range(S)])

    def over_sides(x, k):
        return lax.ppermute(
            x,
            "ctx",
            [(h * S + a * 2 + c, h * S + (a + k) % S2 * 2 + c) for h in range(PLANES) for a in range(S2) for c in range(2)],
        )

    def over_cores(x):
        return lax.ppermute(x, "ctx", [(i, i ^ 1) for i in range(n)])

    def over_groups(x, k):
        return lax.ppermute(x, "fsdp", [(f, (f + k) % groups) for f in range(groups)])

    def pick(x, index):
        return lax.dynamic_index_in_dim(x, index, 0, keepdims=False)

    def turned(x, shift):
        return lax.dynamic_slice_in_dim(jnp.concatenate([x, x], axis=0), shift, x.shape[0], 0)

    def whole_of(shard):
        parts = [shard] + [over_groups(shard, k) for k in range(1, groups)]
        return turned(jnp.stack(parts[::-1]), groups - 1 - gy).reshape(-1, *shard.shape[1:])

    def whole_by_cores(shard):
        half = shard.shape[0] // 2
        halves = shard.reshape(2, half, *shard.shape[1:])
        mine = pick(halves, core)
        got = jnp.stack([over_groups(mine, k) for k in range(1, groups)])
        other = over_cores(got)
        low = jnp.where(core == 0, got, other)
        high = jnp.where(core == 0, other, got)
        parts = jnp.concatenate([jnp.stack([low, high], axis=1)[::-1], halves[None]], axis=0)
        return turned(parts, groups - 1 - gy).reshape(-1, *shard.shape[1:])

    tokens_own = tokens[0]
    all_tokens = jnp.stack([tokens_own] + [over_planes(tokens_own, k) for k in range(1, PLANES)])
    joint_cols = lax.dynamic_index_in_dim(
        joint_projection.reshape(-1, 3, PLANES, QW), plane, 2, keepdims=False
    ).reshape(-1, 3 * QW)
    joint = whole_of(joint_cols)
    gains = whole_of(jnp.stack([gain_first, gain_second], axis=1))
    gain_one, gain_two = gains[:, 0].astype(f32), gains[:, 1].astype(f32)
    out_w = whole_by_cores(output_projection)
    exp_w = whole_by_cores(expand_weight)
    con_w = whole_by_cores(contract_weight)

    lens = lengths[0]
    ends, total = [], jnp.int32(0)
    for j in range(lens.shape[0]):
        total = total + lens[j]
        ends.append(total)
    rel_plane = (plane - jnp.arange(PLANES)) % PLANES
    first_token = (rel_plane * S + side) * T
    natural = first_token[:, None] + jnp.arange(T, dtype=jnp.int32)[None]

    def span_of(index):
        begin, end = jnp.zeros_like(index), jnp.full_like(index, ends[0])
        for j in range(1, lens.shape[0]):
            after = index >= ends[j - 1]
            begin = jnp.where(after, ends[j - 1], begin)
            end = jnp.where(after, ends[j], end)
        return begin, end

    begin, end = span_of(natural)
    span = jnp.stack([begin, end] + [jnp.zeros_like(begin)] * 6, axis=1)
    low_bound, _ = span_of(first_token)
    _, high_bound = span_of(first_token + T - 1)
    bounds = jnp.stack([low_bound // T, (high_bound + T - 1) // T], axis=1).astype(jnp.int32)
    unit = jnp.arange(units, dtype=jnp.int32)
    u_plane, u_side = unit // S, unit % S
    u_s2, u_core = u_side // 2, u_side % 2
    table = ((u_core != core) * S2 + (s2 - u_s2) % S2) * PLANES + (plane - u_plane) % PLANES
    table = table.astype(jnp.int32)
    frequencies = rope_base ** (-jnp.arange(0, HEAD_DIM, 2).astype(f32) / HEAD_DIM)
    angles = (natural - begin).astype(f32)[:, None, :] * frequencies[None, :, None]
    cos, sin = jnp.cos(angles)[:, None], jnp.sin(angles)[:, None]

    x_all = all_tokens.astype(f32)
    first = layer_norm(x_all, gain_one).astype(bf)
    mixed = jnp.einsum("bte,ed->bdt", first, joint, preferred_element_type=f32)
    mixed = mixed.reshape(PLANES, 3, HP, HEAD_DIM, T)
    qt = (rotate_rows(mixed[:, 0], cos, sin).astype(bf) * bf(HEAD_DIM**-0.5)).reshape(PLANES, QW, T)
    kt = rotate_rows(mixed[:, 1], cos, sin).astype(bf).reshape(PLANES, QW, T)
    vt = mixed[:, 2].astype(bf).reshape(PLANES, QW, T)
    kv = jnp.concatenate([kt, vt], axis=1)
    near = jnp.stack([kv] + [over_sides(kv, k) for k in range(1, S2)])
    kv_all = jnp.concatenate([near[None], over_cores(near)[None]], axis=0).reshape(units, 2 * QW, T)

    ot, lowt, lse = attn_fwd(bounds, table, span, qt, kv_all)

    parts = [lowt[0]] + [over_planes(lowt[k], -k) for k in range(1, PLANES)]
    attended_t = turned(jnp.stack(parts), (PLANES - plane) % PLANES).reshape(D, T)

    x = tokens_own.astype(f32)
    grad_out = cotangent[0]
    hidden = x + jnp.einsum("dt,de->te", attended_t, out_w, preferred_element_type=f32)
    second = layer_norm(hidden, gain_two).astype(bf)
    expanded = jnp.dot(second, exp_w, preferred_element_type=f32)

    def gated(values):
        return jax.nn.gelu(values[:, :FF], approximate=False) * values[:, FF:]

    activated_f, gated_pull = jax.vjp(gated, expanded)
    activated = activated_f.astype(bf)
    output = (hidden + jnp.dot(activated, con_w, preferred_element_type=f32)).astype(bf)

    grad_activated = jnp.einsum("td,fd->tf", grad_out, con_w, preferred_element_type=f32)
    grad_expanded = gated_pull(grad_activated)[0].astype(bf)
    grad_second = jnp.einsum("tf,df->td", grad_expanded, exp_w, preferred_element_type=f32)
    _, second_pull = jax.vjp(layer_norm, hidden, gain_two)
    grad_hidden_norm, grad_gain_two = second_pull(grad_second)
    grad_hidden = grad_out.astype(f32) + grad_hidden_norm
    grad_branch = grad_hidden.astype(bf)
    grad_attended = jnp.einsum("de,te->dt", out_w, grad_branch, preferred_element_type=f32).astype(bf)
    rel = turned(grad_attended.reshape(PLANES, QW, T), plane)
    gt = jnp.stack([rel[0]] + [over_planes(rel[k], k) for k in range(1, PLANES)])

    grad_contract = jnp.einsum("tf,td->fd", activated, grad_out, preferred_element_type=f32)
    grad_expand = jnp.einsum("td,tf->df", second, grad_expanded, preferred_element_type=f32)
    grad_output = jnp.einsum("dt,te->de", attended_t, grad_branch, preferred_element_type=f32)

    dqt, dkvt = attn_bwd(bounds, table, span, qt, kv_all, ot, lse, gt)

    dkv = dkvt.reshape(2, S2, PLANES, 2 * QW, T)
    dkv = dkv[0].astype(f32) + over_cores(dkv[1]).astype(f32)
    low_dkv = dkv.astype(bf)
    dkv = sum([over_sides(low_dkv[k], -k).astype(f32) for k in range(1, S2)], dkv[0])
    dk_t, dv_t = dkv[:, :QW], dkv[:, QW:]
    unrotated = [
        rotate_rows(part.reshape(PLANES, HP, HEAD_DIM, T), cos, -sin).astype(bf) for part in (dqt, dk_t)
    ] + [dv_t.reshape(PLANES, HP, HEAD_DIM, T).astype(bf)]
    grad_mixed = jnp.concatenate(unrotated, axis=1).reshape(PLANES, 3 * QW, T)
    grad_first_part = jnp.einsum("bdt,ed->bte", grad_mixed, joint, preferred_element_type=f32)
    low_part = grad_first_part.astype(bf)
    grad_first = sum(
        [over_planes(low_part[k], -k).astype(f32) for k in range(1, PLANES)], grad_first_part[0]
    )
    grad_joint = jnp.einsum("bte,bdt->ed", first, grad_mixed, preferred_element_type=f32)
    _, first_pull = jax.vjp(layer_norm, x, gain_one)
    grad_norm, grad_gain_one = first_pull(grad_first)
    input_grad = (grad_hidden + grad_norm).astype(bf)

    blocks = T // BLOCK
    piece = BLOCK // n
    cut = jnp.transpose(input_grad.reshape(blocks, n, piece, D), (1, 0, 2, 3))
    spread = lax.all_to_all(cut, "ctx", 0, 0).reshape(n * blocks, piece, D)
    slots = (deal[0][:, None] == jnp.arange(n * blocks, dtype=jnp.int32)[None]).astype(bf)
    chosen = jnp.einsum("sb,bpd->spd", slots, spread, preferred_element_type=f32).astype(bf)
    chosen = chosen.reshape(n, blocks, piece, D)
    dealt = jnp.transpose(lax.all_to_all(chosen, "ctx", 0, 0), (1, 0, 2, 3)).reshape(1, T, D)

    def to_sides(x):
        x = x.reshape(PLANES, S2, 2, x.shape[0] // n, x.shape[1])
        kept = lax.dynamic_index_in_dim(x, core, 2, keepdims=False)
        sent = lax.dynamic_index_in_dim(x, 1 - core, 2, keepdims=False).astype(bf)
        x = jnp.moveaxis(kept.astype(f32) + over_cores(sent).astype(f32), 1, 0)
        rolled = turned(x, s2)
        low = rolled.astype(bf)
        return sum([over_sides(low[k], k).astype(f32) for k in range(1, S2)], rolled[0])

    def over_fsdp(x):
        low = x.astype(bf)
        return sum([over_groups(low, k).astype(f32) for k in range(1, groups)], low.astype(f32))

    def to_shard(x):
        x = to_sides(x)
        rolled = turned(x, plane)
        low = rolled.astype(bf)
        x = sum([over_planes(low[k], k).astype(f32) for k in range(1, PLANES)], rolled[0])
        return over_fsdp(x)

    shard_contract, shard_expand, shard_output = to_shard(grad_contract), to_shard(grad_expand), to_shard(grad_output)

    own_joint = to_sides(grad_joint)
    rolled = turned(own_joint, plane).astype(bf)
    cols = [rolled[0]] + [over_planes(rolled[k], k) for k in range(1, PLANES)]
    cols = turned(jnp.stack(cols[::-1]), PLANES - 1 - plane)
    rows = cols.shape[1]
    cols = jnp.transpose(cols.reshape(PLANES, rows, 3, QW), (1, 2, 0, 3)).reshape(rows, 3 * PLANES * QW)
    shard_joint = over_fsdp(cols)

    gain_grads = lax.psum(jnp.stack([grad_gain_one, grad_gain_two]), ("ctx", "fsdp"))
    width = D // n
    gain_grads = lax.dynamic_slice_in_dim(gain_grads, me * width, width, axis=1)
    return (
        output[None],
        dealt,
        shard_joint,
        shard_output,
        shard_expand,
        shard_contract,
        gain_grads[0],
        gain_grads[1],
    )


def solution(mesh):
    return jax.shard_map(
        functools.partial(on_device, mesh.shape["ctx"], mesh.shape["fsdp"]),
        mesh=mesh,
        in_specs=(
            P("fsdp", "ctx", None),
            P("fsdp", "ctx", None),
            P("fsdp", None),
            P("fsdp", None),
            P("fsdp", None),
            P("fsdp", None),
            P("fsdp", None),
            P("fsdp", None),
            P("fsdp"),
            P("fsdp"),
        ),
        out_specs=(
            P("fsdp", "ctx", None),
            P("fsdp", "ctx", None),
            P("ctx", None),
            P("ctx", None),
            P("ctx", None),
            P("ctx", None),
            P("ctx"),
            P("ctx"),
        ),
        check_vma=False,
    )
```

```python
import functools

import jax
import jax.numpy as jnp
from jax import lax
from jax.experimental import pallas as pl
from jax.experimental.pallas import tpu as pltpu
from jax.sharding import PartitionSpec as P

FF = 1152
HEADS = 12
HEAD_DIM = 64
BLOCK = 128
PLANES = 4
HD = HEAD_DIM
HALF = HEAD_DIM // 2
HP = HEADS // PLANES
QW = HP * HEAD_DIM
rope_base = 160000.0
norm_eps = 1e-05
MASKED = -1e30


def head_rows(x, head, pad_to=None):
    rows=lax.broadcasted_iota(jnp.int32,x.shape,0)
    return jnp.where((rows>=head*HD)&(rows<(head+1)*HD),x,jnp.zeros_like(x))

def fwd_kernel(bounds_ref, table_ref, span_ref, qt_ref, kvt_ref, ot_ref, lowt_ref, lse_ref, keys, acc):
    units, _, T = kvt_ref.shape
    def flip(u,_):
        keys[u]=kvt_ref[u,:QW,:].T
        return 0
    lax.fori_loop(0,units,flip,0)
    def one_query_block(b,_):
        qt=qt_ref[b]
        qheads=[head_rows(qt,h) for h in range(HP)]
        q_start=span_ref[b,0:1,:]; q_end=span_ref[b,1:2,:]
        acc[...]=jnp.zeros_like(acc)
        def one_unit(u,carry):
            m,l=carry
            pos=table_ref[u]
            k=keys[pos]
            at=u*T+lax.broadcasted_iota(jnp.int32,(T,T),0)
            allowed=(at>=q_start)&(at<q_end)
            ms=[];ls=[]
            for h in range(HP):
                st=jnp.dot(k,qheads[h],preferred_element_type=jnp.float32)
                st=jnp.where(allowed,st,MASKED)
                mn=jnp.maximum(m[h],jnp.max(st,axis=0,keepdims=True))
                p=jnp.exp(st-mn)
                a=jnp.exp(m[h]-mn)
                ls.append(l[h]*a+jnp.sum(p,axis=0,keepdims=True))
                ms.append(mn)
                rows=pl.ds(h*HD,HD)
                acc[rows,:]=acc[rows,:]*a+jnp.dot(kvt_ref[pos,pl.ds(QW+h*HD,HD),:],p.astype(jnp.bfloat16),preferred_element_type=jnp.float32)
            return tuple(ms),tuple(ls)
        init=(tuple(jnp.full((1,T),MASKED,jnp.float32) for _ in range(HP)),tuple(jnp.zeros((1,T),jnp.float32) for _ in range(HP)))
        m,l=lax.fori_loop(bounds_ref[b,0],bounds_ref[b,1],one_unit,init)
        for h in range(HP):
            rows=pl.ds(h*HD,HD)
            o=acc[rows,:]/l[h]
            ot_ref[b,rows,:]=o
            lowt_ref[b,rows,:]=o.astype(jnp.bfloat16)
            lse_ref[b,h:h+1,:]=m[h]+jnp.log(l[h])
        return 0
    lax.fori_loop(0,qt_ref.shape[0],one_query_block,0)

def attn_fwd(bounds,table,span,qt,kvt):
    B,_,T=qt.shape; U=kvt.shape[0]
    sm=pl.BlockSpec(memory_space=pltpu.SMEM); vm=pl.BlockSpec(memory_space=pltpu.VMEM)
    return pl.pallas_call(fwd_kernel,
        out_shape=(jax.ShapeDtypeStruct((B,QW,T),jnp.float32),jax.ShapeDtypeStruct((B,QW,T),jnp.bfloat16),jax.ShapeDtypeStruct((B,8,T),jnp.float32)),
        in_specs=[sm,sm,vm,vm,vm],out_specs=(vm,vm,vm),
        scratch_shapes=[pltpu.VMEM((U,T,QW),jnp.bfloat16),pltpu.VMEM((QW,T),jnp.float32)],
        compiler_params=pltpu.CompilerParams(vmem_limit_bytes=50<<20))(bounds,table,span,qt,kvt)

def bwd_kernel(bounds_ref, table_ref, span_ref, qt_ref, kvt_ref, ot_ref, lse_ref, gt_ref, dqt_ref, dkvt_ref, kv, dk, dv, dq):
    units, _, T = kvt_ref.shape
    def flip(u,_):
        kv[u]=kvt_ref[u].T
        dk[u]=jnp.zeros_like(dk[u]); dv[u]=jnp.zeros_like(dv[u])
        return 0
    lax.fori_loop(0,units,flip,0)
    def one_query_block(b,_):
        qt=qt_ref[b]; gt=gt_ref[b]
        zero=jnp.zeros((HD,T),jnp.bfloat16)
        qheads=[head_rows(qt,h) for h in range(HP)]
        gheads=[head_rows(gt,h) for h in range(HP)]
        q=[x.T for x in qheads]; g=[x.T for x in gheads]
        q_start=span_ref[b,0:1,:]; q_end=span_ref[b,1:2,:]
        prod=gt.astype(jnp.float32)*ot_ref[b]
        delta=[jnp.sum(prod[h*HD:(h+1)*HD],axis=0,keepdims=True) for h in range(HP)]
        lse=[lse_ref[b,h:h+1,:] for h in range(HP)]
        dq[...]=jnp.zeros_like(dq)
        gpad=[jnp.concatenate([zero,x],axis=0) for x in gheads]
        def one_unit(u,_):
            pos=table_ref[u]
            k=kv[pos,:,:QW]; v=kv[pos,:,128:]
            at=u*T+lax.broadcasted_iota(jnp.int32,(T,T),0)
            allowed=(at>=q_start)&(at<q_end)
            dkt=None
            for h in range(HP):
                st=jnp.dot(k,qheads[h],preferred_element_type=jnp.float32)
                p=jnp.exp(jnp.where(allowed,st-lse[h],MASKED))
                dp=jnp.dot(v,gpad[h],preferred_element_type=jnp.float32)
                ds=(p*(dp-delta[h])).astype(jnp.bfloat16)
                pv=jnp.dot(p.astype(jnp.bfloat16),g[h],preferred_element_type=jnp.float32)
                pk=jnp.dot(ds,q[h],preferred_element_type=jnp.float32)
                dvt=pv if h==0 else dvt+pv
                dkt=pk if h==0 else dkt+pk
                rows=pl.ds(h*HD,HD)
                dq[rows,:]+=jnp.dot(kvt_ref[pos,rows,:],ds,preferred_element_type=jnp.float32)
            dk[pos]+=dkt; dv[pos]+=dvt
            return 0
        lax.fori_loop(bounds_ref[b,0],bounds_ref[b,1],one_unit,0)
        dqt_ref[b]=dq[...]*(HD**-0.5)
        return 0
    lax.fori_loop(0,qt_ref.shape[0],one_query_block,0)
    def out(u,_):
        dkvt_ref[u,:QW,:]=dk[u].T.astype(jnp.bfloat16)
        dkvt_ref[u,QW:,:]=dv[u].T.astype(jnp.bfloat16)
        return 0
    lax.fori_loop(0,units,out,0)

def attn_bwd(bounds,table,span,qt,kvt,ot,lse,gt):
    B,_,T=qt.shape; U=kvt.shape[0]
    sm=pl.BlockSpec(memory_space=pltpu.SMEM); vm=pl.BlockSpec(memory_space=pltpu.VMEM)
    return pl.pallas_call(bwd_kernel,
        out_shape=(jax.ShapeDtypeStruct((B,QW,T),jnp.float32),jax.ShapeDtypeStruct((U,2*QW,T),jnp.bfloat16)),
        in_specs=[sm,sm]+[vm]*6,out_specs=(vm,vm),
        scratch_shapes=[pltpu.VMEM((U,T,2*QW),jnp.bfloat16),pltpu.VMEM((U,T,QW),jnp.float32),pltpu.VMEM((U,T,QW),jnp.float32),pltpu.VMEM((QW,T),jnp.float32)],
        compiler_params=pltpu.CompilerParams(vmem_limit_bytes=60<<20))(bounds,table,span,qt,kvt,ot,lse,gt)


def tail_kernel(
    n,
    groups,
    deal_ref,
    dq_ref,
    dkv_ref,
    cos_ref,
    sin_ref,
    joint_hbm,
    joint_t_hbm,
    first_hbm,
    tokens_hbm,
    grad_hidden_hbm,
    gain_ref,
    packed_hbm,
    dealt_ref,
    shard_ref,
    joint_out_ref,
    joint,
    joint_t,
    first,
    tokens,
    grad_hidden,
    w_own,
    local_sems,
    kv_near,
    kv_send,
    kv_far,
    kv_sems,
    mixed,
    z_send,
    z_got,
    z_sems,
    jg_t,
    jg,
    j_core,
    j_side,
    j_plane,
    j_group,
    j_sems,
    w_core,
    w_y1,
    w_x1,
    w_x2,
    w_y2,
    w_plane,
    w_z,
    w_all,
    w_sems,
    d_send,
    d_mid,
    d_back,
    d_got,
    d_sems,
):
    bf, f32 = jnp.bfloat16, jnp.float32
    S = n // PLANES
    S2 = S // 2
    T, D = tokens.shape
    me, group = lax.axis_index("ctx"), lax.axis_index("fsdp")
    plane, side = me // S, lax.rem(me, S)
    s2, core = side // 2, lax.rem(side, 2)

    def at(p, a, c, g):
        return (p * S + a * 2 + c, g)

    def plane_peer(k):
        return at(lax.rem(plane + k, PLANES), s2, core, group)

    def side_peer(k):
        return at(plane, lax.rem(s2 + k, S2), core, group)

    def group_peer(k):
        return at(plane, s2, core, lax.rem(group + k, groups))

    core_peer = at(plane, s2, 1 - core, group)

    def remote(source, target, sems, index, device):
        return pltpu.make_async_remote_copy(
            src_ref=source,
            dst_ref=target,
            send_sem=sems.at[0, index],
            recv_sem=sems.at[1, index],
            device_id=device,
            device_id_type=pl.DeviceIdType.MESH,
        )

    barrier = pltpu.get_barrier_semaphore()

    def greet(k, carry):
        pl.semaphore_signal(
            barrier, inc=1, device_id=(lax.rem(me + k, n), group), device_id_type=pl.DeviceIdType.MESH
        )
        return carry

    lax.fori_loop(1, n, greet, 0)
    for k in range(1, groups):
        pl.semaphore_signal(barrier, inc=1, device_id=group_peer(k), device_id_type=pl.DeviceIdType.MESH)
    pl.semaphore_wait(barrier, n - 1 + groups - 1)

    order = [*range(1, PLANES), 0]
    core_kv = [remote(dkv_ref.at[1, :, j], kv_near.at[j], kv_sems, j, core_peer) for j in range(PLANES)]
    for j in order:
        core_kv[j].start()
    local = [
        pltpu.make_async_copy(source, target, local_sems.at[i])
        for i, (source, target) in enumerate(
            [
                (joint_t_hbm, joint_t),
                (first_hbm, first),
                (joint_hbm, joint),
                (packed_hbm.at[:, :, core], w_own),
                (tokens_hbm, tokens),
                (grad_hidden_hbm, grad_hidden),
            ]
        )
    ]
    for copy in local:
        copy.start()
    half = PLANES // 2
    core_w = [
        remote(
            packed_hbm.at[pl.ds(i * half, half), :, 1 - core],
            w_core.at[pl.ds(i * half, half)],
            w_sems,
            i,
            core_peer,
        )
        for i in range(2)
    ]
    for copy in core_w:
        copy.start()

    side_kv = {}
    for j in order:
        core_kv[j].wait()
        for k in range(S2):
            total = dkv_ref[0, k, j].astype(f32) + kv_near[j, k].astype(f32)
            kv_send[j, k] = total.astype(bf)
        for k in range(1, S2):
            side_kv[j, k] = remote(
                kv_send.at[j, k],
                kv_far.at[j, k - 1],
                kv_sems,
                PLANES + j * (S2 - 1) + k - 1,
                side_peer(S2 - k),
            )
            side_kv[j, k].start()

    local[3].wait()
    w_moves = []

    def w_copy(source, target, device):
        copy = remote(source, target, w_sems, 2 + len(w_moves), device)
        w_moves.append(copy)
        copy.start()
        return copy

    def add_core(i):
        core_w[i].wait()

        def body(step, carry):
            p, a, g = i * half + step // (S2 * groups), lax.rem(step // groups, S2), lax.rem(step, groups)
            w_core[p, a, g] = (w_own[p, a, g].astype(f32) + w_core[p, a, g].astype(f32)).astype(bf)
            return carry

        lax.fori_loop(0, half * S2 * groups, body, 0)

    add_core(0)
    y1 = [
        w_copy(w_core.at[pl.ds(0, half), :, lax.rem(group + k, groups)], w_y1.at[k - 1], group_peer(k))
        for k in range(1, groups)
    ]
    add_core(1)
    x2 = [
        w_copy(w_core.at[pl.ds(half, half), lax.rem(s2 + k, S2)], w_x2.at[k - 1], side_peer(k))
        for k in range(1, S2)
    ]

    plane_parts = {}
    local[0].wait()
    for j in order:
        dk = kv_send[j, 0].astype(f32)
        for k in range(1, S2):
            side_kv[j, k].wait()
            dk = dk + kv_far[j, k - 1].astype(f32)
        cos, sin = cos_ref[j], sin_ref[j]
        rows = []
        for part in (dq_ref[j], dk[:QW]):
            for h in range(HP):
                upper, lower = part[h * HD : h * HD + HALF], part[h * HD + HALF : (h + 1) * HD]
                rows += [upper * cos + lower * sin, lower * cos - upper * sin]
        rows += [dk[QW:], jnp.zeros((mixed.shape[1] - 3 * QW, T), f32)]
        turned = jnp.concatenate(rows, axis=0)
        mixed[j] = turned.astype(bf)
        part = jnp.dot(turned.T.astype(bf), joint_t[...], preferred_element_type=f32)
        z_send[j] = part.astype(bf)
        if j:
            plane_parts[j] = remote(z_send.at[j], z_got.at[j - 1], z_sems, j - 1, plane_peer(PLANES - j))
            plane_parts[j].start()

    local[1].wait()
    jg_t[...] = jnp.dot(mixed[0], first[0], preferred_element_type=f32)
    for j in range(1, PLANES):
        jg_t[...] += jnp.dot(mixed[j], first[j], preferred_element_type=f32)
    local[2].wait()
    width = jg_t.shape[0]
    shard_rows = jg.shape[3]
    per = 128
    for i in range(D // per):
        block = jg_t[:, i * per : (i + 1) * per].T
        gain_part = jnp.sum(block * joint[i * per : (i + 1) * per, :].astype(f32), axis=1, keepdims=True)
        whole = jnp.concatenate([block, jnp.broadcast_to(gain_part, (per, per))], axis=1).astype(bf)
        j_rows = whole.astype(f32)
        first_row = i * per
        row = first_row
        while row < first_row + per:
            shard, offset = divmod(row, shard_rows)
            count = min(shard_rows - offset, first_row + per - row)
            jg[shard // S, shard % S // 2, shard % 2, offset : offset + count] = j_rows[
                row - first_row : row - first_row + count
            ].astype(bf)
            row += count
    j_moves = []

    def j_copy(source, target, device):
        copy = remote(source, target, j_sems, len(j_moves), device)
        j_moves.append(copy)
        copy.start()
        return copy

    j_first = j_copy(jg.at[:, :, 1 - core], j_core, core_peer)

    def sum_into(target, terms):
        total = terms[0].astype(f32)
        for term in terms[1:]:
            total = total + term.astype(f32)
        return total.astype(target)

    for copy in y1:
        copy.wait()
    for p in range(half):
        for a in range(S2):
            w_y1[0, p, a] = sum_into(bf, [w_core[p, a, group]] + [w_y1[k, p, a] for k in range(groups - 1)])
    x1 = [w_copy(w_y1.at[0, :, lax.rem(s2 + k, S2)], w_x1.at[k - 1], side_peer(k)) for k in range(1, S2)]
    for copy in x2:
        copy.wait()
    for p in range(half):
        for g in range(groups):
            w_x2[0, p, g] = sum_into(bf, [w_core[half + p, s2, g]] + [w_x2[k, p, g] for k in range(S2 - 1)])
    y2 = [w_copy(w_x2.at[0, :, lax.rem(group + k, groups)], w_y2.at[k - 1], group_peer(k)) for k in range(1, groups)]

    j_first.wait()
    for p in range(PLANES):
        for a in range(S2):
            j_core[p, a] = sum_into(bf, [jg[p, a, core], j_core[p, a]])
    j_second = [j_copy(j_core.at[:, lax.rem(s2 + k, S2)], j_side.at[k - 1], side_peer(k)) for k in range(1, S2)]

    local[4].wait()
    local[5].wait()
    for j in range(1, PLANES):
        plane_parts[j].wait()
    strip = 64

    def norm_back(i, carry):
        rows = pl.ds(pl.multiple_of(i * strip, strip), strip)
        grad = z_send[0, rows].astype(f32)
        for j in range(1, PLANES):
            grad = grad + z_got[j - 1, rows].astype(f32)
        values = tokens[rows].astype(f32)
        centred = values - jnp.mean(values, axis=-1, keepdims=True)
        scale = lax.rsqrt(jnp.mean(centred * centred, axis=-1, keepdims=True) + norm_eps)
        normal = centred * scale
        grad = grad * gain_ref[...]
        grad = grad - jnp.mean(grad, axis=-1, keepdims=True) - normal * jnp.mean(grad * normal, axis=-1, keepdims=True)
        grad_hidden[rows] = grad_hidden[rows] + grad * scale
        return carry

    lax.fori_loop(0, T // strip, norm_back, 0)

    blocks = T // BLOCK
    piece = BLOCK // n

    def d_copy(source, target, base, k):
        return remote(source.at[lax.rem(me + k, n)], target.at[me], d_sems, base + k, (lax.rem(me + k, n), group))

    for i in range(n):
        d_send[i] = jnp.concatenate(
            [grad_hidden[b * BLOCK + i * piece : b * BLOCK + (i + 1) * piece] for b in range(blocks)], axis=0
        ).astype(bf)
    out_deal = [d_copy(d_send, d_mid, 0, k) for k in range(1, n)]
    for copy in out_deal:
        copy.start()
    d_mid[me] = d_send[me]

    for copy in x1 + y2:
        copy.wait()
    for p in range(half):
        w_plane[p] = sum_into(bf, [w_y1[0, p, s2]] + [w_x1[k, p] for k in range(S2 - 1)])
        w_plane[half + p] = sum_into(bf, [w_x2[0, p, group]] + [w_y2[k, p] for k in range(groups - 1)])
    w_last = [w_copy(w_plane.at[lax.rem(plane + k, PLANES)], w_z.at[k - 1], plane_peer(k)) for k in range(1, PLANES)]
    for copy in j_second:
        copy.wait()
    for p in range(PLANES):
        j_side[0, p] = sum_into(bf, [j_core[p, s2]] + [j_side[k, p] for k in range(S2 - 1)])
    j_third = [j_copy(j_side.at[0, lax.rem(plane + k, PLANES)], j_plane.at[plane], plane_peer(k)) for k in range(1, PLANES)]
    j_plane[plane] = j_side[0, plane]

    for copy in out_deal:
        copy.wait()
    for i in range(n):
        chosen = []
        for b in range(blocks):
            wanted = deal_ref[i * blocks + b]
            held = d_mid[wanted // blocks].astype(f32)
            part = held[:piece]
            for other in range(1, blocks):
                part = jnp.where(lax.rem(wanted, blocks) == other, held[other * piece : (other + 1) * piece], part)
            chosen.append(part)
        d_back[i] = jnp.concatenate(chosen, axis=0).astype(bf)
    back_deal = [d_copy(d_back, d_got, n, k) for k in range(1, n)]
    for copy in back_deal:
        copy.start()
    d_got[me] = d_back[me]

    for copy in w_last:
        copy.wait()
    w_all[group] = sum_into(bf, [w_plane[plane]] + [w_z[k] for k in range(PLANES - 1)])
    w_gather = [w_copy(w_all.at[group], w_all.at[group], group_peer(k)) for k in range(1, groups)]
    for copy in j_third:
        copy.wait()
    j_group[group] = j_plane[...]
    j_last = [j_copy(j_plane, j_group.at[group], group_peer(k)) for k in range(1, groups)]

    for copy in back_deal:
        copy.wait()
    for b in range(blocks):
        for i in range(0, n, 2):
            rows = [d_got[i + e].astype(f32)[b * piece : (b + 1) * piece] for e in range(2)]
            dealt_ref[b * BLOCK + i * piece : b * BLOCK + (i + 2) * piece] = jnp.concatenate(rows, axis=0).astype(bf)
    for copy in w_gather:
        copy.wait()
    for g in range(groups):
        shard_ref[g] = w_all[g].astype(f32)
    for copy in j_last:
        copy.wait()
    for p in range(PLANES):
        total = j_group[0, p].astype(f32)
        for g in range(1, groups):
            total = total + j_group[g, p].astype(f32)
        joint_out_ref[p] = total


def tail(n, groups, deal, dqt, dkv, cos, sin, joint, joint_t, first, tokens, grad_hidden, gain, packed):
    bf, f32 = jnp.bfloat16, jnp.float32
    S2 = n // PLANES // 2
    T, D = tokens.shape
    width = joint.shape[1]
    wide = width + 128
    rows = D // n
    part = packed.shape[4]
    piece_rows = T // n
    half = PLANES // 2
    any_, vm, sm = (pl.BlockSpec(memory_space=m) for m in (pl.ANY, pltpu.VMEM, pltpu.SMEM))
    sems = lambda count: pltpu.SemaphoreType.DMA((2, count))
    return pl.pallas_call(
        functools.partial(tail_kernel, n, groups),
        out_shape=(
            jax.ShapeDtypeStruct((T, D), bf),
            jax.ShapeDtypeStruct((groups, part, D), f32),
            jax.ShapeDtypeStruct((PLANES, rows, wide), f32),
        ),
        in_specs=[sm, vm, vm, vm, vm, any_, any_, any_, any_, any_, vm, any_],
        out_specs=(vm, vm, vm),
        scratch_shapes=[
            pltpu.VMEM((D, width), bf),
            pltpu.VMEM((width, D), bf),
            pltpu.VMEM((PLANES, T, D), bf),
            pltpu.VMEM((T, D), bf),
            pltpu.VMEM((T, D), f32),
            pltpu.VMEM((PLANES, S2, groups, part, D), bf),
            pltpu.SemaphoreType.DMA((6,)),
            pltpu.VMEM((PLANES, S2, 2 * QW, T), bf),
            pltpu.VMEM((PLANES, S2, 2 * QW, T), bf),
            pltpu.VMEM((PLANES, S2 - 1, 2 * QW, T), bf),
            sems(PLANES * S2),
            pltpu.VMEM((PLANES, width, T), bf),
            pltpu.VMEM((PLANES, T, D), bf),
            pltpu.VMEM((PLANES - 1, T, D), bf),
            sems(PLANES - 1),
            pltpu.VMEM((width, D), f32),
            pltpu.VMEM((PLANES, S2, 2, rows, wide), bf),
            pltpu.VMEM((PLANES, S2, rows, wide), bf),
            pltpu.VMEM((S2 - 1, PLANES, rows, wide), bf),
            pltpu.VMEM((PLANES, rows, wide), bf),
            pltpu.VMEM((groups, PLANES, rows, wide), bf),
            sems(S2 + PLANES + groups - 2),
            pltpu.VMEM((PLANES, S2, groups, part, D), bf),
            pltpu.VMEM((groups - 1, half, S2, part, D), bf),
            pltpu.VMEM((S2 - 1, half, part, D), bf),
            pltpu.VMEM((S2 - 1, half, groups, part, D), bf),
            pltpu.VMEM((groups - 1, half, part, D), bf),
            pltpu.VMEM((PLANES, part, D), bf),
            pltpu.VMEM((PLANES - 1, part, D), bf),
            pltpu.VMEM((groups, part, D), bf),
            sems(2 + 3 * (groups - 1) + 2 * (S2 - 1) + PLANES - 1),
            pltpu.VMEM((n, piece_rows, D), bf),
            pltpu.VMEM((n, piece_rows, D), bf),
            pltpu.VMEM((n, piece_rows, D), bf),
            pltpu.VMEM((n, piece_rows, D), bf),
            sems(2 * n),
        ],
        compiler_params=pltpu.CompilerParams(collective_id=0, has_side_effects=True, vmem_limit_bytes=60 << 20),
    )(deal, dqt, dkv, cos, sin, joint, joint_t, first, tokens, grad_hidden, gain, packed)


def layer_norm(values, weights):
    centred = values - jnp.mean(values, axis=-1, keepdims=True)
    spread = jnp.mean(centred * centred, axis=-1, keepdims=True)
    return centred * lax.rsqrt(spread + norm_eps) * weights


def rotate_rows(values, cos, sin):
    upper, lower = values[..., :HALF, :], values[..., HALF:, :]
    return jnp.concatenate([upper * cos - lower * sin, lower * cos + upper * sin], axis=-2)


def on_device(
    n,
    groups,
    tokens,
    cotangent,
    lengths,
    deal,
    joint_projection,
    output_projection,
    expand_weight,
    contract_weight,
    gain_first,
    gain_second,
):
    bf, f32 = jnp.bfloat16, jnp.float32
    T, D = tokens.shape[1:]
    S = n // PLANES
    S2 = S // 2
    units = n
    me, gy = lax.axis_index("ctx"), lax.axis_index("fsdp")
    plane, side = me // S, me % S
    s2, core = side // 2, side % 2

    def over_planes(x, k):
        return lax.ppermute(x, "ctx", [(h * S + s, (h + k) % PLANES * S + s) for h in range(PLANES) for s in range(S)])

    def over_sides(x, k):
        return lax.ppermute(
            x,
            "ctx",
            [(h * S + a * 2 + c, h * S + (a + k) % S2 * 2 + c) for h in range(PLANES) for a in range(S2) for c in range(2)],
        )

    def over_cores(x):
        return lax.ppermute(x, "ctx", [(i, i ^ 1) for i in range(n)])

    def over_groups(x, k):
        return lax.ppermute(x, "fsdp", [(f, (f + k) % groups) for f in range(groups)])

    def pick(x, index):
        return lax.dynamic_index_in_dim(x, index, 0, keepdims=False)

    def turned(x, shift):
        return lax.dynamic_slice_in_dim(jnp.concatenate([x, x], axis=0), shift, x.shape[0], 0)

    def whole_of(shard):
        parts = [shard] + [over_groups(shard, k) for k in range(1, groups)]
        return turned(jnp.stack(parts[::-1]), groups - 1 - gy).reshape(-1, *shard.shape[1:])

    def whole_by_cores(shard):
        half = shard.shape[0] // 2
        halves = shard.reshape(2, half, *shard.shape[1:])
        mine = pick(halves, core)
        got = jnp.stack([over_groups(mine, k) for k in range(1, groups)])
        other = over_cores(got)
        low = jnp.where(core == 0, got, other)
        high = jnp.where(core == 0, other, got)
        parts = jnp.concatenate([jnp.stack([low, high], axis=1)[::-1], halves[None]], axis=0)
        return turned(parts, groups - 1 - gy).reshape(-1, *shard.shape[1:])

    tokens_own = tokens[0]
    all_tokens = jnp.stack([tokens_own] + [over_planes(tokens_own, k) for k in range(1, PLANES)])
    joint_cols = lax.dynamic_index_in_dim(
        joint_projection.reshape(-1, 3, PLANES, QW), plane, 2, keepdims=False
    ).reshape(-1, 3 * QW)
    joint = whole_of(joint_cols)
    gains = whole_of(jnp.stack([gain_first, gain_second], axis=1))
    gain_one, gain_two = gains[:, 0].astype(f32), gains[:, 1].astype(f32)
    out_w = whole_by_cores(output_projection)
    exp_w = whole_by_cores(expand_weight)
    con_w = whole_by_cores(contract_weight)

    lens = lengths[0]
    ends, total = [], jnp.int32(0)
    for j in range(lens.shape[0]):
        total = total + lens[j]
        ends.append(total)
    rel_plane = (plane - jnp.arange(PLANES)) % PLANES
    first_token = (rel_plane * S + side) * T
    natural = first_token[:, None] + jnp.arange(T, dtype=jnp.int32)[None]

    def span_of(index):
        begin, end = jnp.zeros_like(index), jnp.full_like(index, ends[0])
        for j in range(1, lens.shape[0]):
            after = index >= ends[j - 1]
            begin = jnp.where(after, ends[j - 1], begin)
            end = jnp.where(after, ends[j], end)
        return begin, end

    begin, end = span_of(natural)
    span = jnp.stack([begin, end] + [jnp.zeros_like(begin)] * 6, axis=1)
    low_bound, _ = span_of(first_token)
    _, high_bound = span_of(first_token + T - 1)
    bounds = jnp.stack([low_bound // T, (high_bound + T - 1) // T], axis=1).astype(jnp.int32)
    unit = jnp.arange(units, dtype=jnp.int32)
    u_plane, u_side = unit // S, unit % S
    u_s2, u_core = u_side // 2, u_side % 2
    table = ((u_core != core) * S2 + (s2 - u_s2) % S2) * PLANES + (plane - u_plane) % PLANES
    table = table.astype(jnp.int32)
    frequencies = rope_base ** (-jnp.arange(0, HEAD_DIM, 2).astype(f32) / HEAD_DIM)
    angles = (natural - begin).astype(f32)[:, None, :] * frequencies[None, :, None]
    cos, sin = jnp.cos(angles)[:, None], jnp.sin(angles)[:, None]

    x_all = all_tokens.astype(f32)
    first = layer_norm(x_all, gain_one).astype(bf)
    mixed = jnp.einsum("bte,ed->bdt", first, joint, preferred_element_type=f32)
    mixed = mixed.reshape(PLANES, 3, HP, HEAD_DIM, T)
    qt = (rotate_rows(mixed[:, 0], cos, sin).astype(bf) * bf(HEAD_DIM**-0.5)).reshape(PLANES, QW, T)
    kt = rotate_rows(mixed[:, 1], cos, sin).astype(bf).reshape(PLANES, QW, T)
    vt = mixed[:, 2].astype(bf).reshape(PLANES, QW, T)
    kv = jnp.concatenate([kt, vt], axis=1)
    near = jnp.stack([kv] + [over_sides(kv, k) for k in range(1, S2)])
    kv_all = jnp.concatenate([near[None], over_cores(near)[None]], axis=0).reshape(units, 2 * QW, T)

    ot, lowt, lse = attn_fwd(bounds, table, span, qt, kv_all)

    parts = [lowt[0]] + [over_planes(lowt[k], -k) for k in range(1, PLANES)]
    attended_t = turned(jnp.stack(parts), (PLANES - plane) % PLANES).reshape(D, T)

    x = tokens_own.astype(f32)
    grad_out = cotangent[0]
    hidden = x + jnp.einsum("dt,de->te", attended_t, out_w, preferred_element_type=f32)
    second = layer_norm(hidden, gain_two).astype(bf)
    expanded = jnp.dot(second, exp_w, preferred_element_type=f32)

    def gated(values):
        return jax.nn.gelu(values[:, :FF], approximate=False) * values[:, FF:]

    activated_f, gated_pull = jax.vjp(gated, expanded)
    activated = activated_f.astype(bf)
    output = (hidden + jnp.dot(activated, con_w, preferred_element_type=f32)).astype(bf)

    grad_activated = jnp.einsum("td,fd->tf", grad_out, con_w, preferred_element_type=f32)
    grad_expanded = gated_pull(grad_activated)[0].astype(bf)
    grad_second = jnp.einsum("tf,df->td", grad_expanded, exp_w, preferred_element_type=f32)
    _, second_pull = jax.vjp(layer_norm, hidden, gain_two)
    grad_hidden_norm, grad_gain_two = second_pull(grad_second)
    grad_hidden = grad_out.astype(f32) + grad_hidden_norm
    grad_branch = grad_hidden.astype(bf)
    grad_attended = jnp.einsum("de,te->dt", out_w, grad_branch, preferred_element_type=f32).astype(bf)
    rel = turned(grad_attended.reshape(PLANES, QW, T), plane)
    gt = jnp.stack([rel[0]] + [over_planes(rel[k], k) for k in range(1, PLANES)])

    grad_contract = jnp.einsum("tf,td->fd", activated, grad_out, preferred_element_type=f32)
    grad_expand = jnp.einsum("td,tf->df", second, grad_expanded, preferred_element_type=f32)
    grad_output = jnp.einsum("dt,te->de", attended_t, grad_branch, preferred_element_type=f32)

    dqt, dkvt = attn_bwd(bounds, table, span, qt, kv_all, ot, lse, gt)

    def sharded(x):
        return x.astype(bf).reshape(n, x.shape[0] // n, x.shape[1])

    gain_rows = jnp.pad(grad_gain_two.reshape(n, 1, D // n), ((0, 0), (0, 7), (0, D - D // n))).astype(bf)
    rows = D // n
    wide = grad_expand.shape[1] // D
    pieces = [sharded(grad_output)]
    pieces += [sharded(grad_expand[:, i * D : (i + 1) * D]) for i in range(wide)]
    pieces += [sharded(grad_contract), gain_rows]
    used = sum(p.shape[1] for p in pieces)
    part = -(-used // (groups * 16)) * 16
    packed = jnp.concatenate(pieces + [jnp.zeros((n, groups * part - used, D), bf)], axis=1)
    packed = packed.reshape(PLANES, S2, 2, groups, part, D)
    joint_pad = jnp.pad(joint, ((0, 0), (0, 64)))

    dealt, shards, joint_raw = tail(
        n,
        groups,
        deal[0],
        dqt,
        dkvt.reshape(2, S2, PLANES, 2 * QW, T),
        cos[:, 0],
        sin[:, 0],
        joint_pad,
        joint_pad.T,
        first,
        tokens_own,
        grad_hidden,
        gain_one[None],
        packed,
    )
    shards = shards.reshape(groups * part, D)
    shard_output = shards[:rows]
    shard_expand = jnp.concatenate([shards[(1 + i) * rows : (2 + i) * rows] for i in range(wide)], axis=1)
    after = (1 + wide) * rows
    ff_rows = grad_contract.shape[0] // n
    shard_contract = shards[after : after + ff_rows]
    shard_gain_two = shards[after + ff_rows, :rows]
    shard_joint = jnp.transpose(joint_raw[:, :, : 3 * QW].reshape(PLANES, rows, 3, QW), (1, 2, 0, 3))
    shard_joint = shard_joint.reshape(rows, 3 * PLANES * QW)
    shard_gain_one = jnp.sum(joint_raw[:, :, -1], axis=0) / lax.dynamic_slice_in_dim(gain_one, me * rows, rows)
    return (
        output[None],
        dealt[None],
        shard_joint,
        shard_output,
        shard_expand,
        shard_contract,
        shard_gain_one,
        shard_gain_two,
    )


def solution(mesh):
    return jax.shard_map(
        functools.partial(on_device, mesh.shape["ctx"], mesh.shape["fsdp"]),
        mesh=mesh,
        in_specs=(
            P("fsdp", "ctx", None),
            P("fsdp", "ctx", None),
            P("fsdp", None),
            P("fsdp", None),
            P("fsdp", None),
            P("fsdp", None),
            P("fsdp", None),
            P("fsdp", None),
            P("fsdp"),
            P("fsdp"),
        ),
        out_specs=(
            P("fsdp", "ctx", None),
            P("fsdp", "ctx", None),
            P("ctx", None),
            P("ctx", None),
            P("ctx", None),
            P("ctx", None),
            P("ctx"),
            P("ctx"),
        ),
        check_vma=False,
    )
```

```python
import functools

import jax
import jax.numpy as jnp
from jax import lax
from jax.experimental import pallas as pl
from jax.experimental.pallas import tpu as pltpu
from jax.sharding import PartitionSpec as P

FF = 1152
HEADS = 12
HEAD_DIM = 64
BLOCK = 128
PLANES = 4
HD = HEAD_DIM
HALF = HEAD_DIM // 2
HP = HEADS // PLANES
QW = HP * HEAD_DIM
rope_base = 160000.0
norm_eps = 1e-05
MASKED = -1e30


def head_rows(x, head):
    rows = lax.broadcasted_iota(jnp.int32, x.shape, 0)
    return jnp.where((rows >= head * HD) & (rows < (head + 1) * HD), x, jnp.zeros_like(x))


def over_units(bounds_ref, b, step):
    low, full_low, full_high, high = (bounds_ref[b, i] for i in range(4))

    def run(begin, end, masked):
        def body(u, carry):
            step(u, masked)
            return carry

        lax.fori_loop(begin, end, body, 0)

    run(low, full_low, True)
    in_pairs(full_low, full_high, lambda u: step(u, False))
    run(full_high, high, True)


def in_pairs(begin, end, step):
    pairs = (end - begin) // 2

    def two(i, carry):
        step(begin + 2 * i)
        step(begin + 2 * i + 1)
        return carry

    def one(u, carry):
        step(u)
        return carry

    lax.fori_loop(0, pairs, two, 0)
    lax.fori_loop(begin + 2 * pairs, end, one, 0)


def fwd_kernel(bounds_ref, table_ref, span_ref, qt_ref, kvt_ref, ot_ref, lowt_ref, lse_ref, keys, scores, top, total, acc):
    units, _, T = kvt_ref.shape

    def flip(u, carry):
        keys[u] = kvt_ref[u, :QW, :].T
        return carry

    lax.fori_loop(0, units, flip, 0, unroll=4)

    def one_query_block(b, carry):
        qt = qt_ref[b]
        qheads = [head_rows(qt, h) for h in range(HP)]
        q_start, q_end = span_ref[b, 0:1, :], span_ref[b, 1:2, :]
        top[...] = jnp.full_like(top, MASKED)
        total[...] = jnp.zeros_like(total)
        acc[...] = jnp.zeros_like(acc)

        def score(u, masked):
            k = keys[table_ref[u]]
            st = [jnp.dot(k, qheads[h], preferred_element_type=jnp.float32) for h in range(HP)]
            if masked:
                at = u * T + lax.broadcasted_iota(jnp.int32, (T, T), 0)
                allowed = (at >= q_start) & (at < q_end)
                st = [jnp.where(allowed, s, MASKED) for s in st]
            for h in range(HP):
                scores[u, h] = st[h]
                top[h] = jnp.maximum(top[h], jnp.max(st[h].reshape(T // 8, 8, T), axis=0))

        over_units(bounds_ref, b, score)
        m = [jnp.max(top[h], axis=0, keepdims=True) for h in range(HP)]

        def gather(u):
            pos = table_ref[u]
            p = [jnp.exp(scores[u, h] - m[h]) for h in range(HP)]
            for h in range(HP):
                total[h] += jnp.sum(p[h].reshape(T // 8, 8, T), axis=0)
                rows = pl.ds(h * HD, HD)
                acc[rows, :] += jnp.dot(
                    kvt_ref[pos, pl.ds(QW + h * HD, HD), :], p[h].astype(jnp.bfloat16), preferred_element_type=jnp.float32
                )

        in_pairs(bounds_ref[b, 0], bounds_ref[b, 3], gather)
        for h in range(HP):
            rows = pl.ds(h * HD, HD)
            l = jnp.sum(total[h], axis=0, keepdims=True)
            o = acc[rows, :] / l
            ot_ref[b, rows, :] = o
            lowt_ref[b, rows, :] = o.astype(jnp.bfloat16)
            lse_ref[b, h : h + 1, :] = m[h] + jnp.log(l)
        return carry

    lax.fori_loop(0, qt_ref.shape[0], one_query_block, 0)


def attn_fwd(bounds, table, span, qt, kvt):
    B, _, T = qt.shape
    U = kvt.shape[0]
    sm, vm = pl.BlockSpec(memory_space=pltpu.SMEM), pl.BlockSpec(memory_space=pltpu.VMEM)
    return pl.pallas_call(
        fwd_kernel,
        out_shape=(
            jax.ShapeDtypeStruct((B, QW, T), jnp.float32),
            jax.ShapeDtypeStruct((B, QW, T), jnp.bfloat16),
            jax.ShapeDtypeStruct((B, 8, T), jnp.float32),
        ),
        in_specs=[sm, sm, vm, vm, vm],
        out_specs=(vm, vm, vm),
        scratch_shapes=[
            pltpu.VMEM((U, T, QW), jnp.bfloat16),
            pltpu.VMEM((U, HP, T, T), jnp.float32),
            pltpu.VMEM((HP, 8, T), jnp.float32),
            pltpu.VMEM((HP, 8, T), jnp.float32),
            pltpu.VMEM((QW, T), jnp.float32),
        ],
        compiler_params=pltpu.CompilerParams(vmem_limit_bytes=60 << 20),
    )(bounds, table, span, qt, kvt)


def bwd_kernel(
    bounds_ref, table_ref, span_ref, qt_ref, kvt_ref, ot_ref, lse_ref, gt_ref, dqt_ref, dkvt_ref, kv, dk, dv, dq
):
    units, _, T = kvt_ref.shape

    def flip(u, carry):
        kv[u] = kvt_ref[u].T
        dk[u] = jnp.zeros_like(dk[u])
        dv[u] = jnp.zeros_like(dv[u])
        return carry

    lax.fori_loop(0, units, flip, 0, unroll=4)

    def one_query_block(b, carry):
        qt, gt = qt_ref[b], gt_ref[b]
        zero = jnp.zeros((HD, T), jnp.bfloat16)
        qheads = [head_rows(qt, h) for h in range(HP)]
        gheads = [head_rows(gt, h) for h in range(HP)]
        gpad = [jnp.concatenate([zero, x], axis=0) for x in gheads]
        q = jnp.concatenate([jnp.concatenate([x, zero], axis=0).T for x in qheads], axis=0)
        g = jnp.concatenate([x.T for x in gpad], axis=0)
        q_start, q_end = span_ref[b, 0:1, :], span_ref[b, 1:2, :]
        prod = gt.astype(jnp.float32) * ot_ref[b]
        delta = [jnp.sum(prod[h * HD : (h + 1) * HD], axis=0, keepdims=True) for h in range(HP)]
        lse = [lse_ref[b, h : h + 1, :] for h in range(HP)]
        dq[...] = jnp.zeros_like(dq)

        def one_unit(u, masked):
            pos = table_ref[u]
            k, v = kv[pos, :, :QW], kv[pos, :, 128:]
            st = [jnp.dot(k, qheads[h], preferred_element_type=jnp.float32) for h in range(HP)]
            dp = [jnp.dot(v, gpad[h], preferred_element_type=jnp.float32) for h in range(HP)]
            st = [st[h] - lse[h] for h in range(HP)]
            if masked:
                at = u * T + lax.broadcasted_iota(jnp.int32, (T, T), 0)
                allowed = (at >= q_start) & (at < q_end)
                st = [jnp.where(allowed, s, MASKED) for s in st]
            p = [jnp.exp(s) for s in st]
            ds = [(p[h] * (dp[h] - delta[h])).astype(jnp.bfloat16) for h in range(HP)]
            p = [x.astype(jnp.bfloat16) for x in p]
            dv[pos] += jnp.dot(jnp.concatenate(p, axis=1), g, preferred_element_type=jnp.float32)
            dk[pos] += jnp.dot(jnp.concatenate(ds, axis=1), q, preferred_element_type=jnp.float32)
            for h in range(HP):
                rows = pl.ds(h * HD, HD)
                dq[rows, :] += jnp.dot(kvt_ref[pos, rows, :], ds[h], preferred_element_type=jnp.float32)

        over_units(bounds_ref, b, one_unit)
        dqt_ref[b] = dq[...] * (HD**-0.5)
        return carry

    lax.fori_loop(0, qt_ref.shape[0], one_query_block, 0)

    def out(u, carry):
        dkvt_ref[u, :, :128] = dk[u, :, :128].astype(jnp.bfloat16)
        dkvt_ref[u, :, 128:256] = (dk[u, :, 128:] + dv[u, :, :128]).astype(jnp.bfloat16)
        dkvt_ref[u, :, 256:] = dv[u, :, 128:].astype(jnp.bfloat16)
        return carry

    lax.fori_loop(0, units, out, 0, unroll=2)


def attn_bwd(bounds, table, span, qt, kvt, ot, lse, gt):
    B, _, T = qt.shape
    U = kvt.shape[0]
    sm, vm = pl.BlockSpec(memory_space=pltpu.SMEM), pl.BlockSpec(memory_space=pltpu.VMEM)
    return pl.pallas_call(
        bwd_kernel,
        out_shape=(jax.ShapeDtypeStruct((B, QW, T), jnp.float32), jax.ShapeDtypeStruct((U, T, 2 * QW), jnp.bfloat16)),
        in_specs=[sm, sm] + [vm] * 6,
        out_specs=(vm, vm),
        scratch_shapes=[
            pltpu.VMEM((U, T, 2 * QW), jnp.bfloat16),
            pltpu.VMEM((U, T, 256), jnp.float32),
            pltpu.VMEM((U, T, 256), jnp.float32),
            pltpu.VMEM((QW, T), jnp.float32),
        ],
        compiler_params=pltpu.CompilerParams(vmem_limit_bytes=60 << 20),
    )(bounds, table, span, qt, kvt, ot, lse, gt)


def tail_kernel(
    n,
    groups,
    deal_ref,
    dq_ref,
    dkv_ref,
    cos_ref,
    sin_ref,
    joint_hbm,
    joint_t_hbm,
    first_hbm,
    tokens_hbm,
    grad_hidden_hbm,
    gain_ref,
    packed_hbm,
    dealt_ref,
    shard_ref,
    joint_out_ref,
    joint,
    joint_t,
    first,
    tokens,
    grad_hidden,
    w_own,
    local_sems,
    kv_near,
    kv_send,
    kv_far,
    kv_sems,
    mixed,
    z_send,
    z_got,
    z_sems,
    jg_t,
    jg,
    j_core,
    j_side,
    j_plane,
    j_group,
    j_sems,
    w_core,
    w_y1,
    w_x1,
    w_x2,
    w_y2,
    w_plane,
    w_z,
    w_all,
    w_sems,
    d_send,
    d_mid,
    d_back,
    d_got,
    d_sems,
):
    bf, f32 = jnp.bfloat16, jnp.float32
    S = n // PLANES
    S2 = S // 2
    T, D = tokens.shape
    me, group = lax.axis_index("ctx"), lax.axis_index("fsdp")
    plane, side = me // S, lax.rem(me, S)
    s2, core = side // 2, lax.rem(side, 2)

    def at(p, a, c, g):
        return (p * S + a * 2 + c, g)

    def plane_peer(k):
        return at(lax.rem(plane + k, PLANES), s2, core, group)

    def side_peer(k):
        return at(plane, lax.rem(s2 + k, S2), core, group)

    def group_peer(k):
        return at(plane, s2, core, lax.rem(group + k, groups))

    core_peer = at(plane, s2, 1 - core, group)

    def remote(source, target, sems, index, device):
        return pltpu.make_async_remote_copy(
            src_ref=source,
            dst_ref=target,
            send_sem=sems.at[0, index],
            recv_sem=sems.at[1, index],
            device_id=device,
            device_id_type=pl.DeviceIdType.MESH,
        )

    barrier = pltpu.get_barrier_semaphore()

    def greet(k, carry):
        pl.semaphore_signal(
            barrier, inc=1, device_id=(lax.rem(me + k, n), group), device_id_type=pl.DeviceIdType.MESH
        )
        return carry

    lax.fori_loop(1, n, greet, 0)
    for k in range(1, groups):
        pl.semaphore_signal(barrier, inc=1, device_id=group_peer(k), device_id_type=pl.DeviceIdType.MESH)
    pl.semaphore_wait(barrier, n - 1 + groups - 1)

    order = [*range(1, PLANES), 0]
    core_kv = [remote(dkv_ref.at[1, :, j], kv_near.at[j], kv_sems, j, core_peer) for j in range(PLANES)]
    for j in order:
        core_kv[j].start()
    local = [
        pltpu.make_async_copy(source, target, local_sems.at[i])
        for i, (source, target) in enumerate(
            [
                (joint_t_hbm, joint_t),
                (first_hbm, first),
                (joint_hbm, joint),
                (packed_hbm.at[:, :, core], w_own),
                (tokens_hbm, tokens),
                (grad_hidden_hbm, grad_hidden),
            ]
        )
    ]
    for copy in local:
        copy.start()
    half = PLANES // 2
    core_w = [
        remote(
            packed_hbm.at[pl.ds(i * half, half), :, 1 - core],
            w_core.at[pl.ds(i * half, half)],
            w_sems,
            i,
            core_peer,
        )
        for i in range(2)
    ]
    for copy in core_w:
        copy.start()

    side_kv = {}
    for j in order:
        core_kv[j].wait()
        for k in range(S2):
            total = dkv_ref[0, k, j].astype(f32) + kv_near[j, k].astype(f32)
            kv_send[j, k] = total.astype(bf)
        for k in range(1, S2):
            side_kv[j, k] = remote(
                kv_send.at[j, k],
                kv_far.at[j, k - 1],
                kv_sems,
                PLANES + j * (S2 - 1) + k - 1,
                side_peer(S2 - k),
            )
            side_kv[j, k].start()

    local[3].wait()
    w_moves = []

    def w_copy(source, target, device):
        copy = remote(source, target, w_sems, 2 + len(w_moves), device)
        w_moves.append(copy)
        copy.start()
        return copy

    def add_core(i):
        core_w[i].wait()

        def body(step, carry):
            p, a, g = i * half + step // (S2 * groups), lax.rem(step // groups, S2), lax.rem(step, groups)
            w_core[p, a, g] = (w_own[p, a, g].astype(f32) + w_core[p, a, g].astype(f32)).astype(bf)
            return carry

        lax.fori_loop(0, half * S2 * groups, body, 0)

    add_core(0)
    y1 = [
        w_copy(w_core.at[pl.ds(0, half), :, lax.rem(group + k, groups)], w_y1.at[k - 1], group_peer(k))
        for k in range(1, groups)
    ]
    add_core(1)
    x2 = [
        w_copy(w_core.at[pl.ds(half, half), lax.rem(s2 + k, S2)], w_x2.at[k - 1], side_peer(k))
        for k in range(1, S2)
    ]

    plane_parts = {}
    local[0].wait()
    for j in order:
        dk = kv_send[j, 0].astype(f32)
        for k in range(1, S2):
            side_kv[j, k].wait()
            dk = dk + kv_far[j, k - 1].astype(f32)
        dk = dk.T
        cos, sin = cos_ref[j], sin_ref[j]
        rows = []
        for part in (dq_ref[j], dk[:QW]):
            for h in range(HP):
                upper, lower = part[h * HD : h * HD + HALF], part[h * HD + HALF : (h + 1) * HD]
                rows += [upper * cos + lower * sin, lower * cos - upper * sin]
        rows += [dk[QW:], jnp.zeros((mixed.shape[1] - 3 * QW, T), f32)]
        turned = jnp.concatenate(rows, axis=0)
        mixed[j] = turned.astype(bf)
        part = jnp.dot(turned.T.astype(bf), joint_t[...], preferred_element_type=f32)
        z_send[j] = part.astype(bf)
        if j:
            plane_parts[j] = remote(z_send.at[j], z_got.at[j - 1], z_sems, j - 1, plane_peer(PLANES - j))
            plane_parts[j].start()

    local[1].wait()
    jg_t[...] = jnp.dot(mixed[0], first[0], preferred_element_type=f32)
    for j in range(1, PLANES):
        jg_t[...] += jnp.dot(mixed[j], first[j], preferred_element_type=f32)
    local[2].wait()
    width = jg_t.shape[0]
    shard_rows = jg.shape[3]
    per = 128
    for i in range(D // per):
        block = jg_t[:, i * per : (i + 1) * per].T
        gain_part = jnp.sum(block * joint[i * per : (i + 1) * per, :].astype(f32), axis=1, keepdims=True)
        whole = jnp.concatenate([block, jnp.broadcast_to(gain_part, (per, per))], axis=1).astype(bf)
        j_rows = whole.astype(f32)
        first_row = i * per
        row = first_row
        while row < first_row + per:
            shard, offset = divmod(row, shard_rows)
            count = min(shard_rows - offset, first_row + per - row)
            jg[shard // S, shard % S // 2, shard % 2, offset : offset + count] = j_rows[
                row - first_row : row - first_row + count
            ].astype(bf)
            row += count
    j_moves = []

    def j_copy(source, target, device):
        copy = remote(source, target, j_sems, len(j_moves), device)
        j_moves.append(copy)
        copy.start()
        return copy

    j_first = j_copy(jg.at[:, :, 1 - core], j_core, core_peer)

    def sum_into(target, terms):
        total = terms[0].astype(f32)
        for term in terms[1:]:
            total = total + term.astype(f32)
        return total.astype(target)

    for copy in y1:
        copy.wait()
    for p in range(half):
        for a in range(S2):
            w_y1[0, p, a] = sum_into(bf, [w_core[p, a, group]] + [w_y1[k, p, a] for k in range(groups - 1)])
    x1 = [w_copy(w_y1.at[0, :, lax.rem(s2 + k, S2)], w_x1.at[k - 1], side_peer(k)) for k in range(1, S2)]
    for copy in x2:
        copy.wait()
    for p in range(half):
        for g in range(groups):
            w_x2[0, p, g] = sum_into(bf, [w_core[half + p, s2, g]] + [w_x2[k, p, g] for k in range(S2 - 1)])
    y2 = [w_copy(w_x2.at[0, :, lax.rem(group + k, groups)], w_y2.at[k - 1], group_peer(k)) for k in range(1, groups)]

    j_first.wait()
    for p in range(PLANES):
        for a in range(S2):
            j_core[p, a] = sum_into(bf, [jg[p, a, core], j_core[p, a]])
    j_second = [j_copy(j_core.at[:, lax.rem(s2 + k, S2)], j_side.at[k - 1], side_peer(k)) for k in range(1, S2)]

    local[4].wait()
    local[5].wait()
    for j in range(1, PLANES):
        plane_parts[j].wait()
    strip = 64

    def norm_back(i, carry):
        rows = pl.ds(pl.multiple_of(i * strip, strip), strip)
        grad = z_send[0, rows].astype(f32)
        for j in range(1, PLANES):
            grad = grad + z_got[j - 1, rows].astype(f32)
        values = tokens[rows].astype(f32)
        centred = values - jnp.mean(values, axis=-1, keepdims=True)
        scale = lax.rsqrt(jnp.mean(centred * centred, axis=-1, keepdims=True) + norm_eps)
        normal = centred * scale
        grad = grad * gain_ref[...]
        grad = grad - jnp.mean(grad, axis=-1, keepdims=True) - normal * jnp.mean(grad * normal, axis=-1, keepdims=True)
        grad_hidden[rows] = grad_hidden[rows] + grad * scale
        return carry

    lax.fori_loop(0, T // strip, norm_back, 0)

    blocks = T // BLOCK
    piece = BLOCK // n

    def d_copy(source, target, base, k):
        return remote(source.at[lax.rem(me + k, n)], target.at[me], d_sems, base + k, (lax.rem(me + k, n), group))

    for i in range(n):
        d_send[i] = jnp.concatenate(
            [grad_hidden[b * BLOCK + i * piece : b * BLOCK + (i + 1) * piece] for b in range(blocks)], axis=0
        ).astype(bf)
    out_deal = [d_copy(d_send, d_mid, 0, k) for k in range(1, n)]
    for copy in out_deal:
        copy.start()
    d_mid[me] = d_send[me]

    for copy in x1 + y2:
        copy.wait()
    for p in range(half):
        w_plane[p] = sum_into(bf, [w_y1[0, p, s2]] + [w_x1[k, p] for k in range(S2 - 1)])
        w_plane[half + p] = sum_into(bf, [w_x2[0, p, group]] + [w_y2[k, p] for k in range(groups - 1)])
    w_last = [w_copy(w_plane.at[lax.rem(plane + k, PLANES)], w_z.at[k - 1], plane_peer(k)) for k in range(1, PLANES)]
    for copy in j_second:
        copy.wait()
    for p in range(PLANES):
        j_side[0, p] = sum_into(bf, [j_core[p, s2]] + [j_side[k, p] for k in range(S2 - 1)])
    j_third = [j_copy(j_side.at[0, lax.rem(plane + k, PLANES)], j_plane.at[plane], plane_peer(k)) for k in range(1, PLANES)]
    j_plane[plane] = j_side[0, plane]

    for copy in out_deal:
        copy.wait()
    for i in range(n):
        chosen = []
        for b in range(blocks):
            wanted = deal_ref[i * blocks + b]
            held = d_mid[wanted // blocks].astype(f32)
            part = held[:piece]
            for other in range(1, blocks):
                part = jnp.where(lax.rem(wanted, blocks) == other, held[other * piece : (other + 1) * piece], part)
            chosen.append(part)
        d_back[i] = jnp.concatenate(chosen, axis=0).astype(bf)
    back_deal = [d_copy(d_back, d_got, n, k) for k in range(1, n)]
    for copy in back_deal:
        copy.start()
    d_got[me] = d_back[me]

    for copy in w_last:
        copy.wait()
    w_all[group] = sum_into(bf, [w_plane[plane]] + [w_z[k] for k in range(PLANES - 1)])
    w_gather = [w_copy(w_all.at[group], w_all.at[group], group_peer(k)) for k in range(1, groups)]
    for copy in j_third:
        copy.wait()
    j_group[group] = j_plane[...]
    j_last = [j_copy(j_plane, j_group.at[group], group_peer(k)) for k in range(1, groups)]

    for copy in back_deal:
        copy.wait()
    for b in range(blocks):
        for i in range(0, n, 2):
            rows = [d_got[i + e].astype(f32)[b * piece : (b + 1) * piece] for e in range(2)]
            dealt_ref[b * BLOCK + i * piece : b * BLOCK + (i + 2) * piece] = jnp.concatenate(rows, axis=0).astype(bf)
    for copy in w_gather:
        copy.wait()
    for g in range(groups):
        shard_ref[g] = w_all[g].astype(f32)
    for copy in j_last:
        copy.wait()
    for p in range(PLANES):
        total = j_group[0, p].astype(f32)
        for g in range(1, groups):
            total = total + j_group[g, p].astype(f32)
        joint_out_ref[p] = total


def tail(n, groups, deal, dqt, dkv, cos, sin, joint, joint_t, first, tokens, grad_hidden, gain, packed):
    bf, f32 = jnp.bfloat16, jnp.float32
    S2 = n // PLANES // 2
    T, D = tokens.shape
    width = joint.shape[1]
    wide = width + 128
    rows = D // n
    part = packed.shape[4]
    piece_rows = T // n
    half = PLANES // 2
    any_, vm, sm = (pl.BlockSpec(memory_space=m) for m in (pl.ANY, pltpu.VMEM, pltpu.SMEM))
    sems = lambda count: pltpu.SemaphoreType.DMA((2, count))
    return pl.pallas_call(
        functools.partial(tail_kernel, n, groups),
        out_shape=(
            jax.ShapeDtypeStruct((T, D), bf),
            jax.ShapeDtypeStruct((groups, part, D), f32),
            jax.ShapeDtypeStruct((PLANES, rows, wide), f32),
        ),
        in_specs=[sm, vm, vm, vm, vm, any_, any_, any_, any_, any_, vm, any_],
        out_specs=(vm, vm, vm),
        scratch_shapes=[
            pltpu.VMEM((D, width), bf),
            pltpu.VMEM((width, D), bf),
            pltpu.VMEM((PLANES, T, D), bf),
            pltpu.VMEM((T, D), bf),
            pltpu.VMEM((T, D), f32),
            pltpu.VMEM((PLANES, S2, groups, part, D), bf),
            pltpu.SemaphoreType.DMA((6,)),
            pltpu.VMEM((PLANES, S2, T, 2 * QW), bf),
            pltpu.VMEM((PLANES, S2, T, 2 * QW), bf),
            pltpu.VMEM((PLANES, S2 - 1, T, 2 * QW), bf),
            sems(PLANES * S2),
            pltpu.VMEM((PLANES, width, T), bf),
            pltpu.VMEM((PLANES, T, D), bf),
            pltpu.VMEM((PLANES - 1, T, D), bf),
            sems(PLANES - 1),
            pltpu.VMEM((width, D), f32),
            pltpu.VMEM((PLANES, S2, 2, rows, wide), bf),
            pltpu.VMEM((PLANES, S2, rows, wide), bf),
            pltpu.VMEM((S2 - 1, PLANES, rows, wide), bf),
            pltpu.VMEM((PLANES, rows, wide), bf),
            pltpu.VMEM((groups, PLANES, rows, wide), bf),
            sems(S2 + PLANES + groups - 2),
            pltpu.VMEM((PLANES, S2, groups, part, D), bf),
            pltpu.VMEM((groups - 1, half, S2, part, D), bf),
            pltpu.VMEM((S2 - 1, half, part, D), bf),
            pltpu.VMEM((S2 - 1, half, groups, part, D), bf),
            pltpu.VMEM((groups - 1, half, part, D), bf),
            pltpu.VMEM((PLANES, part, D), bf),
            pltpu.VMEM((PLANES - 1, part, D), bf),
            pltpu.VMEM((groups, part, D), bf),
            sems(2 + 3 * (groups - 1) + 2 * (S2 - 1) + PLANES - 1),
            pltpu.VMEM((n, piece_rows, D), bf),
            pltpu.VMEM((n, piece_rows, D), bf),
            pltpu.VMEM((n, piece_rows, D), bf),
            pltpu.VMEM((n, piece_rows, D), bf),
            sems(2 * n),
        ],
        compiler_params=pltpu.CompilerParams(collective_id=0, has_side_effects=True, vmem_limit_bytes=60 << 20),
    )(deal, dqt, dkv, cos, sin, joint, joint_t, first, tokens, grad_hidden, gain, packed)


def layer_norm(values, weights):
    centred = values - jnp.mean(values, axis=-1, keepdims=True)
    spread = jnp.mean(centred * centred, axis=-1, keepdims=True)
    return centred * lax.rsqrt(spread + norm_eps) * weights


def rotate_rows(values, cos, sin):
    upper, lower = values[..., :HALF, :], values[..., HALF:, :]
    return jnp.concatenate([upper * cos - lower * sin, lower * cos + upper * sin], axis=-2)


def on_device(
    n,
    groups,
    tokens,
    cotangent,
    lengths,
    deal,
    joint_projection,
    output_projection,
    expand_weight,
    contract_weight,
    gain_first,
    gain_second,
):
    bf, f32 = jnp.bfloat16, jnp.float32
    T, D = tokens.shape[1:]
    S = n // PLANES
    S2 = S // 2
    units = n
    me, gy = lax.axis_index("ctx"), lax.axis_index("fsdp")
    plane, side = me // S, me % S
    s2, core = side // 2, side % 2

    def over_planes(x, k):
        return lax.ppermute(x, "ctx", [(h * S + s, (h + k) % PLANES * S + s) for h in range(PLANES) for s in range(S)])

    def over_sides(x, k):
        return lax.ppermute(
            x,
            "ctx",
            [(h * S + a * 2 + c, h * S + (a + k) % S2 * 2 + c) for h in range(PLANES) for a in range(S2) for c in range(2)],
        )

    def over_cores(x):
        return lax.ppermute(x, "ctx", [(i, i ^ 1) for i in range(n)])

    def over_groups(x, k):
        return lax.ppermute(x, "fsdp", [(f, (f + k) % groups) for f in range(groups)])

    def pick(x, index):
        return lax.dynamic_index_in_dim(x, index, 0, keepdims=False)

    def turned(x, shift):
        return lax.dynamic_slice_in_dim(jnp.concatenate([x, x], axis=0), shift, x.shape[0], 0)

    def whole_of(shard):
        parts = [shard] + [over_groups(shard, k) for k in range(1, groups)]
        return turned(jnp.stack(parts[::-1]), groups - 1 - gy).reshape(-1, *shard.shape[1:])

    def whole_by_cores(shard):
        half = shard.shape[0] // 2
        halves = shard.reshape(2, half, *shard.shape[1:])
        mine = pick(halves, core)
        got = jnp.stack([over_groups(mine, k) for k in range(1, groups)])
        other = over_cores(got)
        low = jnp.where(core == 0, got, other)
        high = jnp.where(core == 0, other, got)
        parts = jnp.concatenate([jnp.stack([low, high], axis=1)[::-1], halves[None]], axis=0)
        return turned(parts, groups - 1 - gy).reshape(-1, *shard.shape[1:])

    tokens_own = tokens[0]
    all_tokens = jnp.stack([tokens_own] + [over_planes(tokens_own, k) for k in range(1, PLANES)])
    joint_cols = lax.dynamic_index_in_dim(
        joint_projection.reshape(-1, 3, PLANES, QW), plane, 2, keepdims=False
    ).reshape(-1, 3 * QW)
    joint = whole_of(joint_cols)
    gains = whole_of(jnp.stack([gain_first, gain_second], axis=1))
    gain_one, gain_two = gains[:, 0].astype(f32), gains[:, 1].astype(f32)
    out_w = whole_by_cores(output_projection)
    exp_w = whole_by_cores(expand_weight)
    con_w = whole_by_cores(contract_weight)

    lens = lengths[0]
    ends, total = [], jnp.int32(0)
    for j in range(lens.shape[0]):
        total = total + lens[j]
        ends.append(total)
    rel_plane = (plane - jnp.arange(PLANES)) % PLANES
    first_token = (rel_plane * S + side) * T
    natural = first_token[:, None] + jnp.arange(T, dtype=jnp.int32)[None]

    def span_of(index):
        begin, end = jnp.zeros_like(index), jnp.full_like(index, ends[0])
        for j in range(1, lens.shape[0]):
            after = index >= ends[j - 1]
            begin = jnp.where(after, ends[j - 1], begin)
            end = jnp.where(after, ends[j], end)
        return begin, end

    begin, end = span_of(natural)
    span = jnp.stack([begin, end] + [jnp.zeros_like(begin)] * 6, axis=1)
    low_bound, low_end = span_of(first_token)
    high_begin, high_bound = span_of(first_token + T - 1)
    low, high = low_bound // T, (high_bound + T - 1) // T
    full_low = jnp.clip((high_begin + T - 1) // T, low, high)
    full_high = jnp.clip(low_end // T, full_low, high)
    bounds = jnp.stack([low, full_low, full_high, high], axis=1).astype(jnp.int32)
    unit = jnp.arange(units, dtype=jnp.int32)
    u_plane, u_side = unit // S, unit % S
    u_s2, u_core = u_side // 2, u_side % 2
    table = ((u_core != core) * S2 + (s2 - u_s2) % S2) * PLANES + (plane - u_plane) % PLANES
    table = table.astype(jnp.int32)
    frequencies = rope_base ** (-jnp.arange(0, HEAD_DIM, 2).astype(f32) / HEAD_DIM)
    angles = (natural - begin).astype(f32)[:, None, :] * frequencies[None, :, None]
    cos, sin = jnp.cos(angles)[:, None], jnp.sin(angles)[:, None]

    x_all = all_tokens.astype(f32)
    first = layer_norm(x_all, gain_one).astype(bf)
    mixed = jnp.einsum("bte,ed->bdt", first, joint, preferred_element_type=f32)
    mixed = mixed.reshape(PLANES, 3, HP, HEAD_DIM, T)
    qt = (rotate_rows(mixed[:, 0], cos, sin).astype(bf) * bf(HEAD_DIM**-0.5)).reshape(PLANES, QW, T)
    kt = rotate_rows(mixed[:, 1], cos, sin).astype(bf).reshape(PLANES, QW, T)
    vt = mixed[:, 2].astype(bf).reshape(PLANES, QW, T)
    kv = jnp.concatenate([kt, vt], axis=1)
    near = jnp.stack([kv] + [over_sides(kv, k) for k in range(1, S2)])
    kv_all = jnp.concatenate([near[None], over_cores(near)[None]], axis=0).reshape(units, 2 * QW, T)

    ot, lowt, lse = attn_fwd(bounds, table, span, qt, kv_all)

    parts = [lowt[0]] + [over_planes(lowt[k], -k) for k in range(1, PLANES)]
    attended_t = turned(jnp.stack(parts), (PLANES - plane) % PLANES).reshape(D, T)

    x = tokens_own.astype(f32)
    grad_out = cotangent[0]
    hidden = x + jnp.einsum("dt,de->te", attended_t, out_w, preferred_element_type=f32)
    second = layer_norm(hidden, gain_two).astype(bf)
    expanded = jnp.dot(second, exp_w, preferred_element_type=f32)

    def gated(values):
        return jax.nn.gelu(values[:, :FF], approximate=False) * values[:, FF:]

    activated_f, gated_pull = jax.vjp(gated, expanded)
    activated = activated_f.astype(bf)
    output = (hidden + jnp.dot(activated, con_w, preferred_element_type=f32)).astype(bf)

    grad_activated = jnp.einsum("td,fd->tf", grad_out, con_w, preferred_element_type=f32)
    grad_expanded = gated_pull(grad_activated)[0].astype(bf)
    grad_second = jnp.einsum("tf,df->td", grad_expanded, exp_w, preferred_element_type=f32)
    _, second_pull = jax.vjp(layer_norm, hidden, gain_two)
    grad_hidden_norm, grad_gain_two = second_pull(grad_second)
    grad_hidden = grad_out.astype(f32) + grad_hidden_norm
    grad_branch = grad_hidden.astype(bf)
    grad_attended = jnp.einsum("de,te->dt", out_w, grad_branch, preferred_element_type=f32).astype(bf)
    rel = turned(grad_attended.reshape(PLANES, QW, T), plane)
    gt = jnp.stack([rel[0]] + [over_planes(rel[k], k) for k in range(1, PLANES)])

    grad_contract = jnp.einsum("tf,td->fd", activated, grad_out, preferred_element_type=f32)
    grad_expand = jnp.einsum("td,tf->df", second, grad_expanded, preferred_element_type=f32)
    grad_output = jnp.einsum("dt,te->de", attended_t, grad_branch, preferred_element_type=f32)

    dqt, dkv = attn_bwd(bounds, table, span, qt, kv_all, ot, lse, gt)

    def sharded(x):
        return x.astype(bf).reshape(n, x.shape[0] // n, x.shape[1])

    gain_rows = jnp.pad(grad_gain_two.reshape(n, 1, D // n), ((0, 0), (0, 7), (0, D - D // n))).astype(bf)
    rows = D // n
    wide = grad_expand.shape[1] // D
    pieces = [sharded(grad_output)]
    pieces += [sharded(grad_expand[:, i * D : (i + 1) * D]) for i in range(wide)]
    pieces += [sharded(grad_contract), gain_rows]
    used = sum(p.shape[1] for p in pieces)
    part = -(-used // (groups * 16)) * 16
    packed = jnp.concatenate(pieces + [jnp.zeros((n, groups * part - used, D), bf)], axis=1)
    packed = packed.reshape(PLANES, S2, 2, groups, part, D)
    joint_pad = jnp.pad(joint, ((0, 0), (0, 64)))

    dealt, shards, joint_raw = tail(
        n,
        groups,
        deal[0],
        dqt,
        dkv.reshape(2, S2, PLANES, T, 2 * QW),
        cos[:, 0],
        sin[:, 0],
        joint_pad,
        joint_pad.T,
        first,
        tokens_own,
        grad_hidden,
        gain_one[None],
        packed,
    )
    shards = shards.reshape(groups * part, D)
    shard_output = shards[:rows]
    shard_expand = jnp.concatenate([shards[(1 + i) * rows : (2 + i) * rows] for i in range(wide)], axis=1)
    after = (1 + wide) * rows
    ff_rows = grad_contract.shape[0] // n
    shard_contract = shards[after : after + ff_rows]
    shard_gain_two = shards[after + ff_rows, :rows]
    shard_joint = jnp.transpose(joint_raw[:, :, : 3 * QW].reshape(PLANES, rows, 3, QW), (1, 2, 0, 3))
    shard_joint = shard_joint.reshape(rows, 3 * PLANES * QW)
    shard_gain_one = jnp.sum(joint_raw[:, :, -1], axis=0) / lax.dynamic_slice_in_dim(gain_one, me * rows, rows)
    return (
        output[None],
        dealt[None],
        shard_joint,
        shard_output,
        shard_expand,
        shard_contract,
        shard_gain_one,
        shard_gain_two,
    )


def solution(mesh):
    return jax.shard_map(
        functools.partial(on_device, mesh.shape["ctx"], mesh.shape["fsdp"]),
        mesh=mesh,
        in_specs=(
            P("fsdp", "ctx", None),
            P("fsdp", "ctx", None),
            P("fsdp", None),
            P("fsdp", None),
            P("fsdp", None),
            P("fsdp", None),
            P("fsdp", None),
            P("fsdp", None),
            P("fsdp"),
            P("fsdp"),
        ),
        out_specs=(
            P("fsdp", "ctx", None),
            P("fsdp", "ctx", None),
            P("ctx", None),
            P("ctx", None),
            P("ctx", None),
            P("ctx", None),
            P("ctx"),
            P("ctx"),
        ),
        check_vma=False,
    )
```

```python
import functools

import jax
import jax.numpy as jnp
from jax import lax
from jax.experimental import pallas as pl
from jax.experimental.pallas import tpu as pltpu
from jax.sharding import PartitionSpec as P

FF = 1152
HEADS = 12
HEAD_DIM = 64
BLOCK = 128
PLANES = 4
HD = HEAD_DIM
HALF = HEAD_DIM // 2
HP = HEADS // PLANES
QW = HP * HEAD_DIM
rope_base = 160000.0
norm_eps = 1e-05
MASKED = -1e30


def ends_of(lengths_ref, count):
    ends, total = [], 0
    for i in range(count):
        total = total + lengths_ref[0, i]
        ends.append(total)
    return ends


def span_of(index, ends):
    begin, end = jnp.zeros_like(index), jnp.full_like(index, ends[0])
    for before, after in zip(ends[:-1], ends[1:]):
        begin = jnp.where(index >= before, before, begin)
        end = jnp.where(index >= before, after, end)
    return begin, end


def head_rows(x, head):
    rows = lax.broadcasted_iota(jnp.int32, x.shape, 0)
    return jnp.where((rows >= head * HD) & (rows < (head + 1) * HD), x, jnp.zeros_like(x))


def query_block(n, b, T, ends):
    S = n // PLANES
    me = lax.axis_index("ctx")
    base = (lax.rem(me // S + PLANES - b, PLANES) * S + lax.rem(me, S)) * T
    low_begin, low_end = span_of(base, ends)
    high_begin, high_end = span_of(base + T - 1, ends)
    low, high = low_begin // T, (high_end + T - 1) // T
    full_low = jnp.clip((high_begin + T - 1) // T, low, high)
    full_high = jnp.clip(low_end // T, full_low, high)
    begin, end = span_of(base + lax.broadcasted_iota(jnp.int32, (8, T), 1), ends)
    return (low, full_low, full_high, high), begin[0:1], end[0:1]


def over_units(bounds, step):
    low, full_low, full_high, high = bounds

    def run(begin, end, masked):
        def body(u, carry):
            step(u, masked)
            return carry

        lax.fori_loop(begin, end, body, 0)

    run(low, full_low, True)
    in_pairs(full_low, full_high, lambda u: step(u, False))
    run(full_high, high, True)


def in_pairs(begin, end, step):
    pairs = (end - begin) // 2

    def two(i, carry):
        step(begin + 2 * i)
        step(begin + 2 * i + 1)
        return carry

    def one(u, carry):
        step(u)
        return carry

    lax.fori_loop(0, pairs, two, 0)
    lax.fori_loop(begin + 2 * pairs, end, one, 0)


def fwd_kernel(n, count, lengths_ref, qt_ref, kv_ref, ot_ref, lowt_ref, lse_ref, values, scores, top, total, acc):
    units, T, _ = kv_ref.shape
    ends = ends_of(lengths_ref, count)

    def flip(u, carry):
        values[u] = kv_ref[u, :, 128:].T
        return carry

    lax.fori_loop(0, units, flip, 0, unroll=4)

    def one_query_block(b, carry):
        qt = qt_ref[b]
        qheads = [head_rows(qt, h) for h in range(HP)]
        bounds, q_start, q_end = query_block(n, b, T, ends)
        top[...] = jnp.full_like(top, MASKED)
        total[...] = jnp.zeros_like(total)
        acc[...] = jnp.zeros_like(acc)

        def score(u, masked):
            k = kv_ref[u, :, :QW]
            st = [jnp.dot(k, qheads[h], preferred_element_type=jnp.float32) for h in range(HP)]
            if masked:
                at = u * T + lax.broadcasted_iota(jnp.int32, (T, T), 0)
                allowed = (at >= q_start) & (at < q_end)
                st = [jnp.where(allowed, s, MASKED) for s in st]
            for h in range(HP):
                scores[u, h] = st[h]
                top[h] = jnp.maximum(top[h], jnp.max(st[h].reshape(T // 8, 8, T), axis=0))

        over_units(bounds, score)
        m = [jnp.max(top[h], axis=0, keepdims=True) for h in range(HP)]

        def gather(u):
            p = [jnp.exp(scores[u, h] - m[h]) for h in range(HP)]
            for h in range(HP):
                total[h] += jnp.sum(p[h].reshape(T // 8, 8, T), axis=0)
                rows = pl.ds(h * HD, HD)
                acc[rows, :] += jnp.dot(
                    values[u, pl.ds(HD + h * HD, HD), :], p[h].astype(jnp.bfloat16), preferred_element_type=jnp.float32
                )

        in_pairs(bounds[0], bounds[3], gather)
        for h in range(HP):
            rows = pl.ds(h * HD, HD)
            l = jnp.sum(total[h], axis=0, keepdims=True)
            o = acc[rows, :] / l
            ot_ref[b, rows, :] = o
            lowt_ref[b, rows, :] = o.astype(jnp.bfloat16)
            lse_ref[b, h : h + 1, :] = m[h] + jnp.log(l)
        return carry

    lax.fori_loop(0, qt_ref.shape[0], one_query_block, 0)


def attn_fwd(n, lengths, qt, kv):
    B, _, T = qt.shape
    U = kv.shape[0]
    sm, vm = pl.BlockSpec(memory_space=pltpu.SMEM), pl.BlockSpec(memory_space=pltpu.VMEM)
    return pl.pallas_call(
        functools.partial(fwd_kernel, n, lengths.shape[1]),
        out_shape=(
            jax.ShapeDtypeStruct((B, QW, T), jnp.float32),
            jax.ShapeDtypeStruct((B, QW, T), jnp.bfloat16),
            jax.ShapeDtypeStruct((B, 8, T), jnp.float32),
        ),
        in_specs=[sm, vm, vm],
        out_specs=(vm, vm, vm),
        scratch_shapes=[
            pltpu.VMEM((U, 256, T), jnp.bfloat16),
            pltpu.VMEM((U, HP, T, T), jnp.float32),
            pltpu.VMEM((HP, 8, T), jnp.float32),
            pltpu.VMEM((HP, 8, T), jnp.float32),
            pltpu.VMEM((QW, T), jnp.float32),
        ],
        compiler_params=pltpu.CompilerParams(vmem_limit_bytes=60 << 20),
    )(lengths, qt, kv)


def bwd_kernel(n, count, lengths_ref, qt_ref, kv_ref, ot_ref, lse_ref, gt_ref, dqt_ref, dkv_ref, keys, dk, dv, dq):
    units, T, _ = kv_ref.shape
    ends = ends_of(lengths_ref, count)

    def flip(u, carry):
        keys[u] = kv_ref[u, :, :256].T
        dk[u] = jnp.zeros_like(dk[u])
        dv[u] = jnp.zeros_like(dv[u])
        return carry

    lax.fori_loop(0, units, flip, 0, unroll=4)

    def one_query_block(b, carry):
        qt, gt = qt_ref[b], gt_ref[b]
        zero = jnp.zeros((HD, T), jnp.bfloat16)
        qheads = [head_rows(qt, h) for h in range(HP)]
        gheads = [head_rows(gt, h) for h in range(HP)]
        gpad = [jnp.concatenate([zero, x], axis=0) for x in gheads]
        q = jnp.concatenate([jnp.concatenate([x, zero], axis=0).T for x in qheads], axis=0)
        g = jnp.concatenate([x.T for x in gpad], axis=0)
        bounds, q_start, q_end = query_block(n, b, T, ends)
        prod = gt.astype(jnp.float32) * ot_ref[b]
        delta = [jnp.sum(prod[h * HD : (h + 1) * HD], axis=0, keepdims=True) for h in range(HP)]
        lse = [lse_ref[b, h : h + 1, :] for h in range(HP)]
        dq[...] = jnp.zeros_like(dq)

        def one_unit(u, masked):
            k, v = kv_ref[u, :, :QW], kv_ref[u, :, 128:]
            st = [jnp.dot(k, qheads[h], preferred_element_type=jnp.float32) for h in range(HP)]
            dp = [jnp.dot(v, gpad[h], preferred_element_type=jnp.float32) for h in range(HP)]
            st = [st[h] - lse[h] for h in range(HP)]
            if masked:
                at = u * T + lax.broadcasted_iota(jnp.int32, (T, T), 0)
                allowed = (at >= q_start) & (at < q_end)
                st = [jnp.where(allowed, s, MASKED) for s in st]
            p = [jnp.exp(s) for s in st]
            ds = [(p[h] * (dp[h] - delta[h])).astype(jnp.bfloat16) for h in range(HP)]
            p = [x.astype(jnp.bfloat16) for x in p]
            dv[u] += jnp.dot(jnp.concatenate(p, axis=1), g, preferred_element_type=jnp.float32)
            dk[u] += jnp.dot(jnp.concatenate(ds, axis=1), q, preferred_element_type=jnp.float32)
            for h in range(HP):
                rows = pl.ds(h * HD, HD)
                dq[rows, :] += jnp.dot(keys[u, rows, :], ds[h], preferred_element_type=jnp.float32)

        over_units(bounds, one_unit)
        dqt_ref[b] = dq[...] * (HD**-0.5)
        return carry

    lax.fori_loop(0, qt_ref.shape[0], one_query_block, 0)

    def out(u, carry):
        dkv_ref[u, :, :128] = dk[u, :, :128].astype(jnp.bfloat16)
        dkv_ref[u, :, 128:256] = (dk[u, :, 128:] + dv[u, :, :128]).astype(jnp.bfloat16)
        dkv_ref[u, :, 256:] = dv[u, :, 128:].astype(jnp.bfloat16)
        return carry

    lax.fori_loop(0, units, out, 0, unroll=2)


def attn_bwd(n, lengths, qt, kv, ot, lse, gt):
    B, _, T = qt.shape
    U = kv.shape[0]
    sm, vm = pl.BlockSpec(memory_space=pltpu.SMEM), pl.BlockSpec(memory_space=pltpu.VMEM)
    return pl.pallas_call(
        functools.partial(bwd_kernel, n, lengths.shape[1]),
        out_shape=(jax.ShapeDtypeStruct((B, QW, T), jnp.float32), jax.ShapeDtypeStruct((U, T, 2 * QW), jnp.bfloat16)),
        in_specs=[sm] + [vm] * 5,
        out_specs=(vm, vm),
        scratch_shapes=[
            pltpu.VMEM((U, 256, T), jnp.bfloat16),
            pltpu.VMEM((U, T, 256), jnp.float32),
            pltpu.VMEM((U, T, 256), jnp.float32),
            pltpu.VMEM((QW, T), jnp.float32),
        ],
        compiler_params=pltpu.CompilerParams(vmem_limit_bytes=60 << 20),
    )(lengths, qt, kv, ot, lse, gt)
def front_kernel(
    n,
    groups,
    count,
    lengths_ref,
    tokens_ref,
    joint_ref,
    gain_one_ref,
    gain_two_ref,
    freq_ref,
    out_hbm,
    exp_hbm,
    con_hbm,
    first_ref,
    qt_ref,
    kv_ref,
    joint_out,
    joint_t_out,
    turn_ref,
    gains_ref,
    out_all,
    exp_all,
    con_all,
    held,
    t_sems,
    cols,
    cols_all,
    gain_held,
    g_sems,
    kv_own,
    kv_sems,
    own_sems,
    w_sems,
    w_local,
):
    bf, f32 = jnp.bfloat16, jnp.float32
    S = n // PLANES
    S2 = S // 2
    T, D = tokens_ref.shape
    me, group = lax.axis_index("ctx"), lax.axis_index("fsdp")
    plane, side = me // S, lax.rem(me, S)
    s2, core = side // 2, lax.rem(side, 2)

    def at(p, a, c, g):
        return (p * S + a * 2 + c, g)

    def side_peer(k):
        return at(plane, lax.rem(s2 + k, S2), core, group)

    def group_peer(k):
        return at(plane, s2, core, lax.rem(group + k, groups))

    core_peer = at(plane, s2, 1 - core, group)

    def remote(source, target, sems, index, device):
        return pltpu.make_async_remote_copy(
            src_ref=source,
            dst_ref=target,
            send_sem=sems.at[0, index],
            recv_sem=sems.at[1, index],
            device_id=device,
            device_id_type=pl.DeviceIdType.MESH,
        )

    barrier = pltpu.get_barrier_semaphore()

    def greet(device):
        pl.semaphore_signal(barrier, inc=1, device_id=device, device_id_type=pl.DeviceIdType.MESH)

    for k in range(1, PLANES):
        greet(at(lax.rem(plane + k, PLANES), s2, core, group))
    for k in range(1, S2):
        greet(side_peer(k))
    for k in range(1, groups):
        greet(group_peer(k))
    greet(core_peer)
    pl.semaphore_wait(barrier, PLANES - 1 + S2 - 1 + groups - 1 + 1)

    def up(p):
        return remote(held.at[p], held.at[p], t_sems, p, at(plane + 1, s2, core, group))

    def down(p):
        return remote(held.at[p], held.at[p], t_sems, PLANES + p, at(plane - 1, s2, core, group))

    held[plane] = tokens_ref[...]

    @pl.when(plane < PLANES - 1)
    def _():
        up(plane).start()

    @pl.when(plane > 0)
    def _():
        down(plane).start()

    pair = 2 * QW
    for part in range(3):
        window = joint_ref[:, pl.ds(pl.multiple_of(part * D + plane // 2 * pair, 128), pair)].T
        chosen = jnp.where(lax.rem(plane, 2) == 0, window[:QW].astype(f32), window[QW:].astype(f32))
        cols[part * QW : (part + 1) * QW] = chosen.astype(bf)
    gain_held[group] = jnp.zeros_like(gain_held[group])
    gain_held[group, 0:1] = gain_one_ref[...].astype(f32)
    gain_held[group, 1:2] = gain_two_ref[...].astype(f32)
    col_moves = [remote(cols, cols_all.at[group], g_sems, k - 1, group_peer(k)) for k in range(1, groups)]
    gain_moves = [
        remote(gain_held.at[group], gain_held.at[group], g_sems, groups - 1 + k - 1, group_peer(k))
        for k in range(1, groups)
    ]
    for copy in gain_moves + col_moves:
        copy.start()
    cols_all[group] = cols[...]

    weights = [(out_hbm, out_all), (exp_hbm, exp_all), (con_hbm, con_all)]
    w_own, w_first, w_second = [], [], []
    for i, (source, target) in enumerate(weights):
        w_own.append(pltpu.make_async_copy(source, target.at[group], w_local.at[i]))
        for k in range(1, groups):
            index = (i * (groups - 1) + k - 1) * 2
            w_first.append(remote(source.at[core], target.at[group, core], w_sems, index, group_peer(k)))
            came = lax.rem(group + groups - k, groups)
            w_second.append(remote(target.at[came, core], target.at[came, core], w_sems, index + 1, core_peer))
    for copy in w_own:
        copy.start()

    ends = ends_of(lengths_ref, count)
    for j in range(PLANES):
        base = (lax.rem(plane + PLANES - j, PLANES) * S + side) * T
        index = base + lax.broadcasted_iota(jnp.int32, (8, T), 1)
        begin, _ = span_of(index, ends)
        angles = (index - begin)[0:1].astype(f32) * freq_ref[...]
        turn_ref[j, :HALF] = jnp.cos(angles)
        turn_ref[j, HALF:] = jnp.sin(angles)

    for copy in gain_moves:
        copy.wait()
    share = D // groups
    total = jnp.zeros((8, D), f32)
    for g in range(groups):
        rows = lax.broadcasted_iota(jnp.int32, (share, D), 0)
        lanes = lax.broadcasted_iota(jnp.int32, (share, D), 1)
        place = jnp.where(lanes == rows + g * share, 1.0, 0.0).astype(bf)
        total = total + jnp.dot(gain_held[g].astype(bf), place, preferred_element_type=f32)
    gains_ref[...] = total
    for copy in col_moves:
        copy.wait()
    for copy in w_first:
        copy.start()
    width = joint_t_out.shape[0]
    for g in range(groups):
        padded = jnp.concatenate([cols_all[g], jnp.zeros((width - 3 * QW, share), bf)], axis=0)
        joint_out[g * share : (g + 1) * share] = padded.T
    for i in range(D // 128):
        joint_t_out[:, i * 128 : (i + 1) * 128] = joint_out[i * 128 : (i + 1) * 128].T

    strip = 64

    def kv_unit(p, a, c):
        return p * S + a * 2 + c

    def side_kv(j, k):
        p = lax.rem(plane + PLANES - j, PLANES)
        return remote(kv_own.at[j], kv_ref.at[kv_unit(p, s2, core)], kv_sems, j * (2 * S2 - 1) + k - 1, side_peer(k))

    def core_kv(j, k):
        p = lax.rem(plane + PLANES - j, PLANES)
        unit = kv_unit(p, lax.rem(s2 + S2 - k, S2), core)
        source = kv_own.at[j] if k == 0 else kv_ref.at[unit]
        return remote(source, kv_ref.at[unit], kv_sems, j * (2 * S2 - 1) + S2 - 1 + k, core_peer)

    def own_kv(j):
        p = lax.rem(plane + PLANES - j, PLANES)
        return pltpu.make_async_copy(kv_own.at[j], kv_ref.at[kv_unit(p, s2, core)], own_sems.at[j])

    def process(p):
        j = lax.rem(plane + PLANES - p, PLANES)

        def norm(i, carry):
            rows = pl.ds(pl.multiple_of(i * strip, strip), strip)
            values = held[p, rows].astype(f32)
            centred = values - jnp.mean(values, axis=-1, keepdims=True)
            spread = jnp.mean(centred * centred, axis=-1, keepdims=True)
            first_ref[j, rows] = (centred * lax.rsqrt(spread + norm_eps) * gains_ref[0:1]).astype(bf)
            return carry

        lax.fori_loop(0, T // strip, norm, 0)
        mixed = lax.dot_general(
            joint_t_out[: 3 * QW], first_ref[j], (((1,), (1,)), ((), ())), preferred_element_type=f32
        )
        cos, sin = turn_ref[j, :HALF], turn_ref[j, HALF:]
        turned = []
        for h in range(2 * HP):
            upper, lower = mixed[h * HD : h * HD + HALF], mixed[h * HD + HALF : (h + 1) * HD]
            turned += [upper * cos - lower * sin, lower * cos + upper * sin]
        q = jnp.concatenate(turned[: 2 * HP], axis=0).astype(bf)
        qt_ref[j] = (q.astype(f32) * HEAD_DIM**-0.5).astype(bf)
        kv_own[j] = jnp.concatenate(turned[2 * HP :] + [mixed[2 * QW :]], axis=0).T.astype(bf)
        for k in range(1, S2):
            side_kv(j, k).start()
        core_kv(j, 0).start()
        own_kv(j).start()

    process(plane)
    for t in range(1, PLANES):

        @pl.when(plane >= t)
        def _(t=t):
            up(plane - t).wait_recv()

            @pl.when(plane < PLANES - 1)
            def _():
                up(plane - t).start()

        @pl.when(plane + t < PLANES)
        def _(t=t):
            down(plane + t).wait_recv()

            @pl.when(plane > 0)
            def _():
                down(plane + t).start()

        below = jnp.where(plane >= t, 1, 0)
        above = jnp.where(plane + t < PLANES, 1, 0)

        def arrived(i, carry, t=t, below=below):
            process(jnp.where(i < below, plane - t, plane + t))
            return carry

        lax.fori_loop(0, below + above, arrived, 0)

    for j in range(PLANES):
        for k in range(1, S2):
            side_kv(j, k).wait_recv()
            core_kv(j, k).start()
    for first_move, second_move in zip(w_first, w_second):
        first_move.wait_recv()
        second_move.start()

    for j in range(PLANES):
        own_kv(j).wait()
        for k in range(1, S2):
            side_kv(j, k).wait_send()
        for k in range(S2):
            core_kv(j, k).wait()
    for p in range(PLANES):

        @pl.when((plane < PLANES - 1) & (plane >= p))
        def _(p=p):
            up(p).wait_send()

        @pl.when((plane > 0) & (plane <= p))
        def _(p=p):
            down(p).wait_send()

    for copy in w_own:
        copy.wait()
    for first_move, second_move in zip(w_first, w_second):
        first_move.wait_send()
        second_move.wait()


def front(n, groups, lengths, tokens, joint_shard, gain_first, gain_second, out_w, exp_w, con_w):
    bf, f32 = jnp.bfloat16, jnp.float32
    S2 = n // PLANES // 2
    T, D = tokens.shape
    width = 3 * QW + 64
    share = D // groups
    any_, vm, sm = (pl.BlockSpec(memory_space=m) for m in (pl.ANY, pltpu.VMEM, pltpu.SMEM))
    sems = lambda count: pltpu.SemaphoreType.DMA((2, count))
    halves = lambda w: w.reshape(2, w.shape[0] // 2, w.shape[1])
    frequencies = rope_base ** (-jnp.arange(0, HEAD_DIM, 2).astype(f32) / HEAD_DIM)
    weights = [halves(w) for w in (out_w, exp_w, con_w)]
    return pl.pallas_call(
        functools.partial(front_kernel, n, groups, lengths.shape[1]),
        out_shape=(
            jax.ShapeDtypeStruct((PLANES, T, D), bf),
            jax.ShapeDtypeStruct((PLANES, QW, T), bf),
            jax.ShapeDtypeStruct((n, T, 2 * QW), bf),
            jax.ShapeDtypeStruct((D, width), bf),
            jax.ShapeDtypeStruct((width, D), bf),
            jax.ShapeDtypeStruct((PLANES, 2 * HALF, T), f32),
            jax.ShapeDtypeStruct((8, D), f32),
            *[jax.ShapeDtypeStruct((groups, *w.shape), bf) for w in weights],
        ),
        in_specs=[sm, vm, vm, vm, vm, vm, any_, any_, any_],
        out_specs=(vm, vm, any_, vm, vm, vm, vm, any_, any_, any_),
        scratch_shapes=[
            pltpu.VMEM((PLANES, T, D), bf),
            sems(2 * PLANES),
            pltpu.VMEM((3 * QW, share), bf),
            pltpu.VMEM((groups, 3 * QW, share), bf),
            pltpu.VMEM((groups, 8, share), f32),
            sems(2 * (groups - 1)),
            pltpu.VMEM((PLANES, T, 2 * QW), bf),
            sems(PLANES * (2 * S2 - 1)),
            pltpu.SemaphoreType.DMA((PLANES,)),
            sems(2 * len(weights) * (groups - 1)),
            pltpu.SemaphoreType.DMA((len(weights),)),
        ],
        compiler_params=pltpu.CompilerParams(collective_id=1, has_side_effects=True, vmem_limit_bytes=50 << 20),
    )(
        lengths,
        tokens,
        joint_shard,
        gain_first[None],
        gain_second[None],
        frequencies[:, None],
        *weights,
    )


def tail_kernel(
    n,
    groups,
    deal_ref,
    dq_ref,
    dkv_ref,
    turn_ref,
    joint_hbm,
    joint_t_hbm,
    first_hbm,
    tokens_hbm,
    grad_hidden_hbm,
    gain_ref,
    packed_hbm,
    dealt_ref,
    shard_ref,
    joint_out_ref,
    joint,
    joint_t,
    first,
    tokens,
    grad_hidden,
    w_own,
    local_sems,
    kv_near,
    kv_send,
    kv_far,
    kv_sems,
    mixed,
    z_send,
    z_got,
    z_sems,
    jg_t,
    jg,
    j_core,
    j_side,
    j_plane,
    j_group,
    j_sems,
    w_core,
    w_y1,
    w_x1,
    w_x2,
    w_y2,
    w_plane,
    w_z,
    w_all,
    w_sems,
    d_send,
    d_mid,
    d_back,
    d_got,
    d_sems,
):
    bf, f32 = jnp.bfloat16, jnp.float32
    S = n // PLANES
    S2 = S // 2
    T, D = tokens.shape
    me, group = lax.axis_index("ctx"), lax.axis_index("fsdp")
    plane, side = me // S, lax.rem(me, S)
    s2, core = side // 2, lax.rem(side, 2)

    def at(p, a, c, g):
        return (p * S + a * 2 + c, g)

    def plane_peer(k):
        return at(lax.rem(plane + k, PLANES), s2, core, group)

    def side_peer(k):
        return at(plane, lax.rem(s2 + k, S2), core, group)

    def group_peer(k):
        return at(plane, s2, core, lax.rem(group + k, groups))

    core_peer = at(plane, s2, 1 - core, group)

    def remote(source, target, sems, index, device):
        return pltpu.make_async_remote_copy(
            src_ref=source,
            dst_ref=target,
            send_sem=sems.at[0, index],
            recv_sem=sems.at[1, index],
            device_id=device,
            device_id_type=pl.DeviceIdType.MESH,
        )

    barrier = pltpu.get_barrier_semaphore()

    def greet(k, carry):
        pl.semaphore_signal(
            barrier, inc=1, device_id=(lax.rem(me + k, n), group), device_id_type=pl.DeviceIdType.MESH
        )
        return carry

    lax.fori_loop(1, n, greet, 0)
    for k in range(1, groups):
        pl.semaphore_signal(barrier, inc=1, device_id=group_peer(k), device_id_type=pl.DeviceIdType.MESH)
    pl.semaphore_wait(barrier, n - 1 + groups - 1)

    order = [*range(1, PLANES), 0]
    planes = [lax.rem(plane + PLANES - j, PLANES) for j in range(PLANES)]
    core_kv = [remote(dkv_ref.at[planes[j], :, 1 - core], kv_near.at[j], kv_sems, j, core_peer) for j in range(PLANES)]
    for j in order:
        core_kv[j].start()
    local = [
        pltpu.make_async_copy(source, target, local_sems.at[i])
        for i, (source, target) in enumerate(
            [
                (joint_t_hbm, joint_t),
                (first_hbm, first),
                (joint_hbm, joint),
                (packed_hbm.at[:, :, core], w_own),
                (tokens_hbm, tokens),
                (grad_hidden_hbm, grad_hidden),
            ]
        )
    ]
    for copy in local:
        copy.start()
    half = PLANES // 2
    core_w = [
        remote(
            packed_hbm.at[pl.ds(i * half, half), :, 1 - core],
            w_core.at[pl.ds(i * half, half)],
            w_sems,
            i,
            core_peer,
        )
        for i in range(2)
    ]
    for copy in core_w:
        copy.start()

    side_kv = {}
    for j in order:
        core_kv[j].wait()
        for k in range(S2):
            total = dkv_ref[planes[j], k, core].astype(f32) + kv_near[j, k].astype(f32)
            kv_send[j, k] = total.astype(bf)
        for k in range(1, S2):
            side_kv[j, k] = remote(
                kv_send.at[j, lax.rem(s2 + S2 - k, S2)],
                kv_far.at[j, k - 1],
                kv_sems,
                PLANES + j * (S2 - 1) + k - 1,
                side_peer(S2 - k),
            )
            side_kv[j, k].start()

    local[3].wait()
    w_moves = []

    def w_copy(source, target, device):
        copy = remote(source, target, w_sems, 2 + len(w_moves), device)
        w_moves.append(copy)
        copy.start()
        return copy

    def add_core(i):
        core_w[i].wait()

        def body(step, carry):
            p, a, g = i * half + step // (S2 * groups), lax.rem(step // groups, S2), lax.rem(step, groups)
            w_core[p, a, g] = (w_own[p, a, g].astype(f32) + w_core[p, a, g].astype(f32)).astype(bf)
            return carry

        lax.fori_loop(0, half * S2 * groups, body, 0)

    add_core(0)
    y1 = [
        w_copy(w_core.at[pl.ds(0, half), :, lax.rem(group + k, groups)], w_y1.at[k - 1], group_peer(k))
        for k in range(1, groups)
    ]
    add_core(1)
    x2 = [
        w_copy(w_core.at[pl.ds(half, half), lax.rem(s2 + k, S2)], w_x2.at[k - 1], side_peer(k))
        for k in range(1, S2)
    ]

    plane_parts = {}
    local[0].wait()
    for j in order:
        dk = kv_send[j, s2].astype(f32)
        for k in range(1, S2):
            side_kv[j, k].wait()
            dk = dk + kv_far[j, k - 1].astype(f32)
        dk = dk.T
        cos, sin = turn_ref[j, :HALF], turn_ref[j, HALF:]
        rows = []
        for part in (dq_ref[j], dk[:QW]):
            for h in range(HP):
                upper, lower = part[h * HD : h * HD + HALF], part[h * HD + HALF : (h + 1) * HD]
                rows += [upper * cos + lower * sin, lower * cos - upper * sin]
        rows += [dk[QW:], jnp.zeros((mixed.shape[1] - 3 * QW, T), f32)]
        turned = jnp.concatenate(rows, axis=0)
        mixed[j] = turned.astype(bf)
        part = jnp.dot(turned.T.astype(bf), joint_t[...], preferred_element_type=f32)
        z_send[j] = part.astype(bf)
        if j:
            plane_parts[j] = remote(z_send.at[j], z_got.at[j - 1], z_sems, j - 1, plane_peer(PLANES - j))
            plane_parts[j].start()

    local[1].wait()
    jg_t[...] = jnp.dot(mixed[0], first[0], preferred_element_type=f32)
    for j in range(1, PLANES):
        jg_t[...] += jnp.dot(mixed[j], first[j], preferred_element_type=f32)
    local[2].wait()
    width = jg_t.shape[0]
    shard_rows = jg.shape[3]
    per = 128
    for i in range(D // per):
        block = jg_t[:, i * per : (i + 1) * per].T
        gain_part = jnp.sum(block * joint[i * per : (i + 1) * per, :].astype(f32), axis=1, keepdims=True)
        whole = jnp.concatenate([block, jnp.broadcast_to(gain_part, (per, per))], axis=1).astype(bf)
        j_rows = whole.astype(f32)
        first_row = i * per
        row = first_row
        while row < first_row + per:
            shard, offset = divmod(row, shard_rows)
            count = min(shard_rows - offset, first_row + per - row)
            jg[shard // S, shard % S // 2, shard % 2, offset : offset + count] = j_rows[
                row - first_row : row - first_row + count
            ].astype(bf)
            row += count
    j_moves = []

    def j_copy(source, target, device):
        copy = remote(source, target, j_sems, len(j_moves), device)
        j_moves.append(copy)
        copy.start()
        return copy

    j_first = j_copy(jg.at[:, :, 1 - core], j_core, core_peer)

    def sum_into(target, terms):
        total = terms[0].astype(f32)
        for term in terms[1:]:
            total = total + term.astype(f32)
        return total.astype(target)

    for copy in y1:
        copy.wait()
    for p in range(half):
        for a in range(S2):
            w_y1[0, p, a] = sum_into(bf, [w_core[p, a, group]] + [w_y1[k, p, a] for k in range(groups - 1)])
    x1 = [w_copy(w_y1.at[0, :, lax.rem(s2 + k, S2)], w_x1.at[k - 1], side_peer(k)) for k in range(1, S2)]
    for copy in x2:
        copy.wait()
    for p in range(half):
        for g in range(groups):
            w_x2[0, p, g] = sum_into(bf, [w_core[half + p, s2, g]] + [w_x2[k, p, g] for k in range(S2 - 1)])
    y2 = [w_copy(w_x2.at[0, :, lax.rem(group + k, groups)], w_y2.at[k - 1], group_peer(k)) for k in range(1, groups)]

    j_first.wait()
    for p in range(PLANES):
        for a in range(S2):
            j_core[p, a] = sum_into(bf, [jg[p, a, core], j_core[p, a]])
    j_second = [j_copy(j_core.at[:, lax.rem(s2 + k, S2)], j_side.at[k - 1], side_peer(k)) for k in range(1, S2)]

    local[4].wait()
    local[5].wait()
    for j in range(1, PLANES):
        plane_parts[j].wait()
    strip = 64

    def norm_back(i, carry):
        rows = pl.ds(pl.multiple_of(i * strip, strip), strip)
        grad = z_send[0, rows].astype(f32)
        for j in range(1, PLANES):
            grad = grad + z_got[j - 1, rows].astype(f32)
        values = tokens[rows].astype(f32)
        centred = values - jnp.mean(values, axis=-1, keepdims=True)
        scale = lax.rsqrt(jnp.mean(centred * centred, axis=-1, keepdims=True) + norm_eps)
        normal = centred * scale
        grad = grad * gain_ref[0:1]
        grad = grad - jnp.mean(grad, axis=-1, keepdims=True) - normal * jnp.mean(grad * normal, axis=-1, keepdims=True)
        grad_hidden[rows] = grad_hidden[rows] + grad * scale
        return carry

    lax.fori_loop(0, T // strip, norm_back, 0)

    blocks = T // BLOCK
    piece = BLOCK // n

    def d_copy(source, target, base, k):
        return remote(source.at[lax.rem(me + k, n)], target.at[me], d_sems, base + k, (lax.rem(me + k, n), group))

    for i in range(n):
        d_send[i] = jnp.concatenate(
            [grad_hidden[b * BLOCK + i * piece : b * BLOCK + (i + 1) * piece] for b in range(blocks)], axis=0
        ).astype(bf)
    out_deal = [d_copy(d_send, d_mid, 0, k) for k in range(1, n)]
    for copy in out_deal:
        copy.start()
    d_mid[me] = d_send[me]

    for copy in x1 + y2:
        copy.wait()
    for p in range(half):
        w_plane[p] = sum_into(bf, [w_y1[0, p, s2]] + [w_x1[k, p] for k in range(S2 - 1)])
        w_plane[half + p] = sum_into(bf, [w_x2[0, p, group]] + [w_y2[k, p] for k in range(groups - 1)])
    w_last = [w_copy(w_plane.at[lax.rem(plane + k, PLANES)], w_z.at[k - 1], plane_peer(k)) for k in range(1, PLANES)]
    for copy in j_second:
        copy.wait()
    for p in range(PLANES):
        j_side[0, p] = sum_into(bf, [j_core[p, s2]] + [j_side[k, p] for k in range(S2 - 1)])
    j_third = [j_copy(j_side.at[0, lax.rem(plane + k, PLANES)], j_plane.at[plane], plane_peer(k)) for k in range(1, PLANES)]
    j_plane[plane] = j_side[0, plane]

    for copy in out_deal:
        copy.wait()
    for i in range(n):
        chosen = []
        for b in range(blocks):
            wanted = deal_ref[i * blocks + b]
            held = d_mid[wanted // blocks].astype(f32)
            part = held[:piece]
            for other in range(1, blocks):
                part = jnp.where(lax.rem(wanted, blocks) == other, held[other * piece : (other + 1) * piece], part)
            chosen.append(part)
        d_back[i] = jnp.concatenate(chosen, axis=0).astype(bf)
    back_deal = [d_copy(d_back, d_got, n, k) for k in range(1, n)]
    for copy in back_deal:
        copy.start()
    d_got[me] = d_back[me]

    for copy in w_last:
        copy.wait()
    w_all[group] = sum_into(bf, [w_plane[plane]] + [w_z[k] for k in range(PLANES - 1)])
    w_gather = [w_copy(w_all.at[group], w_all.at[group], group_peer(k)) for k in range(1, groups)]
    for copy in j_third:
        copy.wait()
    j_group[group] = j_plane[...]
    j_last = [j_copy(j_plane, j_group.at[group], group_peer(k)) for k in range(1, groups)]

    for copy in back_deal:
        copy.wait()
    for b in range(blocks):
        for i in range(0, n, 2):
            rows = [d_got[i + e].astype(f32)[b * piece : (b + 1) * piece] for e in range(2)]
            dealt_ref[b * BLOCK + i * piece : b * BLOCK + (i + 2) * piece] = jnp.concatenate(rows, axis=0).astype(bf)
    for copy in w_gather:
        copy.wait()
    for g in range(groups):
        shard_ref[g] = w_all[g].astype(f32)
    for copy in j_last:
        copy.wait()
    for p in range(PLANES):
        total = j_group[0, p].astype(f32)
        for g in range(1, groups):
            total = total + j_group[g, p].astype(f32)
        joint_out_ref[p] = total


def tail(n, groups, deal, dqt, dkv, turn, joint, joint_t, first, tokens, grad_hidden, gain, packed):
    bf, f32 = jnp.bfloat16, jnp.float32
    S2 = n // PLANES // 2
    T, D = tokens.shape
    width = joint.shape[1]
    wide = width + 128
    rows = D // n
    part = packed.shape[4]
    piece_rows = T // n
    half = PLANES // 2
    any_, vm, sm = (pl.BlockSpec(memory_space=m) for m in (pl.ANY, pltpu.VMEM, pltpu.SMEM))
    sems = lambda count: pltpu.SemaphoreType.DMA((2, count))
    return pl.pallas_call(
        functools.partial(tail_kernel, n, groups),
        out_shape=(
            jax.ShapeDtypeStruct((T, D), bf),
            jax.ShapeDtypeStruct((groups, part, D), f32),
            jax.ShapeDtypeStruct((PLANES, rows, wide), f32),
        ),
        in_specs=[sm, vm, vm, vm, any_, any_, any_, any_, any_, vm, any_],
        out_specs=(vm, vm, vm),
        scratch_shapes=[
            pltpu.VMEM((D, width), bf),
            pltpu.VMEM((width, D), bf),
            pltpu.VMEM((PLANES, T, D), bf),
            pltpu.VMEM((T, D), bf),
            pltpu.VMEM((T, D), f32),
            pltpu.VMEM((PLANES, S2, groups, part, D), bf),
            pltpu.SemaphoreType.DMA((6,)),
            pltpu.VMEM((PLANES, S2, T, 2 * QW), bf),
            pltpu.VMEM((PLANES, S2, T, 2 * QW), bf),
            pltpu.VMEM((PLANES, S2 - 1, T, 2 * QW), bf),
            sems(PLANES * S2),
            pltpu.VMEM((PLANES, width, T), bf),
            pltpu.VMEM((PLANES, T, D), bf),
            pltpu.VMEM((PLANES - 1, T, D), bf),
            sems(PLANES - 1),
            pltpu.VMEM((width, D), f32),
            pltpu.VMEM((PLANES, S2, 2, rows, wide), bf),
            pltpu.VMEM((PLANES, S2, rows, wide), bf),
            pltpu.VMEM((S2 - 1, PLANES, rows, wide), bf),
            pltpu.VMEM((PLANES, rows, wide), bf),
            pltpu.VMEM((groups, PLANES, rows, wide), bf),
            sems(S2 + PLANES + groups - 2),
            pltpu.VMEM((PLANES, S2, groups, part, D), bf),
            pltpu.VMEM((groups - 1, half, S2, part, D), bf),
            pltpu.VMEM((S2 - 1, half, part, D), bf),
            pltpu.VMEM((S2 - 1, half, groups, part, D), bf),
            pltpu.VMEM((groups - 1, half, part, D), bf),
            pltpu.VMEM((PLANES, part, D), bf),
            pltpu.VMEM((PLANES - 1, part, D), bf),
            pltpu.VMEM((groups, part, D), bf),
            sems(2 + 3 * (groups - 1) + 2 * (S2 - 1) + PLANES - 1),
            pltpu.VMEM((n, piece_rows, D), bf),
            pltpu.VMEM((n, piece_rows, D), bf),
            pltpu.VMEM((n, piece_rows, D), bf),
            pltpu.VMEM((n, piece_rows, D), bf),
            sems(2 * n),
        ],
        compiler_params=pltpu.CompilerParams(collective_id=0, has_side_effects=True, vmem_limit_bytes=60 << 20),
    )(deal, dqt, dkv, turn, joint, joint_t, first, tokens, grad_hidden, gain, packed)


def layer_norm(values, weights):
    centred = values - jnp.mean(values, axis=-1, keepdims=True)
    spread = jnp.mean(centred * centred, axis=-1, keepdims=True)
    return centred * lax.rsqrt(spread + norm_eps) * weights


def on_device(
    n,
    groups,
    tokens,
    cotangent,
    lengths,
    deal,
    joint_projection,
    output_projection,
    expand_weight,
    contract_weight,
    gain_first,
    gain_second,
):
    bf, f32 = jnp.bfloat16, jnp.float32
    T, D = tokens.shape[1:]
    S = n // PLANES
    S2 = S // 2
    me = lax.axis_index("ctx")
    plane = me // S

    def over_planes(x, k):
        return lax.ppermute(x, "ctx", [(h * S + s, (h + k) % PLANES * S + s) for h in range(PLANES) for s in range(S)])

    def turned(x, shift):
        return lax.dynamic_slice_in_dim(jnp.concatenate([x, x], axis=0), shift, x.shape[0], 0)

    tokens_own = tokens[0]
    first, qt, kv, joint, joint_t, turn, gains, out_w, exp_w, con_w = front(
        n,
        groups,
        lengths,
        tokens_own,
        joint_projection,
        gain_first,
        gain_second,
        output_projection,
        expand_weight,
        contract_weight,
    )
    out_w, exp_w, con_w = (w.reshape(-1, w.shape[-1]) for w in (out_w, exp_w, con_w))
    gain_one, gain_two = gains[0], gains[1]
    ot, lowt, lse = attn_fwd(n, lengths, qt, kv)

    parts = [lowt[0]] + [over_planes(lowt[k], -k) for k in range(1, PLANES)]
    attended_t = turned(jnp.stack(parts), (PLANES - plane) % PLANES).reshape(D, T)

    x = tokens_own.astype(f32)
    grad_out = cotangent[0]
    hidden = x + jnp.einsum("dt,de->te", attended_t, out_w, preferred_element_type=f32)
    second = layer_norm(hidden, gain_two).astype(bf)
    expanded = jnp.dot(second, exp_w, preferred_element_type=f32)

    def gated(values):
        return jax.nn.gelu(values[:, :FF], approximate=False) * values[:, FF:]

    activated_f, gated_pull = jax.vjp(gated, expanded)
    activated = activated_f.astype(bf)
    output = (hidden + jnp.dot(activated, con_w, preferred_element_type=f32)).astype(bf)

    grad_activated = jnp.einsum("td,fd->tf", grad_out, con_w, preferred_element_type=f32)
    grad_expanded = gated_pull(grad_activated)[0].astype(bf)
    grad_second = jnp.einsum("tf,df->td", grad_expanded, exp_w, preferred_element_type=f32)
    _, second_pull = jax.vjp(layer_norm, hidden, gain_two)
    grad_hidden_norm, grad_gain_two = second_pull(grad_second)
    grad_hidden = grad_out.astype(f32) + grad_hidden_norm
    grad_branch = grad_hidden.astype(bf)
    grad_attended = jnp.einsum("de,te->dt", out_w, grad_branch, preferred_element_type=f32).astype(bf)
    rel = turned(grad_attended.reshape(PLANES, QW, T), plane)
    gt = jnp.stack([rel[0]] + [over_planes(rel[k], k) for k in range(1, PLANES)])

    grad_contract = jnp.einsum("tf,td->fd", activated, grad_out, preferred_element_type=f32)
    grad_expand = jnp.einsum("td,tf->df", second, grad_expanded, preferred_element_type=f32)
    grad_output = jnp.einsum("dt,te->de", attended_t, grad_branch, preferred_element_type=f32)

    dqt, dkv = attn_bwd(n, lengths, qt, kv, ot, lse, gt)

    def sharded(x):
        return x.astype(bf).reshape(n, x.shape[0] // n, x.shape[1])

    gain_rows = jnp.pad(grad_gain_two.reshape(n, 1, D // n), ((0, 0), (0, 7), (0, D - D // n))).astype(bf)
    rows = D // n
    wide = grad_expand.shape[1] // D
    pieces = [sharded(grad_output)]
    pieces += [sharded(grad_expand[:, i * D : (i + 1) * D]) for i in range(wide)]
    pieces += [sharded(grad_contract), gain_rows]
    used = sum(p.shape[1] for p in pieces)
    part = -(-used // (groups * 16)) * 16
    packed = jnp.concatenate(pieces + [jnp.zeros((n, groups * part - used, D), bf)], axis=1)
    packed = packed.reshape(PLANES, S2, 2, groups, part, D)

    dealt, shards, joint_raw = tail(
        n,
        groups,
        deal[0],
        dqt,
        dkv.reshape(PLANES, S2, 2, T, 2 * QW),
        turn,
        joint,
        joint_t,
        first,
        tokens_own,
        grad_hidden,
        gains,
        packed,
    )
    shards = shards.reshape(groups * part, D)
    shard_output = shards[:rows]
    shard_expand = jnp.concatenate([shards[(1 + i) * rows : (2 + i) * rows] for i in range(wide)], axis=1)
    after = (1 + wide) * rows
    ff_rows = grad_contract.shape[0] // n
    shard_contract = shards[after : after + ff_rows]
    shard_gain_two = shards[after + ff_rows, :rows]
    shard_joint = jnp.transpose(joint_raw[:, :, : 3 * QW].reshape(PLANES, rows, 3, QW), (1, 2, 0, 3))
    shard_joint = shard_joint.reshape(rows, 3 * PLANES * QW)
    shard_gain_one = jnp.sum(joint_raw[:, :, -1], axis=0) / lax.dynamic_slice_in_dim(gain_one, me * rows, rows)
    return (
        output[None],
        dealt[None],
        shard_joint,
        shard_output,
        shard_expand,
        shard_contract,
        shard_gain_one,
        shard_gain_two,
    )


def solution(mesh):
    return jax.shard_map(
        functools.partial(on_device, mesh.shape["ctx"], mesh.shape["fsdp"]),
        mesh=mesh,
        in_specs=(
            P("fsdp", "ctx", None),
            P("fsdp", "ctx", None),
            P("fsdp", None),
            P("fsdp", None),
            P("fsdp", None),
            P("fsdp", None),
            P("fsdp", None),
            P("fsdp", None),
            P("fsdp"),
            P("fsdp"),
        ),
        out_specs=(
            P("fsdp", "ctx", None),
            P("fsdp", "ctx", None),
            P("ctx", None),
            P("ctx", None),
            P("ctx", None),
            P("ctx", None),
            P("ctx"),
            P("ctx"),
        ),
        check_vma=False,
    )
```

```python
import functools

import jax
import jax.numpy as jnp
from jax import lax
from jax.experimental import pallas as pl
from jax.experimental.pallas import tpu as pltpu
from jax.sharding import PartitionSpec as P

FF = 1152
HEADS = 12
HEAD_DIM = 64
BLOCK = 128
PLANES = 4
HD = HEAD_DIM
HALF = HEAD_DIM // 2
HP = HEADS // PLANES
QW = HP * HEAD_DIM
rope_base = 160000.0
norm_eps = 1e-05
MASKED = -1e30


def ends_of(lengths_ref, count):
    ends, total = [], 0
    for i in range(count):
        total = total + lengths_ref[0, i]
        ends.append(total)
    return ends


def span_of(index, ends):
    begin, end = jnp.zeros_like(index), jnp.full_like(index, ends[0])
    for before, after in zip(ends[:-1], ends[1:]):
        begin = jnp.where(index >= before, before, begin)
        end = jnp.where(index >= before, after, end)
    return begin, end


def head_rows(x, head):
    rows = lax.broadcasted_iota(jnp.int32, x.shape, 0)
    return jnp.where((rows >= head * HD) & (rows < (head + 1) * HD), x, jnp.zeros_like(x))


def query_block(n, b, T, ends):
    S = n // PLANES
    me = lax.axis_index("ctx")
    base = (lax.rem(me // S + PLANES - b, PLANES) * S + lax.rem(me, S)) * T
    low_begin, low_end = span_of(base, ends)
    high_begin, high_end = span_of(base + T - 1, ends)
    low, high = low_begin // T, (high_end + T - 1) // T
    full_low = jnp.clip((high_begin + T - 1) // T, low, high)
    full_high = jnp.clip(low_end // T, full_low, high)
    begin, end = span_of(base + lax.broadcasted_iota(jnp.int32, (8, T), 1), ends)
    return (low, full_low, full_high, high), begin[0:1], end[0:1]


def over_units(bounds, step):
    low, full_low, full_high, high = bounds

    def run(begin, end, masked):
        def body(u, carry):
            step(u, masked)
            return carry

        lax.fori_loop(begin, end, body, 0)

    run(low, full_low, True)
    in_pairs(full_low, full_high, lambda u: step(u, False))
    run(full_high, high, True)


def in_pairs(begin, end, step):
    pairs = (end - begin) // 2

    def two(i, carry):
        step(begin + 2 * i)
        step(begin + 2 * i + 1)
        return carry

    def one(u, carry):
        step(u)
        return carry

    lax.fori_loop(0, pairs, two, 0)
    lax.fori_loop(begin + 2 * pairs, end, one, 0)


def fwd_kernel(n, count, lengths_ref, qt_ref, kv_ref, ot_ref, lowt_ref, lse_ref, values, scores, top, total, acc):
    units, T, _ = kv_ref.shape
    ends = ends_of(lengths_ref, count)

    def flip(u, carry):
        values[u] = kv_ref[u, :, 128:].T
        return carry

    lax.fori_loop(0, units, flip, 0, unroll=4)

    def one_query_block(b, carry):
        qt = qt_ref[b]
        qheads = [head_rows(qt, h) for h in range(HP)]
        bounds, q_start, q_end = query_block(n, b, T, ends)
        top[...] = jnp.full_like(top, MASKED)
        total[...] = jnp.zeros_like(total)
        acc[...] = jnp.zeros_like(acc)

        def score(u, masked):
            k = kv_ref[u, :, :QW]
            st = [jnp.dot(k, qheads[h], preferred_element_type=jnp.float32) for h in range(HP)]
            if masked:
                at = u * T + lax.broadcasted_iota(jnp.int32, (T, T), 0)
                allowed = (at >= q_start) & (at < q_end)
                st = [jnp.where(allowed, s, MASKED) for s in st]
            for h in range(HP):
                scores[u, h] = st[h]
                top[h] = jnp.maximum(top[h], jnp.max(st[h].reshape(T // 8, 8, T), axis=0))

        over_units(bounds, score)
        m = [jnp.max(top[h], axis=0, keepdims=True) for h in range(HP)]

        def gather(u):
            p = [jnp.exp(scores[u, h] - m[h]) for h in range(HP)]
            for h in range(HP):
                total[h] += jnp.sum(p[h].reshape(T // 8, 8, T), axis=0)
                rows = pl.ds(h * HD, HD)
                acc[rows, :] += jnp.dot(
                    values[u, pl.ds(HD + h * HD, HD), :], p[h].astype(jnp.bfloat16), preferred_element_type=jnp.float32
                )

        in_pairs(bounds[0], bounds[3], gather)
        for h in range(HP):
            rows = pl.ds(h * HD, HD)
            l = jnp.sum(total[h], axis=0, keepdims=True)
            o = acc[rows, :] / l
            ot_ref[b, rows, :] = o
            lowt_ref[b, rows, :] = o.astype(jnp.bfloat16)
            lse_ref[b, h : h + 1, :] = m[h] + jnp.log(l)
        return carry

    lax.fori_loop(0, qt_ref.shape[0], one_query_block, 0)


def attn_fwd(n, lengths, qt, kv):
    B, _, T = qt.shape
    U = kv.shape[0]
    sm, vm = pl.BlockSpec(memory_space=pltpu.SMEM), pl.BlockSpec(memory_space=pltpu.VMEM)
    return pl.pallas_call(
        functools.partial(fwd_kernel, n, lengths.shape[1]),
        out_shape=(
            jax.ShapeDtypeStruct((B, QW, T), jnp.float32),
            jax.ShapeDtypeStruct((B, QW, T), jnp.bfloat16),
            jax.ShapeDtypeStruct((B, 8, T), jnp.float32),
        ),
        in_specs=[sm, vm, vm],
        out_specs=(vm, vm, vm),
        scratch_shapes=[
            pltpu.VMEM((U, 256, T), jnp.bfloat16),
            pltpu.VMEM((U, HP, T, T), jnp.float32),
            pltpu.VMEM((HP, 8, T), jnp.float32),
            pltpu.VMEM((HP, 8, T), jnp.float32),
            pltpu.VMEM((QW, T), jnp.float32),
        ],
        compiler_params=pltpu.CompilerParams(vmem_limit_bytes=60 << 20),
    )(lengths, qt, kv)


def bwd_kernel(n, count, lengths_ref, qt_ref, kv_ref, ot_ref, lse_ref, gt_ref, dqt_ref, dkv_ref, keys, dk, dv, dq):
    units, T, _ = kv_ref.shape
    ends = ends_of(lengths_ref, count)

    def flip(u, carry):
        keys[u] = kv_ref[u, :, :256].T
        dk[u] = jnp.zeros_like(dk[u])
        dv[u] = jnp.zeros_like(dv[u])
        return carry

    lax.fori_loop(0, units, flip, 0, unroll=4)

    def one_query_block(b, carry):
        qt, gt = qt_ref[b], gt_ref[b]
        zero = jnp.zeros((HD, T), jnp.bfloat16)
        qheads = [head_rows(qt, h) for h in range(HP)]
        gheads = [head_rows(gt, h) for h in range(HP)]
        gpad = [jnp.concatenate([zero, x], axis=0) for x in gheads]
        q = jnp.concatenate([jnp.concatenate([x, zero], axis=0).T for x in qheads], axis=0)
        g = jnp.concatenate([x.T for x in gpad], axis=0)
        bounds, q_start, q_end = query_block(n, b, T, ends)
        prod = gt.astype(jnp.float32) * ot_ref[b]
        delta = [jnp.sum(prod[h * HD : (h + 1) * HD], axis=0, keepdims=True) for h in range(HP)]
        lse = [lse_ref[b, h : h + 1, :] for h in range(HP)]
        dq[...] = jnp.zeros_like(dq)

        def one_unit(u, masked):
            k, v = kv_ref[u, :, :QW], kv_ref[u, :, 128:]
            st = [jnp.dot(k, qheads[h], preferred_element_type=jnp.float32) for h in range(HP)]
            dp = [jnp.dot(v, gpad[h], preferred_element_type=jnp.float32) for h in range(HP)]
            st = [st[h] - lse[h] for h in range(HP)]
            if masked:
                at = u * T + lax.broadcasted_iota(jnp.int32, (T, T), 0)
                allowed = (at >= q_start) & (at < q_end)
                st = [jnp.where(allowed, s, MASKED) for s in st]
            p = [jnp.exp(s) for s in st]
            ds = [(p[h] * (dp[h] - delta[h])).astype(jnp.bfloat16) for h in range(HP)]
            p = [x.astype(jnp.bfloat16) for x in p]
            dv[u] += jnp.dot(jnp.concatenate(p, axis=1), g, preferred_element_type=jnp.float32)
            dk[u] += jnp.dot(jnp.concatenate(ds, axis=1), q, preferred_element_type=jnp.float32)
            for h in range(HP):
                rows = pl.ds(h * HD, HD)
                dq[rows, :] += jnp.dot(keys[u, rows, :], ds[h], preferred_element_type=jnp.float32)

        over_units(bounds, one_unit)
        dqt_ref[b] = dq[...] * (HD**-0.5)
        return carry

    lax.fori_loop(0, qt_ref.shape[0], one_query_block, 0)

    def out(u, carry):
        dkv_ref[u, :, :128] = dk[u, :, :128].astype(jnp.bfloat16)
        dkv_ref[u, :, 128:256] = (dk[u, :, 128:] + dv[u, :, :128]).astype(jnp.bfloat16)
        dkv_ref[u, :, 256:] = dv[u, :, 128:].astype(jnp.bfloat16)
        return carry

    lax.fori_loop(0, units, out, 0, unroll=2)


def attn_bwd(n, lengths, qt, kv, ot, lse, gt):
    B, _, T = qt.shape
    U = kv.shape[0]
    sm, vm = pl.BlockSpec(memory_space=pltpu.SMEM), pl.BlockSpec(memory_space=pltpu.VMEM)
    return pl.pallas_call(
        functools.partial(bwd_kernel, n, lengths.shape[1]),
        out_shape=(jax.ShapeDtypeStruct((B, QW, T), jnp.float32), jax.ShapeDtypeStruct((U, T, 2 * QW), jnp.bfloat16)),
        in_specs=[sm] + [vm] * 5,
        out_specs=(vm, vm),
        scratch_shapes=[
            pltpu.VMEM((U, 256, T), jnp.bfloat16),
            pltpu.VMEM((U, T, 256), jnp.float32),
            pltpu.VMEM((U, T, 256), jnp.float32),
            pltpu.VMEM((QW, T), jnp.float32),
        ],
        compiler_params=pltpu.CompilerParams(vmem_limit_bytes=60 << 20),
    )(lengths, qt, kv, ot, lse, gt)
def front_kernel(
    n,
    groups,
    count,
    lengths_ref,
    tokens_ref,
    joint_ref,
    gain_one_ref,
    gain_two_ref,
    freq_ref,
    out_hbm,
    exp_hbm,
    con_hbm,
    first_ref,
    qt_ref,
    kv_ref,
    joint_t_out,
    turn_ref,
    gains_ref,
    out_all,
    exp_all,
    con_all,
    held,
    t_sems,
    cols,
    cols_all,
    gain_held,
    g_sems,
    kv_own,
    kv_sems,
    own_sems,
    w_sems,
    w_local,
    joint_rows,
    out_held,
    exp_held,
    con_held,
):
    bf, f32 = jnp.bfloat16, jnp.float32
    S = n // PLANES
    S2 = S // 2
    T, D = tokens_ref.shape
    me, group = lax.axis_index("ctx"), lax.axis_index("fsdp")
    plane, side = me // S, lax.rem(me, S)
    s2, core = side // 2, lax.rem(side, 2)

    def at(p, a, c, g):
        return (p * S + a * 2 + c, g)

    def side_peer(k):
        return at(plane, lax.rem(s2 + k, S2), core, group)

    def group_peer(k):
        return at(plane, s2, core, lax.rem(group + k, groups))

    core_peer = at(plane, s2, 1 - core, group)

    def remote(source, target, sems, index, device):
        return pltpu.make_async_remote_copy(
            src_ref=source,
            dst_ref=target,
            send_sem=sems.at[0, index],
            recv_sem=sems.at[1, index],
            device_id=device,
            device_id_type=pl.DeviceIdType.MESH,
        )

    barrier = pltpu.get_barrier_semaphore()

    def greet(device):
        pl.semaphore_signal(barrier, inc=1, device_id=device, device_id_type=pl.DeviceIdType.MESH)

    for k in range(1, PLANES):
        greet(at(lax.rem(plane + k, PLANES), s2, core, group))
    for k in range(1, S2):
        greet(side_peer(k))
    for k in range(1, groups):
        greet(group_peer(k))
    greet(core_peer)
    pl.semaphore_wait(barrier, PLANES - 1 + S2 - 1 + groups - 1 + 1)

    def up(p):
        return remote(held.at[p], held.at[p], t_sems, p, at(plane + 1, s2, core, group))

    def down(p):
        return remote(held.at[p], held.at[p], t_sems, PLANES + p, at(plane - 1, s2, core, group))

    held[plane] = tokens_ref[...]

    @pl.when(plane < PLANES - 1)
    def _():
        up(plane).start()

    @pl.when(plane > 0)
    def _():
        down(plane).start()

    pair = 2 * QW
    for part in range(3):
        window = joint_ref[:, pl.ds(pl.multiple_of(part * D + plane // 2 * pair, 128), pair)].T
        chosen = jnp.where(lax.rem(plane, 2) == 0, window[:QW].astype(f32), window[QW:].astype(f32))
        half = 3 * QW // 2
        low, high = part * QW, (part + 1) * QW
        for c in range(2):
            begin, end = max(low, c * half), min(high, (c + 1) * half)
            if begin < end:
                cols[c, begin - c * half : end - c * half] = chosen[begin - low : end - low].astype(bf)
    gain_held[group] = jnp.zeros_like(gain_held[group])
    gain_held[group, 0:1] = gain_one_ref[...].astype(f32)
    gain_held[group, 1:2] = gain_two_ref[...].astype(f32)
    col_moves = [
        remote(cols.at[core], cols_all.at[group, core], g_sems, k - 1, group_peer(k)) for k in range(1, groups)
    ]
    col_hands = []
    for k in range(1, groups):
        came = cols_all.at[lax.rem(group + groups - k, groups), core]
        col_hands.append(remote(came, came, g_sems, 2 * (groups - 1) + k - 1, core_peer))
    gain_moves = [
        remote(gain_held.at[group], gain_held.at[group], g_sems, groups - 1 + k - 1, group_peer(k))
        for k in range(1, groups)
    ]
    for copy in gain_moves + col_moves:
        copy.start()
    cols_all[group] = cols[...]

    weights = [(out_hbm, out_all, out_held), (exp_hbm, exp_all, exp_held), (con_hbm, con_all, con_held)]
    w_in, w_own, w_first, w_second = [], [], [], []
    for i, (source, target, bounce) in enumerate(weights):
        w_in.append(pltpu.make_async_copy(source, bounce, w_local.at[0, i]))
        w_own.append(pltpu.make_async_copy(bounce, target.at[group], w_local.at[1, i]))
        for k in range(1, groups):
            index = (i * (groups - 1) + k - 1) * 2
            w_first.append(remote(source.at[core], target.at[group, core], w_sems, index, group_peer(k)))
            came = lax.rem(group + groups - k, groups)
            w_second.append(remote(target.at[came, core], target.at[came, core], w_sems, index + 1, core_peer))
    for copy in w_in:
        copy.start()

    ends = ends_of(lengths_ref, count)
    for j in range(PLANES):
        base = (lax.rem(plane + PLANES - j, PLANES) * S + side) * T
        index = base + lax.broadcasted_iota(jnp.int32, (8, T), 1)
        begin, _ = span_of(index, ends)
        angles = (index - begin)[0:1].astype(f32) * freq_ref[...]
        turn_ref[j, :HALF] = jnp.cos(angles)
        turn_ref[j, HALF:] = jnp.sin(angles)

    strip = 64

    def kv_unit(p, a, c):
        return p * S + a * 2 + c

    def side_kv(j, k):
        p = lax.rem(plane + PLANES - j, PLANES)
        return remote(kv_own.at[j], kv_ref.at[kv_unit(p, s2, core)], kv_sems, j * (2 * S2 - 1) + k - 1, side_peer(k))

    def core_kv(j, k):
        p = lax.rem(plane + PLANES - j, PLANES)
        unit = kv_unit(p, lax.rem(s2 + S2 - k, S2), core)
        source = kv_own.at[j] if k == 0 else kv_ref.at[unit]
        return remote(source, kv_ref.at[unit], kv_sems, j * (2 * S2 - 1) + S2 - 1 + k, core_peer)

    def own_kv(j):
        p = lax.rem(plane + PLANES - j, PLANES)
        return pltpu.make_async_copy(kv_own.at[j], kv_ref.at[kv_unit(p, s2, core)], own_sems.at[j])

    def process(p):
        j = lax.rem(plane + PLANES - p, PLANES)

        def norm(i, carry):
            rows = pl.ds(pl.multiple_of(i * strip, strip), strip)
            values = held[p, rows].astype(f32)
            centred = values - jnp.mean(values, axis=-1, keepdims=True)
            spread = jnp.mean(centred * centred, axis=-1, keepdims=True)
            first_ref[j, rows] = (centred * lax.rsqrt(spread + norm_eps) * gains_ref[0:1]).astype(bf)
            return carry

        lax.fori_loop(0, T // strip, norm, 0)
        mixed = lax.dot_general(
            joint_t_out[: 3 * QW], first_ref[j], (((1,), (1,)), ((), ())), preferred_element_type=f32
        )
        cos, sin = turn_ref[j, :HALF], turn_ref[j, HALF:]
        turned = []
        for h in range(2 * HP):
            upper, lower = mixed[h * HD : h * HD + HALF], mixed[h * HD + HALF : (h + 1) * HD]
            turned += [upper * cos - lower * sin, lower * cos + upper * sin]
        q = jnp.concatenate(turned[: 2 * HP], axis=0).astype(bf)
        qt_ref[j] = (q.astype(f32) * HEAD_DIM**-0.5).astype(bf)
        kv_own[j] = jnp.concatenate(turned[2 * HP :] + [mixed[2 * QW :]], axis=0).T.astype(bf)
        for k in range(1, S2):
            side_kv(j, k).start()
        core_kv(j, 0).start()
        own_kv(j).start()

    def hand_on(t):
        @pl.when(plane >= t)
        def _():
            up(plane - t).wait_recv()

            @pl.when(plane < PLANES - 1)
            def _():
                up(plane - t).start()

        @pl.when(plane + t < PLANES)
        def _():
            down(plane + t).wait_recv()

            @pl.when(plane > 0)
            def _():
                down(plane + t).start()

    def process_arrived(t):
        below = jnp.where(plane >= t, 1, 0)
        above = jnp.where(plane + t < PLANES, 1, 0)

        def arrived(i, carry):
            process(jnp.where(i < below, plane - t, plane + t))
            return carry

        lax.fori_loop(0, below + above, arrived, 0)

    hand_on(1)
    for copy in gain_moves:
        copy.wait()
    share = D // groups
    total = jnp.zeros((8, D), f32)
    for g in range(groups):
        rows = lax.broadcasted_iota(jnp.int32, (share, D), 0)
        lanes = lax.broadcasted_iota(jnp.int32, (share, D), 1)
        place = jnp.where(lanes == rows + g * share, 1.0, 0.0).astype(bf)
        total = total + jnp.dot(gain_held[g].astype(bf), place, preferred_element_type=f32)
    gains_ref[...] = total
    for copy, hand in zip(col_moves, col_hands):
        copy.wait()
        hand.start()
    for copy in w_first:
        copy.start()
    for copy in w_in:
        copy.wait()
    for copy in w_own:
        copy.start()
    for copy in col_hands:
        copy.wait()
    width = joint_t_out.shape[0]
    for g in range(groups):
        whole = jnp.concatenate([cols_all[g, 0], cols_all[g, 1], jnp.zeros((width - 3 * QW, share), bf)], axis=0)
        if share % 128 == 0:
            joint_t_out[:, g * share : (g + 1) * share] = whole
        else:
            joint_rows[g * share : (g + 1) * share] = whole.T
    if share % 128:
        for i in range(D // 128):
            joint_t_out[:, i * 128 : (i + 1) * 128] = joint_rows[i * 128 : (i + 1) * 128].T

    process(plane)
    hand_on(2)
    process_arrived(1)
    hand_on(3)
    process_arrived(2)
    process_arrived(3)

    for j in range(PLANES):
        for k in range(1, S2):
            side_kv(j, k).wait_recv()
            core_kv(j, k).start()
    for first_move, second_move in zip(w_first, w_second):
        first_move.wait_recv()
        second_move.start()

    for j in range(PLANES):
        own_kv(j).wait()
        for k in range(1, S2):
            side_kv(j, k).wait_send()
        for k in range(S2):
            core_kv(j, k).wait()
    for p in range(PLANES):

        @pl.when((plane < PLANES - 1) & (plane >= p))
        def _(p=p):
            up(p).wait_send()

        @pl.when((plane > 0) & (plane <= p))
        def _(p=p):
            down(p).wait_send()

    for copy in w_own:
        copy.wait()
    for first_move, second_move in zip(w_first, w_second):
        first_move.wait_send()
        second_move.wait()


def front(n, groups, lengths, tokens, joint_shard, gain_first, gain_second, out_w, exp_w, con_w):
    bf, f32 = jnp.bfloat16, jnp.float32
    S2 = n // PLANES // 2
    T, D = tokens.shape
    width = 3 * QW + 64
    share = D // groups
    any_, vm, sm = (pl.BlockSpec(memory_space=m) for m in (pl.ANY, pltpu.VMEM, pltpu.SMEM))
    sems = lambda count: pltpu.SemaphoreType.DMA((2, count))
    halves = lambda w: w.reshape(2, w.shape[0] // 2, w.shape[1])
    frequencies = rope_base ** (-jnp.arange(0, HEAD_DIM, 2).astype(f32) / HEAD_DIM)
    weights = [halves(w) for w in (out_w, exp_w, con_w)]
    return pl.pallas_call(
        functools.partial(front_kernel, n, groups, lengths.shape[1]),
        out_shape=(
            jax.ShapeDtypeStruct((PLANES, T, D), bf),
            jax.ShapeDtypeStruct((PLANES, QW, T), bf),
            jax.ShapeDtypeStruct((n, T, 2 * QW), bf),
            jax.ShapeDtypeStruct((width, D), bf),
            jax.ShapeDtypeStruct((PLANES, 2 * HALF, T), f32),
            jax.ShapeDtypeStruct((8, D), f32),
            *[jax.ShapeDtypeStruct((groups, *w.shape), bf) for w in weights],
        ),
        in_specs=[sm, vm, vm, vm, vm, vm, any_, any_, any_],
        out_specs=(vm, vm, any_, vm, vm, vm, any_, any_, any_),
        scratch_shapes=[
            pltpu.VMEM((PLANES, T, D), bf),
            sems(2 * PLANES),
            pltpu.VMEM((2, 3 * QW // 2, share), bf),
            pltpu.VMEM((groups, 2, 3 * QW // 2, share), bf),
            pltpu.VMEM((groups, 8, share), f32),
            sems(3 * (groups - 1)),
            pltpu.VMEM((PLANES, T, 2 * QW), bf),
            sems(PLANES * (2 * S2 - 1)),
            pltpu.SemaphoreType.DMA((PLANES,)),
            sems(2 * len(weights) * (groups - 1)),
            pltpu.SemaphoreType.DMA((2, len(weights))),
            pltpu.VMEM((D, width), bf),
            *[pltpu.VMEM(w.shape, bf) for w in weights],
        ],
        compiler_params=pltpu.CompilerParams(collective_id=1, has_side_effects=True, vmem_limit_bytes=60 << 20),
    )(
        lengths,
        tokens,
        joint_shard,
        gain_first[None],
        gain_second[None],
        frequencies[:, None],
        *weights,
    )


def tail_kernel(
    n,
    groups,
    deal_ref,
    dq_ref,
    dkv_ref,
    turn_ref,
    joint_t_hbm,
    first_hbm,
    tokens_hbm,
    grad_hidden_hbm,
    gain_ref,
    packed_hbm,
    dealt_ref,
    shard_ref,
    joint_out_ref,
    joint_t,
    first,
    tokens,
    grad_hidden,
    w_own,
    local_sems,
    kv_near,
    kv_send,
    kv_far,
    kv_sems,
    mixed,
    z_send,
    z_got,
    z_sems,
    jg_t,
    jg,
    j_core,
    j_side,
    j_plane,
    j_group,
    j_sems,
    w_core,
    w_y1,
    w_x1,
    w_x2,
    w_y2,
    w_plane,
    w_z,
    w_all,
    w_sems,
    d_send,
    d_mid,
    d_back,
    d_got,
    d_sems,
):
    bf, f32 = jnp.bfloat16, jnp.float32
    S = n // PLANES
    S2 = S // 2
    T, D = tokens.shape
    me, group = lax.axis_index("ctx"), lax.axis_index("fsdp")
    plane, side = me // S, lax.rem(me, S)
    s2, core = side // 2, lax.rem(side, 2)

    def at(p, a, c, g):
        return (p * S + a * 2 + c, g)

    def plane_peer(k):
        return at(lax.rem(plane + k, PLANES), s2, core, group)

    def side_peer(k):
        return at(plane, lax.rem(s2 + k, S2), core, group)

    def group_peer(k):
        return at(plane, s2, core, lax.rem(group + k, groups))

    core_peer = at(plane, s2, 1 - core, group)

    def remote(source, target, sems, index, device):
        return pltpu.make_async_remote_copy(
            src_ref=source,
            dst_ref=target,
            send_sem=sems.at[0, index],
            recv_sem=sems.at[1, index],
            device_id=device,
            device_id_type=pl.DeviceIdType.MESH,
        )

    barrier = pltpu.get_barrier_semaphore()

    def greet(k, carry):
        pl.semaphore_signal(
            barrier, inc=1, device_id=(lax.rem(me + k, n), group), device_id_type=pl.DeviceIdType.MESH
        )
        return carry

    lax.fori_loop(1, n, greet, 0)
    for k in range(1, groups):
        pl.semaphore_signal(barrier, inc=1, device_id=group_peer(k), device_id_type=pl.DeviceIdType.MESH)
    pl.semaphore_wait(barrier, n - 1 + groups - 1)

    order = [*range(1, PLANES), 0]
    planes = [lax.rem(plane + PLANES - j, PLANES) for j in range(PLANES)]
    core_kv = [remote(dkv_ref.at[planes[j], :, 1 - core], kv_near.at[j], kv_sems, j, core_peer) for j in range(PLANES)]
    for j in order:
        core_kv[j].start()
    local = [
        pltpu.make_async_copy(source, target, local_sems.at[i])
        for i, (source, target) in enumerate(
            [
                (joint_t_hbm, joint_t),
                (first_hbm, first),
                (packed_hbm.at[:, :, core], w_own),
                (tokens_hbm, tokens),
                (grad_hidden_hbm, grad_hidden),
            ]
        )
    ]
    for copy in local:
        copy.start()
    half = PLANES // 2
    core_w = [
        remote(
            packed_hbm.at[pl.ds(i * half, half), :, 1 - core],
            w_core.at[pl.ds(i * half, half)],
            w_sems,
            i,
            core_peer,
        )
        for i in range(2)
    ]
    for copy in core_w:
        copy.start()

    side_kv = {}
    for j in order:
        core_kv[j].wait()
        for k in range(S2):
            total = dkv_ref[planes[j], k, core].astype(f32) + kv_near[j, k].astype(f32)
            kv_send[j, k] = total.astype(bf)
        for k in range(1, S2):
            side_kv[j, k] = remote(
                kv_send.at[j, lax.rem(s2 + S2 - k, S2)],
                kv_far.at[j, k - 1],
                kv_sems,
                PLANES + j * (S2 - 1) + k - 1,
                side_peer(S2 - k),
            )
            side_kv[j, k].start()

    w_moves = []

    def w_copy(source, target, device):
        copy = remote(source, target, w_sems, 2 + len(w_moves), device)
        w_moves.append(copy)
        copy.start()
        return copy

    def add_core(i):
        core_w[i].wait()
        if i == 0:
            local[2].wait()

        def body(step, carry):
            p, a, g = i * half + step // (S2 * groups), lax.rem(step // groups, S2), lax.rem(step, groups)
            w_core[p, a, g] = (w_own[p, a, g].astype(f32) + w_core[p, a, g].astype(f32)).astype(bf)
            return carry

        lax.fori_loop(0, half * S2 * groups, body, 0)

    plane_parts = {}
    local[0].wait()
    for j in order:
        dk = kv_send[j, s2].astype(f32)
        for k in range(1, S2):
            side_kv[j, k].wait()
            dk = dk + kv_far[j, k - 1].astype(f32)
        dk = dk.T
        cos, sin = turn_ref[j, :HALF], turn_ref[j, HALF:]
        rows = []
        for part in (dq_ref[j], dk[:QW]):
            for h in range(HP):
                upper, lower = part[h * HD : h * HD + HALF], part[h * HD + HALF : (h + 1) * HD]
                rows += [upper * cos + lower * sin, lower * cos - upper * sin]
        rows += [dk[QW:], jnp.zeros((mixed.shape[1] - 3 * QW, T), f32)]
        turned = jnp.concatenate(rows, axis=0)
        mixed[j] = turned.astype(bf)
        part = jnp.dot(turned.T.astype(bf), joint_t[...], preferred_element_type=f32)
        z_send[j] = part.astype(bf)
        if j:
            plane_parts[j] = remote(z_send.at[j], z_got.at[j - 1], z_sems, j - 1, plane_peer(PLANES - j))
            plane_parts[j].start()
        if j == order[0]:
            add_core(0)
            y1 = [
                w_copy(w_core.at[pl.ds(0, half), :, lax.rem(group + k, groups)], w_y1.at[k - 1], group_peer(k))
                for k in range(1, groups)
            ]
        elif j == order[1]:
            add_core(1)
            x2 = [
                w_copy(w_core.at[pl.ds(half, half), lax.rem(s2 + k, S2)], w_x2.at[k - 1], side_peer(k))
                for k in range(1, S2)
            ]

    local[1].wait()
    jg_t[...] = jnp.dot(mixed[0], first[0], preferred_element_type=f32)
    for j in range(1, PLANES):
        jg_t[...] += jnp.dot(mixed[j], first[j], preferred_element_type=f32)
    width = jg_t.shape[0]
    shard_rows = jg.shape[3]
    per = 128
    for i in range(D // per):
        block = jg_t[:, i * per : (i + 1) * per]
        gain_part = jnp.sum(block * joint_t[:, i * per : (i + 1) * per].astype(f32), axis=0, keepdims=True)
        whole = jnp.concatenate([block, jnp.broadcast_to(gain_part, (per, per))], axis=0).T.astype(bf)
        j_rows = whole.astype(f32)
        first_row = i * per
        row = first_row
        while row < first_row + per:
            shard, offset = divmod(row, shard_rows)
            count = min(shard_rows - offset, first_row + per - row)
            jg[shard // S, shard % S // 2, shard % 2, offset : offset + count] = j_rows[
                row - first_row : row - first_row + count
            ].astype(bf)
            row += count
    j_moves = []

    def j_copy(source, target, device):
        copy = remote(source, target, j_sems, len(j_moves), device)
        j_moves.append(copy)
        copy.start()
        return copy

    j_first = j_copy(jg.at[:, :, 1 - core], j_core, core_peer)

    def sum_into(target, terms):
        total = terms[0].astype(f32)
        for term in terms[1:]:
            total = total + term.astype(f32)
        return total.astype(target)

    for copy in y1:
        copy.wait()
    for p in range(half):
        for a in range(S2):
            w_y1[0, p, a] = sum_into(bf, [w_core[p, a, group]] + [w_y1[k, p, a] for k in range(groups - 1)])
    x1 = [w_copy(w_y1.at[0, :, lax.rem(s2 + k, S2)], w_x1.at[k - 1], side_peer(k)) for k in range(1, S2)]
    for copy in x2:
        copy.wait()
    for p in range(half):
        for g in range(groups):
            w_x2[0, p, g] = sum_into(bf, [w_core[half + p, s2, g]] + [w_x2[k, p, g] for k in range(S2 - 1)])
    y2 = [w_copy(w_x2.at[0, :, lax.rem(group + k, groups)], w_y2.at[k - 1], group_peer(k)) for k in range(1, groups)]

    j_first.wait()
    for p in range(PLANES):
        for a in range(S2):
            j_core[p, a] = sum_into(bf, [jg[p, a, core], j_core[p, a]])
    j_second = [j_copy(j_core.at[:, lax.rem(s2 + k, S2)], j_side.at[k - 1], side_peer(k)) for k in range(1, S2)]

    local[3].wait()
    local[4].wait()
    for j in range(1, PLANES):
        plane_parts[j].wait()
    strip = 64

    def norm_back(i, carry):
        rows = pl.ds(pl.multiple_of(i * strip, strip), strip)
        grad = z_send[0, rows].astype(f32)
        for j in range(1, PLANES):
            grad = grad + z_got[j - 1, rows].astype(f32)
        values = tokens[rows].astype(f32)
        centred = values - jnp.mean(values, axis=-1, keepdims=True)
        scale = lax.rsqrt(jnp.mean(centred * centred, axis=-1, keepdims=True) + norm_eps)
        normal = centred * scale
        grad = grad * gain_ref[0:1]
        grad = grad - jnp.mean(grad, axis=-1, keepdims=True) - normal * jnp.mean(grad * normal, axis=-1, keepdims=True)
        grad_hidden[rows] = grad_hidden[rows] + grad * scale
        return carry

    lax.fori_loop(0, T // strip, norm_back, 0)

    blocks = T // BLOCK
    piece = BLOCK // n

    def d_copy(source, target, base, k):
        return remote(source.at[lax.rem(me + k, n)], target.at[me], d_sems, base + k, (lax.rem(me + k, n), group))

    for i in range(n):
        d_send[i] = jnp.concatenate(
            [grad_hidden[b * BLOCK + i * piece : b * BLOCK + (i + 1) * piece] for b in range(blocks)], axis=0
        ).astype(bf)
    out_deal = [d_copy(d_send, d_mid, 0, k) for k in range(1, n)]
    for copy in out_deal:
        copy.start()
    d_mid[me] = d_send[me]

    for copy in x1 + y2:
        copy.wait()
    for p in range(half):
        w_plane[p] = sum_into(bf, [w_y1[0, p, s2]] + [w_x1[k, p] for k in range(S2 - 1)])
        w_plane[half + p] = sum_into(bf, [w_x2[0, p, group]] + [w_y2[k, p] for k in range(groups - 1)])
    w_last = [w_copy(w_plane.at[lax.rem(plane + k, PLANES)], w_z.at[k - 1], plane_peer(k)) for k in range(1, PLANES)]
    for copy in j_second:
        copy.wait()
    for p in range(PLANES):
        j_side[0, p] = sum_into(bf, [j_core[p, s2]] + [j_side[k, p] for k in range(S2 - 1)])
    j_third = [j_copy(j_side.at[0, lax.rem(plane + k, PLANES)], j_plane.at[plane], plane_peer(k)) for k in range(1, PLANES)]
    j_plane[plane] = j_side[0, plane]

    for copy in out_deal:
        copy.wait()
    for i in range(n):
        chosen = []
        for b in range(blocks):
            wanted = deal_ref[i * blocks + b]
            held = d_mid[wanted // blocks].astype(f32)
            part = held[:piece]
            for other in range(1, blocks):
                part = jnp.where(lax.rem(wanted, blocks) == other, held[other * piece : (other + 1) * piece], part)
            chosen.append(part)
        d_back[i] = jnp.concatenate(chosen, axis=0).astype(bf)
    back_deal = [d_copy(d_back, d_got, n, k) for k in range(1, n)]
    for copy in back_deal:
        copy.start()
    d_got[me] = d_back[me]

    for copy in w_last:
        copy.wait()
    w_all[group] = sum_into(bf, [w_plane[plane]] + [w_z[k] for k in range(PLANES - 1)])
    w_gather = [w_copy(w_all.at[group], w_all.at[group], group_peer(k)) for k in range(1, groups)]
    for copy in j_third:
        copy.wait()
    j_group[group] = j_plane[...]
    j_last = [j_copy(j_plane, j_group.at[group], group_peer(k)) for k in range(1, groups)]

    for copy in back_deal:
        copy.wait()
    for b in range(blocks):
        for i in range(0, n, 2):
            rows = [d_got[i + e].astype(f32)[b * piece : (b + 1) * piece] for e in range(2)]
            dealt_ref[b * BLOCK + i * piece : b * BLOCK + (i + 2) * piece] = jnp.concatenate(rows, axis=0).astype(bf)
    for copy in w_gather:
        copy.wait()
    for g in range(groups):
        shard_ref[g] = w_all[g].astype(f32)
    for copy in j_last:
        copy.wait()
    for p in range(PLANES):
        total = j_group[0, p].astype(f32)
        for g in range(1, groups):
            total = total + j_group[g, p].astype(f32)
        joint_out_ref[p] = total


def tail(n, groups, deal, dqt, dkv, turn, joint_t, first, tokens, grad_hidden, gain, packed):
    bf, f32 = jnp.bfloat16, jnp.float32
    S2 = n // PLANES // 2
    T, D = tokens.shape
    width = joint_t.shape[0]
    wide = width + 128
    rows = D // n
    part = packed.shape[4]
    piece_rows = T // n
    half = PLANES // 2
    any_, vm, sm = (pl.BlockSpec(memory_space=m) for m in (pl.ANY, pltpu.VMEM, pltpu.SMEM))
    sems = lambda count: pltpu.SemaphoreType.DMA((2, count))
    return pl.pallas_call(
        functools.partial(tail_kernel, n, groups),
        out_shape=(
            jax.ShapeDtypeStruct((T, D), bf),
            jax.ShapeDtypeStruct((groups, part, D), f32),
            jax.ShapeDtypeStruct((PLANES, rows, wide), f32),
        ),
        in_specs=[sm, vm, vm, vm, any_, any_, any_, any_, vm, any_],
        out_specs=(vm, vm, vm),
        scratch_shapes=[
            pltpu.VMEM((width, D), bf),
            pltpu.VMEM((PLANES, T, D), bf),
            pltpu.VMEM((T, D), bf),
            pltpu.VMEM((T, D), f32),
            pltpu.VMEM((PLANES, S2, groups, part, D), bf),
            pltpu.SemaphoreType.DMA((5,)),
            pltpu.VMEM((PLANES, S2, T, 2 * QW), bf),
            pltpu.VMEM((PLANES, S2, T, 2 * QW), bf),
            pltpu.VMEM((PLANES, S2 - 1, T, 2 * QW), bf),
            sems(PLANES * S2),
            pltpu.VMEM((PLANES, width, T), bf),
            pltpu.VMEM((PLANES, T, D), bf),
            pltpu.VMEM((PLANES - 1, T, D), bf),
            sems(PLANES - 1),
            pltpu.VMEM((width, D), f32),
            pltpu.VMEM((PLANES, S2, 2, rows, wide), bf),
            pltpu.VMEM((PLANES, S2, rows, wide), bf),
            pltpu.VMEM((S2 - 1, PLANES, rows, wide), bf),
            pltpu.VMEM((PLANES, rows, wide), bf),
            pltpu.VMEM((groups, PLANES, rows, wide), bf),
            sems(S2 + PLANES + groups - 2),
            pltpu.VMEM((PLANES, S2, groups, part, D), bf),
            pltpu.VMEM((groups - 1, half, S2, part, D), bf),
            pltpu.VMEM((S2 - 1, half, part, D), bf),
            pltpu.VMEM((S2 - 1, half, groups, part, D), bf),
            pltpu.VMEM((groups - 1, half, part, D), bf),
            pltpu.VMEM((PLANES, part, D), bf),
            pltpu.VMEM((PLANES - 1, part, D), bf),
            pltpu.VMEM((groups, part, D), bf),
            sems(2 + 3 * (groups - 1) + 2 * (S2 - 1) + PLANES - 1),
            pltpu.VMEM((n, piece_rows, D), bf),
            pltpu.VMEM((n, piece_rows, D), bf),
            pltpu.VMEM((n, piece_rows, D), bf),
            pltpu.VMEM((n, piece_rows, D), bf),
            sems(2 * n),
        ],
        compiler_params=pltpu.CompilerParams(collective_id=0, has_side_effects=True, vmem_limit_bytes=60 << 20),
    )(deal, dqt, dkv, turn, joint_t, first, tokens, grad_hidden, gain, packed)


def layer_norm(values, weights):
    centred = values - jnp.mean(values, axis=-1, keepdims=True)
    spread = jnp.mean(centred * centred, axis=-1, keepdims=True)
    return centred * lax.rsqrt(spread + norm_eps) * weights


def on_device(
    n,
    groups,
    tokens,
    cotangent,
    lengths,
    deal,
    joint_projection,
    output_projection,
    expand_weight,
    contract_weight,
    gain_first,
    gain_second,
):
    bf, f32 = jnp.bfloat16, jnp.float32
    T, D = tokens.shape[1:]
    S = n // PLANES
    S2 = S // 2
    me = lax.axis_index("ctx")
    plane = me // S

    def over_planes(x, k):
        return lax.ppermute(x, "ctx", [(h * S + s, (h + k) % PLANES * S + s) for h in range(PLANES) for s in range(S)])

    def turned(x, shift):
        return lax.dynamic_slice_in_dim(jnp.concatenate([x, x], axis=0), shift, x.shape[0], 0)

    tokens_own = tokens[0]
    first, qt, kv, joint_t, turn, gains, out_w, exp_w, con_w = front(
        n,
        groups,
        lengths,
        tokens_own,
        joint_projection,
        gain_first,
        gain_second,
        output_projection,
        expand_weight,
        contract_weight,
    )
    out_w, exp_w, con_w = (w.reshape(-1, w.shape[-1]) for w in (out_w, exp_w, con_w))
    gain_one, gain_two = gains[0], gains[1]
    ot, lowt, lse = attn_fwd(n, lengths, qt, kv)

    parts = [lowt[0]] + [over_planes(lowt[k], -k) for k in range(1, PLANES)]
    attended_t = turned(jnp.stack(parts), (PLANES - plane) % PLANES).reshape(D, T)

    x = tokens_own.astype(f32)
    grad_out = cotangent[0]
    hidden = x + jnp.einsum("dt,de->te", attended_t, out_w, preferred_element_type=f32)
    second = layer_norm(hidden, gain_two).astype(bf)
    expanded = jnp.dot(second, exp_w, preferred_element_type=f32)

    def gated(values):
        return jax.nn.gelu(values[:, :FF], approximate=False) * values[:, FF:]

    activated_f, gated_pull = jax.vjp(gated, expanded)
    activated = activated_f.astype(bf)
    output = (hidden + jnp.dot(activated, con_w, preferred_element_type=f32)).astype(bf)

    grad_activated = jnp.einsum("td,fd->tf", grad_out, con_w, preferred_element_type=f32)
    grad_expanded = gated_pull(grad_activated)[0].astype(bf)
    grad_second = jnp.einsum("tf,df->td", grad_expanded, exp_w, preferred_element_type=f32)
    _, second_pull = jax.vjp(layer_norm, hidden, gain_two)
    grad_hidden_norm, grad_gain_two = second_pull(grad_second)
    grad_hidden = grad_out.astype(f32) + grad_hidden_norm
    grad_branch = grad_hidden.astype(bf)
    grad_attended = jnp.einsum("de,te->dt", out_w, grad_branch, preferred_element_type=f32).astype(bf)
    rel = turned(grad_attended.reshape(PLANES, QW, T), plane)
    gt = jnp.stack([rel[0]] + [over_planes(rel[k], k) for k in range(1, PLANES)])

    grad_contract = jnp.einsum("tf,td->fd", activated, grad_out, preferred_element_type=f32)
    grad_expand = jnp.einsum("td,tf->df", second, grad_expanded, preferred_element_type=f32)
    grad_output = jnp.einsum("dt,te->de", attended_t, grad_branch, preferred_element_type=f32)

    dqt, dkv = attn_bwd(n, lengths, qt, kv, ot, lse, gt)

    def sharded(x):
        return x.astype(bf).reshape(n, x.shape[0] // n, x.shape[1])

    gain_rows = jnp.pad(grad_gain_two.reshape(n, 1, D // n), ((0, 0), (0, 7), (0, D - D // n))).astype(bf)
    rows = D // n
    wide = grad_expand.shape[1] // D
    pieces = [sharded(grad_output)]
    pieces += [sharded(grad_expand[:, i * D : (i + 1) * D]) for i in range(wide)]
    pieces += [sharded(grad_contract), gain_rows]
    used = sum(p.shape[1] for p in pieces)
    part = -(-used // (groups * 16)) * 16
    packed = jnp.concatenate(pieces + [jnp.zeros((n, groups * part - used, D), bf)], axis=1)
    packed = packed.reshape(PLANES, S2, 2, groups, part, D)

    dealt, shards, joint_raw = tail(
        n,
        groups,
        deal[0],
        dqt,
        dkv.reshape(PLANES, S2, 2, T, 2 * QW),
        turn,
        joint_t,
        first,
        tokens_own,
        grad_hidden,
        gains,
        packed,
    )
    shards = shards.reshape(groups * part, D)
    shard_output = shards[:rows]
    shard_expand = jnp.concatenate([shards[(1 + i) * rows : (2 + i) * rows] for i in range(wide)], axis=1)
    after = (1 + wide) * rows
    ff_rows = grad_contract.shape[0] // n
    shard_contract = shards[after : after + ff_rows]
    shard_gain_two = shards[after + ff_rows, :rows]
    shard_joint = jnp.transpose(joint_raw[:, :, : 3 * QW].reshape(PLANES, rows, 3, QW), (1, 2, 0, 3))
    shard_joint = shard_joint.reshape(rows, 3 * PLANES * QW)
    shard_gain_one = jnp.sum(joint_raw[:, :, -1], axis=0) / lax.dynamic_slice_in_dim(gain_one, me * rows, rows)
    return (
        output[None],
        dealt[None],
        shard_joint,
        shard_output,
        shard_expand,
        shard_contract,
        shard_gain_one,
        shard_gain_two,
    )


def solution(mesh):
    return jax.shard_map(
        functools.partial(on_device, mesh.shape["ctx"], mesh.shape["fsdp"]),
        mesh=mesh,
        in_specs=(
            P("fsdp", "ctx", None),
            P("fsdp", "ctx", None),
            P("fsdp", None),
            P("fsdp", None),
            P("fsdp", None),
            P("fsdp", None),
            P("fsdp", None),
            P("fsdp", None),
            P("fsdp"),
            P("fsdp"),
        ),
        out_specs=(
            P("fsdp", "ctx", None),
            P("fsdp", "ctx", None),
            P("ctx", None),
            P("ctx", None),
            P("ctx", None),
            P("ctx", None),
            P("ctx"),
            P("ctx"),
        ),
        check_vma=False,
    )
```

```python
import functools
import math

import jax
import jax.numpy as jnp
from jax import lax
from jax.experimental import pallas as pl
from jax.experimental.pallas import tpu as pltpu
from jax.sharding import PartitionSpec as P

FF = 1152
HEADS = 12
HEAD_DIM = 64
BLOCK = 128
PLANES = 4
HD = HEAD_DIM
HALF = HEAD_DIM // 2
HP = HEADS // PLANES
QW = HP * HEAD_DIM
rope_base = 160000.0
norm_eps = 1e-05
MASKED = -1e30


def ends_of(lengths_ref, count):
    ends, total = [], 0
    for i in range(count):
        total = total + lengths_ref[0, i]
        ends.append(total)
    return ends


def span_of(index, ends):
    begin, end = jnp.zeros_like(index), jnp.full_like(index, ends[0])
    for before, after in zip(ends[:-1], ends[1:]):
        begin = jnp.where(index >= before, before, begin)
        end = jnp.where(index >= before, after, end)
    return begin, end


def head_rows(x, head):
    rows = lax.broadcasted_iota(jnp.int32, x.shape, 0)
    return jnp.where((rows >= head * HD) & (rows < (head + 1) * HD), x, jnp.zeros_like(x))


def query_block(n, b, T, ends):
    S = n // PLANES
    me = lax.axis_index("ctx")
    base = (lax.rem(me // S + PLANES - b, PLANES) * S + lax.rem(me, S)) * T
    low_begin, low_end = span_of(base, ends)
    high_begin, high_end = span_of(base + T - 1, ends)
    low, high = low_begin // T, (high_end + T - 1) // T
    full_low = jnp.clip((high_begin + T - 1) // T, low, high)
    full_high = jnp.clip(low_end // T, full_low, high)
    begin, end = span_of(base + lax.broadcasted_iota(jnp.int32, (8, T), 1), ends)
    return (low, full_low, full_high, high), begin[0:1], end[0:1]


def over_units(bounds, step):
    low, full_low, full_high, high = bounds

    def run(begin, end, masked):
        def body(u, carry):
            step(u, masked)
            return carry

        lax.fori_loop(begin, end, body, 0)

    run(low, full_low, True)
    in_pairs(full_low, full_high, lambda u: step(u, False))
    run(full_high, high, True)


def in_pairs(begin, end, step):
    pairs = (end - begin) // 2

    def two(i, carry):
        step(begin + 2 * i)
        step(begin + 2 * i + 1)
        return carry

    def one(u, carry):
        step(u)
        return carry

    lax.fori_loop(0, pairs, two, 0)
    lax.fori_loop(begin + 2 * pairs, end, one, 0)


def fwd_kernel(n, count, lengths_ref, qt_ref, kv_ref, ot_ref, lowt_ref, lse_ref, values, scores, top, total, acc):
    units, T, _ = kv_ref.shape
    ends = ends_of(lengths_ref, count)

    def flip(u, carry):
        values[u] = kv_ref[u, :, 128:].T
        return carry

    lax.fori_loop(0, units, flip, 0, unroll=4)

    def one_query_block(b, carry):
        qt = qt_ref[b]
        qheads = [head_rows(qt, h) for h in range(HP)]
        bounds, q_start, q_end = query_block(n, b, T, ends)
        top[...] = jnp.full_like(top, MASKED)
        total[...] = jnp.zeros_like(total)
        acc[...] = jnp.zeros_like(acc)

        def score(u, masked):
            k = kv_ref[u, :, :QW]
            st = [jnp.dot(k, qheads[h], preferred_element_type=jnp.float32) for h in range(HP)]
            if masked:
                at = u * T + lax.broadcasted_iota(jnp.int32, (T, T), 0)
                allowed = (at >= q_start) & (at < q_end)
                st = [jnp.where(allowed, s, MASKED) for s in st]
            for h in range(HP):
                scores[u, h] = st[h]
                top[h] = jnp.maximum(top[h], jnp.max(st[h].reshape(T // 8, 8, T), axis=0))

        over_units(bounds, score)
        m = [jnp.max(top[h], axis=0, keepdims=True) for h in range(HP)]

        def gather(u):
            p = [jnp.exp(scores[u, h] - m[h]) for h in range(HP)]
            for h in range(HP):
                total[h] += jnp.sum(p[h].reshape(T // 8, 8, T), axis=0)
                rows = pl.ds(h * HD, HD)
                acc[rows, :] += jnp.dot(
                    values[u, pl.ds(HD + h * HD, HD), :], p[h].astype(jnp.bfloat16), preferred_element_type=jnp.float32
                )

        in_pairs(bounds[0], bounds[3], gather)
        for h in range(HP):
            rows = pl.ds(h * HD, HD)
            l = jnp.sum(total[h], axis=0, keepdims=True)
            o = acc[rows, :] / l
            ot_ref[b, rows, :] = o
            lowt_ref[b, rows, :] = o.astype(jnp.bfloat16)
            lse_ref[b, h : h + 1, :] = m[h] + jnp.log(l)
        return carry

    lax.fori_loop(0, qt_ref.shape[0], one_query_block, 0)


def attn_fwd(n, lengths, qt, kv):
    B, _, T = qt.shape
    U = kv.shape[0]
    sm, vm = pl.BlockSpec(memory_space=pltpu.SMEM), pl.BlockSpec(memory_space=pltpu.VMEM)
    return pl.pallas_call(
        functools.partial(fwd_kernel, n, lengths.shape[1]),
        out_shape=(
            jax.ShapeDtypeStruct((B, QW, T), jnp.float32),
            jax.ShapeDtypeStruct((B, QW, T), jnp.bfloat16),
            jax.ShapeDtypeStruct((B, 8, T), jnp.float32),
        ),
        in_specs=[sm, vm, vm],
        out_specs=(vm, vm, vm),
        scratch_shapes=[
            pltpu.VMEM((U, 256, T), jnp.bfloat16),
            pltpu.VMEM((U, HP, T, T), jnp.float32),
            pltpu.VMEM((HP, 8, T), jnp.float32),
            pltpu.VMEM((HP, 8, T), jnp.float32),
            pltpu.VMEM((QW, T), jnp.float32),
        ],
        compiler_params=pltpu.CompilerParams(vmem_limit_bytes=60 << 20),
    )(lengths, qt, kv)


def bwd_kernel(n, count, lengths_ref, qt_ref, kv_ref, ot_ref, lse_ref, gt_ref, dqt_ref, dkv_ref, keys, dk, dv, dq):
    units, T, _ = kv_ref.shape
    ends = ends_of(lengths_ref, count)

    def flip(u, carry):
        keys[u] = kv_ref[u, :, :256].T
        dk[u] = jnp.zeros_like(dk[u])
        dv[u] = jnp.zeros_like(dv[u])
        return carry

    lax.fori_loop(0, units, flip, 0, unroll=4)

    def one_query_block(b, carry):
        qt, gt = qt_ref[b], gt_ref[b]
        zero = jnp.zeros((HD, T), jnp.bfloat16)
        qheads = [head_rows(qt, h) for h in range(HP)]
        gheads = [head_rows(gt, h) for h in range(HP)]
        gpad = [jnp.concatenate([zero, x], axis=0) for x in gheads]
        q = jnp.concatenate([jnp.concatenate([x, zero], axis=0).T for x in qheads], axis=0)
        g = jnp.concatenate([x.T for x in gpad], axis=0)
        bounds, q_start, q_end = query_block(n, b, T, ends)
        prod = gt.astype(jnp.float32) * ot_ref[b]
        delta = [jnp.sum(prod[h * HD : (h + 1) * HD], axis=0, keepdims=True) for h in range(HP)]
        lse = [lse_ref[b, h : h + 1, :] for h in range(HP)]
        dq[...] = jnp.zeros_like(dq)

        def one_unit(u, masked):
            k, v = kv_ref[u, :, :QW], kv_ref[u, :, 128:]
            st = [jnp.dot(k, qheads[h], preferred_element_type=jnp.float32) for h in range(HP)]
            dp = [jnp.dot(v, gpad[h], preferred_element_type=jnp.float32) for h in range(HP)]
            st = [st[h] - lse[h] for h in range(HP)]
            if masked:
                at = u * T + lax.broadcasted_iota(jnp.int32, (T, T), 0)
                allowed = (at >= q_start) & (at < q_end)
                st = [jnp.where(allowed, s, MASKED) for s in st]
            p = [jnp.exp(s) for s in st]
            ds = [(p[h] * (dp[h] - delta[h])).astype(jnp.bfloat16) for h in range(HP)]
            p = [x.astype(jnp.bfloat16) for x in p]
            dv[u] += jnp.dot(jnp.concatenate(p, axis=1), g, preferred_element_type=jnp.float32)
            dk[u] += jnp.dot(jnp.concatenate(ds, axis=1), q, preferred_element_type=jnp.float32)
            for h in range(HP):
                rows = pl.ds(h * HD, HD)
                dq[rows, :] += jnp.dot(keys[u, rows, :], ds[h], preferred_element_type=jnp.float32)

        over_units(bounds, one_unit)
        dqt_ref[b] = dq[...] * (HD**-0.5)
        return carry

    lax.fori_loop(0, qt_ref.shape[0], one_query_block, 0)

    def out(u, carry):
        dkv_ref[u, :, :128] = dk[u, :, :128].astype(jnp.bfloat16)
        dkv_ref[u, :, 128:256] = (dk[u, :, 128:] + dv[u, :, :128]).astype(jnp.bfloat16)
        dkv_ref[u, :, 256:] = dv[u, :, 128:].astype(jnp.bfloat16)
        return carry

    lax.fori_loop(0, units, out, 0, unroll=2)


def attn_bwd(n, lengths, qt, kv, ot, lse, gt):
    B, _, T = qt.shape
    U = kv.shape[0]
    sm, vm = pl.BlockSpec(memory_space=pltpu.SMEM), pl.BlockSpec(memory_space=pltpu.VMEM)
    return pl.pallas_call(
        functools.partial(bwd_kernel, n, lengths.shape[1]),
        out_shape=(jax.ShapeDtypeStruct((B, QW, T), jnp.float32), jax.ShapeDtypeStruct((U, T, 2 * QW), jnp.bfloat16)),
        in_specs=[sm] + [vm] * 5,
        out_specs=(vm, vm),
        scratch_shapes=[
            pltpu.VMEM((U, 256, T), jnp.bfloat16),
            pltpu.VMEM((U, T, 256), jnp.float32),
            pltpu.VMEM((U, T, 256), jnp.float32),
            pltpu.VMEM((QW, T), jnp.float32),
        ],
        compiler_params=pltpu.CompilerParams(vmem_limit_bytes=60 << 20),
    )(lengths, qt, kv, ot, lse, gt)
def front_kernel(
    n,
    groups,
    count,
    lengths_ref,
    tokens_ref,
    joint_ref,
    gain_one_ref,
    gain_two_ref,
    freq_ref,
    out_hbm,
    exp_hbm,
    con_hbm,
    first_ref,
    qt_ref,
    kv_ref,
    joint_t_out,
    turn_ref,
    gains_ref,
    out_all,
    exp_all,
    con_all,
    held,
    t_sems,
    cols,
    cols_all,
    gain_held,
    g_sems,
    kv_own,
    kv_sems,
    own_sems,
    w_sems,
    w_local,
    joint_rows,
    out_held,
    exp_held,
    con_held,
):
    bf, f32 = jnp.bfloat16, jnp.float32
    S = n // PLANES
    S2 = S // 2
    T, D = tokens_ref.shape
    me, group = lax.axis_index("ctx"), lax.axis_index("fsdp")
    plane, side = me // S, lax.rem(me, S)
    s2, core = side // 2, lax.rem(side, 2)

    def at(p, a, c, g):
        return (p * S + a * 2 + c, g)

    def side_peer(k):
        return at(plane, lax.rem(s2 + k, S2), core, group)

    def group_peer(k):
        return at(plane, s2, core, lax.rem(group + k, groups))

    core_peer = at(plane, s2, 1 - core, group)

    def remote(source, target, sems, index, device):
        return pltpu.make_async_remote_copy(
            src_ref=source,
            dst_ref=target,
            send_sem=sems.at[0, index],
            recv_sem=sems.at[1, index],
            device_id=device,
            device_id_type=pl.DeviceIdType.MESH,
        )

    barrier = pltpu.get_barrier_semaphore()

    def greet(device):
        pl.semaphore_signal(barrier, inc=1, device_id=device, device_id_type=pl.DeviceIdType.MESH)

    for k in range(1, PLANES):
        greet(at(lax.rem(plane + k, PLANES), s2, core, group))
    for k in range(1, S2):
        greet(side_peer(k))
    for k in range(1, groups):
        greet(group_peer(k))
    greet(core_peer)
    pl.semaphore_wait(barrier, PLANES - 1 + S2 - 1 + groups - 1 + 1)

    def up(p):
        return remote(held.at[p], held.at[p], t_sems, p, at(plane + 1, s2, core, group))

    def down(p):
        return remote(held.at[p], held.at[p], t_sems, PLANES + p, at(plane - 1, s2, core, group))

    held[plane] = tokens_ref[...]

    @pl.when(plane < PLANES - 1)
    def _():
        up(plane).start()

    @pl.when(plane > 0)
    def _():
        down(plane).start()

    pair = 2 * QW
    for part in range(3):
        window = joint_ref[:, pl.ds(pl.multiple_of(part * D + plane // 2 * pair, 128), pair)].T
        chosen = jnp.where(lax.rem(plane, 2) == 0, window[:QW].astype(f32), window[QW:].astype(f32))
        half = 3 * QW // 2
        low, high = part * QW, (part + 1) * QW
        for c in range(2):
            begin, end = max(low, c * half), min(high, (c + 1) * half)
            if begin < end:
                cols[c, begin - c * half : end - c * half] = chosen[begin - low : end - low].astype(bf)
    gain_held[group] = jnp.zeros_like(gain_held[group])
    gain_held[group, 0:1] = gain_one_ref[...].astype(f32)
    gain_held[group, 1:2] = gain_two_ref[...].astype(f32)
    col_moves = [
        remote(cols.at[core], cols_all.at[group, core], g_sems, k - 1, group_peer(k)) for k in range(1, groups)
    ]
    col_hands = []
    for k in range(1, groups):
        came = cols_all.at[lax.rem(group + groups - k, groups), core]
        col_hands.append(remote(came, came, g_sems, 2 * (groups - 1) + k - 1, core_peer))
    gain_moves = [
        remote(gain_held.at[group], gain_held.at[group], g_sems, groups - 1 + k - 1, group_peer(k))
        for k in range(1, groups)
    ]
    for copy in gain_moves + col_moves:
        copy.start()
    cols_all[group] = cols[...]

    weights = [(out_hbm, out_all, out_held), (exp_hbm, exp_all, exp_held), (con_hbm, con_all, con_held)]
    w_in, w_own, w_first, w_second = [], [], [], []
    for i, (source, target, bounce) in enumerate(weights):
        w_in.append(pltpu.make_async_copy(source, bounce, w_local.at[0, i]))
        w_own.append(pltpu.make_async_copy(bounce, target.at[group], w_local.at[1, i]))
        for k in range(1, groups):
            index = (i * (groups - 1) + k - 1) * 2
            w_first.append(remote(source.at[core], target.at[group, core], w_sems, index, group_peer(k)))
            came = lax.rem(group + groups - k, groups)
            w_second.append(remote(target.at[came, core], target.at[came, core], w_sems, index + 1, core_peer))
    for copy in w_in:
        copy.start()

    ends = ends_of(lengths_ref, count)
    for j in range(PLANES):
        base = (lax.rem(plane + PLANES - j, PLANES) * S + side) * T
        index = base + lax.broadcasted_iota(jnp.int32, (8, T), 1)
        begin, _ = span_of(index, ends)
        angles = (index - begin)[0:1].astype(f32) * freq_ref[...]
        turn_ref[j, :HALF] = jnp.cos(angles)
        turn_ref[j, HALF:] = jnp.sin(angles)

    strip = 64

    def kv_unit(p, a, c):
        return p * S + a * 2 + c

    def side_kv(j, k):
        p = lax.rem(plane + PLANES - j, PLANES)
        return remote(kv_own.at[j], kv_ref.at[kv_unit(p, s2, core)], kv_sems, j * (2 * S2 - 1) + k - 1, side_peer(k))

    def core_kv(j, k):
        p = lax.rem(plane + PLANES - j, PLANES)
        unit = kv_unit(p, lax.rem(s2 + S2 - k, S2), core)
        source = kv_own.at[j] if k == 0 else kv_ref.at[unit]
        return remote(source, kv_ref.at[unit], kv_sems, j * (2 * S2 - 1) + S2 - 1 + k, core_peer)

    def own_kv(j):
        p = lax.rem(plane + PLANES - j, PLANES)
        return pltpu.make_async_copy(kv_own.at[j], kv_ref.at[kv_unit(p, s2, core)], own_sems.at[j])

    def process(p):
        j = lax.rem(plane + PLANES - p, PLANES)

        def norm(i, carry):
            rows = pl.ds(pl.multiple_of(i * strip, strip), strip)
            values = held[p, rows].astype(f32)
            centred = values - jnp.mean(values, axis=-1, keepdims=True)
            spread = jnp.mean(centred * centred, axis=-1, keepdims=True)
            first_ref[j, rows] = (centred * lax.rsqrt(spread + norm_eps) * gains_ref[0:1]).astype(bf)
            return carry

        lax.fori_loop(0, T // strip, norm, 0)
        mixed = lax.dot_general(
            joint_t_out[: 3 * QW], first_ref[j], (((1,), (1,)), ((), ())), preferred_element_type=f32
        )
        cos, sin = turn_ref[j, :HALF], turn_ref[j, HALF:]
        turned = []
        for h in range(2 * HP):
            upper, lower = mixed[h * HD : h * HD + HALF], mixed[h * HD + HALF : (h + 1) * HD]
            turned += [upper * cos - lower * sin, lower * cos + upper * sin]
        q = jnp.concatenate(turned[: 2 * HP], axis=0).astype(bf)
        qt_ref[j] = (q.astype(f32) * HEAD_DIM**-0.5).astype(bf)
        kv_own[j] = jnp.concatenate(turned[2 * HP :] + [mixed[2 * QW :]], axis=0).T.astype(bf)
        for k in range(1, S2):
            side_kv(j, k).start()
        core_kv(j, 0).start()
        own_kv(j).start()

    def hand_on(t):
        @pl.when(plane >= t)
        def _():
            up(plane - t).wait_recv()

            @pl.when(plane < PLANES - 1)
            def _():
                up(plane - t).start()

        @pl.when(plane + t < PLANES)
        def _():
            down(plane + t).wait_recv()

            @pl.when(plane > 0)
            def _():
                down(plane + t).start()

    def process_arrived(t):
        below = jnp.where(plane >= t, 1, 0)
        above = jnp.where(plane + t < PLANES, 1, 0)

        def arrived(i, carry):
            process(jnp.where(i < below, plane - t, plane + t))
            return carry

        lax.fori_loop(0, below + above, arrived, 0)

    hand_on(1)
    for copy in gain_moves:
        copy.wait()
    share = D // groups
    total = jnp.zeros((8, D), f32)
    for g in range(groups):
        rows = lax.broadcasted_iota(jnp.int32, (share, D), 0)
        lanes = lax.broadcasted_iota(jnp.int32, (share, D), 1)
        place = jnp.where(lanes == rows + g * share, 1.0, 0.0).astype(bf)
        total = total + jnp.dot(gain_held[g].astype(bf), place, preferred_element_type=f32)
    gains_ref[...] = total
    for copy, hand in zip(col_moves, col_hands):
        copy.wait()
        hand.start()
    for copy in w_first:
        copy.start()
    for copy in w_in:
        copy.wait()
    for copy in w_own:
        copy.start()
    for copy in col_hands:
        copy.wait()
    width = joint_t_out.shape[0]
    for g in range(groups):
        whole = jnp.concatenate([cols_all[g, 0], cols_all[g, 1], jnp.zeros((width - 3 * QW, share), bf)], axis=0)
        if share % 128 == 0:
            joint_t_out[:, g * share : (g + 1) * share] = whole
        else:
            joint_rows[g * share : (g + 1) * share] = whole.T
    if share % 128:
        for i in range(D // 128):
            joint_t_out[:, i * 128 : (i + 1) * 128] = joint_rows[i * 128 : (i + 1) * 128].T

    process(plane)
    hand_on(2)
    process_arrived(1)
    hand_on(3)
    process_arrived(2)
    process_arrived(3)

    for j in range(PLANES):
        for k in range(1, S2):
            side_kv(j, k).wait_recv()
            core_kv(j, k).start()
    for first_move, second_move in zip(w_first, w_second):
        first_move.wait_recv()
        second_move.start()

    for j in range(PLANES):
        own_kv(j).wait()
        for k in range(1, S2):
            side_kv(j, k).wait_send()
        for k in range(S2):
            core_kv(j, k).wait()
    for p in range(PLANES):

        @pl.when((plane < PLANES - 1) & (plane >= p))
        def _(p=p):
            up(p).wait_send()

        @pl.when((plane > 0) & (plane <= p))
        def _(p=p):
            down(p).wait_send()

    for copy in w_own:
        copy.wait()
    for first_move, second_move in zip(w_first, w_second):
        first_move.wait_send()
        second_move.wait()


def front(n, groups, lengths, tokens, joint_shard, gain_first, gain_second, out_w, exp_w, con_w):
    bf, f32 = jnp.bfloat16, jnp.float32
    S2 = n // PLANES // 2
    T, D = tokens.shape
    width = 3 * QW + 64
    share = D // groups
    any_, vm, sm = (pl.BlockSpec(memory_space=m) for m in (pl.ANY, pltpu.VMEM, pltpu.SMEM))
    sems = lambda count: pltpu.SemaphoreType.DMA((2, count))
    halves = lambda w: w.reshape(2, w.shape[0] // 2, w.shape[1])
    frequencies = rope_base ** (-jnp.arange(0, HEAD_DIM, 2).astype(f32) / HEAD_DIM)
    weights = [halves(w) for w in (out_w, exp_w, con_w)]
    return pl.pallas_call(
        functools.partial(front_kernel, n, groups, lengths.shape[1]),
        out_shape=(
            jax.ShapeDtypeStruct((PLANES, T, D), bf),
            jax.ShapeDtypeStruct((PLANES, QW, T), bf),
            jax.ShapeDtypeStruct((n, T, 2 * QW), bf),
            jax.ShapeDtypeStruct((width, D), bf),
            jax.ShapeDtypeStruct((PLANES, 2 * HALF, T), f32),
            jax.ShapeDtypeStruct((8, D), f32),
            *[jax.ShapeDtypeStruct((groups, *w.shape), bf) for w in weights],
        ),
        in_specs=[sm, vm, vm, vm, vm, vm, any_, any_, any_],
        out_specs=(vm, vm, any_, vm, vm, vm, any_, any_, any_),
        scratch_shapes=[
            pltpu.VMEM((PLANES, T, D), bf),
            sems(2 * PLANES),
            pltpu.VMEM((2, 3 * QW // 2, share), bf),
            pltpu.VMEM((groups, 2, 3 * QW // 2, share), bf),
            pltpu.VMEM((groups, 8, share), f32),
            sems(3 * (groups - 1)),
            pltpu.VMEM((PLANES, T, 2 * QW), bf),
            sems(PLANES * (2 * S2 - 1)),
            pltpu.SemaphoreType.DMA((PLANES,)),
            sems(2 * len(weights) * (groups - 1)),
            pltpu.SemaphoreType.DMA((2, len(weights))),
            pltpu.VMEM((D, width), bf),
            *[pltpu.VMEM(w.shape, bf) for w in weights],
        ],
        compiler_params=pltpu.CompilerParams(collective_id=1, has_side_effects=True, vmem_limit_bytes=60 << 20),
    )(
        lengths,
        tokens,
        joint_shard,
        gain_first[None],
        gain_second[None],
        frequencies[:, None],
        *weights,
    )


def middle_kernel(
    n,
    groups,
    low_ref,
    tokens_ref,
    cot_ref,
    gains_ref,
    out_hbm,
    exp_hbm,
    con_hbm,
    output_ref,
    grad_hidden_ref,
    gt_ref,
    gain_ref,
    y_keep,
    y_send,
    x_keep,
    x_send,
    z_keep,
    z_send,
    out_w,
    exp_w,
    con_w,
    local_sems,
    att,
    a_sems,
    g_send,
    g_sems,
    hidden,
    second,
    branch,
    ga,
    act,
    gexp,
    acc,
    w_own,
    w_other,
    w_got,
    w_sems,
):
    bf, f32 = jnp.bfloat16, jnp.float32
    S = n // PLANES
    S2 = S // 2
    T, D = tokens_ref.shape
    FFN = act.shape[1]
    me, group = lax.axis_index("ctx"), lax.axis_index("fsdp")
    plane, side = me // S, lax.rem(me, S)
    s2, core = side // 2, lax.rem(side, 2)

    def plane_peer(k):
        return (lax.rem(plane + k, PLANES) * S + side, group)

    core_peer = (plane * S + s2 * 2 + 1 - core, group)

    def remote(source, target, sems, index, device):
        return pltpu.make_async_remote_copy(
            src_ref=source,
            dst_ref=target,
            send_sem=sems.at[0, index],
            recv_sem=sems.at[1, index],
            device_id=device,
            device_id_type=pl.DeviceIdType.MESH,
        )

    local = [
        pltpu.make_async_copy(source, target, local_sems.at[i])
        for i, (source, target) in enumerate([(con_hbm, con_w), (out_hbm, out_w), (exp_hbm, exp_w)])
    ]
    for copy in local:
        copy.start()
    barrier = pltpu.get_barrier_semaphore()
    for k in range(1, PLANES):
        pl.semaphore_signal(barrier, inc=1, device_id=plane_peer(k), device_id_type=pl.DeviceIdType.MESH)
    pl.semaphore_signal(barrier, inc=1, device_id=core_peer, device_id_type=pl.DeviceIdType.MESH)
    pl.semaphore_wait(barrier, PLANES)

    home = [remote(low_ref.at[j], att.at[plane], a_sems, j - 1, plane_peer(PLANES - j)) for j in range(1, PLANES)]
    for copy in home:
        copy.start()
    att[plane] = low_ref[0]

    def nt(a, b):
        return lax.dot_general(a, b, (((1,), (1,)), ((), ())), preferred_element_type=f32)

    chunk = 384
    local[0].wait()
    cot = cot_ref[...]
    for c in range(0, FFN, chunk):
        ga[:, c : c + chunk] = nt(cot, con_w[c : c + chunk])
    local[1].wait()
    for copy in home:
        copy.wait()
    attended = att[...].reshape(D, T)
    hidden[...] = tokens_ref[...].astype(f32) + jnp.dot(attended.T, out_w[...], preferred_element_type=f32)

    strip = 64

    def norm(i, carry):
        rows = pl.ds(pl.multiple_of(i * strip, strip), strip)
        values = hidden[rows]
        centred = values - jnp.mean(values, axis=-1, keepdims=True)
        spread = jnp.mean(centred * centred, axis=-1, keepdims=True)
        second[rows] = (centred * lax.rsqrt(spread + norm_eps) * gains_ref[1:2]).astype(bf)
        return carry

    lax.fori_loop(0, T // strip, norm, 0)
    local[2].wait()
    for c in range(0, FFN, chunk):
        cols, gate_cols = slice(c, c + chunk), slice(FFN + c, FFN + c + chunk)
        inner = jnp.dot(second[...], exp_w[:, cols], preferred_element_type=f32)
        gate = jnp.dot(second[...], exp_w[:, gate_cols], preferred_element_type=f32)
        share = 0.5 * (1.0 + lax.erf(inner * (0.5**0.5)))
        bent = inner * share
        act[:, cols] = (bent * gate).astype(bf)
        grad = ga[:, cols]
        slope = share + inner * jnp.exp(-0.5 * inner * inner) * ((2.0 * math.pi) ** -0.5)
        gexp[:, cols] = (grad * gate * slope).astype(bf)
        gexp[:, gate_cols] = (grad * bent).astype(bf)
    output_ref[...] = (hidden[...] + jnp.dot(act[...], con_w[...], preferred_element_type=f32)).astype(bf)
    acc[:T] = nt(gexp[...], exp_w[...])

    def norm_back(i, total):
        rows = pl.ds(pl.multiple_of(i * strip, strip), strip)
        values = hidden[rows]
        centred = values - jnp.mean(values, axis=-1, keepdims=True)
        scale = lax.rsqrt(jnp.mean(centred * centred, axis=-1, keepdims=True) + norm_eps)
        normal = centred * scale
        grad = acc[rows]
        total = total + jnp.sum(grad * normal, axis=0, keepdims=True)
        grad = grad * gains_ref[1:2]
        grad = grad - jnp.mean(grad, axis=-1, keepdims=True) - normal * jnp.mean(grad * normal, axis=-1, keepdims=True)
        back = cot_ref[rows].astype(f32) + grad * scale
        grad_hidden_ref[rows] = back
        branch[rows] = back.astype(bf)
        return total

    total = lax.fori_loop(0, T // strip, norm_back, jnp.zeros((1, D), f32))
    gain_ref[...] = jnp.broadcast_to(total, gain_ref.shape)
    for p in range(PLANES):
        g_send[p] = nt(out_w[p * QW : (p + 1) * QW], branch[...]).astype(bf)
    away = [
        remote(g_send.at[lax.rem(plane + k, PLANES)], gt_ref.at[k], g_sems, k - 1, plane_peer(k))
        for k in range(1, PLANES)
    ]
    for copy in away:
        copy.start()
    gt_ref[0] = g_send[plane]

    sent = []

    def place(rows, offset, height):
        for target, parity in ((w_other, 1 - core), (w_own, core)):

            def body(m, carry):
                if rows % 8:
                    pair = acc[pl.ds(pl.multiple_of(2 * m * rows, 8), 2 * rows)]
                    value = jnp.where(parity == 0, pair[:rows], pair[rows:])
                else:
                    value = acc[pl.ds(pl.multiple_of((2 * m + parity) * rows, 8), rows)]
                if height > rows:
                    value = jnp.concatenate([value, jnp.zeros((height - rows, D), f32)], axis=0)
                value = value.astype(bf)
                target[m, offset : offset + height] = value
                return carry

            lax.fori_loop(0, n // 2, body, 0)
        part = pl.ds(offset, height)
        sent.append(remote(w_other.at[:, part], w_got.at[:, part], w_sems, len(sent), core_peer))
        sent[-1].start()

    rows = D // n
    acc[:D] = jnp.dot(attended, branch[...], preferred_element_type=f32)
    place(rows, 0, rows)
    second_t = second[...].T
    wide = 2 * FFN // D
    for i in range(wide):
        acc[:D] = jnp.dot(second_t, gexp[:, i * D : (i + 1) * D], preferred_element_type=f32)
        place(rows, (1 + i) * rows, rows)
    for c in range(0, FFN, chunk):
        acc[c : c + chunk] = jnp.dot(act[:, c : c + chunk].T, cot_ref[...], preferred_element_type=f32)
    used = (1 + wide) * rows
    place(FFN // n, used, w_own.shape[1] - used)

    for copy in sent:
        copy.wait()
    height = y_keep.shape[2]
    third = lambda g, i: pl.ds(pl.multiple_of((3 * g + i) * height, 16), height)

    def summed(m, part):
        return (w_own[m, part].astype(f32) + w_got[m, part].astype(f32)).astype(bf)

    def each(count, body):
        def step(i, carry):
            body(i)
            return carry

        lax.fori_loop(0, count, step, 0)

    for k in range(groups):
        g = lax.rem(group + k, groups)

        def first(m, k=k, g=g):
            (y_send.at[k - 1] if k else y_keep)[m // S2, lax.rem(m, S2)] = summed(m, third(g, 0))

        each(PLANES * S2, first)
    for k in range(S2):
        a = lax.rem(s2 + k, S2)

        def second_part(i, k=k, a=a):
            p, g = i // groups, lax.rem(i, groups)
            (x_send.at[k - 1] if k else x_keep)[p, g] = summed(p * S2 + a, third(g, 1))

        each(PLANES * groups, second_part)
    for k in range(PLANES):
        p = lax.rem(plane + k, PLANES)

        def third_part(i, k=k, p=p):
            a, g = i // groups, lax.rem(i, groups)
            (z_send.at[k - 1] if k else z_keep)[a, g] = summed(p * S2 + a, third(g, 2))

        each(S2 * groups, third_part)
    for copy in away:
        copy.wait()


def middle(n, groups, lowt, tokens, cotangent, gains, out_w, exp_w, con_w):
    bf, f32 = jnp.bfloat16, jnp.float32
    S2 = n // PLANES // 2
    T, D = tokens.shape
    ffn = con_w.shape[0]
    used = (D + 2 * ffn + ffn) // n
    height = -(-used // (groups * 48)) * 16
    any_, vm = pl.BlockSpec(memory_space=pl.ANY), pl.BlockSpec(memory_space=pltpu.VMEM)
    sems = lambda count: pltpu.SemaphoreType.DMA((2, count))
    shape = lambda *s: jax.ShapeDtypeStruct(s, bf)
    half = (n // 2, 3 * groups * height, D)
    return pl.pallas_call(
        functools.partial(middle_kernel, n, groups),
        out_shape=(
            shape(T, D),
            jax.ShapeDtypeStruct((T, D), f32),
            shape(PLANES, QW, T),
            jax.ShapeDtypeStruct((8, D), f32),
            shape(PLANES, S2, height, D),
            shape(groups - 1, PLANES, S2, height, D),
            shape(PLANES, groups, height, D),
            shape(S2 - 1, PLANES, groups, height, D),
            shape(S2, groups, height, D),
            shape(PLANES - 1, S2, groups, height, D),
        ),
        in_specs=[vm, vm, vm, vm, any_, any_, any_],
        out_specs=tuple([vm] * 10),
        scratch_shapes=[
            pltpu.VMEM(out_w.shape, bf),
            pltpu.VMEM(exp_w.shape, bf),
            pltpu.VMEM(con_w.shape, bf),
            pltpu.SemaphoreType.DMA((3,)),
            pltpu.VMEM((PLANES, QW, T), bf),
            sems(PLANES - 1),
            pltpu.VMEM((PLANES, QW, T), bf),
            sems(PLANES - 1),
            pltpu.VMEM((T, D), f32),
            pltpu.VMEM((T, D), bf),
            pltpu.VMEM((T, D), bf),
            pltpu.VMEM((T, ffn), f32),
            pltpu.VMEM((T, ffn), bf),
            pltpu.VMEM((T, 2 * ffn), bf),
            pltpu.VMEM((ffn, D), f32),
            pltpu.VMEM(half, bf),
            pltpu.VMEM(half, bf),
            pltpu.VMEM(half, bf),
            sems(2 + 2 * ffn // D),
        ],
        compiler_params=pltpu.CompilerParams(collective_id=2, has_side_effects=True, vmem_limit_bytes=60 << 20),
    )(lowt, tokens, cotangent, gains, out_w, exp_w, con_w)


def tail_kernel(
    n,
    groups,
    deal_ref,
    dq_ref,
    dkv_ref,
    turn_ref,
    gains_ref,
    gain_two_ref,
    joint_t_hbm,
    first_hbm,
    tokens_hbm,
    grad_hidden_hbm,
    y_keep_hbm,
    y_got_hbm,
    x_keep_hbm,
    x_got_hbm,
    z_keep_hbm,
    z_got_hbm,
    d_got,
    w_all,
    jq_all,
    jk_all,
    gain_all,
    joint_t,
    first,
    tokens,
    grad_hidden,
    y_keep,
    y_got,
    x_keep,
    x_got,
    z_keep,
    z_came,
    local_sems,
    kv_near,
    kv_send,
    kv_far,
    kv_sems,
    mixed_q,
    mixed_kv,
    part,
    part_got,
    part_send_sems,
    part_recv_sems,
    j_acc,
    jq,
    jq_core,
    jq_side,
    jq_plane,
    jk,
    jk_core,
    jk_side,
    jk_plane,
    j_sems,
    x1_got,
    y2_got,
    y3_got,
    x3_got,
    w_plane,
    w_plane_got,
    w_sems,
    d_send,
    d_mid,
    d_back,
    d_sems,
    gain_part,
    gain_got,
    gain_sems,
):
    bf, f32 = jnp.bfloat16, jnp.float32
    S = n // PLANES
    S2 = S // 2
    T, D = tokens.shape
    me, group = lax.axis_index("ctx"), lax.axis_index("fsdp")
    plane, side = me // S, lax.rem(me, S)
    s2, core = side // 2, lax.rem(side, 2)
    MESH = pl.DeviceIdType.MESH

    def at(p, a, c, g):
        return (p * S + a * 2 + c, g)

    def plane_peer(k):
        return at(lax.rem(plane + k, PLANES), s2, core, group)

    def side_peer(k):
        return at(plane, lax.rem(s2 + k, S2), core, group)

    def group_peer(k):
        return at(plane, s2, core, lax.rem(group + k, groups))

    core_peer = at(plane, s2, 1 - core, group)

    def send(source, target, send_sem, recv_sem, device):
        return pltpu.make_async_remote_copy(
            src_ref=source, dst_ref=target, send_sem=send_sem, recv_sem=recv_sem, device_id=device, device_id_type=MESH
        )

    def remote(source, target, sems, index, device):
        return send(source, target, sems.at[0, index], sems.at[1, index], device)

    def total_of(terms):
        total = terms[0].astype(f32)
        for term in terms[1:]:
            total = total + term.astype(f32)
        return total

    local = [
        pltpu.make_async_copy(source, target, local_sems.at[i])
        for i, (source, target) in enumerate(
            [
                (first_hbm, first),
                (joint_t_hbm, joint_t),
                (y_keep_hbm, y_keep),
                (y_got_hbm, y_got),
                (x_keep_hbm, x_keep),
                (x_got_hbm, x_got),
                (z_keep_hbm, z_keep),
                (z_got_hbm, z_came),
                (tokens_hbm, tokens),
                (grad_hidden_hbm, grad_hidden),
            ]
        )
    ]
    for copy in local:
        copy.start()
    barrier = pltpu.get_barrier_semaphore()

    def greet(k, carry):
        pl.semaphore_signal(barrier, inc=1, device_id=(lax.rem(me + k, n), group), device_id_type=MESH)
        return carry

    lax.fori_loop(1, n, greet, 0)
    for k in range(1, groups):
        pl.semaphore_signal(barrier, inc=1, device_id=group_peer(k), device_id_type=MESH)
    pl.semaphore_wait(barrier, n - 1 + groups - 1)

    lower = plane < 2
    middle = (plane == 1) | (plane == 2)
    order = [
        jnp.where(lower, 3, 0),
        jnp.where(plane == 0, 2, jnp.where(plane == 1, 0, jnp.where(plane == 2, 3, 1))),
        jnp.where((plane == 0) | (plane == 2), 1, 2),
        plane,
    ]
    steps = range(PLANES)
    back = [lax.rem(plane + PLANES - p, PLANES) for p in order]
    main = jnp.where(lower, 0, 1)
    main_plane = plane + 1 - 2 * main

    core_kv = [remote(dkv_ref.at[order[t], :, 1 - core], kv_near.at[t], kv_sems, t, core_peer) for t in steps]
    for copy in core_kv:
        copy.start()

    def turned_back(x, t):
        cos, sin = turn_ref[back[t], :HALF], turn_ref[back[t], HALF:]
        rows = []
        for h in range(HP):
            upper, lower = x[h * HD : h * HD + HALF], x[h * HD + HALF : (h + 1) * HD]
            rows += [upper * cos + lower * sin, lower * cos - upper * sin]
        return jnp.concatenate(rows, axis=0)

    side_kv = {}
    for t in steps:
        core_kv[t].wait()
        for a in range(S2):
            kv_send[t, a] = total_of([dkv_ref[order[t], a, core], kv_near[t, a]]).astype(bf)
        for k in range(1, S2):
            side_kv[t, k] = remote(
                kv_send.at[t, lax.rem(s2 + S2 - k, S2)],
                kv_far.at[t, k - 1],
                kv_sems,
                PLANES + t * (S2 - 1) + k - 1,
                side_peer(S2 - k),
            )
            side_kv[t, k].start()
    for t in steps:
        mixed_q[t] = turned_back(dq_ref[back[t]], t).astype(bf)

    w_moves = []

    def w_copy(source, target, device):
        copy = remote(source, target, w_sems, len(w_moves), device)
        w_moves.append(copy)
        copy.start()
        return copy

    local[4].wait()
    local[5].wait()
    for p in range(PLANES):
        for g in range(groups):
            x_keep[p, g] = total_of([x_keep[p, g]] + [x_got[k, p, g] for k in range(S2 - 1)]).astype(bf)
    y2 = [w_copy(x_keep.at[:, lax.rem(group + k, groups)], y2_got.at[k - 1], group_peer(k)) for k in range(1, groups)]
    local[2].wait()
    local[3].wait()
    for p in range(PLANES):
        for a in range(S2):
            y_keep[p, a] = total_of([y_keep[p, a]] + [y_got[k, p, a] for k in range(groups - 1)]).astype(bf)
    x1 = [w_copy(y_keep.at[:, lax.rem(s2 + k, S2)], x1_got.at[k - 1], side_peer(k)) for k in range(1, S2)]
    local[6].wait()
    local[7].wait()
    for a in range(S2):
        for g in range(groups):
            z_keep[a, g] = total_of([z_keep[a, g]] + [z_came[k, a, g] for k in range(PLANES - 1)]).astype(bf)
    y3 = [w_copy(z_keep.at[:, lax.rem(group + k, groups)], y3_got.at[k - 1], group_peer(k)) for k in range(1, groups)]

    j_moves = []

    def j_copy(source, target, device):
        copy = remote(source, target, j_sems, len(j_moves), device)
        j_moves.append(copy)
        copy.start()
        return copy

    def j_core_stage(mixed, grads, near):
        height = mixed.shape[1]
        j_acc[:height] = total_of(
            [jnp.dot(mixed[t], first[back[t]], preferred_element_type=f32) for t in steps]
        )
        shard_rows = D // n
        for i in range(D // 128):
            block = j_acc[:height, i * 128 : (i + 1) * 128].T
            row = i * 128
            while row < (i + 1) * 128:
                shard, offset = divmod(row, shard_rows)
                count = min(shard_rows - offset, (i + 1) * 128 - row)
                begin = row - i * 128
                grads[shard // S, shard % S // 2, shard % 2, offset : offset + count] = block[
                    begin : begin + count
                ].astype(bf)
                row += count
        return [j_copy(grads.at[:, :, 1 - core], near, core_peer)]

    def j_side_stage(moves, grads, near, far):
        for copy in moves:
            copy.wait()
        for p in range(PLANES):
            for a in range(S2):
                near[p, a] = total_of([grads[p, a, core], near[p, a]]).astype(bf)
        return [j_copy(near.at[:, lax.rem(s2 + k, S2)], far.at[k - 1], side_peer(k)) for k in range(1, S2)]

    def j_plane_stage(moves, near, far, gathered):
        for copy in moves:
            copy.wait()
        for p in range(PLANES):
            far[0, p] = total_of([near[p, s2]] + [far[k, p] for k in range(S2 - 1)]).astype(bf)
        gathered[plane] = far[0, plane]
        return [
            j_copy(far.at[0, lax.rem(plane + k, PLANES)], gathered.at[plane], plane_peer(k)) for k in range(1, PLANES)
        ]

    def j_group_stage(moves, gathered, every):
        for copy in moves:
            copy.wait()
        every[group] = gathered[...]
        return [j_copy(gathered, every.at[group], group_peer(k)) for k in range(1, groups)]

    local[0].wait()
    jq_moves = j_core_stage(mixed_q, jq, jq_core)

    local[1].wait()

    def main_send(t):
        return send(
            part.at[t],
            part_got.at[main, order[t]],
            part_send_sems.at[t],
            part_recv_sems.at[main * PLANES + order[t]],
            at(main_plane, s2, core, group),
        )

    def other_send(t):
        return send(
            part.at[t],
            part_got.at[1 - main, order[t]],
            part_send_sems.at[t],
            part_recv_sems.at[(1 - main) * PLANES + order[t]],
            at(2 * plane - main_plane, s2, core, group),
        )

    def came(direction, p):
        return send(
            part.at[0],
            part_got.at[direction, p],
            part_send_sems.at[0],
            part_recv_sems.at[direction * PLANES + p],
            core_peer,
        )

    strip = 64

    def add_part(t, direction, p):
        def body(i, carry):
            rows = pl.ds(pl.multiple_of(i * strip, strip), strip)
            part[t, rows] = total_of([part[t, rows], part_got[direction, p, rows]]).astype(bf)
            return carry

        lax.fori_loop(0, T // strip, body, 0)

    def relay(t, secondary):
        @pl.when(middle)
        def _():
            direction = 1 - main if secondary else main
            came(direction, order[t]).wait_recv()
            add_part(t, direction, order[t])
            (other_send if secondary else main_send)(t).start()

    def key_step(t):
        for k in range(1, S2):
            side_kv[t, k].wait()
        dk = total_of([kv_send[t, s2]] + [kv_far[t, k] for k in range(S2 - 1)]).T
        mixed_kv[t, :QW] = turned_back(dk[:QW], t).astype(bf)
        mixed_kv[t, QW:] = dk[QW:].astype(bf)
        grads = jnp.concatenate([mixed_q[t], mixed_kv[t]], axis=0)
        part[t] = jnp.dot(grads.T, joint_t[: 3 * QW], preferred_element_type=f32).astype(bf)
        if t < PLANES - 1:

            @pl.when(jnp.logical_not(middle))
            def _():
                main_send(t).start()

    key_step(0)
    jq_moves = j_side_stage(jq_moves, jq, jq_core, jq_side)
    key_step(1)
    key_step(2)
    relay(0, False)
    jq_moves = j_plane_stage(jq_moves, jq_core, jq_side, jq_plane)
    key_step(3)
    relay(2, False)
    jk_moves = j_core_stage(mixed_kv, jk, jk_core)

    for copy in y3:
        copy.wait()
    for a in range(S2):
        z_keep[a, group] = total_of([z_keep[a, group]] + [y3_got[k, a] for k in range(groups - 1)]).astype(bf)
    x3 = [w_copy(z_keep.at[lax.rem(s2 + k, S2), group], x3_got.at[k - 1], side_peer(k)) for k in range(1, S2)]
    relay(1, True)
    for copy in y2 + x1:
        copy.wait()
    for p in range(PLANES):
        w_plane[p, 0] = total_of([y_keep[p, s2]] + [x1_got[k, p] for k in range(S2 - 1)]).astype(bf)
        w_plane[p, 1] = total_of([x_keep[p, group]] + [y2_got[k, p] for k in range(groups - 1)]).astype(bf)
    jk_moves = j_side_stage(jk_moves, jk, jk_core, jk_side)
    w_last = [
        w_copy(w_plane.at[lax.rem(plane + k, PLANES)], w_plane_got.at[k - 1], plane_peer(k)) for k in range(1, PLANES)
    ]
    jq_moves = j_group_stage(jq_moves, jq_plane, jq_all)

    local[8].wait()
    local[9].wait()
    came(1 - main, plane).wait_recv()
    add_part(PLANES - 1, 1 - main, plane)

    @pl.when(middle)
    def _():
        came(main, plane).wait_recv()
        add_part(PLANES - 1, main, plane)

    def norm_back(i, total):
        rows = pl.ds(pl.multiple_of(i * strip, strip), strip)
        grad = part[PLANES - 1, rows].astype(f32)
        values = tokens[rows].astype(f32)
        centred = values - jnp.mean(values, axis=-1, keepdims=True)
        scale = lax.rsqrt(jnp.mean(centred * centred, axis=-1, keepdims=True) + norm_eps)
        normal = centred * scale
        total = total + jnp.sum(grad * normal, axis=0, keepdims=True)
        grad = grad * gains_ref[0:1]
        grad = grad - jnp.mean(grad, axis=-1, keepdims=True) - normal * jnp.mean(grad * normal, axis=-1, keepdims=True)
        grad_hidden[rows] = grad_hidden[rows] + grad * scale
        return total

    gain_one = lax.fori_loop(0, T // strip, norm_back, jnp.zeros((1, D), f32))

    blocks = T // BLOCK
    piece = BLOCK // n

    def d_copy(source, target, base, k):
        return remote(source.at[lax.rem(me + k, n)], target.at[me], d_sems, base + k, (lax.rem(me + k, n), group))

    for i in range(n):
        d_send[i] = jnp.concatenate(
            [grad_hidden[b * BLOCK + i * piece : b * BLOCK + (i + 1) * piece] for b in range(blocks)], axis=0
        ).astype(bf)
    out_deal = [d_copy(d_send, d_mid, 0, k) for k in range(1, n)]
    for copy in out_deal:
        copy.start()
    d_mid[me] = d_send[me]

    per = D // 128
    gain_part[...] = jnp.zeros_like(gain_part)
    for i in range(per):
        gain_part[i : i + 1] = gain_one[:, i * 128 : (i + 1) * 128]
        gain_part[per + i : per + i + 1] = gain_two_ref[0:1, i * 128 : (i + 1) * 128]
    gain_moves = [
        remote(gain_part, gain_got.at[me], gain_sems, k - 1, (lax.rem(me + k, n), group)) for k in range(1, n)
    ]
    for copy in gain_moves:
        copy.start()
    gain_got[me] = gain_part[...]
    jk_moves = j_plane_stage(jk_moves, jk_core, jk_side, jk_plane)

    for copy in out_deal:
        copy.wait()
    for i in range(n):
        chosen = []
        for b in range(blocks):
            wanted = deal_ref[i * blocks + b]
            held = d_mid[wanted // blocks].astype(f32)
            rows = held[:piece]
            for other in range(1, blocks):
                rows = jnp.where(lax.rem(wanted, blocks) == other, held[other * piece : (other + 1) * piece], rows)
            chosen.append(rows)
        d_back[i] = jnp.concatenate(chosen, axis=0).astype(bf)
    back_deal = [d_copy(d_back, d_got, n, k) for k in range(1, n)]
    for copy in back_deal:
        copy.start()
    d_got[me] = d_back[me]

    for copy in gain_moves:
        copy.wait()
    gain_part[...] = total_of([gain_got[i] for i in range(n)])
    gain_all[group] = gain_part[...]
    gain_last = [
        remote(gain_part, gain_all.at[group], gain_sems, n - 1 + k - 1, group_peer(k)) for k in range(1, groups)
    ]
    for copy in gain_last:
        copy.start()
    for copy in w_last + x3:
        copy.wait()
    height = w_plane.shape[2]
    for i in range(2):
        w_all[group, i * height : (i + 1) * height] = total_of(
            [w_plane[plane, i]] + [w_plane_got[k, i] for k in range(PLANES - 1)]
        ).astype(bf)
    w_all[group, 2 * height :] = total_of([z_keep[s2, group]] + [x3_got[k] for k in range(S2 - 1)]).astype(bf)
    w_gather = [w_copy(w_all.at[group], w_all.at[group], group_peer(k)) for k in range(1, groups)]
    jk_moves = j_group_stage(jk_moves, jk_plane, jk_all)

    for copy in back_deal + gain_last + w_gather + jq_moves + jk_moves:
        copy.wait()
    for t in range(PLANES - 1):
        came_from = send(part.at[t], part.at[t], part_send_sems.at[t], part_recv_sems.at[0], core_peer)
        came_from.wait_send()


def tail(n, groups, deal, dqt, dkv, turn, gains, gain_two, joint_t, first, tokens, grad_hidden, pieces):
    bf, f32 = jnp.bfloat16, jnp.float32
    S2 = n // PLANES // 2
    T, D = tokens.shape
    rows = D // n
    height = pieces[0].shape[2]
    piece_rows = T // n
    gain_rows = -(-2 * D // 128 // 8) * 8
    any_, vm, sm = (pl.BlockSpec(memory_space=m) for m in (pl.ANY, pltpu.VMEM, pltpu.SMEM))
    sems = lambda count: pltpu.SemaphoreType.DMA((2, count))
    small = lambda *s: pltpu.VMEM(s, bf)
    j_buffers = lambda w: [
        small(PLANES, S2, 2, rows, w),
        small(PLANES, S2, rows, w),
        small(S2 - 1, PLANES, rows, w),
        small(PLANES, rows, w),
    ]
    return pl.pallas_call(
        functools.partial(tail_kernel, n, groups),
        out_shape=(
            jax.ShapeDtypeStruct((n, piece_rows, D), bf),
            jax.ShapeDtypeStruct((groups, 3 * height, D), bf),
            jax.ShapeDtypeStruct((groups, PLANES, rows, QW), bf),
            jax.ShapeDtypeStruct((groups, PLANES, rows, 2 * QW), bf),
            jax.ShapeDtypeStruct((groups, gain_rows, 128), f32),
        ),
        in_specs=[sm, vm, vm, vm, vm, vm] + [any_] * 10,
        out_specs=tuple([vm] * 5),
        scratch_shapes=[
            pltpu.VMEM(joint_t.shape, bf),
            pltpu.VMEM((PLANES, T, D), bf),
            pltpu.VMEM((T, D), bf),
            pltpu.VMEM((T, D), f32),
            *[pltpu.VMEM(p.shape, bf) for p in pieces],
            pltpu.SemaphoreType.DMA((10,)),
            small(PLANES, S2, T, 2 * QW),
            small(PLANES, S2, T, 2 * QW),
            small(PLANES, S2 - 1, T, 2 * QW),
            sems(PLANES * S2),
            small(PLANES, QW, T),
            small(PLANES, 2 * QW, T),
            small(PLANES, T, D),
            small(2, PLANES, T, D),
            pltpu.SemaphoreType.DMA((PLANES - 1,)),
            pltpu.SemaphoreType.DMA((2 * PLANES,)),
            pltpu.VMEM((2 * QW, D), f32),
            *j_buffers(QW),
            *j_buffers(2 * QW),
            sems(2 * (1 + S2 - 1 + PLANES - 1 + groups - 1)),
            small(S2 - 1, PLANES, height, D),
            small(groups - 1, PLANES, height, D),
            small(groups - 1, S2, height, D),
            small(S2 - 1, height, D),
            small(PLANES, 2, height, D),
            small(PLANES - 1, 2, height, D),
            sems(3 * (groups - 1) + 2 * (S2 - 1) + PLANES - 1),
            small(n, piece_rows, D),
            small(n, piece_rows, D),
            small(n, piece_rows, D),
            sems(2 * n),
            pltpu.VMEM((gain_rows, 128), f32),
            pltpu.VMEM((n, gain_rows, 128), f32),
            sems(n - 1 + groups - 1),
        ],
        compiler_params=pltpu.CompilerParams(collective_id=0, has_side_effects=True, vmem_limit_bytes=60 << 20),
    )(deal, dqt, dkv, turn, gains, gain_two, joint_t, first, tokens, grad_hidden, *pieces)


def finish_kernel(n, d_ref, w_ref, jq_ref, jk_ref, dealt_ref, joint_ref, output_ref, expand_ref, contract_ref):
    f32 = jnp.float32
    T, D = dealt_ref.shape
    blocks = T // BLOCK
    piece = BLOCK // n
    for b in range(blocks):
        for i in range(0, n, 2):
            rows = [d_ref[i + e].astype(f32)[b * piece : (b + 1) * piece] for e in range(2)]
            dealt_ref[b * BLOCK + i * piece : b * BLOCK + (i + 2) * piece] = jnp.concatenate(rows, axis=0).astype(
                dealt_ref.dtype
            )

    def summed(ref, p):
        total = ref[0, p].astype(f32)
        for g in range(1, ref.shape[0]):
            total = total + ref[g, p].astype(f32)
        return total.T

    for i in range(PLANES // 2):
        pair = [summed(jq_ref, 2 * i + e) for e in range(2)]
        joint_ref[:, i * 2 * QW : (i + 1) * 2 * QW] = jnp.concatenate(pair, axis=0).T
        pair = [summed(jk_ref, 2 * i + e) for e in range(2)]
        for part in range(2):
            cols = (part + 1) * D + i * 2 * QW
            rows = [x[part * QW : (part + 1) * QW] for x in pair]
            joint_ref[:, cols : cols + 2 * QW] = jnp.concatenate(rows, axis=0).T
    height = w_ref.shape[1]
    rows = D // n
    targets = [(output_ref, 0, rows)]
    targets += [(expand_ref, i * D, rows) for i in range(expand_ref.shape[1] // D)]
    targets += [(contract_ref, 0, contract_ref.shape[0])]
    row = 0
    for target, column, count in targets:
        done = 0
        while done < count:
            g, offset = divmod(row, height)
            part = min(count - done, height - offset)
            target[done : done + part, column : column + D] = w_ref[g, offset : offset + part].astype(f32)
            done += part
            row += part


def finish(n, T, wide, contract_rows, d_got, w_all, jq_all, jk_all):
    D = d_got.shape[-1]
    rows = D // n
    f32 = jnp.float32
    vm = pl.BlockSpec(memory_space=pltpu.VMEM)
    return pl.pallas_call(
        functools.partial(finish_kernel, n),
        out_shape=(
            jax.ShapeDtypeStruct((T, D), jnp.bfloat16),
            jax.ShapeDtypeStruct((rows, 3 * D), f32),
            jax.ShapeDtypeStruct((rows, D), f32),
            jax.ShapeDtypeStruct((rows, wide), f32),
            jax.ShapeDtypeStruct((contract_rows, D), f32),
        ),
        in_specs=[vm] * 4,
        out_specs=tuple([vm] * 5),
    )(d_got, w_all, jq_all, jk_all)


def on_device(
    n,
    groups,
    tokens,
    cotangent,
    lengths,
    deal,
    joint_projection,
    output_projection,
    expand_weight,
    contract_weight,
    gain_first,
    gain_second,
):
    T, D = tokens.shape[1:]
    S = n // PLANES
    S2 = S // 2
    me = lax.axis_index("ctx")

    def over_planes(x, k):
        return lax.ppermute(x, "ctx", [(h * S + s, (h + k) % PLANES * S + s) for h in range(PLANES) for s in range(S)])

    def over_sides(x, k):
        pairs = [
            (h * S + a * 2 + c, h * S + (a + k) % S2 * 2 + c) for h in range(PLANES) for a in range(S2) for c in range(2)
        ]
        return lax.ppermute(x, "ctx", pairs)

    def over_groups(x, k):
        return lax.ppermute(x, "fsdp", [(f, (f + k) % groups) for f in range(groups)])

    def moved(x, over):
        if x.shape[0] == 1:
            return over(x, 1)
        return jnp.stack([over(x[k], k + 1) for k in range(x.shape[0])])

    first, qt, kv, joint_t, turn, gains, out_w, exp_w, con_w = front(
        n,
        groups,
        lengths,
        tokens[0],
        joint_projection,
        gain_first,
        gain_second,
        output_projection,
        expand_weight,
        contract_weight,
    )
    out_w, exp_w, con_w = (w.reshape(-1, w.shape[-1]) for w in (out_w, exp_w, con_w))
    ot, lowt, lse = attn_fwd(n, lengths, qt, kv)
    output, grad_hidden, gt, gain_two, y_keep, y_send, x_keep, x_send, z_keep, z_send = middle(
        n, groups, lowt, tokens[0], cotangent[0], gains, out_w, exp_w, con_w
    )
    y_got, x_got, z_got = moved(y_send, over_groups), moved(x_send, over_sides), moved(z_send, over_planes)
    dqt, dkv = attn_bwd(n, lengths, qt, kv, ot, lse, gt)
    d_got, w_all, jq_all, jk_all, gain_all = tail(
        n,
        groups,
        deal[0],
        dqt,
        dkv.reshape(PLANES, S2, 2, T, 2 * QW),
        turn,
        gains,
        gain_two,
        joint_t,
        first,
        tokens[0],
        grad_hidden,
        [y_keep, y_got, x_keep, x_got, z_keep, z_got],
    )
    dealt, shard_joint, shard_output, shard_expand, shard_contract = finish(
        n, T, exp_w.shape[1], con_w.shape[0] // n, d_got, w_all, jq_all, jk_all
    )
    width = D // n
    gain_grads = jnp.sum(gain_all, axis=0).reshape(-1)[: 2 * D].reshape(2, D)
    gain_grads = lax.dynamic_slice_in_dim(gain_grads, me * width, width, axis=1)
    return (
        output[None],
        dealt[None],
        shard_joint,
        shard_output,
        shard_expand,
        shard_contract,
        gain_grads[0],
        gain_grads[1],
    )


def solution(mesh):
    return jax.shard_map(
        functools.partial(on_device, mesh.shape["ctx"], mesh.shape["fsdp"]),
        mesh=mesh,
        in_specs=(
            P("fsdp", "ctx", None),
            P("fsdp", "ctx", None),
            P("fsdp", None),
            P("fsdp", None),
            P("fsdp", None),
            P("fsdp", None),
            P("fsdp", None),
            P("fsdp", None),
            P("fsdp"),
            P("fsdp"),
        ),
        out_specs=(
            P("fsdp", "ctx", None),
            P("fsdp", "ctx", None),
            P("ctx", None),
            P("ctx", None),
            P("ctx", None),
            P("ctx", None),
            P("ctx"),
            P("ctx"),
        ),
        check_vma=False,
    )
```

```python
import functools
import math

import jax
import jax.numpy as jnp
import numpy as np
from jax import lax
from jax.experimental import pallas as pl
from jax.experimental.pallas import tpu as pltpu
from jax.sharding import PartitionSpec as P

FF = 1152
HEADS = 12
HEAD_DIM = 64
BLOCK = 128
PLANES = 4
HD = HEAD_DIM
HALF = HEAD_DIM // 2
HP = HEADS // PLANES
QW = HP * HEAD_DIM
rope_base = 160000.0
norm_eps = 1e-05
MASKED = -1e30


def ends_of(lengths_ref, count):
    ends, total = [], 0
    for i in range(count):
        total = total + lengths_ref[0, i]
        ends.append(total)
    return ends


def span_of(index, ends):
    begin, end = jnp.zeros_like(index), jnp.full_like(index, ends[0])
    for before, after in zip(ends[:-1], ends[1:]):
        begin = jnp.where(index >= before, before, begin)
        end = jnp.where(index >= before, after, end)
    return begin, end


def head_rows(x, head):
    rows = lax.broadcasted_iota(jnp.int32, x.shape, 0)
    return jnp.where((rows >= head * HD) & (rows < (head + 1) * HD), x, jnp.zeros_like(x))


def query_block(n, b, T, ends):
    S = n // PLANES
    me = lax.axis_index("ctx")
    base = (lax.rem(me // S + PLANES - b, PLANES) * S + lax.rem(me, S)) * T
    low_begin, low_end = span_of(base, ends)
    high_begin, high_end = span_of(base + T - 1, ends)
    low, high = low_begin // T, (high_end + T - 1) // T
    full_low = jnp.clip((high_begin + T - 1) // T, low, high)
    full_high = jnp.clip(low_end // T, full_low, high)
    begin, end = span_of(base + lax.broadcasted_iota(jnp.int32, (8, T), 1), ends)
    return (low, full_low, full_high, high), begin[0:1], end[0:1]


def over_units(bounds, step):
    low, full_low, full_high, high = bounds

    def run(begin, end, masked):
        def body(u, carry):
            step(u, masked)
            return carry

        lax.fori_loop(begin, end, body, 0)

    run(low, full_low, True)
    in_pairs(full_low, full_high, lambda u: step(u, False))
    run(full_high, high, True)


def in_pairs(begin, end, step):
    pairs = (end - begin) // 2

    def two(i, carry):
        step(begin + 2 * i)
        step(begin + 2 * i + 1)
        return carry

    def one(u, carry):
        step(u)
        return carry

    lax.fori_loop(0, pairs, two, 0)
    lax.fori_loop(begin + 2 * pairs, end, one, 0)


def fwd_kernel(n, count, lengths_ref, qt_ref, kv_ref, ot_ref, lowt_ref, lse_ref, values, scores, top, total, acc):
    units, T, _ = kv_ref.shape
    ends = ends_of(lengths_ref, count)

    def flip(u, carry):
        values[u] = kv_ref[u, :, 128:].T
        return carry

    lax.fori_loop(0, units, flip, 0, unroll=4)

    def one_query_block(b, carry):
        qt = qt_ref[b]
        qheads = [head_rows(qt, h) for h in range(HP)]
        bounds, q_start, q_end = query_block(n, b, T, ends)
        top[...] = jnp.full_like(top, MASKED)
        total[...] = jnp.zeros_like(total)
        acc[...] = jnp.zeros_like(acc)

        def score(u, masked):
            k = kv_ref[u, :, :QW]
            st = [jnp.dot(k, qheads[h], preferred_element_type=jnp.float32) for h in range(HP)]
            if masked:
                at = u * T + lax.broadcasted_iota(jnp.int32, (T, T), 0)
                allowed = (at >= q_start) & (at < q_end)
                st = [jnp.where(allowed, s, MASKED) for s in st]
            for h in range(HP):
                scores[u, h] = st[h]
                top[h] = jnp.maximum(top[h], jnp.max(st[h].reshape(T // 8, 8, T), axis=0))

        over_units(bounds, score)
        m = [jnp.max(top[h], axis=0, keepdims=True) for h in range(HP)]

        def gather(u):
            p = [jnp.exp(scores[u, h] - m[h]) for h in range(HP)]
            for h in range(HP):
                total[h] += jnp.sum(p[h].reshape(T // 8, 8, T), axis=0)
                rows = pl.ds(h * HD, HD)
                acc[rows, :] += jnp.dot(
                    values[u, pl.ds(HD + h * HD, HD), :], p[h].astype(jnp.bfloat16), preferred_element_type=jnp.float32
                )

        in_pairs(bounds[0], bounds[3], gather)
        for h in range(HP):
            rows = pl.ds(h * HD, HD)
            l = jnp.sum(total[h], axis=0, keepdims=True)
            o = acc[rows, :] / l
            ot_ref[b, rows, :] = o
            lowt_ref[b, rows, :] = o.astype(jnp.bfloat16)
            lse_ref[b, h : h + 1, :] = m[h] + jnp.log(l)
        return carry

    lax.fori_loop(0, qt_ref.shape[0], one_query_block, 0)


def attn_fwd(n, lengths, qt, kv):
    B, _, T = qt.shape
    U = kv.shape[0]
    sm, vm = pl.BlockSpec(memory_space=pltpu.SMEM), pl.BlockSpec(memory_space=pltpu.VMEM)
    return pl.pallas_call(
        functools.partial(fwd_kernel, n, lengths.shape[1]),
        out_shape=(
            jax.ShapeDtypeStruct((B, QW, T), jnp.float32),
            jax.ShapeDtypeStruct((B, QW, T), jnp.bfloat16),
            jax.ShapeDtypeStruct((B, 8, T), jnp.float32),
        ),
        in_specs=[sm, vm, vm],
        out_specs=(vm, vm, vm),
        scratch_shapes=[
            pltpu.VMEM((U, 256, T), jnp.bfloat16),
            pltpu.VMEM((U, HP, T, T), jnp.float32),
            pltpu.VMEM((HP, 8, T), jnp.float32),
            pltpu.VMEM((HP, 8, T), jnp.float32),
            pltpu.VMEM((QW, T), jnp.float32),
        ],
        compiler_params=pltpu.CompilerParams(vmem_limit_bytes=60 << 20),
    )(lengths, qt, kv)


def bwd_kernel(n, count, lengths_ref, qt_ref, kv_ref, ot_ref, lse_ref, gt_ref, dqt_ref, dkv_ref, keys, dk, dv, dq):
    units, T, _ = kv_ref.shape
    ends = ends_of(lengths_ref, count)

    def flip(u, carry):
        keys[u] = kv_ref[u, :, :256].T
        dk[u] = jnp.zeros_like(dk[u])
        dv[u] = jnp.zeros_like(dv[u])
        return carry

    lax.fori_loop(0, units, flip, 0, unroll=4)

    def one_query_block(b, carry):
        qt, gt = qt_ref[b], gt_ref[b]
        zero = jnp.zeros((HD, T), jnp.bfloat16)
        qheads = [head_rows(qt, h) for h in range(HP)]
        gheads = [head_rows(gt, h) for h in range(HP)]
        gpad = [jnp.concatenate([zero, x], axis=0) for x in gheads]
        q = jnp.concatenate([jnp.concatenate([x, zero], axis=0).T for x in qheads], axis=0)
        g = jnp.concatenate([x.T for x in gpad], axis=0)
        bounds, q_start, q_end = query_block(n, b, T, ends)
        prod = gt.astype(jnp.float32) * ot_ref[b]
        delta = [jnp.sum(prod[h * HD : (h + 1) * HD], axis=0, keepdims=True) for h in range(HP)]
        lse = [lse_ref[b, h : h + 1, :] for h in range(HP)]
        dq[...] = jnp.zeros_like(dq)

        def one_unit(u, masked):
            k, v = kv_ref[u, :, :QW], kv_ref[u, :, 128:]
            st = [jnp.dot(k, qheads[h], preferred_element_type=jnp.float32) for h in range(HP)]
            dp = [jnp.dot(v, gpad[h], preferred_element_type=jnp.float32) for h in range(HP)]
            st = [st[h] - lse[h] for h in range(HP)]
            if masked:
                at = u * T + lax.broadcasted_iota(jnp.int32, (T, T), 0)
                allowed = (at >= q_start) & (at < q_end)
                st = [jnp.where(allowed, s, MASKED) for s in st]
            p = [jnp.exp(s) for s in st]
            ds = [(p[h] * (dp[h] - delta[h])).astype(jnp.bfloat16) for h in range(HP)]
            p = [x.astype(jnp.bfloat16) for x in p]
            dv[u] += jnp.dot(jnp.concatenate(p, axis=1), g, preferred_element_type=jnp.float32)
            dk[u] += jnp.dot(jnp.concatenate(ds, axis=1), q, preferred_element_type=jnp.float32)
            for h in range(HP):
                rows = pl.ds(h * HD, HD)
                dq[rows, :] += jnp.dot(keys[u, rows, :], ds[h], preferred_element_type=jnp.float32)

        over_units(bounds, one_unit)
        dqt_ref[b] = dq[...] * (HD**-0.5)
        return carry

    lax.fori_loop(0, qt_ref.shape[0], one_query_block, 0)

    def out(u, carry):
        dkv_ref[u, :, :128] = dk[u, :, :128].astype(jnp.bfloat16)
        dkv_ref[u, :, 128:256] = (dk[u, :, 128:] + dv[u, :, :128]).astype(jnp.bfloat16)
        dkv_ref[u, :, 256:] = dv[u, :, 128:].astype(jnp.bfloat16)
        return carry

    lax.fori_loop(0, units, out, 0, unroll=2)


def attn_bwd(n, lengths, qt, kv, ot, lse, gt):
    B, _, T = qt.shape
    U = kv.shape[0]
    sm, vm = pl.BlockSpec(memory_space=pltpu.SMEM), pl.BlockSpec(memory_space=pltpu.VMEM)
    return pl.pallas_call(
        functools.partial(bwd_kernel, n, lengths.shape[1]),
        out_shape=(jax.ShapeDtypeStruct((B, QW, T), jnp.float32), jax.ShapeDtypeStruct((U, T, 2 * QW), jnp.bfloat16)),
        in_specs=[sm] + [vm] * 5,
        out_specs=(vm, vm),
        scratch_shapes=[
            pltpu.VMEM((U, 256, T), jnp.bfloat16),
            pltpu.VMEM((U, T, 256), jnp.float32),
            pltpu.VMEM((U, T, 256), jnp.float32),
            pltpu.VMEM((QW, T), jnp.float32),
        ],
        compiler_params=pltpu.CompilerParams(vmem_limit_bytes=60 << 20),
    )(lengths, qt, kv, ot, lse, gt)
def front_kernel(
    n,
    groups,
    count,
    lengths_ref,
    tokens_ref,
    joint_ref,
    gain_one_ref,
    gain_two_ref,
    out_hbm,
    exp_hbm,
    con_hbm,
    first_ref,
    qt_ref,
    kv_ref,
    joint_t_out,
    turn_ref,
    gains_ref,
    out_all,
    exp_all,
    con_all,
    held,
    t_sems,
    cols,
    cols_all,
    gain_held,
    g_sems,
    kv_own,
    kv_sems,
    own_sems,
    w_sems,
    w_local,
    joint_rows,
    out_held,
    exp_held,
    con_held,
):
    bf, f32 = jnp.bfloat16, jnp.float32
    S = n // PLANES
    S2 = S // 2
    T, D = tokens_ref.shape
    me, group = lax.axis_index("ctx"), lax.axis_index("fsdp")
    plane, side = me // S, lax.rem(me, S)
    s2, core = side // 2, lax.rem(side, 2)

    def at(p, a, c, g):
        return (p * S + a * 2 + c, g)

    def side_peer(k):
        return at(plane, lax.rem(s2 + k, S2), core, group)

    def group_peer(k):
        return at(plane, s2, core, lax.rem(group + k, groups))

    core_peer = at(plane, s2, 1 - core, group)

    def remote(source, target, sems, index, device):
        return pltpu.make_async_remote_copy(
            src_ref=source,
            dst_ref=target,
            send_sem=sems.at[0, index],
            recv_sem=sems.at[1, index],
            device_id=device,
            device_id_type=pl.DeviceIdType.MESH,
        )

    barrier = pltpu.get_barrier_semaphore()

    def greet(device):
        pl.semaphore_signal(barrier, inc=1, device_id=device, device_id_type=pl.DeviceIdType.MESH)

    for k in range(1, PLANES):
        greet(at(lax.rem(plane + k, PLANES), s2, core, group))
    for k in range(1, S2):
        greet(side_peer(k))
    for k in range(1, groups):
        greet(group_peer(k))
    greet(core_peer)
    pl.semaphore_wait(barrier, PLANES - 1 + S2 - 1 + groups - 1 + 1)

    def up(p):
        return remote(held.at[p], held.at[p], t_sems, p, at(plane + 1, s2, core, group))

    def down(p):
        return remote(held.at[p], held.at[p], t_sems, PLANES + p, at(plane - 1, s2, core, group))

    held[plane] = tokens_ref[...]

    @pl.when(plane < PLANES - 1)
    def _():
        up(plane).start()

    @pl.when(plane > 0)
    def _():
        down(plane).start()

    pair = 2 * QW
    for part in range(3):
        window = joint_ref[:, pl.ds(pl.multiple_of(part * D + plane // 2 * pair, 128), pair)].T
        chosen = jnp.where(lax.rem(plane, 2) == 0, window[:QW].astype(f32), window[QW:].astype(f32))
        half = 3 * QW // 2
        low, high = part * QW, (part + 1) * QW
        for c in range(2):
            begin, end = max(low, c * half), min(high, (c + 1) * half)
            if begin < end:
                cols[c, begin - c * half : end - c * half] = chosen[begin - low : end - low].astype(bf)
    gain_held[group] = jnp.zeros_like(gain_held[group])
    gain_held[group, 0:1] = gain_one_ref[...].astype(f32).reshape(1, -1)
    gain_held[group, 1:2] = gain_two_ref[...].astype(f32).reshape(1, -1)
    col_moves = [
        remote(cols.at[core], cols_all.at[group, core], g_sems, k - 1, group_peer(k)) for k in range(1, groups)
    ]
    col_hands = []
    for k in range(1, groups):
        came = cols_all.at[lax.rem(group + groups - k, groups), core]
        col_hands.append(remote(came, came, g_sems, 2 * (groups - 1) + k - 1, core_peer))
    gain_moves = [
        remote(gain_held.at[group], gain_held.at[group], g_sems, groups - 1 + k - 1, group_peer(k))
        for k in range(1, groups)
    ]
    for copy in gain_moves + col_moves:
        copy.start()
    cols_all[group] = cols[...]

    weights = [(out_hbm, out_all, out_held), (exp_hbm, exp_all, exp_held), (con_hbm, con_all, con_held)]
    w_in, w_own, w_first, w_second = [], [], [], []
    for i, (source, target, bounce) in enumerate(weights):
        w_in.append(pltpu.make_async_copy(source, bounce, w_local.at[0, i]))
        w_own.append(pltpu.make_async_copy(bounce, target.at[group], w_local.at[1, i]))
        for k in range(1, groups):
            index = (i * (groups - 1) + k - 1) * 2
            w_first.append(remote(source.at[core], target.at[group, core], w_sems, index, group_peer(k)))
            came = lax.rem(group + groups - k, groups)
            w_second.append(remote(target.at[came, core], target.at[came, core], w_sems, index + 1, core_peer))
    for copy in w_in:
        copy.start()

    ends = ends_of(lengths_ref, count)
    row = lax.broadcasted_iota(jnp.int32, (HALF, T), 0)
    frequencies = jnp.zeros((HALF, T), f32)
    for i in range(HALF):
        frequencies = jnp.where(row == i, float(np.float32(rope_base ** (-2.0 * i / HEAD_DIM))), frequencies)
    for j in range(PLANES):
        base = (lax.rem(plane + PLANES - j, PLANES) * S + side) * T
        index = base + lax.broadcasted_iota(jnp.int32, (8, T), 1)
        begin, _ = span_of(index, ends)
        angles = (index - begin)[0:1].astype(f32) * frequencies
        turn_ref[j, :HALF] = jnp.cos(angles)
        turn_ref[j, HALF:] = jnp.sin(angles)

    strip = 64

    def kv_unit(p, a, c):
        return p * S + a * 2 + c

    def side_kv(j, k):
        p = lax.rem(plane + PLANES - j, PLANES)
        return remote(kv_own.at[j], kv_ref.at[kv_unit(p, s2, core)], kv_sems, j * (2 * S2 - 1) + k - 1, side_peer(k))

    def core_kv(j, k):
        p = lax.rem(plane + PLANES - j, PLANES)
        unit = kv_unit(p, lax.rem(s2 + S2 - k, S2), core)
        source = kv_own.at[j] if k == 0 else kv_ref.at[unit]
        return remote(source, kv_ref.at[unit], kv_sems, j * (2 * S2 - 1) + S2 - 1 + k, core_peer)

    def own_kv(j):
        p = lax.rem(plane + PLANES - j, PLANES)
        return pltpu.make_async_copy(kv_own.at[j], kv_ref.at[kv_unit(p, s2, core)], own_sems.at[j])

    def process(p):
        j = lax.rem(plane + PLANES - p, PLANES)

        def norm(i, carry):
            rows = pl.ds(pl.multiple_of(i * strip, strip), strip)
            values = held[p, rows].astype(f32)
            centred = values - jnp.mean(values, axis=-1, keepdims=True)
            spread = jnp.mean(centred * centred, axis=-1, keepdims=True)
            first_ref[j, rows] = (centred * lax.rsqrt(spread + norm_eps) * gains_ref[0:1]).astype(bf)
            return carry

        lax.fori_loop(0, T // strip, norm, 0)
        mixed = lax.dot_general(
            joint_t_out[: 3 * QW], first_ref[j], (((1,), (1,)), ((), ())), preferred_element_type=f32
        )
        cos, sin = turn_ref[j, :HALF], turn_ref[j, HALF:]
        turned = []
        for h in range(2 * HP):
            upper, lower = mixed[h * HD : h * HD + HALF], mixed[h * HD + HALF : (h + 1) * HD]
            turned += [upper * cos - lower * sin, lower * cos + upper * sin]
        q = jnp.concatenate(turned[: 2 * HP], axis=0).astype(bf)
        qt_ref[j] = (q.astype(f32) * HEAD_DIM**-0.5).astype(bf)
        kv_own[j] = jnp.concatenate(turned[2 * HP :] + [mixed[2 * QW :]], axis=0).T.astype(bf)
        for k in range(1, S2):
            side_kv(j, k).start()
        core_kv(j, 0).start()
        own_kv(j).start()

    def hand_on(t):
        @pl.when(plane >= t)
        def _():
            up(plane - t).wait_recv()

            @pl.when(plane < PLANES - 1)
            def _():
                up(plane - t).start()

        @pl.when(plane + t < PLANES)
        def _():
            down(plane + t).wait_recv()

            @pl.when(plane > 0)
            def _():
                down(plane + t).start()

    def process_arrived(t):
        below = jnp.where(plane >= t, 1, 0)
        above = jnp.where(plane + t < PLANES, 1, 0)

        def arrived(i, carry):
            process(jnp.where(i < below, plane - t, plane + t))
            return carry

        lax.fori_loop(0, below + above, arrived, 0)

    hand_on(1)
    for copy in gain_moves:
        copy.wait()
    share = D // groups
    total = jnp.zeros((8, D), f32)
    for g in range(groups):
        rows = lax.broadcasted_iota(jnp.int32, (share, D), 0)
        lanes = lax.broadcasted_iota(jnp.int32, (share, D), 1)
        place = jnp.where(lanes == rows + g * share, 1.0, 0.0).astype(bf)
        total = total + jnp.dot(gain_held[g].astype(bf), place, preferred_element_type=f32)
    gains_ref[...] = total
    for copy, hand in zip(col_moves, col_hands):
        copy.wait()
        hand.start()
    for copy in w_first:
        copy.start()
    for copy in w_in:
        copy.wait()
    for copy in w_own:
        copy.start()
    for copy in col_hands:
        copy.wait()
    width = joint_t_out.shape[0]
    for g in range(groups):
        whole = jnp.concatenate([cols_all[g, 0], cols_all[g, 1], jnp.zeros((width - 3 * QW, share), bf)], axis=0)
        if share % 128 == 0:
            joint_t_out[:, g * share : (g + 1) * share] = whole
        else:
            joint_rows[g * share : (g + 1) * share] = whole.T
    if share % 128:
        for i in range(D // 128):
            joint_t_out[:, i * 128 : (i + 1) * 128] = joint_rows[i * 128 : (i + 1) * 128].T

    process(plane)
    hand_on(2)
    process_arrived(1)
    hand_on(3)
    process_arrived(2)
    process_arrived(3)

    for j in range(PLANES):
        for k in range(1, S2):
            side_kv(j, k).wait_recv()
            core_kv(j, k).start()
    for first_move, second_move in zip(w_first, w_second):
        first_move.wait_recv()
        second_move.start()

    for j in range(PLANES):
        own_kv(j).wait()
        for k in range(1, S2):
            side_kv(j, k).wait_send()
        for k in range(S2):
            core_kv(j, k).wait()
    for p in range(PLANES):

        @pl.when((plane < PLANES - 1) & (plane >= p))
        def _(p=p):
            up(p).wait_send()

        @pl.when((plane > 0) & (plane <= p))
        def _(p=p):
            down(p).wait_send()

    for copy in w_own:
        copy.wait()
    for first_move, second_move in zip(w_first, w_second):
        first_move.wait_send()
        second_move.wait()


def front(n, groups, lengths, tokens, joint_shard, gain_first, gain_second, out_w, exp_w, con_w):
    bf, f32 = jnp.bfloat16, jnp.float32
    S2 = n // PLANES // 2
    T, D = tokens.shape
    width = 3 * QW + 64
    share = D // groups
    any_, vm, sm = (pl.BlockSpec(memory_space=m) for m in (pl.ANY, pltpu.VMEM, pltpu.SMEM))
    sems = lambda count: pltpu.SemaphoreType.DMA((2, count))
    halves = lambda w: w.reshape(2, w.shape[0] // 2, w.shape[1])
    weights = [halves(w) for w in (out_w, exp_w, con_w)]
    return pl.pallas_call(
        functools.partial(front_kernel, n, groups, lengths.shape[1]),
        out_shape=(
            jax.ShapeDtypeStruct((PLANES, T, D), bf),
            jax.ShapeDtypeStruct((PLANES, QW, T), bf),
            jax.ShapeDtypeStruct((n, T, 2 * QW), bf),
            jax.ShapeDtypeStruct((width, D), bf),
            jax.ShapeDtypeStruct((PLANES, 2 * HALF, T), f32),
            jax.ShapeDtypeStruct((8, D), f32),
            *[jax.ShapeDtypeStruct((groups, *w.shape), bf) for w in weights],
        ),
        in_specs=[sm, vm, vm, vm, vm, any_, any_, any_],
        out_specs=(vm, vm, any_, vm, vm, vm, any_, any_, any_),
        scratch_shapes=[
            pltpu.VMEM((PLANES, T, D), bf),
            sems(2 * PLANES),
            pltpu.VMEM((2, 3 * QW // 2, share), bf),
            pltpu.VMEM((groups, 2, 3 * QW // 2, share), bf),
            pltpu.VMEM((groups, 8, share), f32),
            sems(3 * (groups - 1)),
            pltpu.VMEM((PLANES, T, 2 * QW), bf),
            sems(PLANES * (2 * S2 - 1)),
            pltpu.SemaphoreType.DMA((PLANES,)),
            sems(2 * len(weights) * (groups - 1)),
            pltpu.SemaphoreType.DMA((2, len(weights))),
            pltpu.VMEM((D, width), bf),
            *[pltpu.VMEM(w.shape, bf) for w in weights],
        ],
        compiler_params=pltpu.CompilerParams(collective_id=1, has_side_effects=True, vmem_limit_bytes=60 << 20),
    )(
        lengths,
        tokens,
        joint_shard,
        gain_first,
        gain_second,
        *weights,
    )


def middle_kernel(
    n,
    groups,
    low_ref,
    tokens_ref,
    cot_ref,
    gains_ref,
    out_hbm,
    exp_hbm,
    con_hbm,
    output_ref,
    grad_hidden_ref,
    gt_ref,
    y_keep,
    y_send,
    x_keep,
    x_send,
    z_keep,
    z_send_1,
    z_send_2,
    z_send_3,
    out_w,
    exp_w,
    con_w,
    local_sems,
    att,
    a_sems,
    g_send,
    g_sems,
    hidden,
    second,
    branch,
    ga,
    act,
    gexp,
    acc,
    w_own,
    w_other,
    w_got,
    w_sems,
):
    bf, f32 = jnp.bfloat16, jnp.float32
    S = n // PLANES
    S2 = S // 2
    T, D = tokens_ref.shape
    FFN = act.shape[1]
    me, group = lax.axis_index("ctx"), lax.axis_index("fsdp")
    plane, side = me // S, lax.rem(me, S)
    s2, core = side // 2, lax.rem(side, 2)

    def plane_peer(k):
        return (lax.rem(plane + k, PLANES) * S + side, group)

    core_peer = (plane * S + s2 * 2 + 1 - core, group)

    def remote(source, target, sems, index, device):
        return pltpu.make_async_remote_copy(
            src_ref=source,
            dst_ref=target,
            send_sem=sems.at[0, index],
            recv_sem=sems.at[1, index],
            device_id=device,
            device_id_type=pl.DeviceIdType.MESH,
        )

    local = [
        pltpu.make_async_copy(source, target, local_sems.at[i])
        for i, (source, target) in enumerate([(con_hbm, con_w), (out_hbm, out_w), (exp_hbm, exp_w)])
    ]
    for copy in local:
        copy.start()
    barrier = pltpu.get_barrier_semaphore()
    for k in range(1, PLANES):
        pl.semaphore_signal(barrier, inc=1, device_id=plane_peer(k), device_id_type=pl.DeviceIdType.MESH)
    pl.semaphore_signal(barrier, inc=1, device_id=core_peer, device_id_type=pl.DeviceIdType.MESH)
    pl.semaphore_wait(barrier, PLANES)

    home = [remote(low_ref.at[j], att.at[plane], a_sems, j - 1, plane_peer(PLANES - j)) for j in range(1, PLANES)]
    for copy in home:
        copy.start()
    att[plane] = low_ref[0]

    def nt(a, b):
        return lax.dot_general(a, b, (((1,), (1,)), ((), ())), preferred_element_type=f32)

    chunk = 384
    local[0].wait()
    cot = cot_ref[...]
    for c in range(0, FFN, chunk):
        ga[:, c : c + chunk] = nt(cot, con_w[c : c + chunk])
    local[1].wait()
    for copy in home:
        copy.wait()
    attended = att[...].reshape(D, T)
    hidden[...] = tokens_ref[...].astype(f32) + jnp.dot(attended.T, out_w[...], preferred_element_type=f32)

    strip = 64

    def norm(i, carry):
        rows = pl.ds(pl.multiple_of(i * strip, strip), strip)
        values = hidden[rows]
        centred = values - jnp.mean(values, axis=-1, keepdims=True)
        spread = jnp.mean(centred * centred, axis=-1, keepdims=True)
        second[rows] = (centred * lax.rsqrt(spread + norm_eps) * gains_ref[1:2]).astype(bf)
        return carry

    lax.fori_loop(0, T // strip, norm, 0)
    local[2].wait()
    for c in range(0, FFN, chunk):
        cols, gate_cols = slice(c, c + chunk), slice(FFN + c, FFN + c + chunk)
        inner = jnp.dot(second[...], exp_w[:, cols], preferred_element_type=f32)
        gate = jnp.dot(second[...], exp_w[:, gate_cols], preferred_element_type=f32)
        share = 0.5 * (1.0 + lax.erf(inner * (0.5**0.5)))
        bent = inner * share
        act[:, cols] = (bent * gate).astype(bf)
        grad = ga[:, cols]
        slope = share + inner * jnp.exp(-0.5 * inner * inner) * ((2.0 * math.pi) ** -0.5)
        gexp[:, cols] = (grad * gate * slope).astype(bf)
        gexp[:, gate_cols] = (grad * bent).astype(bf)
    output_ref[...] = (hidden[...] + jnp.dot(act[...], con_w[...], preferred_element_type=f32)).astype(bf)
    acc[:T] = nt(gexp[...], exp_w[...])

    def norm_back(i, total):
        rows = pl.ds(pl.multiple_of(i * strip, strip), strip)
        values = hidden[rows]
        centred = values - jnp.mean(values, axis=-1, keepdims=True)
        scale = lax.rsqrt(jnp.mean(centred * centred, axis=-1, keepdims=True) + norm_eps)
        normal = centred * scale
        grad = acc[rows]
        total = total + jnp.sum(grad * normal, axis=0, keepdims=True)
        grad = grad * gains_ref[1:2]
        grad = grad - jnp.mean(grad, axis=-1, keepdims=True) - normal * jnp.mean(grad * normal, axis=-1, keepdims=True)
        back = cot_ref[rows].astype(f32) + grad * scale
        grad_hidden_ref[rows] = back
        branch[rows] = back.astype(bf)
        return total

    total = lax.fori_loop(0, T // strip, norm_back, jnp.zeros((1, D), f32))
    gain_two = jnp.broadcast_to(total, (8, D))
    for p in range(PLANES):
        g_send[p] = nt(out_w[p * QW : (p + 1) * QW], branch[...]).astype(bf)
    away = [
        remote(g_send.at[lax.rem(plane + k, PLANES)], gt_ref.at[k], g_sems, k - 1, plane_peer(k))
        for k in range(1, PLANES)
    ]
    for copy in away:
        copy.start()
    gt_ref[0] = g_send[plane]

    sent = []

    def place(rows, offset, height):
        for target, parity in ((w_other, 1 - core), (w_own, core)):

            def body(m, carry):
                if rows % 8:
                    pair = acc[pl.ds(pl.multiple_of(2 * m * rows, 8), 2 * rows)]
                    value = jnp.where(parity == 0, pair[:rows], pair[rows:])
                else:
                    value = acc[pl.ds(pl.multiple_of((2 * m + parity) * rows, 8), rows)]
                if height > rows:
                    rest = jnp.zeros((height - rows - 8, D), f32)
                    value = jnp.concatenate([value, gain_two, rest], axis=0)
                value = value.astype(bf)
                target[m, offset : offset + height] = value
                return carry

            lax.fori_loop(0, n // 2, body, 0)
        part = pl.ds(offset, height)
        sent.append(remote(w_other.at[:, part], w_got.at[:, part], w_sems, len(sent), core_peer))
        sent[-1].start()

    rows = D // n
    acc[:D] = jnp.dot(attended, branch[...], preferred_element_type=f32)
    place(rows, 0, rows)
    second_t = second[...].T
    wide = 2 * FFN // D
    for i in range(wide):
        acc[:D] = jnp.dot(second_t, gexp[:, i * D : (i + 1) * D], preferred_element_type=f32)
        place(rows, (1 + i) * rows, rows)
    for c in range(0, FFN, chunk):
        acc[c : c + chunk] = jnp.dot(act[:, c : c + chunk].T, cot_ref[...], preferred_element_type=f32)
    used = (1 + wide) * rows
    place(FFN // n, used, w_own.shape[1] - used)

    for copy in sent:
        copy.wait()
    height = y_keep.shape[2]
    third = lambda g, i: pl.ds(pl.multiple_of((3 * g + i) * height, 16), height)

    def summed(m, part):
        return (w_own[m, part].astype(f32) + w_got[m, part].astype(f32)).astype(bf)

    def each(count, body):
        def step(i, carry):
            body(i)
            return carry

        lax.fori_loop(0, count, step, 0)

    for k in range(groups):
        g = lax.rem(group + k, groups)

        def first(m, k=k, g=g):
            (y_send.at[k - 1] if k else y_keep)[m // S2, lax.rem(m, S2)] = summed(m, third(g, 0))

        each(PLANES * S2, first)
    for k in range(S2):
        a = lax.rem(s2 + k, S2)

        def second_part(i, k=k, a=a):
            p, g = i // groups, lax.rem(i, groups)
            (x_send.at[k - 1] if k else x_keep)[p, g] = summed(p * S2 + a, third(g, 1))

        each(PLANES * groups, second_part)
    z_parts = [z_keep, z_send_1, z_send_2, z_send_3]
    for k in range(PLANES):
        p = lax.rem(plane + k, PLANES)

        def third_part(i, k=k, p=p):
            a, g = i // groups, lax.rem(i, groups)
            z_parts[k][a, g] = summed(p * S2 + a, third(g, 2))

        each(S2 * groups, third_part)
    for copy in away:
        copy.wait()


def middle(n, groups, lowt, tokens, cotangent, gains, out_w, exp_w, con_w):
    bf, f32 = jnp.bfloat16, jnp.float32
    S2 = n // PLANES // 2
    T, D = tokens.shape
    ffn = con_w.shape[0]
    used = (D + 2 * ffn + ffn) // n + 8
    height = -(-used // (groups * 48)) * 16
    any_, vm = pl.BlockSpec(memory_space=pl.ANY), pl.BlockSpec(memory_space=pltpu.VMEM)
    sems = lambda count: pltpu.SemaphoreType.DMA((2, count))
    shape = lambda *s: jax.ShapeDtypeStruct(s, bf)
    half = (n // 2, 3 * groups * height, D)
    return pl.pallas_call(
        functools.partial(middle_kernel, n, groups),
        out_shape=(
            shape(T, D),
            jax.ShapeDtypeStruct((T, D), f32),
            shape(PLANES, QW, T),
            shape(PLANES, S2, height, D),
            shape(groups - 1, PLANES, S2, height, D),
            shape(PLANES, groups, height, D),
            shape(S2 - 1, PLANES, groups, height, D),
            shape(S2, groups, height, D),
            *[shape(S2, groups, height, D)] * (PLANES - 1),
        ),
        in_specs=[vm, vm, vm, vm, any_, any_, any_],
        out_specs=tuple([vm] * 11),
        scratch_shapes=[
            pltpu.VMEM(out_w.shape, bf),
            pltpu.VMEM(exp_w.shape, bf),
            pltpu.VMEM(con_w.shape, bf),
            pltpu.SemaphoreType.DMA((3,)),
            pltpu.VMEM((PLANES, QW, T), bf),
            sems(PLANES - 1),
            pltpu.VMEM((PLANES, QW, T), bf),
            sems(PLANES - 1),
            pltpu.VMEM((T, D), f32),
            pltpu.VMEM((T, D), bf),
            pltpu.VMEM((T, D), bf),
            pltpu.VMEM((T, ffn), f32),
            pltpu.VMEM((T, ffn), bf),
            pltpu.VMEM((T, 2 * ffn), bf),
            pltpu.VMEM((ffn, D), f32),
            pltpu.VMEM(half, bf),
            pltpu.VMEM(half, bf),
            pltpu.VMEM(half, bf),
            sems(2 + 2 * ffn // D),
        ],
        compiler_params=pltpu.CompilerParams(collective_id=2, has_side_effects=True, vmem_limit_bytes=60 << 20),
    )(lowt, tokens, cotangent, gains, out_w, exp_w, con_w)


def tail_kernel(
    n,
    groups,
    deal_ref,
    dq_ref,
    dkv_ref,
    turn_ref,
    gains_ref,
    joint_hbm,
    joint_t_hbm,
    first_hbm,
    tokens_hbm,
    grad_hidden_hbm,
    y_keep_hbm,
    y_got_hbm,
    x_keep_hbm,
    x_got_hbm,
    z_keep_hbm,
    z_got_1,
    z_got_2,
    z_got_3,
    d_got,
    w_all,
    jq_all,
    jk_all,
    joint_rows,
    joint_t,
    first,
    tokens,
    grad_hidden,
    y_keep,
    y_got,
    x_keep,
    x_got,
    z_keep,
    z_came,
    local_sems,
    kv_near,
    kv_send,
    kv_far,
    kv_sems,
    mixed_q,
    mixed_kv,
    part,
    part_got,
    part_send_sems,
    part_recv_sems,
    j_acc,
    jq,
    jq_core,
    jq_side,
    jq_plane,
    jk,
    jk_core,
    jk_side,
    jk_plane,
    j_sems,
    x1_got,
    y2_got,
    y3_got,
    z1_got,
    x3_got,
    w_plane,
    w_plane_got,
    w_sems,
    d_send,
    d_mid,
    d_back,
    d_sems,
    row_sems,
    row_local,
):
    bf, f32 = jnp.bfloat16, jnp.float32
    S = n // PLANES
    S2 = S // 2
    T, D = tokens.shape
    me, group = lax.axis_index("ctx"), lax.axis_index("fsdp")
    plane, side = me // S, lax.rem(me, S)
    s2, core = side // 2, lax.rem(side, 2)
    MESH = pl.DeviceIdType.MESH

    def at(p, a, c, g):
        return (p * S + a * 2 + c, g)

    def plane_peer(k):
        return at(lax.rem(plane + k, PLANES), s2, core, group)

    def side_peer(k):
        return at(plane, lax.rem(s2 + k, S2), core, group)

    def group_peer(k):
        return at(plane, s2, core, lax.rem(group + k, groups))

    core_peer = at(plane, s2, 1 - core, group)

    def send(source, target, send_sem, recv_sem, device):
        return pltpu.make_async_remote_copy(
            src_ref=source, dst_ref=target, send_sem=send_sem, recv_sem=recv_sem, device_id=device, device_id_type=MESH
        )

    def remote(source, target, sems, index, device):
        return send(source, target, sems.at[0, index], sems.at[1, index], device)

    def total_of(terms):
        total = terms[0].astype(f32)
        for term in terms[1:]:
            total = total + term.astype(f32)
        return total

    local = [
        pltpu.make_async_copy(source, target, local_sems.at[i])
        for i, (source, target) in enumerate(
            [
                (first_hbm, first),
                (joint_t_hbm, joint_t),
                (y_keep_hbm, y_keep),
                (y_got_hbm, y_got),
                (x_keep_hbm, x_keep),
                (x_got_hbm, x_got),
                (z_keep_hbm, z_keep),
                (z_got_1, z_came.at[0]),
                (z_got_2, z_came.at[1]),
                (z_got_3, z_came.at[2]),
                (tokens_hbm, tokens),
                (grad_hidden_hbm, grad_hidden),
            ]
        )
    ]
    for copy in local:
        copy.start()
    barrier = pltpu.get_barrier_semaphore()

    def greet(k, carry):
        pl.semaphore_signal(barrier, inc=1, device_id=(lax.rem(me + k, n), group), device_id_type=MESH)
        return carry

    lax.fori_loop(1, n, greet, 0)
    for k in range(1, groups):
        pl.semaphore_signal(barrier, inc=1, device_id=group_peer(k), device_id_type=MESH)
    pl.semaphore_wait(barrier, n - 1 + groups - 1)

    lower = plane < 2
    middle = (plane == 1) | (plane == 2)
    order = [
        jnp.where(lower, 3, 0),
        jnp.where(plane == 0, 2, jnp.where(plane == 1, 0, jnp.where(plane == 2, 3, 1))),
        jnp.where((plane == 0) | (plane == 2), 1, 2),
        plane,
    ]
    steps = range(PLANES)
    back = [lax.rem(plane + PLANES - p, PLANES) for p in order]
    main = jnp.where(lower, 0, 1)
    main_plane = plane + 1 - 2 * main

    core_kv = [remote(dkv_ref.at[order[t], :, 1 - core], kv_near.at[t], kv_sems, t, core_peer) for t in steps]
    for copy in core_kv:
        copy.start()

    per_group = joint_hbm.shape[0]
    index = me - group * per_group
    held_here = (index >= 0) & (index < per_group)
    row_own = pltpu.make_async_copy(joint_hbm.at[jnp.clip(index, 0, per_group - 1)], joint_rows, row_local.at[0])
    row_moves = [
        send(
            joint_hbm.at[jnp.clip(index, 0, per_group - 1)],
            joint_rows,
            row_sems.at[k - 1],
            row_sems.at[groups - 1],
            group_peer(k),
        )
        for k in range(1, groups)
    ]

    @pl.when(held_here)
    def _():
        row_own.start()
        for copy in row_moves:
            copy.start()

    w_moves = []

    def w_copy(source, target, device):
        copy = remote(source, target, w_sems, len(w_moves), device)
        w_moves.append(copy)
        copy.start()
        return copy

    local[2].wait()
    local[3].wait()
    for p in range(PLANES):
        for a in range(S2):
            y_keep[p, a] = total_of([y_keep[p, a]] + [y_got[k, p, a] for k in range(groups - 1)]).astype(bf)
    z1 = [w_copy(y_keep.at[lax.rem(plane + k, PLANES)], z1_got.at[k - 1], plane_peer(k)) for k in range(1, PLANES)]

    def turned_back(x, t):
        cos, sin = turn_ref[back[t], :HALF], turn_ref[back[t], HALF:]
        rows = []
        for h in range(HP):
            upper, lower = x[h * HD : h * HD + HALF], x[h * HD + HALF : (h + 1) * HD]
            rows += [upper * cos + lower * sin, lower * cos - upper * sin]
        return jnp.concatenate(rows, axis=0)

    side_kv = {}
    for t in steps:
        core_kv[t].wait()
        for a in range(S2):
            kv_send[t, a] = total_of([dkv_ref[order[t], a, core], kv_near[t, a]]).astype(bf)
        for k in range(1, S2):
            side_kv[t, k] = remote(
                kv_send.at[t, lax.rem(s2 + S2 - k, S2)],
                kv_far.at[t, k - 1],
                kv_sems,
                PLANES + t * (S2 - 1) + k - 1,
                side_peer(S2 - k),
            )
            side_kv[t, k].start()
    for t in steps:
        mixed_q[t] = turned_back(dq_ref[back[t]], t).astype(bf)

    local[4].wait()
    local[5].wait()
    for p in range(PLANES):
        for g in range(groups):
            x_keep[p, g] = total_of([x_keep[p, g]] + [x_got[k, p, g] for k in range(S2 - 1)]).astype(bf)
    y2 = [w_copy(x_keep.at[:, lax.rem(group + k, groups)], y2_got.at[k - 1], group_peer(k)) for k in range(1, groups)]
    for i in range(6, 10):
        local[i].wait()
    for a in range(S2):
        for g in range(groups):
            z_keep[a, g] = total_of([z_keep[a, g]] + [z_came[k, a, g] for k in range(PLANES - 1)]).astype(bf)
    y3 = [w_copy(z_keep.at[:, lax.rem(group + k, groups)], y3_got.at[k - 1], group_peer(k)) for k in range(1, groups)]

    j_moves = []

    def j_copy(source, target, device):
        copy = remote(source, target, j_sems, len(j_moves), device)
        j_moves.append(copy)
        copy.start()
        return copy

    def j_core_stage(mixed, grads, near):
        height = mixed.shape[1]
        j_acc[:height] = total_of(
            [jnp.dot(mixed[t], first[back[t]], preferred_element_type=f32) for t in steps]
        )
        shard_rows = D // n
        for i in range(D // 128):
            block = j_acc[:height, i * 128 : (i + 1) * 128].T
            row = i * 128
            while row < (i + 1) * 128:
                shard, offset = divmod(row, shard_rows)
                count = min(shard_rows - offset, (i + 1) * 128 - row)
                begin = row - i * 128
                grads[shard // S, shard % S // 2, shard % 2, offset : offset + count] = block[
                    begin : begin + count
                ].astype(bf)
                row += count
        return [j_copy(grads.at[:, :, 1 - core], near, core_peer)]

    def j_side_stage(moves, grads, near, far):
        for copy in moves:
            copy.wait()
        for p in range(PLANES):
            for a in range(S2):
                near[p, a] = total_of([grads[p, a, core], near[p, a]]).astype(bf)
        return [j_copy(near.at[:, lax.rem(s2 + k, S2)], far.at[k - 1], side_peer(k)) for k in range(1, S2)]

    def j_plane_stage(moves, near, far, gathered):
        for copy in moves:
            copy.wait()
        for p in range(PLANES):
            far[0, p] = total_of([near[p, s2]] + [far[k, p] for k in range(S2 - 1)]).astype(bf)
        gathered[plane] = far[0, plane]
        return [
            j_copy(far.at[0, lax.rem(plane + k, PLANES)], gathered.at[plane], plane_peer(k)) for k in range(1, PLANES)
        ]

    def j_group_stage(moves, gathered, every):
        for copy in moves:
            copy.wait()
        every[group] = gathered[...]
        return [j_copy(gathered, every.at[group], group_peer(k)) for k in range(1, groups)]

    local[0].wait()
    jq_moves = j_core_stage(mixed_q, jq, jq_core)

    local[1].wait()

    def main_send(t):
        return send(
            part.at[t],
            part_got.at[main, order[t]],
            part_send_sems.at[t],
            part_recv_sems.at[main * PLANES + order[t]],
            at(main_plane, s2, core, group),
        )

    def other_send(t):
        return send(
            part.at[t],
            part_got.at[1 - main, order[t]],
            part_send_sems.at[t],
            part_recv_sems.at[(1 - main) * PLANES + order[t]],
            at(2 * plane - main_plane, s2, core, group),
        )

    def came(direction, p):
        return send(
            part.at[0],
            part_got.at[direction, p],
            part_send_sems.at[0],
            part_recv_sems.at[direction * PLANES + p],
            core_peer,
        )

    strip = 64

    def add_part(t, direction, p):
        def body(i, carry):
            rows = pl.ds(pl.multiple_of(i * strip, strip), strip)
            part[t, rows] = total_of([part[t, rows], part_got[direction, p, rows]]).astype(bf)
            return carry

        lax.fori_loop(0, T // strip, body, 0)

    def relay(t, secondary):
        @pl.when(middle)
        def _():
            direction = 1 - main if secondary else main
            came(direction, order[t]).wait_recv()
            add_part(t, direction, order[t])
            (other_send if secondary else main_send)(t).start()

    def key_step(t):
        for k in range(1, S2):
            side_kv[t, k].wait()
        dk = total_of([kv_send[t, s2]] + [kv_far[t, k] for k in range(S2 - 1)]).T
        mixed_kv[t, :QW] = turned_back(dk[:QW], t).astype(bf)
        mixed_kv[t, QW:] = dk[QW:].astype(bf)
        grads = jnp.concatenate([mixed_q[t], mixed_kv[t]], axis=0)
        part[t] = jnp.dot(grads.T, joint_t[: 3 * QW], preferred_element_type=f32).astype(bf)
        if t < PLANES - 1:

            @pl.when(jnp.logical_not(middle))
            def _():
                main_send(t).start()

    key_step(0)
    jq_moves = j_side_stage(jq_moves, jq, jq_core, jq_side)
    key_step(1)
    key_step(2)
    relay(0, False)
    jq_moves = j_plane_stage(jq_moves, jq_core, jq_side, jq_plane)
    key_step(3)
    relay(2, False)
    jk_moves = j_core_stage(mixed_kv, jk, jk_core)

    for copy in y3:
        copy.wait()
    for a in range(S2):
        z_keep[a, group] = total_of([z_keep[a, group]] + [y3_got[k, a] for k in range(groups - 1)]).astype(bf)
    x3 = [w_copy(z_keep.at[lax.rem(s2 + k, S2), group], x3_got.at[k - 1], side_peer(k)) for k in range(1, S2)]
    for copy in y2:
        copy.wait()
    for p in range(PLANES):
        w_plane[p] = total_of([x_keep[p, group]] + [y2_got[k, p] for k in range(groups - 1)]).astype(bf)
    w_last = [
        w_copy(w_plane.at[lax.rem(plane + k, PLANES)], w_plane_got.at[k - 1], plane_peer(k)) for k in range(1, PLANES)
    ]
    for copy in z1:
        copy.wait()
    for a in range(S2):
        y_keep[plane, a] = total_of([y_keep[plane, a]] + [z1_got[k, a] for k in range(PLANES - 1)]).astype(bf)
    x1 = [w_copy(y_keep.at[plane, lax.rem(s2 + k, S2)], x1_got.at[k - 1], side_peer(k)) for k in range(1, S2)]
    relay(1, True)
    jk_moves = j_side_stage(jk_moves, jk, jk_core, jk_side)
    jq_moves = j_group_stage(jq_moves, jq_plane, jq_all)

    local[10].wait()
    local[11].wait()
    came(1 - main, plane).wait_recv()
    add_part(PLANES - 1, 1 - main, plane)

    @pl.when(middle)
    def _():
        came(main, plane).wait_recv()
        add_part(PLANES - 1, main, plane)

    def norm_back(i, carry):
        rows = pl.ds(pl.multiple_of(i * strip, strip), strip)
        grad = part[PLANES - 1, rows].astype(f32)
        values = tokens[rows].astype(f32)
        centred = values - jnp.mean(values, axis=-1, keepdims=True)
        scale = lax.rsqrt(jnp.mean(centred * centred, axis=-1, keepdims=True) + norm_eps)
        normal = centred * scale
        grad = grad * gains_ref[0:1]
        grad = grad - jnp.mean(grad, axis=-1, keepdims=True) - normal * jnp.mean(grad * normal, axis=-1, keepdims=True)
        grad_hidden[rows] = grad_hidden[rows] + grad * scale
        return carry

    lax.fori_loop(0, T // strip, norm_back, 0)

    blocks = T // BLOCK
    piece = BLOCK // n

    def d_copy(source, target, base, k):
        return remote(source.at[lax.rem(me + k, n)], target.at[me], d_sems, base + k, (lax.rem(me + k, n), group))

    for i in range(n):
        d_send[i] = jnp.concatenate(
            [grad_hidden[b * BLOCK + i * piece : b * BLOCK + (i + 1) * piece] for b in range(blocks)], axis=0
        ).astype(bf)
    out_deal = [d_copy(d_send, d_mid, 0, k) for k in range(1, n)]
    for copy in out_deal:
        copy.start()
    d_mid[me] = d_send[me]

    jk_moves = j_plane_stage(jk_moves, jk_core, jk_side, jk_plane)

    for copy in out_deal:
        copy.wait()
    for i in range(n):
        chosen = []
        for b in range(blocks):
            wanted = deal_ref[i * blocks + b]
            held = d_mid[wanted // blocks].astype(f32)
            rows = held[:piece]
            for other in range(1, blocks):
                rows = jnp.where(lax.rem(wanted, blocks) == other, held[other * piece : (other + 1) * piece], rows)
            chosen.append(rows)
        d_back[i] = jnp.concatenate(chosen, axis=0).astype(bf)
    back_deal = [d_copy(d_back, d_got, n, k) for k in range(1, n)]
    for copy in back_deal:
        copy.start()
    d_got[me] = d_back[me]

    for copy in x1 + w_last + x3:
        copy.wait()
    height = w_plane.shape[1]
    w_all[group, :height] = total_of([y_keep[plane, s2]] + [x1_got[k] for k in range(S2 - 1)]).astype(bf)
    w_all[group, height : 2 * height] = total_of(
        [w_plane[plane]] + [w_plane_got[k] for k in range(PLANES - 1)]
    ).astype(bf)
    w_all[group, 2 * height :] = total_of([z_keep[s2, group]] + [x3_got[k] for k in range(S2 - 1)]).astype(bf)
    w_gather = [w_copy(w_all.at[group], w_all.at[group], group_peer(k)) for k in range(1, groups)]
    jk_moves = j_group_stage(jk_moves, jk_plane, jk_all)

    for copy in back_deal + w_gather + jq_moves + jk_moves:
        copy.wait()
    for t in range(PLANES - 1):
        came_from = send(part.at[t], part.at[t], part_send_sems.at[t], part_recv_sems.at[0], core_peer)
        came_from.wait_send()

    @pl.when(held_here)
    def _():
        row_own.wait()
        for copy in row_moves:
            copy.wait_send()

    @pl.when(jnp.logical_not(held_here))
    def _():
        row_moves[0].wait_recv()


def tail(n, groups, deal, dqt, dkv, turn, gains, joint_shard, joint_t, first, tokens, grad_hidden, pieces):
    bf, f32 = jnp.bfloat16, jnp.float32
    S2 = n // PLANES // 2
    T, D = tokens.shape
    rows = D // n
    height = pieces[0].shape[2]
    piece_rows = T // n
    joint_shard = joint_shard.reshape(-1, rows, joint_shard.shape[1])
    any_, vm, sm = (pl.BlockSpec(memory_space=m) for m in (pl.ANY, pltpu.VMEM, pltpu.SMEM))
    sems = lambda count: pltpu.SemaphoreType.DMA((2, count))
    small = lambda *s: pltpu.VMEM(s, bf)
    j_buffers = lambda w: [
        small(PLANES, S2, 2, rows, w),
        small(PLANES, S2, rows, w),
        small(S2 - 1, PLANES, rows, w),
        small(PLANES, rows, w),
    ]
    return pl.pallas_call(
        functools.partial(tail_kernel, n, groups),
        out_shape=(
            jax.ShapeDtypeStruct((n, piece_rows, D), bf),
            jax.ShapeDtypeStruct((groups, 3 * height, D), bf),
            jax.ShapeDtypeStruct((groups, PLANES, rows, QW), bf),
            jax.ShapeDtypeStruct((groups, PLANES, rows, 2 * QW), bf),
            jax.ShapeDtypeStruct(joint_shard.shape[1:], bf),
        ),
        in_specs=[sm, vm, vm, vm, vm] + [any_] * 13,
        out_specs=tuple([vm] * 4) + (any_,),
        scratch_shapes=[
            pltpu.VMEM(joint_t.shape, bf),
            pltpu.VMEM((PLANES, T, D), bf),
            pltpu.VMEM((T, D), bf),
            pltpu.VMEM((T, D), f32),
            *[pltpu.VMEM(p.shape, bf) for p in pieces[:5]],
            pltpu.VMEM((PLANES - 1, *pieces[5].shape), bf),
            pltpu.SemaphoreType.DMA((12,)),
            small(PLANES, S2, T, 2 * QW),
            small(PLANES, S2, T, 2 * QW),
            small(PLANES, S2 - 1, T, 2 * QW),
            sems(PLANES * S2),
            small(PLANES, QW, T),
            small(PLANES, 2 * QW, T),
            small(PLANES, T, D),
            small(2, PLANES, T, D),
            pltpu.SemaphoreType.DMA((PLANES - 1,)),
            pltpu.SemaphoreType.DMA((2 * PLANES,)),
            pltpu.VMEM((2 * QW, D), f32),
            *j_buffers(QW),
            *j_buffers(2 * QW),
            sems(2 * (1 + S2 - 1 + PLANES - 1 + groups - 1)),
            small(S2 - 1, height, D),
            small(groups - 1, PLANES, height, D),
            small(groups - 1, S2, height, D),
            small(PLANES - 1, S2, height, D),
            small(S2 - 1, height, D),
            small(PLANES, height, D),
            small(PLANES - 1, height, D),
            sems(3 * (groups - 1) + 2 * (S2 - 1) + 2 * (PLANES - 1)),
            small(n, piece_rows, D),
            small(n, piece_rows, D),
            small(n, piece_rows, D),
            sems(2 * n),
            pltpu.SemaphoreType.DMA((groups,)),
            pltpu.SemaphoreType.DMA((1,)),
        ],
        compiler_params=pltpu.CompilerParams(collective_id=0, has_side_effects=True, vmem_limit_bytes=60 << 20),
    )(deal, dqt, dkv, turn, gains, joint_shard, joint_t, first, tokens, grad_hidden, *pieces)


def finish_kernel(
    n,
    d_ref,
    w_ref,
    jq_ref,
    jk_ref,
    rows_ref,
    dealt_ref,
    joint_ref,
    output_ref,
    expand_ref,
    contract_ref,
    gain_one_ref,
    gain_two_ref,
):
    f32 = jnp.float32
    T, D = dealt_ref.shape
    blocks = T // BLOCK
    piece = BLOCK // n
    for b in range(blocks):
        for i in range(0, n, 2):
            rows = [d_ref[i + e].astype(f32)[b * piece : (b + 1) * piece] for e in range(2)]
            dealt_ref[b * BLOCK + i * piece : b * BLOCK + (i + 2) * piece] = jnp.concatenate(rows, axis=0).astype(
                dealt_ref.dtype
            )

    def summed(ref, p):
        total = ref[0, p].astype(f32)
        for g in range(1, ref.shape[0]):
            total = total + ref[g, p].astype(f32)
        return total.T

    for i in range(PLANES // 2):
        pair = [summed(jq_ref, 2 * i + e) for e in range(2)]
        joint_ref[:, i * 2 * QW : (i + 1) * 2 * QW] = jnp.concatenate(pair, axis=0).T
        pair = [summed(jk_ref, 2 * i + e) for e in range(2)]
        for part in range(2):
            cols = (part + 1) * D + i * 2 * QW
            rows = [x[part * QW : (part + 1) * QW] for x in pair]
            joint_ref[:, cols : cols + 2 * QW] = jnp.concatenate(rows, axis=0).T
    product = jnp.sum(joint_ref[...] * rows_ref[...].astype(f32), axis=1, keepdims=True)
    gain_one_ref[...] = jnp.broadcast_to(product, gain_one_ref.shape)
    height = w_ref.shape[1]
    rows = D // n
    targets = [(output_ref, 0, rows)]
    targets += [(expand_ref, i * D, rows) for i in range(expand_ref.shape[1] // D)]
    targets += [(contract_ref, 0, contract_ref.shape[0])]
    row = 0
    for target, column, count in targets:
        done = 0
        while done < count:
            g, offset = divmod(row, height)
            part = min(count - done, height - offset)
            target[done : done + part, column : column + D] = w_ref[g, offset : offset + part].astype(f32)
            done += part
            row += part
    g, offset = divmod(row, height)
    gain_two_ref[...] = w_ref[g, offset : offset + 1].astype(f32)


def finish(n, T, wide, contract_rows, d_got, w_all, jq_all, jk_all, joint_rows):
    D = d_got.shape[-1]
    rows = D // n
    f32 = jnp.float32
    vm = pl.BlockSpec(memory_space=pltpu.VMEM)
    return pl.pallas_call(
        functools.partial(finish_kernel, n),
        out_shape=(
            jax.ShapeDtypeStruct((T, D), jnp.bfloat16),
            jax.ShapeDtypeStruct((rows, 3 * D), f32),
            jax.ShapeDtypeStruct((rows, D), f32),
            jax.ShapeDtypeStruct((rows, wide), f32),
            jax.ShapeDtypeStruct((contract_rows, D), f32),
            jax.ShapeDtypeStruct((rows, 128), f32),
            jax.ShapeDtypeStruct((1, D), f32),
        ),
        in_specs=[vm] * 5,
        out_specs=tuple([vm] * 7),
    )(d_got, w_all, jq_all, jk_all, joint_rows)


def on_device(
    n,
    groups,
    tokens,
    cotangent,
    lengths,
    deal,
    joint_projection,
    output_projection,
    expand_weight,
    contract_weight,
    gain_first,
    gain_second,
):
    T, D = tokens.shape[1:]
    S = n // PLANES
    S2 = S // 2
    me = lax.axis_index("ctx")

    def over_planes(x, k):
        return lax.ppermute(x, "ctx", [(h * S + s, (h + k) % PLANES * S + s) for h in range(PLANES) for s in range(S)])

    def over_sides(x, k):
        pairs = [
            (h * S + a * 2 + c, h * S + (a + k) % S2 * 2 + c) for h in range(PLANES) for a in range(S2) for c in range(2)
        ]
        return lax.ppermute(x, "ctx", pairs)

    def over_groups(x, k):
        return lax.ppermute(x, "fsdp", [(f, (f + k) % groups) for f in range(groups)])

    def moved(x, over):
        if x.shape[0] == 1:
            return over(x, 1)
        return jnp.stack([over(x[k], k + 1) for k in range(x.shape[0])])

    first, qt, kv, joint_t, turn, gains, out_w, exp_w, con_w = front(
        n,
        groups,
        lengths,
        tokens[0],
        joint_projection,
        gain_first,
        gain_second,
        output_projection,
        expand_weight,
        contract_weight,
    )
    out_w, exp_w, con_w = (w.reshape(-1, w.shape[-1]) for w in (out_w, exp_w, con_w))
    ot, lowt, lse = attn_fwd(n, lengths, qt, kv)
    output, grad_hidden, gt, y_keep, y_send, x_keep, x_send, z_keep, *z_send = middle(
        n, groups, lowt, tokens[0], cotangent[0], gains, out_w, exp_w, con_w
    )
    y_got, x_got = moved(y_send, over_groups), moved(x_send, over_sides)
    z_got = [over_planes(part, k + 1) for k, part in enumerate(z_send)]
    dqt, dkv = attn_bwd(n, lengths, qt, kv, ot, lse, gt)
    d_got, w_all, jq_all, jk_all, joint_rows = tail(
        n,
        groups,
        deal[0],
        dqt,
        dkv.reshape(PLANES, S2, 2, T, 2 * QW),
        turn,
        gains,
        joint_projection,
        joint_t,
        first,
        tokens[0],
        grad_hidden,
        [y_keep, y_got, x_keep, x_got, z_keep, *z_got],
    )
    dealt, shard_joint, shard_output, shard_expand, shard_contract, gain_one, gain_two = finish(
        n, T, exp_w.shape[1], con_w.shape[0] // n, d_got, w_all, jq_all, jk_all, joint_rows
    )
    width = D // n
    gain_one = gain_one[:, 0] / lax.dynamic_slice_in_dim(gains[0], me * width, width)
    gain_two = lax.dynamic_slice_in_dim(gain_two[0], me * width, width)
    return (
        output[None],
        dealt[None],
        shard_joint,
        shard_output,
        shard_expand,
        shard_contract,
        gain_one,
        gain_two,
    )


def solution(mesh):
    return jax.shard_map(
        functools.partial(on_device, mesh.shape["ctx"], mesh.shape["fsdp"]),
        mesh=mesh,
        in_specs=(
            P("fsdp", "ctx", None),
            P("fsdp", "ctx", None),
            P("fsdp", None),
            P("fsdp", None),
            P("fsdp", None),
            P("fsdp", None),
            P("fsdp", None),
            P("fsdp", None),
            P("fsdp"),
            P("fsdp"),
        ),
        out_specs=(
            P("fsdp", "ctx", None),
            P("fsdp", "ctx", None),
            P("ctx", None),
            P("ctx", None),
            P("ctx", None),
            P("ctx", None),
            P("ctx"),
            P("ctx"),
        ),
        check_vma=False,
    )
```

```python
import functools
import math

import jax
import jax.numpy as jnp
import numpy as np
from jax import lax
from jax.experimental import pallas as pl
from jax.experimental.pallas import tpu as pltpu
from jax.sharding import PartitionSpec as P

FF = 1152
HEADS = 12
HEAD_DIM = 64
BLOCK = 128
PLANES = 4
HD = HEAD_DIM
HALF = HEAD_DIM // 2
HP = HEADS // PLANES
QW = HP * HEAD_DIM
rope_base = 160000.0
norm_eps = 1e-05
MASKED = -1e30


def ends_of(lengths_ref, count):
    ends, total = [], 0
    for i in range(count):
        total = total + lengths_ref[0, i]
        ends.append(total)
    return ends


def span_of(index, ends):
    begin, end = jnp.zeros_like(index), jnp.full_like(index, ends[0])
    for before, after in zip(ends[:-1], ends[1:]):
        begin = jnp.where(index >= before, before, begin)
        end = jnp.where(index >= before, after, end)
    return begin, end


def head_rows(x, head):
    rows = lax.broadcasted_iota(jnp.int32, x.shape, 0)
    return jnp.where((rows >= head * HD) & (rows < (head + 1) * HD), x, jnp.zeros_like(x))


def query_block(n, b, T, ends):
    S = n // PLANES
    me = lax.axis_index("ctx")
    base = (lax.rem(me // S + PLANES - b, PLANES) * S + lax.rem(me, S)) * T
    low_begin, low_end = span_of(base, ends)
    high_begin, high_end = span_of(base + T - 1, ends)
    low, high = low_begin // T, (high_end + T - 1) // T
    full_low = jnp.clip((high_begin + T - 1) // T, low, high)
    full_high = jnp.clip(low_end // T, full_low, high)
    begin, end = span_of(base + lax.broadcasted_iota(jnp.int32, (8, T), 1), ends)
    return (low, full_low, full_high, high), begin[0:1], end[0:1]


def over_units(bounds, step, sizes):
    low, full_low, full_high, high = bounds

    def run(begin, end, masked):
        def body(u, carry):
            step(u, masked)
            return carry

        lax.fori_loop(begin, end, body, 0)

    run(low, full_low, True)
    in_groups(full_low, full_high, lambda u: step(u, False), sizes)
    run(full_high, high, True)


def in_groups(begin, end, step, sizes):
    for size in sizes:
        count = (end - begin) // size

        def some(i, carry, size=size, begin=begin):
            for e in range(size):
                step(begin + size * i + e)
            return carry

        lax.fori_loop(0, count, some, 0)
        begin = begin + size * count


def fwd_kernel(n, count, lengths_ref, qt_ref, kv_ref, ot_ref, lowt_ref, lse_ref, values, scores, top, total, acc):
    units, T, _ = kv_ref.shape
    ends = ends_of(lengths_ref, count)

    def flip(u, carry):
        values[u] = kv_ref[u, :, 128:].T
        return carry

    lax.fori_loop(0, units, flip, 0, unroll=4)

    def one_query_block(b, carry):
        qt = qt_ref[b]
        qheads = [head_rows(qt, h) for h in range(HP)]
        bounds, q_start, q_end = query_block(n, b, T, ends)
        top[...] = jnp.full_like(top, MASKED)
        total[...] = jnp.zeros_like(total)
        acc[...] = jnp.zeros_like(acc)

        def score(u, masked):
            k = kv_ref[u, :, :QW]
            st = [jnp.dot(k, qheads[h], preferred_element_type=jnp.float32) for h in range(HP)]
            if masked:
                at = u * T + lax.broadcasted_iota(jnp.int32, (T, T), 0)
                allowed = (at >= q_start) & (at < q_end)
                st = [jnp.where(allowed, s, MASKED) for s in st]
            for h in range(HP):
                scores[u, h] = st[h]
                top[h] = jnp.maximum(top[h], jnp.max(st[h].reshape(T // 8, 8, T), axis=0))

        over_units(bounds, score, (2, 1))
        m = [jnp.max(top[h], axis=0, keepdims=True) for h in range(HP)]

        def gather(u):
            p = [jnp.exp(scores[u, h] - m[h]) for h in range(HP)]
            for h in range(HP):
                total[h] += jnp.sum(p[h].reshape(T // 8, 8, T), axis=0)
                rows = pl.ds(h * HD, HD)
                acc[rows, :] += jnp.dot(
                    values[u, pl.ds(HD + h * HD, HD), :], p[h].astype(jnp.bfloat16), preferred_element_type=jnp.float32
                )

        in_groups(bounds[0], bounds[3], gather, (4, 2, 1))
        for h in range(HP):
            rows = pl.ds(h * HD, HD)
            l = jnp.sum(total[h], axis=0, keepdims=True)
            o = acc[rows, :] / l
            ot_ref[b, rows, :] = o
            lowt_ref[b, rows, :] = o.astype(jnp.bfloat16)
            lse_ref[b, h : h + 1, :] = m[h] + jnp.log(l)
        return carry

    lax.fori_loop(0, qt_ref.shape[0], one_query_block, 0)


def attn_fwd(n, lengths, qt, kv):
    B, _, T = qt.shape
    U = kv.shape[0]
    sm, vm = pl.BlockSpec(memory_space=pltpu.SMEM), pl.BlockSpec(memory_space=pltpu.VMEM)
    return pl.pallas_call(
        functools.partial(fwd_kernel, n, lengths.shape[1]),
        out_shape=(
            jax.ShapeDtypeStruct((B, QW, T), jnp.float32),
            jax.ShapeDtypeStruct((B, QW, T), jnp.bfloat16),
            jax.ShapeDtypeStruct((B, 8, T), jnp.float32),
        ),
        in_specs=[sm, vm, vm],
        out_specs=(vm, vm, vm),
        scratch_shapes=[
            pltpu.VMEM((U, 256, T), jnp.bfloat16),
            pltpu.VMEM((U, HP, T, T), jnp.float32),
            pltpu.VMEM((HP, 8, T), jnp.float32),
            pltpu.VMEM((HP, 8, T), jnp.float32),
            pltpu.VMEM((QW, T), jnp.float32),
        ],
        compiler_params=pltpu.CompilerParams(vmem_limit_bytes=60 << 20),
    )(lengths, qt, kv)


def bwd_kernel(n, count, lengths_ref, qt_ref, kv_ref, ot_ref, lse_ref, gt_ref, dqt_ref, dkv_ref, keys, dk, dv, dq):
    units, T, _ = kv_ref.shape
    ends = ends_of(lengths_ref, count)

    def flip(u, carry):
        keys[u] = kv_ref[u, :, :256].T
        dk[u] = jnp.zeros_like(dk[u])
        dv[u] = jnp.zeros_like(dv[u])
        return carry

    lax.fori_loop(0, units, flip, 0, unroll=4)

    def one_query_block(b, carry):
        qt, gt = qt_ref[b], gt_ref[b]
        zero = jnp.zeros((HD, T), jnp.bfloat16)
        qheads = [head_rows(qt, h) for h in range(HP)]
        gheads = [head_rows(gt, h) for h in range(HP)]
        gpad = [jnp.concatenate([zero, x], axis=0) for x in gheads]
        q = jnp.concatenate([jnp.concatenate([x, zero], axis=0).T for x in qheads], axis=0)
        g = jnp.concatenate([x.T for x in gpad], axis=0)
        bounds, q_start, q_end = query_block(n, b, T, ends)
        prod = gt.astype(jnp.float32) * ot_ref[b]
        delta = [jnp.sum(prod[h * HD : (h + 1) * HD], axis=0, keepdims=True) for h in range(HP)]
        lse = [lse_ref[b, h : h + 1, :] for h in range(HP)]
        dq[...] = jnp.zeros_like(dq)

        def one_unit(u, masked):
            k, v = kv_ref[u, :, :QW], kv_ref[u, :, 128:]
            st = [jnp.dot(k, qheads[h], preferred_element_type=jnp.float32) for h in range(HP)]
            dp = [jnp.dot(v, gpad[h], preferred_element_type=jnp.float32) for h in range(HP)]
            st = [st[h] - lse[h] for h in range(HP)]
            if masked:
                at = u * T + lax.broadcasted_iota(jnp.int32, (T, T), 0)
                allowed = (at >= q_start) & (at < q_end)
                st = [jnp.where(allowed, s, MASKED) for s in st]
            p = [jnp.exp(s) for s in st]
            ds = [(p[h] * (dp[h] - delta[h])).astype(jnp.bfloat16) for h in range(HP)]
            p = [x.astype(jnp.bfloat16) for x in p]
            dv[u] += jnp.dot(jnp.concatenate(p, axis=1), g, preferred_element_type=jnp.float32)
            dk[u] += jnp.dot(jnp.concatenate(ds, axis=1), q, preferred_element_type=jnp.float32)
            for h in range(HP):
                rows = pl.ds(h * HD, HD)
                dq[rows, :] += jnp.dot(keys[u, rows, :], ds[h], preferred_element_type=jnp.float32)

        over_units(bounds, one_unit, (4, 2, 1))
        dqt_ref[b] = dq[...] * (HD**-0.5)
        return carry

    lax.fori_loop(0, qt_ref.shape[0], one_query_block, 0)

    def out(u, carry):
        dkv_ref[u, :, :128] = dk[u, :, :128].astype(jnp.bfloat16)
        dkv_ref[u, :, 128:256] = (dk[u, :, 128:] + dv[u, :, :128]).astype(jnp.bfloat16)
        dkv_ref[u, :, 256:] = dv[u, :, 128:].astype(jnp.bfloat16)
        return carry

    lax.fori_loop(0, units, out, 0, unroll=2)


def attn_bwd(n, lengths, qt, kv, ot, lse, gt):
    B, _, T = qt.shape
    U = kv.shape[0]
    sm, vm = pl.BlockSpec(memory_space=pltpu.SMEM), pl.BlockSpec(memory_space=pltpu.VMEM)
    return pl.pallas_call(
        functools.partial(bwd_kernel, n, lengths.shape[1]),
        out_shape=(jax.ShapeDtypeStruct((B, QW, T), jnp.float32), jax.ShapeDtypeStruct((U, T, 2 * QW), jnp.bfloat16)),
        in_specs=[sm] + [vm] * 5,
        out_specs=(vm, vm),
        scratch_shapes=[
            pltpu.VMEM((U, 256, T), jnp.bfloat16),
            pltpu.VMEM((U, T, 256), jnp.float32),
            pltpu.VMEM((U, T, 256), jnp.float32),
            pltpu.VMEM((QW, T), jnp.float32),
        ],
        compiler_params=pltpu.CompilerParams(vmem_limit_bytes=60 << 20),
    )(lengths, qt, kv, ot, lse, gt)
def front_kernel(
    n,
    groups,
    count,
    lengths_ref,
    tokens_ref,
    joint_ref,
    gain_one_ref,
    gain_two_ref,
    out_hbm,
    exp_hbm,
    con_hbm,
    first_ref,
    qt_ref,
    kv_ref,
    joint_t_out,
    turn_ref,
    gains_ref,
    out_all,
    exp_all,
    con_ref,
    held,
    t_sems,
    cols,
    cols_all,
    gain_held,
    g_sems,
    kv_own,
    kv_sems,
    own_sems,
    w_sems,
    w_local,
    joint_rows,
    out_held,
    exp_held,
    con_held,
):
    bf, f32 = jnp.bfloat16, jnp.float32
    S = n // PLANES
    S2 = S // 2
    T, D = tokens_ref.shape
    me, group = lax.axis_index("ctx"), lax.axis_index("fsdp")
    plane, side = me // S, lax.rem(me, S)
    s2, core = side // 2, lax.rem(side, 2)

    def at(p, a, c, g):
        return (p * S + a * 2 + c, g)

    def side_peer(k):
        return at(plane, lax.rem(s2 + k, S2), core, group)

    def group_peer(k):
        return at(plane, s2, core, lax.rem(group + k, groups))

    core_peer = at(plane, s2, 1 - core, group)

    def remote(source, target, sems, index, device):
        return pltpu.make_async_remote_copy(
            src_ref=source,
            dst_ref=target,
            send_sem=sems.at[0, index],
            recv_sem=sems.at[1, index],
            device_id=device,
            device_id_type=pl.DeviceIdType.MESH,
        )

    barrier = pltpu.get_barrier_semaphore()

    def greet(device):
        pl.semaphore_signal(barrier, inc=1, device_id=device, device_id_type=pl.DeviceIdType.MESH)

    for k in range(1, PLANES):
        greet(at(lax.rem(plane + k, PLANES), s2, core, group))
    for k in range(1, S2):
        greet(side_peer(k))
    for k in range(1, groups):
        greet(group_peer(k))
    greet(core_peer)
    pl.semaphore_wait(barrier, PLANES - 1 + S2 - 1 + groups - 1 + 1)

    def up(p):
        return remote(held.at[p], held.at[p], t_sems, p, at(plane + 1, s2, core, group))

    def down(p):
        return remote(held.at[p], held.at[p], t_sems, PLANES + p, at(plane - 1, s2, core, group))

    held[plane] = tokens_ref[...]

    @pl.when(plane < PLANES - 1)
    def _():
        up(plane).start()

    @pl.when(plane > 0)
    def _():
        down(plane).start()

    pair = 2 * QW
    for part in range(3):
        window = joint_ref[:, pl.ds(pl.multiple_of(part * D + plane // 2 * pair, 128), pair)].T
        chosen = jnp.where(lax.rem(plane, 2) == 0, window[:QW].astype(f32), window[QW:].astype(f32))
        half = 3 * QW // 2
        low, high = part * QW, (part + 1) * QW
        for c in range(2):
            begin, end = max(low, c * half), min(high, (c + 1) * half)
            if begin < end:
                cols[c, begin - c * half : end - c * half] = chosen[begin - low : end - low].astype(bf)
    gain_held[group] = jnp.zeros_like(gain_held[group])
    gain_held[group, 0:1] = gain_one_ref[...].astype(f32).reshape(1, -1)
    gain_held[group, 1:2] = gain_two_ref[...].astype(f32).reshape(1, -1)
    col_moves = [
        remote(cols.at[core], cols_all.at[group, core], g_sems, k - 1, group_peer(k)) for k in range(1, groups)
    ]
    col_hands = []
    for k in range(1, groups):
        came = cols_all.at[lax.rem(group + groups - k, groups), core]
        col_hands.append(remote(came, came, g_sems, 2 * (groups - 1) + k - 1, core_peer))
    gain_moves = [
        remote(gain_held.at[group], gain_held.at[group], g_sems, groups - 1 + k - 1, group_peer(k))
        for k in range(1, groups)
    ]
    for copy in gain_moves + col_moves:
        copy.start()
    cols_all[group] = cols[...]

    weights = [(out_hbm, out_all, out_held), (exp_hbm, exp_all, exp_held)]
    part = core if con_hbm.shape[0] == 2 else 0
    w_in = [pltpu.make_async_copy(con_hbm.at[part], con_held, w_local.at[0, len(weights)])]
    w_own = [pltpu.make_async_copy(con_held, con_ref, w_local.at[1, len(weights)])]
    w_first, w_second = [], []
    for i, (source, target, bounce) in enumerate(weights):
        w_in.append(pltpu.make_async_copy(source, bounce, w_local.at[0, i]))
        w_own.append(pltpu.make_async_copy(bounce, target.at[group], w_local.at[1, i]))
        for k in range(1, groups):
            index = (i * (groups - 1) + k - 1) * 2
            w_first.append(remote(source.at[core], target.at[group, core], w_sems, index, group_peer(k)))
            came = lax.rem(group + groups - k, groups)
            w_second.append(remote(target.at[came, core], target.at[came, core], w_sems, index + 1, core_peer))
    for copy in w_in:
        copy.start()

    ends = ends_of(lengths_ref, count)
    row = lax.broadcasted_iota(jnp.int32, (HALF, T), 0)
    frequencies = jnp.zeros((HALF, T), f32)
    for i in range(HALF):
        frequencies = jnp.where(row == i, float(np.float32(rope_base ** (-2.0 * i / HEAD_DIM))), frequencies)
    for j in range(PLANES):
        base = (lax.rem(plane + PLANES - j, PLANES) * S + side) * T
        index = base + lax.broadcasted_iota(jnp.int32, (8, T), 1)
        begin, _ = span_of(index, ends)
        angles = (index - begin)[0:1].astype(f32) * frequencies
        turn_ref[j, :HALF] = jnp.cos(angles)
        turn_ref[j, HALF:] = jnp.sin(angles)

    strip = 64

    def kv_unit(p, a, c):
        return p * S + a * 2 + c

    def side_kv(j, k):
        p = lax.rem(plane + PLANES - j, PLANES)
        return remote(kv_own.at[j], kv_ref.at[kv_unit(p, s2, core)], kv_sems, j * (2 * S2 - 1) + k - 1, side_peer(k))

    def core_kv(j, k):
        p = lax.rem(plane + PLANES - j, PLANES)
        unit = kv_unit(p, lax.rem(s2 + S2 - k, S2), core)
        source = kv_own.at[j] if k == 0 else kv_ref.at[unit]
        return remote(source, kv_ref.at[unit], kv_sems, j * (2 * S2 - 1) + S2 - 1 + k, core_peer)

    def own_kv(j):
        p = lax.rem(plane + PLANES - j, PLANES)
        return pltpu.make_async_copy(kv_own.at[j], kv_ref.at[kv_unit(p, s2, core)], own_sems.at[j])

    def process(p):
        j = lax.rem(plane + PLANES - p, PLANES)

        def norm(i, carry):
            rows = pl.ds(pl.multiple_of(i * strip, strip), strip)
            values = held[p, rows].astype(f32)
            centred = values - jnp.mean(values, axis=-1, keepdims=True)
            spread = jnp.mean(centred * centred, axis=-1, keepdims=True)
            first_ref[j, rows] = (centred * lax.rsqrt(spread + norm_eps) * gains_ref[0:1]).astype(bf)
            return carry

        lax.fori_loop(0, T // strip, norm, 0)
        mixed = lax.dot_general(
            joint_t_out[: 3 * QW], first_ref[j], (((1,), (1,)), ((), ())), preferred_element_type=f32
        )
        cos, sin = turn_ref[j, :HALF], turn_ref[j, HALF:]
        turned = []
        for h in range(2 * HP):
            upper, lower = mixed[h * HD : h * HD + HALF], mixed[h * HD + HALF : (h + 1) * HD]
            turned += [upper * cos - lower * sin, lower * cos + upper * sin]
        q = jnp.concatenate(turned[: 2 * HP], axis=0).astype(bf)
        qt_ref[j] = (q.astype(f32) * HEAD_DIM**-0.5).astype(bf)
        kv_own[j] = jnp.concatenate(turned[2 * HP :] + [mixed[2 * QW :]], axis=0).T.astype(bf)
        for k in range(1, S2):
            side_kv(j, k).start()
        core_kv(j, 0).start()
        own_kv(j).start()

    def hand_on(t):
        @pl.when(plane >= t)
        def _():
            up(plane - t).wait_recv()

            @pl.when(plane < PLANES - 1)
            def _():
                up(plane - t).start()

        @pl.when(plane + t < PLANES)
        def _():
            down(plane + t).wait_recv()

            @pl.when(plane > 0)
            def _():
                down(plane + t).start()

    def process_arrived(t):
        below = jnp.where(plane >= t, 1, 0)
        above = jnp.where(plane + t < PLANES, 1, 0)

        def arrived(i, carry):
            process(jnp.where(i < below, plane - t, plane + t))
            return carry

        lax.fori_loop(0, below + above, arrived, 0)

    hand_on(1)
    for copy in gain_moves:
        copy.wait()
    share = D // groups
    total = jnp.zeros((8, D), f32)
    for g in range(groups):
        rows = lax.broadcasted_iota(jnp.int32, (share, D), 0)
        lanes = lax.broadcasted_iota(jnp.int32, (share, D), 1)
        place = jnp.where(lanes == rows + g * share, 1.0, 0.0).astype(bf)
        total = total + jnp.dot(gain_held[g].astype(bf), place, preferred_element_type=f32)
    gains_ref[...] = total
    for copy, hand in zip(col_moves, col_hands):
        copy.wait()
        hand.start()
    for copy in w_first:
        copy.start()
    for copy in w_in:
        copy.wait()
    for copy in w_own:
        copy.start()
    for copy in col_hands:
        copy.wait()
    width = joint_t_out.shape[0]
    for g in range(groups):
        whole = jnp.concatenate([cols_all[g, 0], cols_all[g, 1], jnp.zeros((width - 3 * QW, share), bf)], axis=0)
        if share % 128 == 0:
            joint_t_out[:, g * share : (g + 1) * share] = whole
        else:
            joint_rows[g * share : (g + 1) * share] = whole.T
    if share % 128:
        for i in range(D // 128):
            joint_t_out[:, i * 128 : (i + 1) * 128] = joint_rows[i * 128 : (i + 1) * 128].T

    process(plane)
    hand_on(2)
    process_arrived(1)
    hand_on(3)
    process_arrived(2)
    process_arrived(3)

    for j in range(PLANES):
        for k in range(1, S2):
            side_kv(j, k).wait_recv()
            core_kv(j, k).start()
    for first_move, second_move in zip(w_first, w_second):
        first_move.wait_recv()
        second_move.start()

    for j in range(PLANES):
        own_kv(j).wait()
        for k in range(1, S2):
            side_kv(j, k).wait_send()
        for k in range(S2):
            core_kv(j, k).wait()
    for p in range(PLANES):

        @pl.when((plane < PLANES - 1) & (plane >= p))
        def _(p=p):
            up(p).wait_send()

        @pl.when((plane > 0) & (plane <= p))
        def _(p=p):
            down(p).wait_send()

    for copy in w_own:
        copy.wait()
    for first_move, second_move in zip(w_first, w_second):
        first_move.wait_send()
        second_move.wait()


def front(n, groups, lengths, tokens, joint_shard, gain_first, gain_second, out_w, exp_w, con_w):
    bf, f32 = jnp.bfloat16, jnp.float32
    S2 = n // PLANES // 2
    T, D = tokens.shape
    width = 3 * QW + 64
    share = D // groups
    any_, vm, sm = (pl.BlockSpec(memory_space=m) for m in (pl.ANY, pltpu.VMEM, pltpu.SMEM))
    sems = lambda count: pltpu.SemaphoreType.DMA((2, count))
    halves = lambda w: w.reshape(2, w.shape[0] // 2, w.shape[1])
    weights = [halves(w) for w in (out_w, exp_w)]
    con_w = con_w.reshape(2 if con_w.shape[0] % 32 == 0 else 1, -1, D)
    return pl.pallas_call(
        functools.partial(front_kernel, n, groups, lengths.shape[1]),
        out_shape=(
            jax.ShapeDtypeStruct((PLANES, T, D), bf),
            jax.ShapeDtypeStruct((PLANES, QW, T), bf),
            jax.ShapeDtypeStruct((n, T, 2 * QW), bf),
            jax.ShapeDtypeStruct((width, D), bf),
            jax.ShapeDtypeStruct((PLANES, 2 * HALF, T), f32),
            jax.ShapeDtypeStruct((8, D), f32),
            *[jax.ShapeDtypeStruct((groups, *w.shape), bf) for w in weights],
            jax.ShapeDtypeStruct(con_w.shape[1:], bf),
        ),
        in_specs=[sm, vm, vm, vm, vm, any_, any_, any_],
        out_specs=(vm, vm, any_, vm, vm, vm, any_, any_, any_),
        scratch_shapes=[
            pltpu.VMEM((PLANES, T, D), bf),
            sems(2 * PLANES),
            pltpu.VMEM((2, 3 * QW // 2, share), bf),
            pltpu.VMEM((groups, 2, 3 * QW // 2, share), bf),
            pltpu.VMEM((groups, 8, share), f32),
            sems(3 * (groups - 1)),
            pltpu.VMEM((PLANES, T, 2 * QW), bf),
            sems(PLANES * (2 * S2 - 1)),
            pltpu.SemaphoreType.DMA((PLANES,)),
            sems(2 * len(weights) * (groups - 1)),
            pltpu.SemaphoreType.DMA((2, len(weights) + 1)),
            pltpu.VMEM((D, width), bf),
            *[pltpu.VMEM(w.shape, bf) for w in weights],
            pltpu.VMEM(con_w.shape[1:], bf),
        ],
        compiler_params=pltpu.CompilerParams(collective_id=1, has_side_effects=True, vmem_limit_bytes=60 << 20),
    )(
        lengths,
        tokens,
        joint_shard,
        gain_first,
        gain_second,
        *weights,
        con_w,
    )


def middle_kernel(
    n,
    groups,
    low_ref,
    tokens_ref,
    cot_ref,
    gains_ref,
    out_hbm,
    exp_hbm,
    con_hbm,
    *refs,
):
    con_got, refs = refs[: groups - 1], refs[groups - 1 :]
    (
        output_ref,
        grad_hidden_ref,
        gt_ref,
        y_keep,
        y_send,
        x_keep,
        x_send,
        z_keep,
        z_send_1,
        z_send_2,
        z_send_3,
        out_w,
        exp_w,
        con_w,
        local_sems,
        c_sems,
        att,
        a_sems,
        g_send,
        g_sems,
        hidden,
        second,
        branch,
        ga,
        act,
        gexp,
        acc,
        w_own,
        w_other,
        w_got,
        w_sems,
    ) = refs
    bf, f32 = jnp.bfloat16, jnp.float32
    S = n // PLANES
    S2 = S // 2
    T, D = tokens_ref.shape
    FFN = act.shape[1]
    me, group = lax.axis_index("ctx"), lax.axis_index("fsdp")
    plane, side = me // S, lax.rem(me, S)
    s2, core = side // 2, lax.rem(side, 2)

    def plane_peer(k):
        return (lax.rem(plane + k, PLANES) * S + side, group)

    core_peer = (plane * S + s2 * 2 + 1 - core, group)

    def group_peer(k):
        return (me, lax.rem(group + k, groups))


    def remote(source, target, sems, index, device):
        return pltpu.make_async_remote_copy(
            src_ref=source,
            dst_ref=target,
            send_sem=sems.at[0, index],
            recv_sem=sems.at[1, index],
            device_id=device,
            device_id_type=pl.DeviceIdType.MESH,
        )

    ff_share = con_hbm.shape[0]
    split = ff_share % 32 == 0

    def rows_of(g):
        return pl.ds(pl.multiple_of(g * ff_share, 16), ff_share)

    def half_of(g):
        if not split:
            return rows_of(g)
        half = ff_share // 2
        return pl.ds(pl.multiple_of(g * ff_share + core * half, 16), half)

    came = [half_of(lax.rem(group + groups - k, groups)) for k in range(1, groups)]
    con_hands = [remote(con_got[k], con_w.at[came[k]], c_sems, k, core_peer) for k in range(groups - 1)]
    con_local = [
        pltpu.make_async_copy(con_got[k], con_w.at[came[k]], local_sems.at[3 + k]) for k in range(groups - 1)
    ]
    local = [
        pltpu.make_async_copy(source, target, local_sems.at[i])
        for i, (source, target) in enumerate([(con_hbm, con_w.at[rows_of(group)]), (out_hbm, out_w), (exp_hbm, exp_w)])
    ]
    for copy in local + con_local:
        copy.start()
    barrier = pltpu.get_barrier_semaphore()
    for k in range(1, PLANES):
        pl.semaphore_signal(barrier, inc=1, device_id=plane_peer(k), device_id_type=pl.DeviceIdType.MESH)
    pl.semaphore_signal(barrier, inc=1, device_id=core_peer, device_id_type=pl.DeviceIdType.MESH)
    pl.semaphore_wait(barrier, PLANES)

    home = [remote(low_ref.at[j], att.at[plane], a_sems, j - 1, plane_peer(PLANES - j)) for j in range(1, PLANES)]
    for copy in home + (con_hands if split else []):
        copy.start()
    att[plane] = low_ref[0]

    def nt(a, b):
        return lax.dot_general(a, b, (((1,), (1,)), ((), ())), preferred_element_type=f32)

    chunk = 384
    cot = cot_ref[...]
    local[0].wait()
    for copy in con_local + (con_hands if split else []):
        copy.wait()
    for c in range(0, FFN, chunk):
        ga[:, c : c + chunk] = nt(cot, con_w[c : c + chunk])
    local[1].wait()
    for copy in home:
        copy.wait()
    attended = att[...].reshape(D, T)
    hidden[...] = tokens_ref[...].astype(f32) + jnp.dot(attended.T, out_w[...], preferred_element_type=f32)

    strip = 64

    def norm(i, carry):
        rows = pl.ds(pl.multiple_of(i * strip, strip), strip)
        values = hidden[rows]
        centred = values - jnp.mean(values, axis=-1, keepdims=True)
        spread = jnp.mean(centred * centred, axis=-1, keepdims=True)
        second[rows] = (centred * lax.rsqrt(spread + norm_eps) * gains_ref[1:2]).astype(bf)
        return carry

    lax.fori_loop(0, T // strip, norm, 0)
    local[2].wait()
    for c in range(0, FFN, chunk):
        cols, gate_cols = slice(c, c + chunk), slice(FFN + c, FFN + c + chunk)
        inner = jnp.dot(second[...], exp_w[:, cols], preferred_element_type=f32)
        gate = jnp.dot(second[...], exp_w[:, gate_cols], preferred_element_type=f32)
        share = 0.5 * (1.0 + lax.erf(inner * (0.5**0.5)))
        bent = inner * share
        act[:, cols] = (bent * gate).astype(bf)
        grad = ga[:, cols]
        slope = share + inner * jnp.exp(-0.5 * inner * inner) * ((2.0 * math.pi) ** -0.5)
        gexp[:, cols] = (grad * gate * slope).astype(bf)
        gexp[:, gate_cols] = (grad * bent).astype(bf)
    output_ref[...] = (hidden[...] + jnp.dot(act[...], con_w[...], preferred_element_type=f32)).astype(bf)
    acc[:T] = nt(gexp[...], exp_w[...])

    def norm_back(i, total):
        rows = pl.ds(pl.multiple_of(i * strip, strip), strip)
        values = hidden[rows]
        centred = values - jnp.mean(values, axis=-1, keepdims=True)
        scale = lax.rsqrt(jnp.mean(centred * centred, axis=-1, keepdims=True) + norm_eps)
        normal = centred * scale
        grad = acc[rows]
        total = total + jnp.sum(grad * normal, axis=0, keepdims=True)
        grad = grad * gains_ref[1:2]
        grad = grad - jnp.mean(grad, axis=-1, keepdims=True) - normal * jnp.mean(grad * normal, axis=-1, keepdims=True)
        back = cot_ref[rows].astype(f32) + grad * scale
        grad_hidden_ref[rows] = back
        branch[rows] = back.astype(bf)
        return total

    total = lax.fori_loop(0, T // strip, norm_back, jnp.zeros((1, D), f32))
    gain_two = jnp.broadcast_to(total, (8, D))
    for p in range(PLANES):
        g_send[p] = nt(out_w[p * QW : (p + 1) * QW], branch[...]).astype(bf)
    away = [
        remote(g_send.at[lax.rem(plane + k, PLANES)], gt_ref.at[k], g_sems, k - 1, plane_peer(k))
        for k in range(1, PLANES)
    ]
    for copy in away:
        copy.start()
    gt_ref[0] = g_send[plane]

    sent = []

    def place(rows, offset, height):
        for target, parity in ((w_other, 1 - core), (w_own, core)):

            def body(m, carry):
                if rows % 8:
                    pair = acc[pl.ds(pl.multiple_of(2 * m * rows, 8), 2 * rows)]
                    value = jnp.where(parity == 0, pair[:rows], pair[rows:])
                else:
                    value = acc[pl.ds(pl.multiple_of((2 * m + parity) * rows, 8), rows)]
                if height > rows:
                    rest = jnp.zeros((height - rows - 8, D), f32)
                    value = jnp.concatenate([value, gain_two, rest], axis=0)
                value = value.astype(bf)
                target[m, offset : offset + height] = value
                return carry

            lax.fori_loop(0, n // 2, body, 0)
        part = pl.ds(offset, height)
        sent.append(remote(w_other.at[:, part], w_got.at[:, part], w_sems, len(sent), core_peer))
        sent[-1].start()

    rows = D // n
    wide = 2 * FFN // D
    for c in range(0, FFN, chunk):
        acc[c : c + chunk] = jnp.dot(act[:, c : c + chunk].T, cot_ref[...], preferred_element_type=f32)
    used = (1 + wide) * rows
    place(FFN // n, used, w_own.shape[1] - used)
    second_t = second[...].T
    for i in range(wide):
        acc[:D] = jnp.dot(second_t, gexp[:, i * D : (i + 1) * D], preferred_element_type=f32)
        place(rows, (1 + i) * rows, rows)
    acc[:D] = jnp.dot(attended, branch[...], preferred_element_type=f32)
    place(rows, 0, rows)

    for copy in sent:
        copy.wait()
    height = y_keep.shape[2]
    third = lambda g, i: pl.ds(pl.multiple_of((3 * g + i) * height, 16), height)

    def summed(m, part):
        return (w_own[m, part].astype(f32) + w_got[m, part].astype(f32)).astype(bf)

    def each(count, body):
        def step(i, carry):
            body(i)
            return carry

        lax.fori_loop(0, count, step, 0)

    for k in range(groups):
        g = lax.rem(group + k, groups)

        def first(m, k=k, g=g):
            (y_send.at[k - 1] if k else y_keep)[m // S2, lax.rem(m, S2)] = summed(m, third(g, 0))

        each(PLANES * S2, first)
    for k in range(S2):
        a = lax.rem(s2 + k, S2)

        def second_part(i, k=k, a=a):
            p, g = i // groups, lax.rem(i, groups)
            (x_send.at[k - 1] if k else x_keep)[p, g] = summed(p * S2 + a, third(g, 1))

        each(PLANES * groups, second_part)
    z_parts = [z_keep, z_send_1, z_send_2, z_send_3]
    for k in range(PLANES):
        p = lax.rem(plane + k, PLANES)

        def third_part(i, k=k, p=p):
            a, g = i // groups, lax.rem(i, groups)
            z_parts[k][a, g] = summed(p * S2 + a, third(g, 2))

        each(S2 * groups, third_part)
    for copy in away:
        copy.wait()


def middle(n, groups, lowt, tokens, cotangent, gains, out_w, exp_w, con_w, con_got):
    bf, f32 = jnp.bfloat16, jnp.float32
    S2 = n // PLANES // 2
    T, D = tokens.shape
    ffn = con_w.shape[0] * groups
    used = (D + 2 * ffn + ffn) // n + 8
    height = -(-used // (groups * 48)) * 16
    any_, vm = pl.BlockSpec(memory_space=pl.ANY), pl.BlockSpec(memory_space=pltpu.VMEM)
    sems = lambda count: pltpu.SemaphoreType.DMA((2, count))
    shape = lambda *s: jax.ShapeDtypeStruct(s, bf)
    half = (n // 2, 3 * groups * height, D)
    return pl.pallas_call(
        functools.partial(middle_kernel, n, groups),
        out_shape=(
            shape(T, D),
            jax.ShapeDtypeStruct((T, D), f32),
            shape(PLANES, QW, T),
            shape(PLANES, S2, height, D),
            shape(groups - 1, PLANES, S2, height, D),
            shape(PLANES, groups, height, D),
            shape(S2 - 1, PLANES, groups, height, D),
            shape(S2, groups, height, D),
            *[shape(S2, groups, height, D)] * (PLANES - 1),
        ),
        in_specs=[vm, vm, vm, vm, any_, any_, any_] + [any_] * (groups - 1),
        out_specs=tuple([vm] * 11),
        scratch_shapes=[
            pltpu.VMEM(out_w.shape, bf),
            pltpu.VMEM(exp_w.shape, bf),
            pltpu.VMEM((ffn, D), bf),
            pltpu.SemaphoreType.DMA((3 + groups - 1,)),
            sems(groups - 1),
            pltpu.VMEM((PLANES, QW, T), bf),
            sems(PLANES - 1),
            pltpu.VMEM((PLANES, QW, T), bf),
            sems(PLANES - 1),
            pltpu.VMEM((T, D), f32),
            pltpu.VMEM((T, D), bf),
            pltpu.VMEM((T, D), bf),
            pltpu.VMEM((T, ffn), f32),
            pltpu.VMEM((T, ffn), bf),
            pltpu.VMEM((T, 2 * ffn), bf),
            pltpu.VMEM((ffn, D), f32),
            pltpu.VMEM(half, bf),
            pltpu.VMEM(half, bf),
            pltpu.VMEM(half, bf),
            sems(2 + 2 * ffn // D),
        ],
        compiler_params=pltpu.CompilerParams(collective_id=2, has_side_effects=True, vmem_limit_bytes=60 << 20),
    )(lowt, tokens, cotangent, gains, out_w, exp_w, con_w, *con_got)


def tail_kernel(
    n,
    groups,
    deal_ref,
    dq_ref,
    dkv_ref,
    turn_ref,
    gains_ref,
    joint_hbm,
    joint_t_hbm,
    first_hbm,
    tokens_hbm,
    grad_hidden_hbm,
    y_keep_hbm,
    y_got_hbm,
    x_keep_hbm,
    x_got_hbm,
    z_keep_hbm,
    z_got_1,
    z_got_2,
    z_got_3,
    d_got,
    w_all,
    jq_all,
    jk_all,
    joint_rows,
    joint_t,
    first,
    tokens,
    grad_hidden,
    y_keep,
    y_got,
    x_keep,
    x_got,
    z_keep,
    z_came,
    local_sems,
    kv_near,
    kv_send,
    kv_far,
    kv_sems,
    mixed_q,
    mixed_kv,
    part,
    part_got,
    part_send_sems,
    part_recv_sems,
    j_acc,
    jq,
    jq_core,
    jq_side,
    jq_plane,
    jk,
    jk_core,
    jk_side,
    jk_plane,
    j_sems,
    x1_got,
    y2_got,
    y3_got,
    z1_got,
    x3_got,
    w_plane,
    w_plane_got,
    w_sems,
    d_send,
    d_mid,
    d_back,
    d_sems,
    row_sems,
    row_local,
):
    bf, f32 = jnp.bfloat16, jnp.float32
    S = n // PLANES
    S2 = S // 2
    T, D = tokens.shape
    me, group = lax.axis_index("ctx"), lax.axis_index("fsdp")
    plane, side = me // S, lax.rem(me, S)
    s2, core = side // 2, lax.rem(side, 2)
    MESH = pl.DeviceIdType.MESH

    def at(p, a, c, g):
        return (p * S + a * 2 + c, g)

    def plane_peer(k):
        return at(lax.rem(plane + k, PLANES), s2, core, group)

    def side_peer(k):
        return at(plane, lax.rem(s2 + k, S2), core, group)

    def group_peer(k):
        return at(plane, s2, core, lax.rem(group + k, groups))

    core_peer = at(plane, s2, 1 - core, group)

    def send(source, target, send_sem, recv_sem, device):
        return pltpu.make_async_remote_copy(
            src_ref=source, dst_ref=target, send_sem=send_sem, recv_sem=recv_sem, device_id=device, device_id_type=MESH
        )

    def remote(source, target, sems, index, device):
        return send(source, target, sems.at[0, index], sems.at[1, index], device)

    def total_of(terms):
        total = terms[0].astype(f32)
        for term in terms[1:]:
            total = total + term.astype(f32)
        return total

    local = [
        pltpu.make_async_copy(source, target, local_sems.at[i])
        for i, (source, target) in enumerate(
            [
                (first_hbm, first),
                (joint_t_hbm, joint_t),
                (y_keep_hbm, y_keep),
                (y_got_hbm, y_got),
                (x_keep_hbm, x_keep),
                (x_got_hbm, x_got),
                (z_keep_hbm, z_keep),
                (z_got_1, z_came.at[0]),
                (z_got_2, z_came.at[1]),
                (z_got_3, z_came.at[2]),
                (tokens_hbm, tokens),
                (grad_hidden_hbm, grad_hidden),
            ]
        )
    ]
    for copy in local:
        copy.start()
    barrier = pltpu.get_barrier_semaphore()

    def greet(k, carry):
        pl.semaphore_signal(barrier, inc=1, device_id=(lax.rem(me + k, n), group), device_id_type=MESH)
        return carry

    lax.fori_loop(1, n, greet, 0)
    for k in range(1, groups):
        pl.semaphore_signal(barrier, inc=1, device_id=group_peer(k), device_id_type=MESH)
    pl.semaphore_wait(barrier, n - 1 + groups - 1)

    lower = plane < 2
    middle = (plane == 1) | (plane == 2)
    order = [
        jnp.where(lower, 3, 0),
        jnp.where(plane == 0, 2, jnp.where(plane == 1, 0, jnp.where(plane == 2, 3, 1))),
        jnp.where((plane == 0) | (plane == 2), 1, 2),
        plane,
    ]
    steps = range(PLANES)
    back = [lax.rem(plane + PLANES - p, PLANES) for p in order]
    main = jnp.where(lower, 0, 1)
    main_plane = plane + 1 - 2 * main

    core_kv = [remote(dkv_ref.at[order[t], :, 1 - core], kv_near.at[t], kv_sems, t, core_peer) for t in steps]
    for copy in core_kv:
        copy.start()

    per_group = joint_hbm.shape[0]
    index = me - group * per_group
    held_here = (index >= 0) & (index < per_group)
    row_own = pltpu.make_async_copy(joint_hbm.at[jnp.clip(index, 0, per_group - 1)], joint_rows, row_local.at[0])
    row_moves = [
        send(
            joint_hbm.at[jnp.clip(index, 0, per_group - 1)],
            joint_rows,
            row_sems.at[k - 1],
            row_sems.at[groups - 1],
            group_peer(k),
        )
        for k in range(1, groups)
    ]

    @pl.when(held_here)
    def _():
        row_own.start()
        for copy in row_moves:
            copy.start()

    w_moves = []

    def w_copy(source, target, device):
        copy = remote(source, target, w_sems, len(w_moves), device)
        w_moves.append(copy)
        copy.start()
        return copy

    local[2].wait()
    local[3].wait()
    for p in range(PLANES):
        for a in range(S2):
            y_keep[p, a] = total_of([y_keep[p, a]] + [y_got[k, p, a] for k in range(groups - 1)]).astype(bf)
    z1 = [w_copy(y_keep.at[lax.rem(plane + k, PLANES)], z1_got.at[k - 1], plane_peer(k)) for k in range(1, PLANES)]

    def turned_back(x, t):
        cos, sin = turn_ref[back[t], :HALF], turn_ref[back[t], HALF:]
        rows = []
        for h in range(HP):
            upper, lower = x[h * HD : h * HD + HALF], x[h * HD + HALF : (h + 1) * HD]
            rows += [upper * cos + lower * sin, lower * cos - upper * sin]
        return jnp.concatenate(rows, axis=0)

    side_kv = {}
    for t in steps:
        core_kv[t].wait()
        for a in range(S2):
            kv_send[t, a] = total_of([dkv_ref[order[t], a, core], kv_near[t, a]]).astype(bf)
        for k in range(1, S2):
            side_kv[t, k] = remote(
                kv_send.at[t, lax.rem(s2 + S2 - k, S2)],
                kv_far.at[t, k - 1],
                kv_sems,
                PLANES + t * (S2 - 1) + k - 1,
                side_peer(S2 - k),
            )
            side_kv[t, k].start()
    for t in steps:
        mixed_q[t] = turned_back(dq_ref[back[t]], t).astype(bf)

    local[4].wait()
    local[5].wait()
    for p in range(PLANES):
        for g in range(groups):
            x_keep[p, g] = total_of([x_keep[p, g]] + [x_got[k, p, g] for k in range(S2 - 1)]).astype(bf)
    y2 = [w_copy(x_keep.at[:, lax.rem(group + k, groups)], y2_got.at[k - 1], group_peer(k)) for k in range(1, groups)]
    for i in range(6, 10):
        local[i].wait()
    for a in range(S2):
        for g in range(groups):
            z_keep[a, g] = total_of([z_keep[a, g]] + [z_came[k, a, g] for k in range(PLANES - 1)]).astype(bf)
    y3 = [w_copy(z_keep.at[:, lax.rem(group + k, groups)], y3_got.at[k - 1], group_peer(k)) for k in range(1, groups)]

    j_moves = []

    def j_copy(source, target, device):
        copy = remote(source, target, j_sems, len(j_moves), device)
        j_moves.append(copy)
        copy.start()
        return copy

    def j_core_stage(mixed, grads, near):
        height = mixed.shape[1]
        j_acc[:height] = total_of(
            [jnp.dot(mixed[t], first[back[t]], preferred_element_type=f32) for t in steps]
        )
        shard_rows = D // n
        for i in range(D // 128):
            block = j_acc[:height, i * 128 : (i + 1) * 128].T
            row = i * 128
            while row < (i + 1) * 128:
                shard, offset = divmod(row, shard_rows)
                count = min(shard_rows - offset, (i + 1) * 128 - row)
                begin = row - i * 128
                grads[shard // S, shard % S // 2, shard % 2, offset : offset + count] = block[
                    begin : begin + count
                ].astype(bf)
                row += count
        return [j_copy(grads.at[:, :, 1 - core], near, core_peer)]

    def j_side_stage(moves, grads, near, far):
        for copy in moves:
            copy.wait()
        for p in range(PLANES):
            for a in range(S2):
                near[p, a] = total_of([grads[p, a, core], near[p, a]]).astype(bf)
        return [j_copy(near.at[:, lax.rem(s2 + k, S2)], far.at[k - 1], side_peer(k)) for k in range(1, S2)]

    def j_plane_stage(moves, near, far, gathered):
        for copy in moves:
            copy.wait()
        for p in range(PLANES):
            far[0, p] = total_of([near[p, s2]] + [far[k, p] for k in range(S2 - 1)]).astype(bf)
        gathered[plane] = far[0, plane]
        return [
            j_copy(far.at[0, lax.rem(plane + k, PLANES)], gathered.at[plane], plane_peer(k)) for k in range(1, PLANES)
        ]

    def j_group_stage(moves, gathered, every):
        for copy in moves:
            copy.wait()
        every[group] = gathered[...]
        return [j_copy(gathered, every.at[group], group_peer(k)) for k in range(1, groups)]

    local[0].wait()
    jq_moves = j_core_stage(mixed_q, jq, jq_core)

    local[1].wait()

    def main_send(t):
        return send(
            part.at[t],
            part_got.at[main, order[t]],
            part_send_sems.at[t],
            part_recv_sems.at[main * PLANES + order[t]],
            at(main_plane, s2, core, group),
        )

    def other_send(t):
        return send(
            part.at[t],
            part_got.at[1 - main, order[t]],
            part_send_sems.at[t],
            part_recv_sems.at[(1 - main) * PLANES + order[t]],
            at(2 * plane - main_plane, s2, core, group),
        )

    def came(direction, p):
        return send(
            part.at[0],
            part_got.at[direction, p],
            part_send_sems.at[0],
            part_recv_sems.at[direction * PLANES + p],
            core_peer,
        )

    strip = 64

    def add_part(t, direction, p):
        def body(i, carry):
            rows = pl.ds(pl.multiple_of(i * strip, strip), strip)
            part[t, rows] = total_of([part[t, rows], part_got[direction, p, rows]]).astype(bf)
            return carry

        lax.fori_loop(0, T // strip, body, 0)

    def relay(t, secondary):
        @pl.when(middle)
        def _():
            direction = 1 - main if secondary else main
            came(direction, order[t]).wait_recv()
            add_part(t, direction, order[t])
            (other_send if secondary else main_send)(t).start()

    def key_step(t):
        for k in range(1, S2):
            side_kv[t, k].wait()
        dk = total_of([kv_send[t, s2]] + [kv_far[t, k] for k in range(S2 - 1)]).T
        mixed_kv[t, :QW] = turned_back(dk[:QW], t).astype(bf)
        mixed_kv[t, QW:] = dk[QW:].astype(bf)
        grads = jnp.concatenate([mixed_q[t], mixed_kv[t]], axis=0)
        part[t] = jnp.dot(grads.T, joint_t[: 3 * QW], preferred_element_type=f32).astype(bf)
        if t < PLANES - 1:

            @pl.when(jnp.logical_not(middle))
            def _():
                main_send(t).start()

    key_step(0)
    jq_moves = j_side_stage(jq_moves, jq, jq_core, jq_side)
    key_step(1)
    key_step(2)
    relay(0, False)
    jq_moves = j_plane_stage(jq_moves, jq_core, jq_side, jq_plane)
    key_step(3)
    relay(2, False)
    jk_moves = j_core_stage(mixed_kv, jk, jk_core)

    for copy in y3:
        copy.wait()
    for a in range(S2):
        z_keep[a, group] = total_of([z_keep[a, group]] + [y3_got[k, a] for k in range(groups - 1)]).astype(bf)
    x3 = [w_copy(z_keep.at[lax.rem(s2 + k, S2), group], x3_got.at[k - 1], side_peer(k)) for k in range(1, S2)]
    for copy in y2:
        copy.wait()
    for p in range(PLANES):
        w_plane[p] = total_of([x_keep[p, group]] + [y2_got[k, p] for k in range(groups - 1)]).astype(bf)
    w_last = [
        w_copy(w_plane.at[lax.rem(plane + k, PLANES)], w_plane_got.at[k - 1], plane_peer(k)) for k in range(1, PLANES)
    ]
    for copy in z1:
        copy.wait()
    for a in range(S2):
        y_keep[plane, a] = total_of([y_keep[plane, a]] + [z1_got[k, a] for k in range(PLANES - 1)]).astype(bf)
    x1 = [w_copy(y_keep.at[plane, lax.rem(s2 + k, S2)], x1_got.at[k - 1], side_peer(k)) for k in range(1, S2)]
    relay(1, True)
    jk_moves = j_side_stage(jk_moves, jk, jk_core, jk_side)
    jq_moves = j_group_stage(jq_moves, jq_plane, jq_all)

    local[10].wait()
    local[11].wait()
    came(1 - main, plane).wait_recv()
    add_part(PLANES - 1, 1 - main, plane)

    @pl.when(middle)
    def _():
        came(main, plane).wait_recv()
        add_part(PLANES - 1, main, plane)

    def norm_back(i, carry):
        rows = pl.ds(pl.multiple_of(i * strip, strip), strip)
        grad = part[PLANES - 1, rows].astype(f32)
        values = tokens[rows].astype(f32)
        centred = values - jnp.mean(values, axis=-1, keepdims=True)
        scale = lax.rsqrt(jnp.mean(centred * centred, axis=-1, keepdims=True) + norm_eps)
        normal = centred * scale
        grad = grad * gains_ref[0:1]
        grad = grad - jnp.mean(grad, axis=-1, keepdims=True) - normal * jnp.mean(grad * normal, axis=-1, keepdims=True)
        grad_hidden[rows] = grad_hidden[rows] + grad * scale
        return carry

    lax.fori_loop(0, T // strip, norm_back, 0)

    blocks = T // BLOCK
    piece = BLOCK // n

    def d_copy(source, target, base, k):
        return remote(source.at[lax.rem(me + k, n)], target.at[me], d_sems, base + k, (lax.rem(me + k, n), group))

    for i in range(n):
        d_send[i] = jnp.concatenate(
            [grad_hidden[b * BLOCK + i * piece : b * BLOCK + (i + 1) * piece] for b in range(blocks)], axis=0
        ).astype(bf)
    out_deal = [d_copy(d_send, d_mid, 0, k) for k in range(1, n)]
    for copy in out_deal:
        copy.start()
    d_mid[me] = d_send[me]

    jk_moves = j_plane_stage(jk_moves, jk_core, jk_side, jk_plane)

    for copy in out_deal:
        copy.wait()
    for i in range(n):
        chosen = []
        for b in range(blocks):
            wanted = deal_ref[i * blocks + b]
            held = d_mid[wanted // blocks].astype(f32)
            rows = held[:piece]
            for other in range(1, blocks):
                rows = jnp.where(lax.rem(wanted, blocks) == other, held[other * piece : (other + 1) * piece], rows)
            chosen.append(rows)
        d_back[i] = jnp.concatenate(chosen, axis=0).astype(bf)
    back_deal = [d_copy(d_back, d_got, n, k) for k in range(1, n)]
    for copy in back_deal:
        copy.start()
    d_got[me] = d_back[me]

    for copy in x1 + w_last + x3:
        copy.wait()
    height = w_plane.shape[1]
    w_all[group, :height] = total_of([y_keep[plane, s2]] + [x1_got[k] for k in range(S2 - 1)]).astype(bf)
    w_all[group, height : 2 * height] = total_of(
        [w_plane[plane]] + [w_plane_got[k] for k in range(PLANES - 1)]
    ).astype(bf)
    w_all[group, 2 * height :] = total_of([z_keep[s2, group]] + [x3_got[k] for k in range(S2 - 1)]).astype(bf)
    w_gather = [w_copy(w_all.at[group], w_all.at[group], group_peer(k)) for k in range(1, groups)]
    jk_moves = j_group_stage(jk_moves, jk_plane, jk_all)

    for copy in back_deal + w_gather + jq_moves + jk_moves:
        copy.wait()
    for t in range(PLANES - 1):
        came_from = send(part.at[t], part.at[t], part_send_sems.at[t], part_recv_sems.at[0], core_peer)
        came_from.wait_send()

    @pl.when(held_here)
    def _():
        row_own.wait()
        for copy in row_moves:
            copy.wait_send()

    @pl.when(jnp.logical_not(held_here))
    def _():
        row_moves[0].wait_recv()


def tail(n, groups, deal, dqt, dkv, turn, gains, joint_shard, joint_t, first, tokens, grad_hidden, pieces):
    bf, f32 = jnp.bfloat16, jnp.float32
    S2 = n // PLANES // 2
    T, D = tokens.shape
    rows = D // n
    height = pieces[0].shape[2]
    piece_rows = T // n
    joint_shard = joint_shard.reshape(-1, rows, joint_shard.shape[1])
    any_, vm, sm = (pl.BlockSpec(memory_space=m) for m in (pl.ANY, pltpu.VMEM, pltpu.SMEM))
    sems = lambda count: pltpu.SemaphoreType.DMA((2, count))
    small = lambda *s: pltpu.VMEM(s, bf)
    j_buffers = lambda w: [
        small(PLANES, S2, 2, rows, w),
        small(PLANES, S2, rows, w),
        small(S2 - 1, PLANES, rows, w),
        small(PLANES, rows, w),
    ]
    return pl.pallas_call(
        functools.partial(tail_kernel, n, groups),
        out_shape=(
            jax.ShapeDtypeStruct((n, piece_rows, D), bf),
            jax.ShapeDtypeStruct((groups, 3 * height, D), bf),
            jax.ShapeDtypeStruct((groups, PLANES, rows, QW), bf),
            jax.ShapeDtypeStruct((groups, PLANES, rows, 2 * QW), bf),
            jax.ShapeDtypeStruct(joint_shard.shape[1:], bf),
        ),
        in_specs=[sm, vm, vm, vm, vm] + [any_] * 13,
        out_specs=tuple([vm] * 4) + (any_,),
        scratch_shapes=[
            pltpu.VMEM(joint_t.shape, bf),
            pltpu.VMEM((PLANES, T, D), bf),
            pltpu.VMEM((T, D), bf),
            pltpu.VMEM((T, D), f32),
            *[pltpu.VMEM(p.shape, bf) for p in pieces[:5]],
            pltpu.VMEM((PLANES - 1, *pieces[5].shape), bf),
            pltpu.SemaphoreType.DMA((12,)),
            small(PLANES, S2, T, 2 * QW),
            small(PLANES, S2, T, 2 * QW),
            small(PLANES, S2 - 1, T, 2 * QW),
            sems(PLANES * S2),
            small(PLANES, QW, T),
            small(PLANES, 2 * QW, T),
            small(PLANES, T, D),
            small(2, PLANES, T, D),
            pltpu.SemaphoreType.DMA((PLANES - 1,)),
            pltpu.SemaphoreType.DMA((2 * PLANES,)),
            pltpu.VMEM((2 * QW, D), f32),
            *j_buffers(QW),
            *j_buffers(2 * QW),
            sems(2 * (1 + S2 - 1 + PLANES - 1 + groups - 1)),
            small(S2 - 1, height, D),
            small(groups - 1, PLANES, height, D),
            small(groups - 1, S2, height, D),
            small(PLANES - 1, S2, height, D),
            small(S2 - 1, height, D),
            small(PLANES, height, D),
            small(PLANES - 1, height, D),
            sems(3 * (groups - 1) + 2 * (S2 - 1) + 2 * (PLANES - 1)),
            small(n, piece_rows, D),
            small(n, piece_rows, D),
            small(n, piece_rows, D),
            sems(2 * n),
            pltpu.SemaphoreType.DMA((groups,)),
            pltpu.SemaphoreType.DMA((1,)),
        ],
        compiler_params=pltpu.CompilerParams(collective_id=0, has_side_effects=True, vmem_limit_bytes=60 << 20),
    )(deal, dqt, dkv, turn, gains, joint_shard, joint_t, first, tokens, grad_hidden, *pieces)


def finish_kernel(
    n,
    d_ref,
    w_ref,
    jq_ref,
    jk_ref,
    rows_ref,
    gains_ref,
    dealt_ref,
    joint_ref,
    output_ref,
    expand_ref,
    contract_ref,
    gain_one_ref,
    gain_two_ref,
):
    f32 = jnp.float32
    T, D = dealt_ref.shape
    blocks = T // BLOCK
    piece = BLOCK // n
    for b in range(blocks):
        for i in range(0, n, 2):
            rows = [d_ref[i + e].astype(f32)[b * piece : (b + 1) * piece] for e in range(2)]
            dealt_ref[b * BLOCK + i * piece : b * BLOCK + (i + 2) * piece] = jnp.concatenate(rows, axis=0).astype(
                dealt_ref.dtype
            )

    def summed(ref, p):
        total = ref[0, p].astype(f32)
        for g in range(1, ref.shape[0]):
            total = total + ref[g, p].astype(f32)
        return total.T

    for i in range(PLANES // 2):
        pair = [summed(jq_ref, 2 * i + e) for e in range(2)]
        joint_ref[:, i * 2 * QW : (i + 1) * 2 * QW] = jnp.concatenate(pair, axis=0).T
        pair = [summed(jk_ref, 2 * i + e) for e in range(2)]
        for part in range(2):
            cols = (part + 1) * D + i * 2 * QW
            rows = [x[part * QW : (part + 1) * QW] for x in pair]
            joint_ref[:, cols : cols + 2 * QW] = jnp.concatenate(rows, axis=0).T
    shift = D - lax.axis_index("ctx") * (D // n)

    def own_lanes(x):
        return pltpu.roll(jnp.broadcast_to(x, (8, D)), shift, 1)[0:1, : D // n]

    product = jnp.sum(joint_ref[...] * rows_ref[...].astype(f32), axis=1, keepdims=True)
    product = jnp.broadcast_to(product, (D // n, 128)).T[0:1]
    gain_one_ref[...] = product / own_lanes(gains_ref[0:1])
    height = w_ref.shape[1]
    rows = D // n
    targets = [(output_ref, 0, rows)]
    targets += [(expand_ref, i * D, rows) for i in range(expand_ref.shape[1] // D)]
    targets += [(contract_ref, 0, contract_ref.shape[0])]
    row = 0
    for target, column, count in targets:
        done = 0
        while done < count:
            g, offset = divmod(row, height)
            part = min(count - done, height - offset)
            target[done : done + part, column : column + D] = w_ref[g, offset : offset + part].astype(f32)
            done += part
            row += part
    g, offset = divmod(row, height)
    gain_two_ref[...] = own_lanes(w_ref[g, offset : offset + 1].astype(f32))


def finish(n, T, wide, contract_rows, d_got, w_all, jq_all, jk_all, joint_rows, gains):
    D = d_got.shape[-1]
    rows = D // n
    f32 = jnp.float32
    vm = pl.BlockSpec(memory_space=pltpu.VMEM)
    return pl.pallas_call(
        functools.partial(finish_kernel, n),
        out_shape=(
            jax.ShapeDtypeStruct((T, D), jnp.bfloat16),
            jax.ShapeDtypeStruct((rows, 3 * D), f32),
            jax.ShapeDtypeStruct((rows, D), f32),
            jax.ShapeDtypeStruct((rows, wide), f32),
            jax.ShapeDtypeStruct((contract_rows, D), f32),
            jax.ShapeDtypeStruct((1, rows), f32),
            jax.ShapeDtypeStruct((1, rows), f32),
        ),
        in_specs=[vm] * 6,
        out_specs=tuple([vm] * 7),
    )(d_got, w_all, jq_all, jk_all, joint_rows, gains)


def on_device(
    n,
    groups,
    tokens,
    cotangent,
    lengths,
    deal,
    joint_projection,
    output_projection,
    expand_weight,
    contract_weight,
    gain_first,
    gain_second,
):
    T, D = tokens.shape[1:]
    S = n // PLANES
    S2 = S // 2

    def over_planes(x, k):
        return lax.ppermute(x, "ctx", [(h * S + s, (h + k) % PLANES * S + s) for h in range(PLANES) for s in range(S)])

    def over_sides(x, k):
        pairs = [
            (h * S + a * 2 + c, h * S + (a + k) % S2 * 2 + c) for h in range(PLANES) for a in range(S2) for c in range(2)
        ]
        return lax.ppermute(x, "ctx", pairs)

    def over_groups(x, k):
        return lax.ppermute(x, "fsdp", [(f, (f + k) % groups) for f in range(groups)])

    def moved(x, over):
        if x.shape[0] == 1:
            return over(x, 1)
        return jnp.stack([over(x[k], k + 1) for k in range(x.shape[0])])

    first, qt, kv, joint_t, turn, gains, out_w, exp_w, con_half = front(
        n,
        groups,
        lengths,
        tokens[0],
        joint_projection,
        gain_first,
        gain_second,
        output_projection,
        expand_weight,
        contract_weight,
    )
    con_got = [over_groups(con_half, k) for k in range(1, groups)]
    out_w, exp_w = (w.reshape(-1, w.shape[-1]) for w in (out_w, exp_w))
    ot, lowt, lse = attn_fwd(n, lengths, qt, kv)
    output, grad_hidden, gt, y_keep, y_send, x_keep, x_send, z_keep, *z_send = middle(
        n, groups, lowt, tokens[0], cotangent[0], gains, out_w, exp_w, contract_weight, con_got
    )
    y_got, x_got = moved(y_send, over_groups), moved(x_send, over_sides)
    z_got = [over_planes(part, k + 1) for k, part in enumerate(z_send)]
    dqt, dkv = attn_bwd(n, lengths, qt, kv, ot, lse, gt)
    d_got, w_all, jq_all, jk_all, joint_rows = tail(
        n,
        groups,
        deal[0],
        dqt,
        dkv.reshape(PLANES, S2, 2, T, 2 * QW),
        turn,
        gains,
        joint_projection,
        joint_t,
        first,
        tokens[0],
        grad_hidden,
        [y_keep, y_got, x_keep, x_got, z_keep, *z_got],
    )
    dealt, shard_joint, shard_output, shard_expand, shard_contract, gain_one, gain_two = finish(
        n, T, exp_w.shape[1], contract_weight.shape[0] * groups // n, d_got, w_all, jq_all, jk_all, joint_rows, gains
    )
    return (
        output[None],
        dealt[None],
        shard_joint,
        shard_output,
        shard_expand,
        shard_contract,
        gain_one[0],
        gain_two[0],
    )


def solution(mesh):
    return jax.shard_map(
        functools.partial(on_device, mesh.shape["ctx"], mesh.shape["fsdp"]),
        mesh=mesh,
        in_specs=(
            P("fsdp", "ctx", None),
            P("fsdp", "ctx", None),
            P("fsdp", None),
            P("fsdp", None),
            P("fsdp", None),
            P("fsdp", None),
            P("fsdp", None),
            P("fsdp", None),
            P("fsdp"),
            P("fsdp"),
        ),
        out_specs=(
            P("fsdp", "ctx", None),
            P("fsdp", "ctx", None),
            P("ctx", None),
            P("ctx", None),
            P("ctx", None),
            P("ctx", None),
            P("ctx"),
            P("ctx"),
        ),
        check_vma=False,
    )
```

```python
import functools
import math

import jax
import jax.numpy as jnp
import numpy as np
from jax import lax
from jax.experimental import pallas as pl
from jax.experimental.pallas import tpu as pltpu
from jax.sharding import PartitionSpec as P

FF = 1152
HEADS = 12
HEAD_DIM = 64
BLOCK = 128
PLANES = 4
HD = HEAD_DIM
HALF = HEAD_DIM // 2
HP = HEADS // PLANES
QW = HP * HEAD_DIM
rope_base = 160000.0
norm_eps = 1e-05
MASKED = -1e30


def ends_of(lengths_ref, count):
    ends, total = [], 0
    for i in range(count):
        total = total + lengths_ref[0, i]
        ends.append(total)
    return ends


def span_of(index, ends):
    begin, end = jnp.zeros_like(index), jnp.full_like(index, ends[0])
    for before, after in zip(ends[:-1], ends[1:]):
        begin = jnp.where(index >= before, before, begin)
        end = jnp.where(index >= before, after, end)
    return begin, end


def head_rows(x, head):
    rows = lax.broadcasted_iota(jnp.int32, x.shape, 0)
    return jnp.where((rows >= head * HD) & (rows < (head + 1) * HD), x, jnp.zeros_like(x))


def query_block(n, b, T, ends):
    S = n // PLANES
    me = lax.axis_index("ctx")
    base = (lax.rem(me // S + PLANES - b, PLANES) * S + lax.rem(me, S)) * T
    low_begin, low_end = span_of(base, ends)
    high_begin, high_end = span_of(base + T - 1, ends)
    low, high = low_begin // T, (high_end + T - 1) // T
    full_low = jnp.clip((high_begin + T - 1) // T, low, high)
    full_high = jnp.clip(low_end // T, full_low, high)
    begin, end = span_of(base + lax.broadcasted_iota(jnp.int32, (8, T), 1), ends)
    return (low, full_low, full_high, high), begin[0:1], end[0:1]


def over_units(bounds, step, sizes):
    low, full_low, full_high, high = bounds

    def run(begin, end, masked):
        def body(u, carry):
            step(u, masked)
            return carry

        lax.fori_loop(begin, end, body, 0)

    run(low, full_low, True)
    in_groups(full_low, full_high, lambda u: step(u, False), sizes)
    run(full_high, high, True)


def in_groups(begin, end, step, sizes):
    for size in sizes:
        count = (end - begin) // size

        def some(i, carry, size=size, begin=begin):
            for e in range(size):
                step(begin + size * i + e)
            return carry

        lax.fori_loop(0, count, some, 0)
        begin = begin + size * count


def fwd_kernel(n, count, lengths_ref, qt_ref, kv_ref, ot_ref, lowt_ref, lse_ref, values, scores, top, total, acc):
    units, T, _ = kv_ref.shape
    ends = ends_of(lengths_ref, count)

    def flip(u, carry):
        values[u] = kv_ref[u, :, 128:].T
        return carry

    lax.fori_loop(0, units, flip, 0, unroll=4)

    def one_query_block(b, carry):
        qt = qt_ref[b]
        qheads = [head_rows(qt, h) for h in range(HP)]
        bounds, q_start, q_end = query_block(n, b, T, ends)
        top[...] = jnp.full_like(top, MASKED)
        total[...] = jnp.zeros_like(total)
        acc[...] = jnp.zeros_like(acc)

        def score(u, masked):
            k = kv_ref[u, :, :QW]
            st = [jnp.dot(k, qheads[h], preferred_element_type=jnp.float32) for h in range(HP)]
            if masked:
                at = u * T + lax.broadcasted_iota(jnp.int32, (T, T), 0)
                allowed = (at >= q_start) & (at < q_end)
                st = [jnp.where(allowed, s, MASKED) for s in st]
            for h in range(HP):
                scores[u, h] = st[h]
                top[h] = jnp.maximum(top[h], jnp.max(st[h].reshape(T // 8, 8, T), axis=0))

        over_units(bounds, score, (2, 1))
        m = [jnp.max(top[h], axis=0, keepdims=True) for h in range(HP)]

        def gather(u):
            p = [jnp.exp(scores[u, h] - m[h]) for h in range(HP)]
            for h in range(HP):
                total[h] += jnp.sum(p[h].reshape(T // 8, 8, T), axis=0)
                rows = pl.ds(h * HD, HD)
                acc[rows, :] += jnp.dot(
                    values[u, pl.ds(HD + h * HD, HD), :], p[h].astype(jnp.bfloat16), preferred_element_type=jnp.float32
                )

        in_groups(bounds[0], bounds[3], gather, (4, 2, 1))
        for h in range(HP):
            rows = pl.ds(h * HD, HD)
            l = jnp.sum(total[h], axis=0, keepdims=True)
            o = acc[rows, :] / l
            ot_ref[b, rows, :] = o
            lowt_ref[b, rows, :] = o.astype(jnp.bfloat16)
            lse_ref[b, h : h + 1, :] = m[h] + jnp.log(l)
        return carry

    lax.fori_loop(0, qt_ref.shape[0], one_query_block, 0)


def attn_fwd(n, lengths, qt, kv):
    B, _, T = qt.shape
    U = kv.shape[0]
    sm, vm = pl.BlockSpec(memory_space=pltpu.SMEM), pl.BlockSpec(memory_space=pltpu.VMEM)
    return pl.pallas_call(
        functools.partial(fwd_kernel, n, lengths.shape[1]),
        out_shape=(
            jax.ShapeDtypeStruct((B, QW, T), jnp.float32),
            jax.ShapeDtypeStruct((B, QW, T), jnp.bfloat16),
            jax.ShapeDtypeStruct((B, 8, T), jnp.float32),
        ),
        in_specs=[sm, vm, vm],
        out_specs=(vm, vm, vm),
        scratch_shapes=[
            pltpu.VMEM((U, 256, T), jnp.bfloat16),
            pltpu.VMEM((U, HP, T, T), jnp.float32),
            pltpu.VMEM((HP, 8, T), jnp.float32),
            pltpu.VMEM((HP, 8, T), jnp.float32),
            pltpu.VMEM((QW, T), jnp.float32),
        ],
        compiler_params=pltpu.CompilerParams(vmem_limit_bytes=60 << 20),
    )(lengths, qt, kv)


def bwd_kernel(n, count, lengths_ref, qt_ref, kv_ref, ot_ref, lse_ref, gt_ref, dqt_ref, dkv_ref, keys, dk, dv, dq):
    units, T, _ = kv_ref.shape
    ends = ends_of(lengths_ref, count)

    def flip(u, carry):
        keys[u] = kv_ref[u, :, :256].T
        dk[u] = jnp.zeros_like(dk[u])
        dv[u] = jnp.zeros_like(dv[u])
        return carry

    lax.fori_loop(0, units, flip, 0, unroll=4)

    def one_query_block(b, carry):
        qt, gt = qt_ref[b], gt_ref[b]
        zero = jnp.zeros((HD, T), jnp.bfloat16)
        qheads = [head_rows(qt, h) for h in range(HP)]
        gheads = [head_rows(gt, h) for h in range(HP)]
        gpad = [jnp.concatenate([zero, x], axis=0) for x in gheads]
        lanes = lax.broadcasted_iota(jnp.int32, (T, 256), 1) // HD
        q, g = jnp.concatenate([qt, zero], axis=0).T, jnp.concatenate([zero, gt], axis=0).T
        q = jnp.concatenate([jnp.where(lanes == h, q, jnp.zeros_like(q)) for h in range(HP)], axis=0)
        g = jnp.concatenate([jnp.where(lanes == h + 1, g, jnp.zeros_like(g)) for h in range(HP)], axis=0)
        bounds, q_start, q_end = query_block(n, b, T, ends)
        prod = gt.astype(jnp.float32) * ot_ref[b]
        delta = [jnp.sum(prod[h * HD : (h + 1) * HD], axis=0, keepdims=True) for h in range(HP)]
        lse = [lse_ref[b, h : h + 1, :] for h in range(HP)]
        dq[...] = jnp.zeros_like(dq)

        def one_unit(u, masked):
            k, v = kv_ref[u, :, :QW], kv_ref[u, :, 128:]
            st = [jnp.dot(k, qheads[h], preferred_element_type=jnp.float32) for h in range(HP)]
            dp = [jnp.dot(v, gpad[h], preferred_element_type=jnp.float32) for h in range(HP)]
            st = [st[h] - lse[h] for h in range(HP)]
            if masked:
                at = u * T + lax.broadcasted_iota(jnp.int32, (T, T), 0)
                allowed = (at >= q_start) & (at < q_end)
                st = [jnp.where(allowed, s, MASKED) for s in st]
            p = [jnp.exp(s) for s in st]
            ds = [(p[h] * (dp[h] - delta[h])).astype(jnp.bfloat16) for h in range(HP)]
            p = [x.astype(jnp.bfloat16) for x in p]
            dv[u] += jnp.dot(jnp.concatenate(p, axis=1), g, preferred_element_type=jnp.float32)
            dk[u] += jnp.dot(jnp.concatenate(ds, axis=1), q, preferred_element_type=jnp.float32)
            for h in range(HP):
                rows = pl.ds(h * HD, HD)
                dq[rows, :] += jnp.dot(keys[u, rows, :], ds[h], preferred_element_type=jnp.float32)

        over_units(bounds, one_unit, (4, 2, 1))
        dqt_ref[b] = dq[...] * (HD**-0.5)
        return carry

    lax.fori_loop(0, qt_ref.shape[0], one_query_block, 0)

    def out(u, carry):
        dkv_ref[u, :, :128] = dk[u, :, :128].astype(jnp.bfloat16)
        dkv_ref[u, :, 128:256] = (dk[u, :, 128:] + dv[u, :, :128]).astype(jnp.bfloat16)
        dkv_ref[u, :, 256:] = dv[u, :, 128:].astype(jnp.bfloat16)
        return carry

    lax.fori_loop(0, units, out, 0, unroll=2)


def attn_bwd(n, lengths, qt, kv, ot, lse, gt):
    B, _, T = qt.shape
    U = kv.shape[0]
    sm, vm = pl.BlockSpec(memory_space=pltpu.SMEM), pl.BlockSpec(memory_space=pltpu.VMEM)
    return pl.pallas_call(
        functools.partial(bwd_kernel, n, lengths.shape[1]),
        out_shape=(jax.ShapeDtypeStruct((B, QW, T), jnp.float32), jax.ShapeDtypeStruct((U, T, 2 * QW), jnp.bfloat16)),
        in_specs=[sm] + [vm] * 5,
        out_specs=(vm, vm),
        scratch_shapes=[
            pltpu.VMEM((U, 256, T), jnp.bfloat16),
            pltpu.VMEM((U, T, 256), jnp.float32),
            pltpu.VMEM((U, T, 256), jnp.float32),
            pltpu.VMEM((QW, T), jnp.float32),
        ],
        compiler_params=pltpu.CompilerParams(vmem_limit_bytes=60 << 20),
    )(lengths, qt, kv, ot, lse, gt)
def front_kernel(
    n,
    groups,
    count,
    lengths_ref,
    tokens_ref,
    joint_ref,
    gain_one_ref,
    gain_two_ref,
    out_hbm,
    exp_hbm,
    con_hbm,
    first_ref,
    qt_ref,
    kv_ref,
    joint_t_out,
    turn_ref,
    gains_ref,
    out_all,
    exp_all,
    con_ref,
    held,
    t_sems,
    cols,
    cols_all,
    gain_held,
    g_sems,
    kv_own,
    kv_sems,
    own_sems,
    w_sems,
    w_local,
    joint_rows,
    out_held,
    exp_held,
    con_held,
):
    bf, f32 = jnp.bfloat16, jnp.float32
    S = n // PLANES
    S2 = S // 2
    T, D = tokens_ref.shape
    me, group = lax.axis_index("ctx"), lax.axis_index("fsdp")
    plane, side = me // S, lax.rem(me, S)
    s2, core = side // 2, lax.rem(side, 2)

    def at(p, a, c, g):
        return (p * S + a * 2 + c, g)

    def side_peer(k):
        return at(plane, lax.rem(s2 + k, S2), core, group)

    def group_peer(k):
        return at(plane, s2, core, lax.rem(group + k, groups))

    core_peer = at(plane, s2, 1 - core, group)

    def remote(source, target, sems, index, device):
        return pltpu.make_async_remote_copy(
            src_ref=source,
            dst_ref=target,
            send_sem=sems.at[0, index],
            recv_sem=sems.at[1, index],
            device_id=device,
            device_id_type=pl.DeviceIdType.MESH,
        )

    barrier = pltpu.get_barrier_semaphore()

    def greet(device):
        pl.semaphore_signal(barrier, inc=1, device_id=device, device_id_type=pl.DeviceIdType.MESH)

    for k in range(1, PLANES):
        greet(at(lax.rem(plane + k, PLANES), s2, core, group))
    for k in range(1, S2):
        greet(side_peer(k))
    for k in range(1, groups):
        greet(group_peer(k))
    greet(core_peer)
    pl.semaphore_wait(barrier, PLANES - 1 + S2 - 1 + groups - 1 + 1)

    def up(p):
        return remote(held.at[p], held.at[p], t_sems, p, at(plane + 1, s2, core, group))

    def down(p):
        return remote(held.at[p], held.at[p], t_sems, PLANES + p, at(plane - 1, s2, core, group))

    held[plane] = tokens_ref[...]

    @pl.when(plane < PLANES - 1)
    def _():
        up(plane).start()

    @pl.when(plane > 0)
    def _():
        down(plane).start()

    pair = 2 * QW
    for part in range(3):
        window = joint_ref[:, pl.ds(pl.multiple_of(part * D + plane // 2 * pair, 128), pair)].T
        chosen = jnp.where(lax.rem(plane, 2) == 0, window[:QW].astype(f32), window[QW:].astype(f32))
        half = 3 * QW // 2
        low, high = part * QW, (part + 1) * QW
        for c in range(2):
            begin, end = max(low, c * half), min(high, (c + 1) * half)
            if begin < end:
                cols[c, begin - c * half : end - c * half] = chosen[begin - low : end - low].astype(bf)
    gain_held[group] = jnp.zeros_like(gain_held[group])
    gain_held[group, 0:1] = gain_one_ref[...].astype(f32).reshape(1, -1)
    gain_held[group, 1:2] = gain_two_ref[...].astype(f32).reshape(1, -1)
    col_moves = [
        remote(cols.at[core], cols_all.at[group, core], g_sems, k - 1, group_peer(k)) for k in range(1, groups)
    ]
    col_hands = []
    for k in range(1, groups):
        came = cols_all.at[lax.rem(group + groups - k, groups), core]
        col_hands.append(remote(came, came, g_sems, 2 * (groups - 1) + k - 1, core_peer))
    gain_moves = [
        remote(gain_held.at[group], gain_held.at[group], g_sems, groups - 1 + k - 1, group_peer(k))
        for k in range(1, groups)
    ]
    for copy in gain_moves + col_moves:
        copy.start()
    cols_all[group] = cols[...]

    weights = [(out_hbm, out_all, out_held), (exp_hbm, exp_all, exp_held)]
    part = core if con_hbm.shape[0] == 2 else 0
    w_in = [pltpu.make_async_copy(con_hbm.at[part], con_held, w_local.at[0, len(weights)])]
    w_own = [pltpu.make_async_copy(con_held, con_ref, w_local.at[1, len(weights)])]
    w_first, w_second = [], []
    for i, (source, target, bounce) in enumerate(weights):
        w_in.append(pltpu.make_async_copy(source, bounce, w_local.at[0, i]))
        w_own.append(pltpu.make_async_copy(bounce, target.at[group], w_local.at[1, i]))
        for k in range(1, groups):
            index = (i * (groups - 1) + k - 1) * 2
            w_first.append(remote(source.at[core], target.at[group, core], w_sems, index, group_peer(k)))
            came = lax.rem(group + groups - k, groups)
            w_second.append(remote(target.at[came, core], target.at[came, core], w_sems, index + 1, core_peer))
    for copy in w_in:
        copy.start()

    ends = ends_of(lengths_ref, count)
    row = lax.broadcasted_iota(jnp.int32, (HALF, T), 0)
    frequencies = jnp.zeros((HALF, T), f32)
    for i in range(HALF):
        frequencies = jnp.where(row == i, float(np.float32(rope_base ** (-2.0 * i / HEAD_DIM))), frequencies)
    for j in range(PLANES):
        base = (lax.rem(plane + PLANES - j, PLANES) * S + side) * T
        index = base + lax.broadcasted_iota(jnp.int32, (8, T), 1)
        begin, _ = span_of(index, ends)
        angles = (index - begin)[0:1].astype(f32) * frequencies
        turn_ref[j, :HALF] = jnp.cos(angles)
        turn_ref[j, HALF:] = jnp.sin(angles)

    strip = 64

    def kv_unit(p, a, c):
        return p * S + a * 2 + c

    def side_kv(j, k):
        p = lax.rem(plane + PLANES - j, PLANES)
        return remote(kv_own.at[j], kv_ref.at[kv_unit(p, s2, core)], kv_sems, j * (2 * S2 - 1) + k - 1, side_peer(k))

    def core_kv(j, k):
        p = lax.rem(plane + PLANES - j, PLANES)
        unit = kv_unit(p, lax.rem(s2 + S2 - k, S2), core)
        source = kv_own.at[j] if k == 0 else kv_ref.at[unit]
        return remote(source, kv_ref.at[unit], kv_sems, j * (2 * S2 - 1) + S2 - 1 + k, core_peer)

    def own_kv(j):
        p = lax.rem(plane + PLANES - j, PLANES)
        return pltpu.make_async_copy(kv_own.at[j], kv_ref.at[kv_unit(p, s2, core)], own_sems.at[j])

    def process(p):
        j = lax.rem(plane + PLANES - p, PLANES)

        def norm(i, carry):
            rows = pl.ds(pl.multiple_of(i * strip, strip), strip)
            values = held[p, rows].astype(f32)
            centred = values - jnp.mean(values, axis=-1, keepdims=True)
            spread = jnp.mean(centred * centred, axis=-1, keepdims=True)
            first_ref[j, rows] = (centred * lax.rsqrt(spread + norm_eps) * gains_ref[0:1]).astype(bf)
            return carry

        lax.fori_loop(0, T // strip, norm, 0)
        mixed = lax.dot_general(
            joint_t_out[: 3 * QW], first_ref[j], (((1,), (1,)), ((), ())), preferred_element_type=f32
        )
        cos, sin = turn_ref[j, :HALF], turn_ref[j, HALF:]
        turned = []
        for h in range(2 * HP):
            upper, lower = mixed[h * HD : h * HD + HALF], mixed[h * HD + HALF : (h + 1) * HD]
            turned += [upper * cos - lower * sin, lower * cos + upper * sin]
        q = jnp.concatenate(turned[: 2 * HP], axis=0).astype(bf)
        qt_ref[j] = (q.astype(f32) * HEAD_DIM**-0.5).astype(bf)
        kv_own[j] = jnp.concatenate(turned[2 * HP :] + [mixed[2 * QW :]], axis=0).T.astype(bf)
        for k in range(1, S2):
            side_kv(j, k).start()
        core_kv(j, 0).start()
        own_kv(j).start()

    def hand_on(t):
        @pl.when(plane >= t)
        def _():
            up(plane - t).wait_recv()

            @pl.when(plane < PLANES - 1)
            def _():
                up(plane - t).start()

        @pl.when(plane + t < PLANES)
        def _():
            down(plane + t).wait_recv()

            @pl.when(plane > 0)
            def _():
                down(plane + t).start()

    def process_arrived(t):
        below = jnp.where(plane >= t, 1, 0)
        above = jnp.where(plane + t < PLANES, 1, 0)

        def arrived(i, carry):
            process(jnp.where(i < below, plane - t, plane + t))
            return carry

        lax.fori_loop(0, below + above, arrived, 0)

    hand_on(1)
    for copy in gain_moves:
        copy.wait()
    share = D // groups
    total = jnp.zeros((8, D), f32)
    for g in range(groups):
        rows = lax.broadcasted_iota(jnp.int32, (share, D), 0)
        lanes = lax.broadcasted_iota(jnp.int32, (share, D), 1)
        place = jnp.where(lanes == rows + g * share, 1.0, 0.0).astype(bf)
        total = total + jnp.dot(gain_held[g].astype(bf), place, preferred_element_type=f32)
    gains_ref[...] = total
    for copy, hand in zip(col_moves, col_hands):
        copy.wait()
        hand.start()
    for copy in w_first:
        copy.start()
    for copy in w_in:
        copy.wait()
    for copy in w_own:
        copy.start()
    for copy in col_hands:
        copy.wait()
    width = joint_t_out.shape[0]
    for g in range(groups):
        whole = jnp.concatenate([cols_all[g, 0], cols_all[g, 1], jnp.zeros((width - 3 * QW, share), bf)], axis=0)
        if share % 128 == 0:
            joint_t_out[:, g * share : (g + 1) * share] = whole
        else:
            joint_rows[g * share : (g + 1) * share] = whole.T
    if share % 128:
        for i in range(D // 128):
            joint_t_out[:, i * 128 : (i + 1) * 128] = joint_rows[i * 128 : (i + 1) * 128].T

    process(plane)
    hand_on(2)
    process_arrived(1)
    hand_on(3)
    process_arrived(2)
    process_arrived(3)

    for j in range(PLANES):
        for k in range(1, S2):
            side_kv(j, k).wait_recv()
            core_kv(j, k).start()
    for first_move, second_move in zip(w_first, w_second):
        first_move.wait_recv()
        second_move.start()

    for j in range(PLANES):
        own_kv(j).wait()
        for k in range(1, S2):
            side_kv(j, k).wait_send()
        for k in range(S2):
            core_kv(j, k).wait()
    for p in range(PLANES):

        @pl.when((plane < PLANES - 1) & (plane >= p))
        def _(p=p):
            up(p).wait_send()

        @pl.when((plane > 0) & (plane <= p))
        def _(p=p):
            down(p).wait_send()

    for copy in w_own:
        copy.wait()
    for first_move, second_move in zip(w_first, w_second):
        first_move.wait_send()
        second_move.wait()


def front(n, groups, lengths, tokens, joint_shard, gain_first, gain_second, out_w, exp_w, con_w):
    bf, f32 = jnp.bfloat16, jnp.float32
    S2 = n // PLANES // 2
    T, D = tokens.shape
    width = 3 * QW + 64
    share = D // groups
    any_, vm, sm = (pl.BlockSpec(memory_space=m) for m in (pl.ANY, pltpu.VMEM, pltpu.SMEM))
    sems = lambda count: pltpu.SemaphoreType.DMA((2, count))
    halves = lambda w: w.reshape(2, w.shape[0] // 2, w.shape[1])
    weights = [halves(w) for w in (out_w, exp_w)]
    con_w = con_w.reshape(2 if con_w.shape[0] % 32 == 0 else 1, -1, D)
    return pl.pallas_call(
        functools.partial(front_kernel, n, groups, lengths.shape[1]),
        out_shape=(
            jax.ShapeDtypeStruct((PLANES, T, D), bf),
            jax.ShapeDtypeStruct((PLANES, QW, T), bf),
            jax.ShapeDtypeStruct((n, T, 2 * QW), bf),
            jax.ShapeDtypeStruct((width, D), bf),
            jax.ShapeDtypeStruct((PLANES, 2 * HALF, T), f32),
            jax.ShapeDtypeStruct((8, D), f32),
            *[jax.ShapeDtypeStruct((groups, *w.shape), bf) for w in weights],
            jax.ShapeDtypeStruct(con_w.shape[1:], bf),
        ),
        in_specs=[sm, vm, vm, vm, vm, any_, any_, any_],
        out_specs=(vm, vm, any_, vm, vm, vm, any_, any_, any_),
        scratch_shapes=[
            pltpu.VMEM((PLANES, T, D), bf),
            sems(2 * PLANES),
            pltpu.VMEM((2, 3 * QW // 2, share), bf),
            pltpu.VMEM((groups, 2, 3 * QW // 2, share), bf),
            pltpu.VMEM((groups, 8, share), f32),
            sems(3 * (groups - 1)),
            pltpu.VMEM((PLANES, T, 2 * QW), bf),
            sems(PLANES * (2 * S2 - 1)),
            pltpu.SemaphoreType.DMA((PLANES,)),
            sems(2 * len(weights) * (groups - 1)),
            pltpu.SemaphoreType.DMA((2, len(weights) + 1)),
            pltpu.VMEM((D, width), bf),
            *[pltpu.VMEM(w.shape, bf) for w in weights],
            pltpu.VMEM(con_w.shape[1:], bf),
        ],
        compiler_params=pltpu.CompilerParams(collective_id=1, has_side_effects=True, vmem_limit_bytes=60 << 20),
    )(
        lengths,
        tokens,
        joint_shard,
        gain_first,
        gain_second,
        *weights,
        con_w,
    )


def middle_kernel(
    n,
    groups,
    low_ref,
    tokens_ref,
    cot_ref,
    gains_ref,
    out_hbm,
    exp_hbm,
    con_hbm,
    joint_hbm,
    *refs,
):
    con_got, refs = refs[: groups - 1], refs[groups - 1 :]
    (
        output_ref,
        grad_hidden_ref,
        gt_ref,
        y_keep,
        y_send,
        x_keep,
        x_send,
        z_keep,
        z_send_1,
        z_send_2,
        z_send_3,
        joint_near,
        out_w,
        exp_w,
        con_w,
        local_sems,
        c_sems,
        joint_shard,
        cols,
        cols_all,
        col_sems,
        joint_rows,
        att,
        a_sems,
        g_send,
        g_sems,
        hidden,
        second,
        branch,
        ga,
        act,
        gexp,
        acc,
        w_own,
        w_other,
        w_got,
        w_sems,
    ) = refs
    bf, f32 = jnp.bfloat16, jnp.float32
    S = n // PLANES
    S2 = S // 2
    T, D = tokens_ref.shape
    FFN = act.shape[1]
    me, group = lax.axis_index("ctx"), lax.axis_index("fsdp")
    plane, side = me // S, lax.rem(me, S)
    s2, core = side // 2, lax.rem(side, 2)

    def plane_peer(k):
        return (lax.rem(plane + k, PLANES) * S + side, group)

    core_peer = (plane * S + s2 * 2 + 1 - core, group)

    def group_peer(k):
        return (me, lax.rem(group + k, groups))


    def remote(source, target, sems, index, device):
        return pltpu.make_async_remote_copy(
            src_ref=source,
            dst_ref=target,
            send_sem=sems.at[0, index],
            recv_sem=sems.at[1, index],
            device_id=device,
            device_id_type=pl.DeviceIdType.MESH,
        )

    ff_share = con_hbm.shape[0]
    split = ff_share % 32 == 0

    def rows_of(g):
        return pl.ds(pl.multiple_of(g * ff_share, 16), ff_share)

    def half_of(g):
        if not split:
            return rows_of(g)
        half = ff_share // 2
        return pl.ds(pl.multiple_of(g * ff_share + core * half, 16), half)

    came = [half_of(lax.rem(group + groups - k, groups)) for k in range(1, groups)]
    con_hands = [remote(con_got[k], con_w.at[came[k]], c_sems, k, core_peer) for k in range(groups - 1)]
    con_local = [
        pltpu.make_async_copy(con_got[k], con_w.at[came[k]], local_sems.at[3 + k]) for k in range(groups - 1)
    ]
    local = [
        pltpu.make_async_copy(source, target, local_sems.at[i])
        for i, (source, target) in enumerate([(con_hbm, con_w.at[rows_of(group)]), (out_hbm, out_w), (exp_hbm, exp_w)])
    ]
    joint_local = pltpu.make_async_copy(joint_hbm, joint_shard, local_sems.at[3 + groups - 1])
    for copy in [joint_local] + local + con_local:
        copy.start()
    barrier = pltpu.get_barrier_semaphore()
    for k in range(1, PLANES):
        pl.semaphore_signal(barrier, inc=1, device_id=plane_peer(k), device_id_type=pl.DeviceIdType.MESH)
    pl.semaphore_signal(barrier, inc=1, device_id=core_peer, device_id_type=pl.DeviceIdType.MESH)
    for k in range(1, groups):
        pl.semaphore_signal(barrier, inc=1, device_id=group_peer(k), device_id_type=pl.DeviceIdType.MESH)
    pl.semaphore_wait(barrier, PLANES + groups - 1)

    home = [remote(low_ref.at[j], att.at[plane], a_sems, j - 1, plane_peer(PLANES - j)) for j in range(1, PLANES)]
    for copy in home + (con_hands if split else []):
        copy.start()
    att[plane] = low_ref[0]

    joint_local.wait()
    pair = 2 * QW
    for part in range(3):
        window = joint_shard[:, pl.ds(pl.multiple_of(part * D + plane // 2 * pair, 128), pair)].T
        chosen = jnp.where(lax.rem(plane, 2) == 1, window[:QW].astype(f32), window[QW:].astype(f32))
        half = 3 * QW // 2
        low, high = part * QW, (part + 1) * QW
        for c in range(2):
            begin, end = max(low, c * half), min(high, (c + 1) * half)
            if begin < end:
                cols[c, begin - c * half : end - c * half] = chosen[begin - low : end - low].astype(bf)
    col_moves = [
        remote(cols.at[core], cols_all.at[group, core], col_sems, k - 1, group_peer(k)) for k in range(1, groups)
    ]
    col_hands = []
    for k in range(1, groups):
        col_came = cols_all.at[lax.rem(group + groups - k, groups), core]
        col_hands.append(remote(col_came, col_came, col_sems, groups - 1 + k - 1, core_peer))
    for copy in col_moves:
        copy.start()
    cols_all[group] = cols[...]

    def nt(a, b):
        return lax.dot_general(a, b, (((1,), (1,)), ((), ())), preferred_element_type=f32)

    chunk = 384
    cot = cot_ref[...]
    local[0].wait()
    for copy in con_local + (con_hands if split else []):
        copy.wait()
    for c in range(0, FFN, chunk):
        ga[:, c : c + chunk] = nt(cot, con_w[c : c + chunk])
    local[1].wait()
    for copy in home:
        copy.wait()
    attended = att[...].reshape(D, T)
    hidden[...] = tokens_ref[...].astype(f32) + jnp.dot(attended.T, out_w[...], preferred_element_type=f32)

    strip = 64

    for copy, hand in zip(col_moves, col_hands):
        copy.wait()
        hand.start()

    def norm(i, carry):
        rows = pl.ds(pl.multiple_of(i * strip, strip), strip)
        values = hidden[rows]
        centred = values - jnp.mean(values, axis=-1, keepdims=True)
        spread = jnp.mean(centred * centred, axis=-1, keepdims=True)
        second[rows] = (centred * lax.rsqrt(spread + norm_eps) * gains_ref[1:2]).astype(bf)
        return carry

    lax.fori_loop(0, T // strip, norm, 0)
    local[2].wait()
    for c in range(0, FFN, chunk):
        cols, gate_cols = slice(c, c + chunk), slice(FFN + c, FFN + c + chunk)
        inner = jnp.dot(second[...], exp_w[:, cols], preferred_element_type=f32)
        gate = jnp.dot(second[...], exp_w[:, gate_cols], preferred_element_type=f32)
        share = 0.5 * (1.0 + lax.erf(inner * (0.5**0.5)))
        bent = inner * share
        act[:, cols] = (bent * gate).astype(bf)
        grad = ga[:, cols]
        slope = share + inner * jnp.exp(-0.5 * inner * inner) * ((2.0 * math.pi) ** -0.5)
        gexp[:, cols] = (grad * gate * slope).astype(bf)
        gexp[:, gate_cols] = (grad * bent).astype(bf)
    output_ref[...] = (hidden[...] + jnp.dot(act[...], con_w[...], preferred_element_type=f32)).astype(bf)
    acc[:T] = nt(gexp[...], exp_w[...])

    def norm_back(i, total):
        rows = pl.ds(pl.multiple_of(i * strip, strip), strip)
        values = hidden[rows]
        centred = values - jnp.mean(values, axis=-1, keepdims=True)
        scale = lax.rsqrt(jnp.mean(centred * centred, axis=-1, keepdims=True) + norm_eps)
        normal = centred * scale
        grad = acc[rows]
        total = total + jnp.sum(grad * normal, axis=0, keepdims=True)
        grad = grad * gains_ref[1:2]
        grad = grad - jnp.mean(grad, axis=-1, keepdims=True) - normal * jnp.mean(grad * normal, axis=-1, keepdims=True)
        back = cot_ref[rows].astype(f32) + grad * scale
        grad_hidden_ref[rows] = back
        branch[rows] = back.astype(bf)
        return total

    total = lax.fori_loop(0, T // strip, norm_back, jnp.zeros((1, D), f32))
    gain_two = jnp.broadcast_to(total, (8, D))
    for p in range(PLANES):
        g_send[p] = nt(out_w[p * QW : (p + 1) * QW], branch[...]).astype(bf)
    away = [
        remote(g_send.at[lax.rem(plane + k, PLANES)], gt_ref.at[k], g_sems, k - 1, plane_peer(k))
        for k in range(1, PLANES)
    ]
    for copy in away:
        copy.start()
    gt_ref[0] = g_send[plane]

    for copy in col_hands:
        copy.wait()
    share = D // groups
    for g in range(groups):
        whole = jnp.concatenate([cols_all[g, 0], cols_all[g, 1]], axis=0)
        if share % 128 == 0:
            joint_near[:, g * share : (g + 1) * share] = whole
        else:
            joint_rows[g * share : (g + 1) * share] = whole.T
    if share % 128:
        for i in range(D // 128):
            joint_near[:, i * 128 : (i + 1) * 128] = joint_rows[i * 128 : (i + 1) * 128].T

    sent = []

    def place(rows, offset, height):
        for target, parity in ((w_other, 1 - core), (w_own, core)):

            def body(m, carry):
                if rows % 8:
                    pair = acc[pl.ds(pl.multiple_of(2 * m * rows, 8), 2 * rows)]
                    value = jnp.where(parity == 0, pair[:rows], pair[rows:])
                else:
                    value = acc[pl.ds(pl.multiple_of((2 * m + parity) * rows, 8), rows)]
                if height > rows:
                    rest = jnp.zeros((height - rows - 8, D), f32)
                    value = jnp.concatenate([value, gain_two, rest], axis=0)
                value = value.astype(bf)
                target[m, offset : offset + height] = value
                return carry

            lax.fori_loop(0, n // 2, body, 0)
        part = pl.ds(offset, height)
        sent.append(remote(w_other.at[:, part], w_got.at[:, part], w_sems, len(sent), core_peer))
        sent[-1].start()

    rows = D // n
    wide = 2 * FFN // D
    for c in range(0, FFN, chunk):
        acc[c : c + chunk] = jnp.dot(act[:, c : c + chunk].T, cot_ref[...], preferred_element_type=f32)
    used = (1 + wide) * rows
    place(FFN // n, used, w_own.shape[1] - used)
    second_t = second[...].T
    for i in range(wide):
        acc[:D] = jnp.dot(second_t, gexp[:, i * D : (i + 1) * D], preferred_element_type=f32)
        place(rows, (1 + i) * rows, rows)
    acc[:D] = jnp.dot(attended, branch[...], preferred_element_type=f32)
    place(rows, 0, rows)

    for copy in sent:
        copy.wait()
    height = y_keep.shape[2]
    third = lambda g, i: pl.ds(pl.multiple_of((3 * g + i) * height, 16), height)

    def summed(m, part):
        return (w_own[m, part].astype(f32) + w_got[m, part].astype(f32)).astype(bf)

    def each(count, body):
        def step(i, carry):
            body(i)
            return carry

        lax.fori_loop(0, count, step, 0)

    for k in range(groups):
        g = lax.rem(group + k, groups)

        def first(m, k=k, g=g):
            (y_send.at[k - 1] if k else y_keep)[m // S2, lax.rem(m, S2)] = summed(m, third(g, 0))

        each(PLANES * S2, first)
    for k in range(S2):
        a = lax.rem(s2 + k, S2)

        def second_part(i, k=k, a=a):
            p, g = i // groups, lax.rem(i, groups)
            (x_send.at[k - 1] if k else x_keep)[p, g] = summed(p * S2 + a, third(g, 1))

        each(PLANES * groups, second_part)
    z_parts = [z_keep, z_send_1, z_send_2, z_send_3]
    for k in range(PLANES):
        p = lax.rem(plane + k, PLANES)

        def third_part(i, k=k, p=p):
            a, g = i // groups, lax.rem(i, groups)
            z_parts[k][a, g] = summed(p * S2 + a, third(g, 2))

        each(S2 * groups, third_part)
    for copy in away:
        copy.wait()


def middle(n, groups, lowt, tokens, cotangent, gains, out_w, exp_w, con_w, joint_shard, con_got):
    bf, f32 = jnp.bfloat16, jnp.float32
    S2 = n // PLANES // 2
    T, D = tokens.shape
    ffn = con_w.shape[0] * groups
    used = (D + 2 * ffn + ffn) // n + 8
    height = -(-used // (groups * 48)) * 16
    any_, vm = pl.BlockSpec(memory_space=pl.ANY), pl.BlockSpec(memory_space=pltpu.VMEM)
    sems = lambda count: pltpu.SemaphoreType.DMA((2, count))
    shape = lambda *s: jax.ShapeDtypeStruct(s, bf)
    half = (n // 2, 3 * groups * height, D)
    return pl.pallas_call(
        functools.partial(middle_kernel, n, groups),
        out_shape=(
            shape(T, D),
            jax.ShapeDtypeStruct((T, D), f32),
            shape(PLANES, QW, T),
            shape(PLANES, S2, height, D),
            shape(groups - 1, PLANES, S2, height, D),
            shape(PLANES, groups, height, D),
            shape(S2 - 1, PLANES, groups, height, D),
            shape(S2, groups, height, D),
            *[shape(S2, groups, height, D)] * (PLANES - 1),
            shape(3 * QW, D),
        ),
        in_specs=[vm, vm, vm, vm, any_, any_, any_, any_] + [any_] * (groups - 1),
        out_specs=tuple([vm] * 12),
        scratch_shapes=[
            pltpu.VMEM(out_w.shape, bf),
            pltpu.VMEM(exp_w.shape, bf),
            pltpu.VMEM((ffn, D), bf),
            pltpu.SemaphoreType.DMA((4 + groups - 1,)),
            sems(groups - 1),
            pltpu.VMEM(joint_shard.shape, bf),
            pltpu.VMEM((2, 3 * QW // 2, D // groups), bf),
            pltpu.VMEM((groups, 2, 3 * QW // 2, D // groups), bf),
            sems(2 * (groups - 1)),
            pltpu.VMEM((D, 3 * QW), bf),
            pltpu.VMEM((PLANES, QW, T), bf),
            sems(PLANES - 1),
            pltpu.VMEM((PLANES, QW, T), bf),
            sems(PLANES - 1),
            pltpu.VMEM((T, D), f32),
            pltpu.VMEM((T, D), bf),
            pltpu.VMEM((T, D), bf),
            pltpu.VMEM((T, ffn), f32),
            pltpu.VMEM((T, ffn), bf),
            pltpu.VMEM((T, 2 * ffn), bf),
            pltpu.VMEM((ffn, D), f32),
            pltpu.VMEM(half, bf),
            pltpu.VMEM(half, bf),
            pltpu.VMEM(half, bf),
            sems(2 + 2 * ffn // D),
        ],
        compiler_params=pltpu.CompilerParams(collective_id=2, has_side_effects=True, vmem_limit_bytes=60 << 20),
    )(lowt, tokens, cotangent, gains, out_w, exp_w, con_w, joint_shard, *con_got)


def tail_kernel(
    n,
    groups,
    deal_ref,
    dq_hbm,
    dkv_hbm,
    turn_ref,
    gains_ref,
    joint_hbm,
    joint_t_hbm,
    joint_near_hbm,
    first_hbm,
    tokens_hbm,
    grad_hidden_hbm,
    y_keep_hbm,
    y_got_hbm,
    x_keep_hbm,
    x_got_hbm,
    z_keep_hbm,
    z_got_1,
    z_got_2,
    z_got_3,
    d_got,
    w_all,
    jq_all,
    jk_all,
    joint_rows,
    joint_t,
    joint_near,
    first,
    tokens,
    grad_hidden,
    y_keep,
    y_got,
    x_keep,
    x_got,
    z_keep,
    z_came,
    local_sems,
    dq_ref,
    kv_own,
    own_sems,
    kv_near,
    kv_send,
    kv_far,
    kv_sems,
    mixed,
    mixed_got,
    mixed_send_sems,
    mixed_recv_sems,
    part,
    part_got,
    part_send_sems,
    part_recv_sems,
    j_acc,
    jq,
    jq_core,
    jq_side,
    jq_plane,
    jk,
    jk_core,
    jk_side,
    jk_plane,
    j_sems,
    x1_got,
    y2_got,
    y3_got,
    z1_got,
    x3_got,
    w_plane,
    w_plane_got,
    w_sems,
    d_send,
    d_mid,
    d_back,
    d_sems,
    row_sems,
    row_local,
):
    bf, f32 = jnp.bfloat16, jnp.float32
    S = n // PLANES
    S2 = S // 2
    T, D = tokens.shape
    me, group = lax.axis_index("ctx"), lax.axis_index("fsdp")
    plane, side = me // S, lax.rem(me, S)
    s2, core = side // 2, lax.rem(side, 2)
    MESH = pl.DeviceIdType.MESH

    def at(p, a, c, g):
        return (p * S + a * 2 + c, g)

    def plane_peer(k):
        return at(lax.rem(plane + k, PLANES), s2, core, group)

    def side_peer(k):
        return at(plane, lax.rem(s2 + k, S2), core, group)

    def group_peer(k):
        return at(plane, s2, core, lax.rem(group + k, groups))

    core_peer = at(plane, s2, 1 - core, group)

    def send(source, target, send_sem, recv_sem, device):
        return pltpu.make_async_remote_copy(
            src_ref=source, dst_ref=target, send_sem=send_sem, recv_sem=recv_sem, device_id=device, device_id_type=MESH
        )

    def remote(source, target, sems, index, device):
        return send(source, target, sems.at[0, index], sems.at[1, index], device)

    def total_of(terms):
        total = terms[0].astype(f32)
        for term in terms[1:]:
            total = total + term.astype(f32)
        return total

    lower = plane < 2
    middle = (plane == 1) | (plane == 2)
    order = [
        jnp.where(lower, 3, 0),
        jnp.where(plane == 0, 2, jnp.where(plane == 1, 0, jnp.where(plane == 2, 3, 1))),
        jnp.where((plane == 0) | (plane == 2), 1, 2),
        plane,
    ]
    steps = range(PLANES)
    back = [lax.rem(plane + PLANES - p, PLANES) for p in order]
    main = jnp.where(lower, 0, 1)
    main_plane = plane + 1 - 2 * main

    own_kv = [
        pltpu.make_async_copy(dkv_hbm.at[order[t], :, core], kv_own.at[t], own_sems.at[t]) for t in steps
    ] + [pltpu.make_async_copy(dq_hbm, dq_ref, own_sems.at[PLANES])]
    for copy in own_kv:
        copy.start()
    local = [
        pltpu.make_async_copy(source, target, local_sems.at[i])
        for i, (source, target) in enumerate(
            [
                (first_hbm, first),
                (joint_t_hbm, joint_t),
                (y_keep_hbm, y_keep),
                (y_got_hbm, y_got),
                (x_keep_hbm, x_keep),
                (x_got_hbm, x_got),
                (z_keep_hbm, z_keep),
                (z_got_1, z_came.at[0]),
                (z_got_2, z_came.at[1]),
                (z_got_3, z_came.at[2]),
                (tokens_hbm, tokens),
                (grad_hidden_hbm, grad_hidden),
                (joint_near_hbm, joint_near),
            ]
        )
    ]
    for copy in local:
        copy.start()
    barrier = pltpu.get_barrier_semaphore()

    def greet(k, carry):
        pl.semaphore_signal(barrier, inc=1, device_id=(lax.rem(me + k, n), group), device_id_type=MESH)
        return carry

    lax.fori_loop(1, n, greet, 0)
    for k in range(1, groups):
        pl.semaphore_signal(barrier, inc=1, device_id=group_peer(k), device_id_type=MESH)
    pl.semaphore_wait(barrier, n - 1 + groups - 1)

    core_kv = [remote(dkv_hbm.at[order[t], :, 1 - core], kv_near.at[t], kv_sems, t, core_peer) for t in steps]
    for copy in core_kv:
        copy.start()

    per_group = joint_hbm.shape[0]
    index = me - group * per_group
    held_here = (index >= 0) & (index < per_group)
    row_own = pltpu.make_async_copy(joint_hbm.at[jnp.clip(index, 0, per_group - 1)], joint_rows, row_local.at[0])
    row_moves = [
        send(
            joint_hbm.at[jnp.clip(index, 0, per_group - 1)],
            joint_rows,
            row_sems.at[k - 1],
            row_sems.at[groups - 1],
            group_peer(k),
        )
        for k in range(1, groups)
    ]

    @pl.when(held_here)
    def _():
        row_own.start()
        for copy in row_moves:
            copy.start()

    w_moves = []

    def w_copy(source, target, device):
        copy = remote(source, target, w_sems, len(w_moves), device)
        w_moves.append(copy)
        copy.start()
        return copy

    local[2].wait()
    local[3].wait()
    for p in range(PLANES):
        for a in range(S2):
            y_keep[p, a] = total_of([y_keep[p, a]] + [y_got[k, p, a] for k in range(groups - 1)]).astype(bf)
    z1 = [w_copy(y_keep.at[lax.rem(plane + k, PLANES)], z1_got.at[k - 1], plane_peer(k)) for k in range(1, PLANES)]

    def turned_back(x, t):
        cos, sin = turn_ref[back[t], :HALF], turn_ref[back[t], HALF:]
        rows = []
        for h in range(HP):
            upper, lower = x[h * HD : h * HD + HALF], x[h * HD + HALF : (h + 1) * HD]
            rows += [upper * cos + lower * sin, lower * cos - upper * sin]
        return jnp.concatenate(rows, axis=0)

    side_kv = {}
    for t in steps:
        own_kv[t].wait()
        core_kv[t].wait()
        for a in range(S2):
            kv_send[t, a] = total_of([kv_own[t, a], kv_near[t, a]]).astype(bf)
        for k in range(1, S2):
            side_kv[t, k] = remote(
                kv_send.at[t, lax.rem(s2 + S2 - k, S2)],
                kv_far.at[t, k - 1],
                kv_sems,
                PLANES + t * (S2 - 1) + k - 1,
                side_peer(S2 - k),
            )
            side_kv[t, k].start()
    own_kv[PLANES].wait()
    for t in steps:
        mixed[t, :QW] = turned_back(dq_ref[back[t]], t).astype(bf)

    local[4].wait()
    local[5].wait()
    for p in range(PLANES):
        for g in range(groups):
            x_keep[p, g] = total_of([x_keep[p, g]] + [x_got[k, p, g] for k in range(S2 - 1)]).astype(bf)
    y2 = [w_copy(x_keep.at[:, lax.rem(group + k, groups)], y2_got.at[k - 1], group_peer(k)) for k in range(1, groups)]
    for i in range(6, 10):
        local[i].wait()
    for a in range(S2):
        for g in range(groups):
            z_keep[a, g] = total_of([z_keep[a, g]] + [z_came[k, a, g] for k in range(PLANES - 1)]).astype(bf)
    y3 = [w_copy(z_keep.at[:, lax.rem(group + k, groups)], y3_got.at[k - 1], group_peer(k)) for k in range(1, groups)]

    j_moves = []

    def j_copy(source, target, device):
        copy = remote(source, target, j_sems, len(j_moves), device)
        j_moves.append(copy)
        copy.start()
        return copy

    def j_core_stage(begin, height, grads, near):
        j_acc[:height] = total_of(
            [
                jnp.dot(mixed[t, begin : begin + height], first[back[t]], preferred_element_type=f32)
                for t in steps
            ]
        )
        shard_rows = D // n
        for i in range(D // 128):
            block = j_acc[:height, i * 128 : (i + 1) * 128].T
            row = i * 128
            while row < (i + 1) * 128:
                shard, offset = divmod(row, shard_rows)
                count = min(shard_rows - offset, (i + 1) * 128 - row)
                source = row - i * 128
                grads[shard // S, shard % S // 2, shard % 2, offset : offset + count] = block[
                    source : source + count
                ].astype(bf)
                row += count
        return [j_copy(grads.at[:, :, 1 - core], near, core_peer)]

    def j_side_stage(moves, grads, near, far):
        for copy in moves:
            copy.wait()
        for p in range(PLANES):
            for a in range(S2):
                near[p, a] = total_of([grads[p, a, core], near[p, a]]).astype(bf)
        return [j_copy(near.at[:, lax.rem(s2 + k, S2)], far.at[k - 1], side_peer(k)) for k in range(1, S2)]

    def j_plane_stage(moves, near, far, gathered):
        for copy in moves:
            copy.wait()
        for p in range(PLANES):
            far[0, p] = total_of([near[p, s2]] + [far[k, p] for k in range(S2 - 1)]).astype(bf)
        gathered[plane] = far[0, plane]
        return [
            j_copy(far.at[0, lax.rem(plane + k, PLANES)], gathered.at[plane], plane_peer(k)) for k in range(1, PLANES)
        ]

    def j_group_stage(moves, gathered, every):
        for copy in moves:
            copy.wait()
        every[group] = gathered[...]
        return [j_copy(gathered, every.at[group], group_peer(k)) for k in range(1, groups)]

    local[0].wait()
    jq_moves = j_core_stage(0, QW, jq, jq_core)

    local[1].wait()

    half = T // 2
    halves = range(2)

    def mixed_send(t, e):
        lanes = pl.ds(e * half, half)
        return send(
            mixed.at[t, :, lanes],
            mixed_got.at[t, :, lanes],
            mixed_send_sems.at[t, e],
            mixed_recv_sems.at[t, e],
            at(main_plane, s2, core, group),
        )

    def part_send(t, e, direction, target):
        rows = pl.ds(e * half, half)
        return send(
            part.at[t, rows],
            part_got.at[direction, order[t], rows],
            part_send_sems.at[t, e],
            part_recv_sems.at[direction * PLANES + order[t], e],
            at(target, s2, core, group),
        )

    def part_came(direction, p, e):
        rows = pl.ds(e * half, half)
        return send(
            part.at[0, rows],
            part_got.at[direction, p, rows],
            part_send_sems.at[0, e],
            part_recv_sems.at[direction * PLANES + p, e],
            core_peer,
        )

    other_plane = 2 * plane - main_plane

    def product(grads, columns):
        return jnp.dot(grads.T, columns, preferred_element_type=f32)

    def add_mixed(t, slot, e):
        mixed_send(slot, e).wait_recv()
        rows = slice(e * half, (e + 1) * half)
        near = product(mixed_got[slot, :, rows], joint_near[...])
        part[t, rows] = (part[t, rows].astype(f32) + near).astype(bf)

    def add_part(t, direction, p, e):
        part_came(direction, p, e).wait_recv()
        rows = slice(e * half, (e + 1) * half)
        part[t, rows] = total_of([part[t, rows], part_got[direction, p, rows]]).astype(bf)

    def relay(t, slot):
        @pl.when(middle)
        def _():
            for e in halves:
                if slot is None:
                    add_part(t, 1 - main, order[t], e)
                    part_send(t, e, 1 - main, other_plane).start()
                else:
                    add_mixed(t, slot, e)
                    part_send(t, e, main, main_plane).start()

    def key_step(t):
        for k in range(1, S2):
            side_kv[t, k].wait()
        dk = total_of([kv_send[t, s2]] + [kv_far[t, k] for k in range(S2 - 1)]).T
        mixed[t, QW : 2 * QW] = turned_back(dk[:QW], t).astype(bf)
        mixed[t, 2 * QW :] = dk[QW:].astype(bf)
        if t < PLANES - 1:

            @pl.when(jnp.logical_not(middle))
            def _():
                for e in halves:
                    mixed_send(t, e).start()

            @pl.when(middle)
            def _():
                part[t] = product(mixed[t], joint_t[: 3 * QW]).astype(bf)

        else:
            part[t] = product(mixed[t], joint_t[: 3 * QW]).astype(bf)

    local[12].wait()
    key_step(0)
    jq_moves = j_side_stage(jq_moves, jq, jq_core, jq_side)
    key_step(1)
    key_step(2)
    relay(0, 0)
    jq_moves = j_plane_stage(jq_moves, jq_core, jq_side, jq_plane)
    key_step(3)
    relay(2, 1)
    jk_moves = j_core_stage(QW, 2 * QW, jk, jk_core)

    for copy in y3:
        copy.wait()
    for a in range(S2):
        z_keep[a, group] = total_of([z_keep[a, group]] + [y3_got[k, a] for k in range(groups - 1)]).astype(bf)
    x3 = [w_copy(z_keep.at[lax.rem(s2 + k, S2), group], x3_got.at[k - 1], side_peer(k)) for k in range(1, S2)]
    for copy in y2:
        copy.wait()
    for p in range(PLANES):
        w_plane[p] = total_of([x_keep[p, group]] + [y2_got[k, p] for k in range(groups - 1)]).astype(bf)
    w_last = [
        w_copy(w_plane.at[lax.rem(plane + k, PLANES)], w_plane_got.at[k - 1], plane_peer(k)) for k in range(1, PLANES)
    ]
    for copy in z1:
        copy.wait()
    for a in range(S2):
        y_keep[plane, a] = total_of([y_keep[plane, a]] + [z1_got[k, a] for k in range(PLANES - 1)]).astype(bf)
    x1 = [w_copy(y_keep.at[plane, lax.rem(s2 + k, S2)], x1_got.at[k - 1], side_peer(k)) for k in range(1, S2)]
    relay(1, None)
    jk_moves = j_side_stage(jk_moves, jk, jk_core, jk_side)
    jq_moves = j_group_stage(jq_moves, jq_plane, jq_all)

    local[10].wait()
    local[11].wait()
    @pl.when(middle)
    def _():
        for e in halves:
            add_mixed(PLANES - 1, 2, e)

    for e in halves:
        add_part(PLANES - 1, 1 - main, plane, e)

    strip = 64

    def norm_back(i, carry):
        rows = pl.ds(pl.multiple_of(i * strip, strip), strip)
        grad = part[PLANES - 1, rows].astype(f32)
        values = tokens[rows].astype(f32)
        centred = values - jnp.mean(values, axis=-1, keepdims=True)
        scale = lax.rsqrt(jnp.mean(centred * centred, axis=-1, keepdims=True) + norm_eps)
        normal = centred * scale
        grad = grad * gains_ref[0:1]
        grad = grad - jnp.mean(grad, axis=-1, keepdims=True) - normal * jnp.mean(grad * normal, axis=-1, keepdims=True)
        grad_hidden[rows] = grad_hidden[rows] + grad * scale
        return carry

    lax.fori_loop(0, T // strip, norm_back, 0)

    blocks = T // BLOCK
    piece = BLOCK // n

    def d_copy(source, target, base, k):
        return remote(source.at[lax.rem(me + k, n)], target.at[me], d_sems, base + k, (lax.rem(me + k, n), group))

    for i in range(n):
        d_send[i] = jnp.concatenate(
            [grad_hidden[b * BLOCK + i * piece : b * BLOCK + (i + 1) * piece] for b in range(blocks)], axis=0
        ).astype(bf)
    out_deal = [d_copy(d_send, d_mid, 0, k) for k in range(1, n)]
    for copy in out_deal:
        copy.start()
    d_mid[me] = d_send[me]

    jk_moves = j_plane_stage(jk_moves, jk_core, jk_side, jk_plane)

    for copy in out_deal:
        copy.wait()
    for i in range(n):
        chosen = []
        for b in range(blocks):
            wanted = deal_ref[i * blocks + b]
            held = d_mid[wanted // blocks].astype(f32)
            rows = held[:piece]
            for other in range(1, blocks):
                rows = jnp.where(lax.rem(wanted, blocks) == other, held[other * piece : (other + 1) * piece], rows)
            chosen.append(rows)
        d_back[i] = jnp.concatenate(chosen, axis=0).astype(bf)
    back_deal = [d_copy(d_back, d_got, n, k) for k in range(1, n)]
    for copy in back_deal:
        copy.start()
    d_got[me] = d_back[me]

    for copy in x1 + w_last + x3:
        copy.wait()
    height = w_plane.shape[1]
    w_all[group, :height] = total_of([y_keep[plane, s2]] + [x1_got[k] for k in range(S2 - 1)]).astype(bf)
    w_all[group, height : 2 * height] = total_of(
        [w_plane[plane]] + [w_plane_got[k] for k in range(PLANES - 1)]
    ).astype(bf)
    w_all[group, 2 * height :] = total_of([z_keep[s2, group]] + [x3_got[k] for k in range(S2 - 1)]).astype(bf)
    w_gather = [w_copy(w_all.at[group], w_all.at[group], group_peer(k)) for k in range(1, groups)]
    jk_moves = j_group_stage(jk_moves, jk_plane, jk_all)

    for copy in back_deal + w_gather + jq_moves + jk_moves:
        copy.wait()
    for t in range(PLANES - 1):
        for e in halves:

            @pl.when(middle)
            def _(t=t, e=e):
                part_send(t, e, main, main_plane).wait_send()

            @pl.when(jnp.logical_not(middle))
            def _(t=t, e=e):
                mixed_send(t, e).wait_send()

    @pl.when(held_here)
    def _():
        row_own.wait()
        for copy in row_moves:
            copy.wait_send()

    @pl.when(jnp.logical_not(held_here))
    def _():
        row_moves[0].wait_recv()


def tail(n, groups, deal, dqt, dkv, turn, gains, joint_shard, joint_t, joint_near, first, tokens, grad_hidden, pieces):
    bf, f32 = jnp.bfloat16, jnp.float32
    S2 = n // PLANES // 2
    T, D = tokens.shape
    rows = D // n
    height = pieces[0].shape[2]
    piece_rows = T // n
    joint_shard = joint_shard.reshape(-1, rows, joint_shard.shape[1])
    any_, vm, sm = (pl.BlockSpec(memory_space=m) for m in (pl.ANY, pltpu.VMEM, pltpu.SMEM))
    sems = lambda count: pltpu.SemaphoreType.DMA((2, count))
    small = lambda *s: pltpu.VMEM(s, bf)
    j_buffers = lambda w: [
        small(PLANES, S2, 2, rows, w),
        small(PLANES, S2, rows, w),
        small(S2 - 1, PLANES, rows, w),
        small(PLANES, rows, w),
    ]
    return pl.pallas_call(
        functools.partial(tail_kernel, n, groups),
        out_shape=(
            jax.ShapeDtypeStruct((n, piece_rows, D), bf),
            jax.ShapeDtypeStruct((groups, 3 * height, D), bf),
            jax.ShapeDtypeStruct((groups, PLANES, rows, QW), bf),
            jax.ShapeDtypeStruct((groups, PLANES, rows, 2 * QW), bf),
            jax.ShapeDtypeStruct(joint_shard.shape[1:], bf),
        ),
        in_specs=[sm, any_, any_, vm, vm] + [any_] * 14,
        out_specs=tuple([vm] * 4) + (any_,),
        scratch_shapes=[
            pltpu.VMEM(joint_t.shape, bf),
            pltpu.VMEM(joint_near.shape, bf),
            pltpu.VMEM((PLANES, T, D), bf),
            pltpu.VMEM((T, D), bf),
            pltpu.VMEM((T, D), f32),
            *[pltpu.VMEM(p.shape, bf) for p in pieces[:5]],
            pltpu.VMEM((PLANES - 1, *pieces[5].shape), bf),
            pltpu.SemaphoreType.DMA((13,)),
            pltpu.VMEM(dqt.shape, f32),
            small(PLANES, S2, T, 2 * QW),
            pltpu.SemaphoreType.DMA((PLANES + 1,)),
            small(PLANES, S2, T, 2 * QW),
            small(PLANES, S2, T, 2 * QW),
            small(PLANES, S2 - 1, T, 2 * QW),
            sems(PLANES * S2),
            small(PLANES, 3 * QW, T),
            small(PLANES - 1, 3 * QW, T),
            pltpu.SemaphoreType.DMA((PLANES - 1, 2)),
            pltpu.SemaphoreType.DMA((PLANES - 1, 2)),
            small(PLANES, T, D),
            small(2, PLANES, T, D),
            pltpu.SemaphoreType.DMA((PLANES - 1, 2)),
            pltpu.SemaphoreType.DMA((2 * PLANES, 2)),
            pltpu.VMEM((2 * QW, D), f32),
            *j_buffers(QW),
            *j_buffers(2 * QW),
            sems(2 * (1 + S2 - 1 + PLANES - 1 + groups - 1)),
            small(S2 - 1, height, D),
            small(groups - 1, PLANES, height, D),
            small(groups - 1, S2, height, D),
            small(PLANES - 1, S2, height, D),
            small(S2 - 1, height, D),
            small(PLANES, height, D),
            small(PLANES - 1, height, D),
            sems(3 * (groups - 1) + 2 * (S2 - 1) + 2 * (PLANES - 1)),
            small(n, piece_rows, D),
            small(n, piece_rows, D),
            small(n, piece_rows, D),
            sems(2 * n),
            pltpu.SemaphoreType.DMA((groups,)),
            pltpu.SemaphoreType.DMA((1,)),
        ],
        compiler_params=pltpu.CompilerParams(collective_id=0, has_side_effects=True, vmem_limit_bytes=60 << 20),
    )(deal, dqt, dkv, turn, gains, joint_shard, joint_t, joint_near, first, tokens, grad_hidden, *pieces)


def finish_kernel(
    n,
    d_ref,
    w_ref,
    jq_ref,
    jk_ref,
    rows_ref,
    gains_ref,
    dealt_ref,
    joint_ref,
    output_ref,
    expand_ref,
    contract_ref,
    gain_one_ref,
    gain_two_ref,
):
    f32 = jnp.float32
    T, D = dealt_ref.shape
    blocks = T // BLOCK
    piece = BLOCK // n
    for b in range(blocks):
        for i in range(0, n, 2):
            rows = [d_ref[i + e].astype(f32)[b * piece : (b + 1) * piece] for e in range(2)]
            dealt_ref[b * BLOCK + i * piece : b * BLOCK + (i + 2) * piece] = jnp.concatenate(rows, axis=0).astype(
                dealt_ref.dtype
            )

    def summed(ref, p):
        total = ref[0, p].astype(f32)
        for g in range(1, ref.shape[0]):
            total = total + ref[g, p].astype(f32)
        return total.T

    for i in range(PLANES // 2):
        pair = [summed(jq_ref, 2 * i + e) for e in range(2)]
        joint_ref[:, i * 2 * QW : (i + 1) * 2 * QW] = jnp.concatenate(pair, axis=0).T
        pair = [summed(jk_ref, 2 * i + e) for e in range(2)]
        for part in range(2):
            cols = (part + 1) * D + i * 2 * QW
            rows = [x[part * QW : (part + 1) * QW] for x in pair]
            joint_ref[:, cols : cols + 2 * QW] = jnp.concatenate(rows, axis=0).T
    shift = D - lax.axis_index("ctx") * (D // n)

    def own_lanes(x):
        return pltpu.roll(jnp.broadcast_to(x, (8, D)), shift, 1)[0:1, : D // n]

    product = jnp.sum(joint_ref[...] * rows_ref[...].astype(f32), axis=1, keepdims=True)
    product = jnp.broadcast_to(product, (D // n, 128)).T[0:1]
    gain_one_ref[...] = product / own_lanes(gains_ref[0:1])
    height = w_ref.shape[1]
    rows = D // n
    targets = [(output_ref, 0, rows)]
    targets += [(expand_ref, i * D, rows) for i in range(expand_ref.shape[1] // D)]
    targets += [(contract_ref, 0, contract_ref.shape[0])]
    row = 0
    for target, column, count in targets:
        done = 0
        while done < count:
            g, offset = divmod(row, height)
            part = min(count - done, height - offset)
            target[done : done + part, column : column + D] = w_ref[g, offset : offset + part].astype(f32)
            done += part
            row += part
    g, offset = divmod(row, height)
    gain_two_ref[...] = own_lanes(w_ref[g, offset : offset + 1].astype(f32))


def finish(n, T, wide, contract_rows, d_got, w_all, jq_all, jk_all, joint_rows, gains):
    D = d_got.shape[-1]
    rows = D // n
    f32 = jnp.float32
    vm = pl.BlockSpec(memory_space=pltpu.VMEM)
    return pl.pallas_call(
        functools.partial(finish_kernel, n),
        out_shape=(
            jax.ShapeDtypeStruct((T, D), jnp.bfloat16),
            jax.ShapeDtypeStruct((rows, 3 * D), f32),
            jax.ShapeDtypeStruct((rows, D), f32),
            jax.ShapeDtypeStruct((rows, wide), f32),
            jax.ShapeDtypeStruct((contract_rows, D), f32),
            jax.ShapeDtypeStruct((1, rows), f32),
            jax.ShapeDtypeStruct((1, rows), f32),
        ),
        in_specs=[vm] * 6,
        out_specs=tuple([vm] * 7),
    )(d_got, w_all, jq_all, jk_all, joint_rows, gains)


def on_device(
    n,
    groups,
    tokens,
    cotangent,
    lengths,
    deal,
    joint_projection,
    output_projection,
    expand_weight,
    contract_weight,
    gain_first,
    gain_second,
):
    T, D = tokens.shape[1:]
    S = n // PLANES
    S2 = S // 2

    def over_planes(x, k):
        return lax.ppermute(x, "ctx", [(h * S + s, (h + k) % PLANES * S + s) for h in range(PLANES) for s in range(S)])

    def over_sides(x, k):
        pairs = [
            (h * S + a * 2 + c, h * S + (a + k) % S2 * 2 + c) for h in range(PLANES) for a in range(S2) for c in range(2)
        ]
        return lax.ppermute(x, "ctx", pairs)

    def over_groups(x, k):
        return lax.ppermute(x, "fsdp", [(f, (f + k) % groups) for f in range(groups)])

    def moved(x, over):
        if x.shape[0] == 1:
            return over(x, 1)
        return jnp.stack([over(x[k], k + 1) for k in range(x.shape[0])])

    first, qt, kv, joint_t, turn, gains, out_w, exp_w, con_half = front(
        n,
        groups,
        lengths,
        tokens[0],
        joint_projection,
        gain_first,
        gain_second,
        output_projection,
        expand_weight,
        contract_weight,
    )
    con_got = [over_groups(con_half, k) for k in range(1, groups)]
    out_w, exp_w = (w.reshape(-1, w.shape[-1]) for w in (out_w, exp_w))
    ot, lowt, lse = attn_fwd(n, lengths, qt, kv)
    output, grad_hidden, gt, y_keep, y_send, x_keep, x_send, z_keep, *z_send, joint_near = middle(
        n, groups, lowt, tokens[0], cotangent[0], gains, out_w, exp_w, contract_weight, joint_projection, con_got
    )
    y_got, x_got = moved(y_send, over_groups), moved(x_send, over_sides)
    z_got = [over_planes(part, k + 1) for k, part in enumerate(z_send)]
    dqt, dkv = attn_bwd(n, lengths, qt, kv, ot, lse, gt)
    d_got, w_all, jq_all, jk_all, joint_rows = tail(
        n,
        groups,
        deal[0],
        dqt,
        dkv.reshape(PLANES, S2, 2, T, 2 * QW),
        turn,
        gains,
        joint_projection,
        joint_t,
        joint_near,
        first,
        tokens[0],
        grad_hidden,
        [y_keep, y_got, x_keep, x_got, z_keep, *z_got],
    )
    dealt, shard_joint, shard_output, shard_expand, shard_contract, gain_one, gain_two = finish(
        n, T, exp_w.shape[1], contract_weight.shape[0] * groups // n, d_got, w_all, jq_all, jk_all, joint_rows, gains
    )
    return (
        output[None],
        dealt[None],
        shard_joint,
        shard_output,
        shard_expand,
        shard_contract,
        gain_one[0],
        gain_two[0],
    )


def solution(mesh):
    return jax.shard_map(
        functools.partial(on_device, mesh.shape["ctx"], mesh.shape["fsdp"]),
        mesh=mesh,
        in_specs=(
            P("fsdp", "ctx", None),
            P("fsdp", "ctx", None),
            P("fsdp", None),
            P("fsdp", None),
            P("fsdp", None),
            P("fsdp", None),
            P("fsdp", None),
            P("fsdp", None),
            P("fsdp"),
            P("fsdp"),
        ),
        out_specs=(
            P("fsdp", "ctx", None),
            P("fsdp", "ctx", None),
            P("ctx", None),
            P("ctx", None),
            P("ctx", None),
            P("ctx", None),
            P("ctx"),
            P("ctx"),
        ),
        check_vma=False,
    )
```

```python
import functools
import math

import jax
import jax.numpy as jnp
import numpy as np
from jax import lax
from jax.experimental import pallas as pl
from jax.experimental.pallas import tpu as pltpu
from jax.sharding import PartitionSpec as P

FF = 1152
HEADS = 12
HEAD_DIM = 64
BLOCK = 128
PLANES = 4
HD = HEAD_DIM
HALF = HEAD_DIM // 2
HP = HEADS // PLANES
QW = HP * HEAD_DIM
rope_base = 160000.0
norm_eps = 1e-05
MASKED = -1e30


def ends_of(lengths_ref, count):
    ends, total = [], 0
    for i in range(count):
        total = total + lengths_ref[0, i]
        ends.append(total)
    return ends


def span_of(index, ends):
    begin, end = jnp.zeros_like(index), jnp.full_like(index, ends[0])
    for before, after in zip(ends[:-1], ends[1:]):
        begin = jnp.where(index >= before, before, begin)
        end = jnp.where(index >= before, after, end)
    return begin, end


def head_rows(x, head):
    rows = lax.broadcasted_iota(jnp.int32, x.shape, 0)
    return jnp.where((rows >= head * HD) & (rows < (head + 1) * HD), x, jnp.zeros_like(x))


def query_block(n, b, T, ends):
    S = n // PLANES
    me = lax.axis_index("ctx")
    base = (lax.rem(me // S + PLANES - b, PLANES) * S + lax.rem(me, S)) * T
    low_begin, low_end = span_of(base, ends)
    high_begin, high_end = span_of(base + T - 1, ends)
    low, high = low_begin // T, (high_end + T - 1) // T
    full_low = jnp.clip((high_begin + T - 1) // T, low, high)
    full_high = jnp.clip(low_end // T, full_low, high)
    begin, end = span_of(base + lax.broadcasted_iota(jnp.int32, (8, T), 1), ends)
    return (low, full_low, full_high, high), begin[0:1], end[0:1]


def over_units(bounds, step, sizes):
    low, full_low, full_high, high = bounds

    def run(begin, end, masked):
        def body(u, carry):
            step(u, masked)
            return carry

        lax.fori_loop(begin, end, body, 0)

    run(low, full_low, True)
    in_groups(full_low, full_high, lambda u: step(u, False), sizes)
    run(full_high, high, True)


def in_groups(begin, end, step, sizes):
    for size in sizes:
        count = (end - begin) // size

        def some(i, carry, size=size, begin=begin):
            for e in range(size):
                step(begin + size * i + e)
            return carry

        lax.fori_loop(0, count, some, 0)
        begin = begin + size * count


def fwd_kernel(n, count, lengths_ref, qt_ref, kv_ref, ot_ref, lowt_ref, lse_ref, values, scores, top, total, acc):
    units, T, _ = kv_ref.shape
    ends = ends_of(lengths_ref, count)

    def flip(u, carry):
        values[u] = kv_ref[u, :, 128:].T
        return carry

    lax.fori_loop(0, units, flip, 0, unroll=4)

    def one_query_block(b, carry):
        qt = qt_ref[b]
        qheads = [head_rows(qt, h) for h in range(HP)]
        bounds, q_start, q_end = query_block(n, b, T, ends)
        top[...] = jnp.full_like(top, MASKED)
        total[...] = jnp.zeros_like(total)
        acc[...] = jnp.zeros_like(acc)

        def score(u, masked):
            k = kv_ref[u, :, :QW]
            st = [jnp.dot(k, qheads[h], preferred_element_type=jnp.float32) for h in range(HP)]
            if masked:
                at = u * T + lax.broadcasted_iota(jnp.int32, (T, T), 0)
                allowed = (at >= q_start) & (at < q_end)
                st = [jnp.where(allowed, s, MASKED) for s in st]
            for h in range(HP):
                scores[u, h] = st[h]
                top[h] = jnp.maximum(top[h], jnp.max(st[h].reshape(T // 8, 8, T), axis=0))

        over_units(bounds, score, (2, 1))
        m = [jnp.max(top[h], axis=0, keepdims=True) for h in range(HP)]

        def gather(u):
            p = [jnp.exp(scores[u, h] - m[h]) for h in range(HP)]
            for h in range(HP):
                total[h] += jnp.sum(p[h].reshape(T // 8, 8, T), axis=0)
                rows = pl.ds(h * HD, HD)
                acc[rows, :] += jnp.dot(
                    values[u, pl.ds(HD + h * HD, HD), :], p[h].astype(jnp.bfloat16), preferred_element_type=jnp.float32
                )

        in_groups(bounds[0], bounds[3], gather, (4, 2, 1))
        for h in range(HP):
            rows = pl.ds(h * HD, HD)
            l = jnp.sum(total[h], axis=0, keepdims=True)
            o = acc[rows, :] / l
            ot_ref[b, rows, :] = o
            lowt_ref[b, rows, :] = o.astype(jnp.bfloat16)
            lse_ref[b, h : h + 1, :] = m[h] + jnp.log(l)
        return carry

    lax.fori_loop(0, qt_ref.shape[0], one_query_block, 0)


def attn_fwd(n, lengths, qt, kv):
    B, _, T = qt.shape
    U = kv.shape[0]
    sm, vm = pl.BlockSpec(memory_space=pltpu.SMEM), pl.BlockSpec(memory_space=pltpu.VMEM)
    return pl.pallas_call(
        functools.partial(fwd_kernel, n, lengths.shape[1]),
        out_shape=(
            jax.ShapeDtypeStruct((B, QW, T), jnp.float32),
            jax.ShapeDtypeStruct((B, QW, T), jnp.bfloat16),
            jax.ShapeDtypeStruct((B, 8, T), jnp.float32),
        ),
        in_specs=[sm, vm, vm],
        out_specs=(vm, vm, vm),
        scratch_shapes=[
            pltpu.VMEM((U, 256, T), jnp.bfloat16),
            pltpu.VMEM((U, HP, T, T), jnp.float32),
            pltpu.VMEM((HP, 8, T), jnp.float32),
            pltpu.VMEM((HP, 8, T), jnp.float32),
            pltpu.VMEM((QW, T), jnp.float32),
        ],
        compiler_params=pltpu.CompilerParams(vmem_limit_bytes=60 << 20),
    )(lengths, qt, kv)


def bwd_kernel(n, count, lengths_ref, qt_ref, kv_ref, ot_ref, lse_ref, gt_ref, dqt_ref, dkv_ref, keys, dk, dv, dq):
    units, T, _ = kv_ref.shape
    ends = ends_of(lengths_ref, count)

    def flip(u, carry):
        keys[u] = kv_ref[u, :, :256].T
        dk[u] = jnp.zeros_like(dk[u])
        dv[u] = jnp.zeros_like(dv[u])
        return carry

    lax.fori_loop(0, units, flip, 0, unroll=4)

    def one_query_block(b, carry):
        qt, gt = qt_ref[b], gt_ref[b]
        zero = jnp.zeros((HD, T), jnp.bfloat16)
        qheads = [head_rows(qt, h) for h in range(HP)]
        gheads = [head_rows(gt, h) for h in range(HP)]
        gpad = [jnp.concatenate([zero, x], axis=0) for x in gheads]
        lanes = lax.broadcasted_iota(jnp.int32, (T, 256), 1) // HD
        q, g = jnp.concatenate([qt, zero], axis=0).T, jnp.concatenate([zero, gt], axis=0).T
        q = jnp.concatenate([jnp.where(lanes == h, q, jnp.zeros_like(q)) for h in range(HP)], axis=0)
        g = jnp.concatenate([jnp.where(lanes == h + 1, g, jnp.zeros_like(g)) for h in range(HP)], axis=0)
        bounds, q_start, q_end = query_block(n, b, T, ends)
        prod = gt.astype(jnp.float32) * ot_ref[b]
        delta = [jnp.sum(prod[h * HD : (h + 1) * HD], axis=0, keepdims=True) for h in range(HP)]
        lse = [lse_ref[b, h : h + 1, :] for h in range(HP)]
        dq[...] = jnp.zeros_like(dq)

        def one_unit(u, masked):
            k, v = kv_ref[u, :, :QW], kv_ref[u, :, 128:]
            st = [jnp.dot(k, qheads[h], preferred_element_type=jnp.float32) for h in range(HP)]
            dp = [jnp.dot(v, gpad[h], preferred_element_type=jnp.float32) for h in range(HP)]
            st = [st[h] - lse[h] for h in range(HP)]
            if masked:
                at = u * T + lax.broadcasted_iota(jnp.int32, (T, T), 0)
                allowed = (at >= q_start) & (at < q_end)
                st = [jnp.where(allowed, s, MASKED) for s in st]
            p = [jnp.exp(s) for s in st]
            ds = [(p[h] * (dp[h] - delta[h])).astype(jnp.bfloat16) for h in range(HP)]
            p = [x.astype(jnp.bfloat16) for x in p]
            dv[u] += jnp.dot(jnp.concatenate(p, axis=1), g, preferred_element_type=jnp.float32)
            dk[u] += jnp.dot(jnp.concatenate(ds, axis=1), q, preferred_element_type=jnp.float32)
            for h in range(HP):
                rows = pl.ds(h * HD, HD)
                dq[rows, :] += jnp.dot(keys[u, rows, :], ds[h], preferred_element_type=jnp.float32)

        over_units(bounds, one_unit, (4, 2, 1))
        dqt_ref[b] = dq[...] * (HD**-0.5)
        return carry

    lax.fori_loop(0, qt_ref.shape[0], one_query_block, 0)

    def out(u, carry):
        dkv_ref[u, :, :128] = dk[u, :, :128].astype(jnp.bfloat16)
        dkv_ref[u, :, 128:256] = (dk[u, :, 128:] + dv[u, :, :128]).astype(jnp.bfloat16)
        dkv_ref[u, :, 256:] = dv[u, :, 128:].astype(jnp.bfloat16)
        return carry

    lax.fori_loop(0, units, out, 0, unroll=2)


def attn_bwd(n, lengths, qt, kv, ot, lse, gt):
    B, _, T = qt.shape
    U = kv.shape[0]
    sm, vm = pl.BlockSpec(memory_space=pltpu.SMEM), pl.BlockSpec(memory_space=pltpu.VMEM)
    return pl.pallas_call(
        functools.partial(bwd_kernel, n, lengths.shape[1]),
        out_shape=(jax.ShapeDtypeStruct((B, QW, T), jnp.float32), jax.ShapeDtypeStruct((U, T, 2 * QW), jnp.bfloat16)),
        in_specs=[sm] + [vm] * 5,
        out_specs=(vm, vm),
        scratch_shapes=[
            pltpu.VMEM((U, 256, T), jnp.bfloat16),
            pltpu.VMEM((U, T, 256), jnp.float32),
            pltpu.VMEM((U, T, 256), jnp.float32),
            pltpu.VMEM((QW, T), jnp.float32),
        ],
        compiler_params=pltpu.CompilerParams(vmem_limit_bytes=60 << 20),
    )(lengths, qt, kv, ot, lse, gt)
def front_kernel(
    n,
    groups,
    count,
    lengths_ref,
    tokens_ref,
    joint_ref,
    gain_one_ref,
    gain_two_ref,
    out_hbm,
    exp_hbm,
    con_hbm,
    first_ref,
    qt_ref,
    kv_ref,
    joint_t_out,
    turn_ref,
    gains_ref,
    out_all,
    exp_all,
    con_ref,
    held,
    t_sems,
    cols,
    cols_all,
    gain_held,
    g_sems,
    kv_own,
    kv_sems,
    own_sems,
    w_sems,
    w_local,
    joint_rows,
    out_held,
    exp_held,
    con_held,
):
    bf, f32 = jnp.bfloat16, jnp.float32
    S = n // PLANES
    S2 = S // 2
    T, D = tokens_ref.shape
    me, group = lax.axis_index("ctx"), lax.axis_index("fsdp")
    plane, side = me // S, lax.rem(me, S)
    s2, core = side // 2, lax.rem(side, 2)

    def at(p, a, c, g):
        return (p * S + a * 2 + c, g)

    def side_peer(k):
        return at(plane, lax.rem(s2 + k, S2), core, group)

    def group_peer(k):
        return at(plane, s2, core, lax.rem(group + k, groups))

    core_peer = at(plane, s2, 1 - core, group)

    def remote(source, target, sems, index, device):
        return pltpu.make_async_remote_copy(
            src_ref=source,
            dst_ref=target,
            send_sem=sems.at[0, index],
            recv_sem=sems.at[1, index],
            device_id=device,
            device_id_type=pl.DeviceIdType.MESH,
        )

    barrier = pltpu.get_barrier_semaphore()

    def greet(device):
        pl.semaphore_signal(barrier, inc=1, device_id=device, device_id_type=pl.DeviceIdType.MESH)

    for k in range(1, PLANES):
        greet(at(lax.rem(plane + k, PLANES), s2, core, group))
    for k in range(1, S2):
        greet(side_peer(k))
    for k in range(1, groups):
        greet(group_peer(k))
    greet(core_peer)
    pl.semaphore_wait(barrier, PLANES - 1 + S2 - 1 + groups - 1 + 1)

    def up(p):
        return remote(held.at[p], held.at[p], t_sems, p, at(plane + 1, s2, core, group))

    def down(p):
        return remote(held.at[p], held.at[p], t_sems, PLANES + p, at(plane - 1, s2, core, group))

    held[plane] = tokens_ref[...]

    @pl.when(plane < PLANES - 1)
    def _():
        up(plane).start()

    @pl.when(plane > 0)
    def _():
        down(plane).start()

    pair = 2 * QW
    for part in range(3):
        window = joint_ref[:, pl.ds(pl.multiple_of(part * D + plane // 2 * pair, 128), pair)].T
        chosen = jnp.where(lax.rem(plane, 2) == 0, window[:QW].astype(f32), window[QW:].astype(f32))
        half = 3 * QW // 2
        low, high = part * QW, (part + 1) * QW
        for c in range(2):
            begin, end = max(low, c * half), min(high, (c + 1) * half)
            if begin < end:
                cols[c, begin - c * half : end - c * half] = chosen[begin - low : end - low].astype(bf)
    gain_held[group] = jnp.zeros_like(gain_held[group])
    gain_held[group, 0:1] = gain_one_ref[...].astype(f32).reshape(1, -1)
    gain_held[group, 1:2] = gain_two_ref[...].astype(f32).reshape(1, -1)
    col_moves = [
        remote(cols.at[core], cols_all.at[group, core], g_sems, k - 1, group_peer(k)) for k in range(1, groups)
    ]
    col_hands = []
    for k in range(1, groups):
        came = cols_all.at[lax.rem(group + groups - k, groups), core]
        col_hands.append(remote(came, came, g_sems, 2 * (groups - 1) + k - 1, core_peer))
    gain_moves = [
        remote(gain_held.at[group], gain_held.at[group], g_sems, groups - 1 + k - 1, group_peer(k))
        for k in range(1, groups)
    ]
    for copy in gain_moves + col_moves:
        copy.start()
    cols_all[group] = cols[...]

    weights = [(out_hbm, out_all, out_held), (exp_hbm, exp_all, exp_held)]
    part = core if con_hbm.shape[0] == 2 else 0
    w_in = [pltpu.make_async_copy(con_hbm.at[part], con_held, w_local.at[0, len(weights)])]
    w_own = [pltpu.make_async_copy(con_held, con_ref, w_local.at[1, len(weights)])]
    w_first, w_second = [], []
    for i, (source, target, bounce) in enumerate(weights):
        w_in.append(pltpu.make_async_copy(source, bounce, w_local.at[0, i]))
        w_own.append(pltpu.make_async_copy(bounce, target.at[group], w_local.at[1, i]))
        for k in range(1, groups):
            index = (i * (groups - 1) + k - 1) * 2
            w_first.append(remote(source.at[core], target.at[group, core], w_sems, index, group_peer(k)))
            came = lax.rem(group + groups - k, groups)
            w_second.append(remote(target.at[came, core], target.at[came, core], w_sems, index + 1, core_peer))
    for copy in w_in:
        copy.start()

    ends = ends_of(lengths_ref, count)
    row = lax.broadcasted_iota(jnp.int32, (HALF, T), 0)
    frequencies = jnp.zeros((HALF, T), f32)
    for i in range(HALF):
        frequencies = jnp.where(row == i, float(np.float32(rope_base ** (-2.0 * i / HEAD_DIM))), frequencies)
    for j in range(PLANES):
        base = (lax.rem(plane + PLANES - j, PLANES) * S + side) * T
        index = base + lax.broadcasted_iota(jnp.int32, (8, T), 1)
        begin, _ = span_of(index, ends)
        angles = (index - begin)[0:1].astype(f32) * frequencies
        turn_ref[j, :HALF] = jnp.cos(angles)
        turn_ref[j, HALF:] = jnp.sin(angles)

    strip = 64

    def kv_unit(p, a, c):
        return p * S + a * 2 + c

    def side_kv(j, k):
        p = lax.rem(plane + PLANES - j, PLANES)
        return remote(kv_own.at[j], kv_ref.at[kv_unit(p, s2, core)], kv_sems, j * (2 * S2 - 1) + k - 1, side_peer(k))

    def core_kv(j, k):
        p = lax.rem(plane + PLANES - j, PLANES)
        unit = kv_unit(p, lax.rem(s2 + S2 - k, S2), core)
        source = kv_own.at[j] if k == 0 else kv_ref.at[unit]
        return remote(source, kv_ref.at[unit], kv_sems, j * (2 * S2 - 1) + S2 - 1 + k, core_peer)

    def own_kv(j):
        p = lax.rem(plane + PLANES - j, PLANES)
        return pltpu.make_async_copy(kv_own.at[j], kv_ref.at[kv_unit(p, s2, core)], own_sems.at[j])

    def process(p):
        j = lax.rem(plane + PLANES - p, PLANES)

        def norm(i, carry):
            rows = pl.ds(pl.multiple_of(i * strip, strip), strip)
            values = held[p, rows].astype(f32)
            centred = values - jnp.mean(values, axis=-1, keepdims=True)
            spread = jnp.mean(centred * centred, axis=-1, keepdims=True)
            first_ref[j, rows] = (centred * lax.rsqrt(spread + norm_eps) * gains_ref[0:1]).astype(bf)
            return carry

        lax.fori_loop(0, T // strip, norm, 0)
        mixed = lax.dot_general(
            joint_t_out[: 3 * QW], first_ref[j], (((1,), (1,)), ((), ())), preferred_element_type=f32
        )
        cos, sin = turn_ref[j, :HALF], turn_ref[j, HALF:]
        turned = []
        for h in range(2 * HP):
            upper, lower = mixed[h * HD : h * HD + HALF], mixed[h * HD + HALF : (h + 1) * HD]
            turned += [upper * cos - lower * sin, lower * cos + upper * sin]
        q = jnp.concatenate(turned[: 2 * HP], axis=0).astype(bf)
        qt_ref[j] = (q.astype(f32) * HEAD_DIM**-0.5).astype(bf)
        kv_own[j] = jnp.concatenate(turned[2 * HP :] + [mixed[2 * QW :]], axis=0).T.astype(bf)
        for k in range(1, S2):
            side_kv(j, k).start()
        core_kv(j, 0).start()
        own_kv(j).start()

    def hand_on(t):
        @pl.when(plane >= t)
        def _():
            up(plane - t).wait_recv()

            @pl.when(plane < PLANES - 1)
            def _():
                up(plane - t).start()

        @pl.when(plane + t < PLANES)
        def _():
            down(plane + t).wait_recv()

            @pl.when(plane > 0)
            def _():
                down(plane + t).start()

    def process_arrived(t):
        below = jnp.where(plane >= t, 1, 0)
        above = jnp.where(plane + t < PLANES, 1, 0)

        def arrived(i, carry):
            process(jnp.where(i < below, plane - t, plane + t))
            return carry

        lax.fori_loop(0, below + above, arrived, 0)

    hand_on(1)
    for copy in gain_moves:
        copy.wait()
    share = D // groups
    total = jnp.zeros((8, D), f32)
    for g in range(groups):
        rows = lax.broadcasted_iota(jnp.int32, (share, D), 0)
        lanes = lax.broadcasted_iota(jnp.int32, (share, D), 1)
        place = jnp.where(lanes == rows + g * share, 1.0, 0.0).astype(bf)
        total = total + jnp.dot(gain_held[g].astype(bf), place, preferred_element_type=f32)
    gains_ref[...] = total
    for copy, hand in zip(col_moves, col_hands):
        copy.wait()
        hand.start()
    for copy in w_first:
        copy.start()
    for copy in w_in:
        copy.wait()
    for copy in w_own:
        copy.start()
    for copy in col_hands:
        copy.wait()
    width = joint_t_out.shape[0]
    for g in range(groups):
        whole = jnp.concatenate([cols_all[g, 0], cols_all[g, 1], jnp.zeros((width - 3 * QW, share), bf)], axis=0)
        if share % 128 == 0:
            joint_t_out[:, g * share : (g + 1) * share] = whole
        else:
            joint_rows[g * share : (g + 1) * share] = whole.T
    if share % 128:
        for i in range(D // 128):
            joint_t_out[:, i * 128 : (i + 1) * 128] = joint_rows[i * 128 : (i + 1) * 128].T

    process(plane)
    hand_on(2)
    process_arrived(1)
    hand_on(3)
    process_arrived(2)
    process_arrived(3)

    for j in range(PLANES):
        for k in range(1, S2):
            side_kv(j, k).wait_recv()
            core_kv(j, k).start()
    for first_move, second_move in zip(w_first, w_second):
        first_move.wait_recv()
        second_move.start()

    for j in range(PLANES):
        own_kv(j).wait()
        for k in range(1, S2):
            side_kv(j, k).wait_send()
        for k in range(S2):
            core_kv(j, k).wait()
    for p in range(PLANES):

        @pl.when((plane < PLANES - 1) & (plane >= p))
        def _(p=p):
            up(p).wait_send()

        @pl.when((plane > 0) & (plane <= p))
        def _(p=p):
            down(p).wait_send()

    for copy in w_own:
        copy.wait()
    for first_move, second_move in zip(w_first, w_second):
        first_move.wait_send()
        second_move.wait()


def front(n, groups, lengths, tokens, joint_shard, gain_first, gain_second, out_w, exp_w, con_w):
    bf, f32 = jnp.bfloat16, jnp.float32
    S2 = n // PLANES // 2
    T, D = tokens.shape
    width = 3 * QW + 64
    share = D // groups
    any_, vm, sm = (pl.BlockSpec(memory_space=m) for m in (pl.ANY, pltpu.VMEM, pltpu.SMEM))
    sems = lambda count: pltpu.SemaphoreType.DMA((2, count))
    halves = lambda w: w.reshape(2, w.shape[0] // 2, w.shape[1])
    weights = [halves(w) for w in (out_w, exp_w)]
    con_w = con_w.reshape(2 if con_w.shape[0] % 32 == 0 else 1, -1, D)
    return pl.pallas_call(
        functools.partial(front_kernel, n, groups, lengths.shape[1]),
        out_shape=(
            jax.ShapeDtypeStruct((PLANES, T, D), bf),
            jax.ShapeDtypeStruct((PLANES, QW, T), bf),
            jax.ShapeDtypeStruct((n, T, 2 * QW), bf),
            jax.ShapeDtypeStruct((width, D), bf),
            jax.ShapeDtypeStruct((PLANES, 2 * HALF, T), f32),
            jax.ShapeDtypeStruct((8, D), f32),
            *[jax.ShapeDtypeStruct((groups, *w.shape), bf) for w in weights],
            jax.ShapeDtypeStruct(con_w.shape[1:], bf),
        ),
        in_specs=[sm, vm, vm, vm, vm, any_, any_, any_],
        out_specs=(vm, vm, any_, vm, vm, vm, any_, any_, any_),
        scratch_shapes=[
            pltpu.VMEM((PLANES, T, D), bf),
            sems(2 * PLANES),
            pltpu.VMEM((2, 3 * QW // 2, share), bf),
            pltpu.VMEM((groups, 2, 3 * QW // 2, share), bf),
            pltpu.VMEM((groups, 8, share), f32),
            sems(3 * (groups - 1)),
            pltpu.VMEM((PLANES, T, 2 * QW), bf),
            sems(PLANES * (2 * S2 - 1)),
            pltpu.SemaphoreType.DMA((PLANES,)),
            sems(2 * len(weights) * (groups - 1)),
            pltpu.SemaphoreType.DMA((2, len(weights) + 1)),
            pltpu.VMEM((D, width), bf),
            *[pltpu.VMEM(w.shape, bf) for w in weights],
            pltpu.VMEM(con_w.shape[1:], bf),
        ],
        compiler_params=pltpu.CompilerParams(collective_id=1, has_side_effects=True, vmem_limit_bytes=60 << 20),
    )(
        lengths,
        tokens,
        joint_shard,
        gain_first,
        gain_second,
        *weights,
        con_w,
    )


def middle_kernel(
    n,
    groups,
    low_ref,
    tokens_ref,
    cot_ref,
    gains_ref,
    out_hbm,
    exp_hbm,
    con_hbm,
    joint_hbm,
    *refs,
):
    con_got, refs = refs[: groups - 1], refs[groups - 1 :]
    (
        output_ref,
        grad_hidden_ref,
        gt_ref,
        y_keep,
        y_send,
        x_keep,
        x_send,
        z_keep,
        z_send_1,
        z_send_2,
        z_send_3,
        joint_near,
        out_w,
        exp_w,
        con_w,
        local_sems,
        c_sems,
        joint_shard,
        cols,
        cols_all,
        col_sems,
        joint_rows,
        att,
        a_sems,
        g_send,
        g_sems,
        hidden,
        second,
        branch,
        ga,
        act,
        gexp,
        acc,
        w_own,
        w_other,
        w_got,
        w_sems,
    ) = refs
    bf, f32 = jnp.bfloat16, jnp.float32
    S = n // PLANES
    S2 = S // 2
    T, D = tokens_ref.shape
    FFN = act.shape[1]
    me, group = lax.axis_index("ctx"), lax.axis_index("fsdp")
    plane, side = me // S, lax.rem(me, S)
    s2, core = side // 2, lax.rem(side, 2)

    def plane_peer(k):
        return (lax.rem(plane + k, PLANES) * S + side, group)

    core_peer = (plane * S + s2 * 2 + 1 - core, group)

    def group_peer(k):
        return (me, lax.rem(group + k, groups))


    def remote(source, target, sems, index, device):
        return pltpu.make_async_remote_copy(
            src_ref=source,
            dst_ref=target,
            send_sem=sems.at[0, index],
            recv_sem=sems.at[1, index],
            device_id=device,
            device_id_type=pl.DeviceIdType.MESH,
        )

    ff_share = con_hbm.shape[0]
    split = ff_share % 32 == 0

    def rows_of(g):
        return pl.ds(pl.multiple_of(g * ff_share, 16), ff_share)

    def half_of(g):
        if not split:
            return rows_of(g)
        half = ff_share // 2
        return pl.ds(pl.multiple_of(g * ff_share + core * half, 16), half)

    came = [half_of(lax.rem(group + groups - k, groups)) for k in range(1, groups)]
    con_hands = [remote(con_got[k], con_w.at[came[k]], c_sems, k, core_peer) for k in range(groups - 1)]
    con_local = [
        pltpu.make_async_copy(con_got[k], con_w.at[came[k]], local_sems.at[3 + k]) for k in range(groups - 1)
    ]
    local = [
        pltpu.make_async_copy(source, target, local_sems.at[i])
        for i, (source, target) in enumerate([(con_hbm, con_w.at[rows_of(group)]), (out_hbm, out_w), (exp_hbm, exp_w)])
    ]
    joint_local = pltpu.make_async_copy(joint_hbm, joint_shard, local_sems.at[3 + groups - 1])
    for copy in [joint_local] + local + con_local:
        copy.start()
    barrier = pltpu.get_barrier_semaphore()
    for k in range(1, PLANES):
        pl.semaphore_signal(barrier, inc=1, device_id=plane_peer(k), device_id_type=pl.DeviceIdType.MESH)
    pl.semaphore_signal(barrier, inc=1, device_id=core_peer, device_id_type=pl.DeviceIdType.MESH)
    for k in range(1, groups):
        pl.semaphore_signal(barrier, inc=1, device_id=group_peer(k), device_id_type=pl.DeviceIdType.MESH)
    pl.semaphore_wait(barrier, PLANES + groups - 1)

    home = [remote(low_ref.at[j], att.at[plane], a_sems, j - 1, plane_peer(PLANES - j)) for j in range(1, PLANES)]
    for copy in home + (con_hands if split else []):
        copy.start()
    att[plane] = low_ref[0]

    joint_local.wait()
    pair = 2 * QW
    for part in range(3):
        window = joint_shard[:, pl.ds(pl.multiple_of(part * D + plane // 2 * pair, 128), pair)].T
        chosen = jnp.where(lax.rem(plane, 2) == 1, window[:QW].astype(f32), window[QW:].astype(f32))
        half = 3 * QW // 2
        low, high = part * QW, (part + 1) * QW
        for c in range(2):
            begin, end = max(low, c * half), min(high, (c + 1) * half)
            if begin < end:
                cols[c, begin - c * half : end - c * half] = chosen[begin - low : end - low].astype(bf)
    col_moves = [
        remote(cols.at[core], cols_all.at[group, core], col_sems, k - 1, group_peer(k)) for k in range(1, groups)
    ]
    col_hands = []
    for k in range(1, groups):
        col_came = cols_all.at[lax.rem(group + groups - k, groups), core]
        col_hands.append(remote(col_came, col_came, col_sems, groups - 1 + k - 1, core_peer))
    for copy in col_moves:
        copy.start()
    cols_all[group] = cols[...]

    def nt(a, b):
        return lax.dot_general(a, b, (((1,), (1,)), ((), ())), preferred_element_type=f32)

    chunk = 384
    cot = cot_ref[...]
    local[0].wait()
    for copy in con_local + (con_hands if split else []):
        copy.wait()
    for c in range(0, FFN, chunk):
        ga[:, c : c + chunk] = nt(cot, con_w[c : c + chunk])
    local[1].wait()
    for copy in home:
        copy.wait()
    attended = att[...].reshape(D, T)
    hidden[...] = tokens_ref[...].astype(f32) + jnp.dot(attended.T, out_w[...], preferred_element_type=f32)

    strip = 64

    for copy, hand in zip(col_moves, col_hands):
        copy.wait()
        hand.start()

    def norm(i, carry):
        rows = pl.ds(pl.multiple_of(i * strip, strip), strip)
        values = hidden[rows]
        centred = values - jnp.mean(values, axis=-1, keepdims=True)
        spread = jnp.mean(centred * centred, axis=-1, keepdims=True)
        second[rows] = (centred * lax.rsqrt(spread + norm_eps) * gains_ref[1:2]).astype(bf)
        return carry

    lax.fori_loop(0, T // strip, norm, 0)
    local[2].wait()
    for c in range(0, FFN, chunk):
        cols, gate_cols = slice(c, c + chunk), slice(FFN + c, FFN + c + chunk)
        inner = jnp.dot(second[...], exp_w[:, cols], preferred_element_type=f32)
        gate = jnp.dot(second[...], exp_w[:, gate_cols], preferred_element_type=f32)
        share = 0.5 * (1.0 + lax.erf(inner * (0.5**0.5)))
        bent = inner * share
        act[:, cols] = (bent * gate).astype(bf)
        grad = ga[:, cols]
        slope = share + inner * jnp.exp(-0.5 * inner * inner) * ((2.0 * math.pi) ** -0.5)
        gexp[:, cols] = (grad * gate * slope).astype(bf)
        gexp[:, gate_cols] = (grad * bent).astype(bf)
    output_ref[...] = (hidden[...] + jnp.dot(act[...], con_w[...], preferred_element_type=f32)).astype(bf)
    acc[:T] = nt(gexp[...], exp_w[...])

    def norm_back(i, total):
        rows = pl.ds(pl.multiple_of(i * strip, strip), strip)
        values = hidden[rows]
        centred = values - jnp.mean(values, axis=-1, keepdims=True)
        scale = lax.rsqrt(jnp.mean(centred * centred, axis=-1, keepdims=True) + norm_eps)
        normal = centred * scale
        grad = acc[rows]
        total = total + jnp.sum(grad * normal, axis=0, keepdims=True)
        grad = grad * gains_ref[1:2]
        grad = grad - jnp.mean(grad, axis=-1, keepdims=True) - normal * jnp.mean(grad * normal, axis=-1, keepdims=True)
        back = cot_ref[rows].astype(f32) + grad * scale
        grad_hidden_ref[rows] = back
        branch[rows] = back.astype(bf)
        return total

    total = lax.fori_loop(0, T // strip, norm_back, jnp.zeros((1, D), f32))
    gain_two = jnp.broadcast_to(total, (8, D))
    for p in range(PLANES):
        g_send[p] = nt(out_w[p * QW : (p + 1) * QW], branch[...]).astype(bf)
    away = [
        remote(g_send.at[lax.rem(plane + k, PLANES)], gt_ref.at[k], g_sems, k - 1, plane_peer(k))
        for k in range(1, PLANES)
    ]
    for copy in away:
        copy.start()
    gt_ref[0] = g_send[plane]

    for copy in col_hands:
        copy.wait()
    share = D // groups
    for g in range(groups):
        whole = jnp.concatenate([cols_all[g, 0], cols_all[g, 1]], axis=0)
        if share % 128 == 0:
            joint_near[:, g * share : (g + 1) * share] = whole
        else:
            joint_rows[g * share : (g + 1) * share] = whole.T
    if share % 128:
        for i in range(D // 128):
            joint_near[:, i * 128 : (i + 1) * 128] = joint_rows[i * 128 : (i + 1) * 128].T

    sent = []

    def place(rows, offset, height):
        for target, parity in ((w_other, 1 - core), (w_own, core)):

            def body(m, carry):
                if rows % 8:
                    pair = acc[pl.ds(pl.multiple_of(2 * m * rows, 8), 2 * rows)]
                    value = jnp.where(parity == 0, pair[:rows], pair[rows:])
                else:
                    value = acc[pl.ds(pl.multiple_of((2 * m + parity) * rows, 8), rows)]
                if height > rows:
                    rest = jnp.zeros((height - rows - 8, D), f32)
                    value = jnp.concatenate([value, gain_two, rest], axis=0)
                value = value.astype(bf)
                target[m, offset : offset + height] = value
                return carry

            lax.fori_loop(0, n // 2, body, 0)
        part = pl.ds(offset, height)
        sent.append(remote(w_other.at[:, part], w_got.at[:, part], w_sems, len(sent), core_peer))
        sent[-1].start()

    rows = D // n
    wide = 2 * FFN // D
    for c in range(0, FFN, chunk):
        acc[c : c + chunk] = jnp.dot(act[:, c : c + chunk].T, cot_ref[...], preferred_element_type=f32)
    used = (1 + wide) * rows
    place(FFN // n, used, w_own.shape[1] - used)
    second_t = second[...].T
    for i in range(wide):
        acc[:D] = jnp.dot(second_t, gexp[:, i * D : (i + 1) * D], preferred_element_type=f32)
        place(rows, (1 + i) * rows, rows)
    acc[:D] = jnp.dot(attended, branch[...], preferred_element_type=f32)
    place(rows, 0, rows)

    for copy in sent:
        copy.wait()
    height = y_keep.shape[2]
    third = lambda g, i: pl.ds(pl.multiple_of((3 * g + i) * height, 16), height)

    def summed(m, part):
        return (w_own[m, part].astype(f32) + w_got[m, part].astype(f32)).astype(bf)

    def each(count, body):
        def step(i, carry):
            body(i)
            return carry

        lax.fori_loop(0, count, step, 0)

    for k in range(groups):
        g = lax.rem(group + k, groups)

        def first(m, k=k, g=g):
            (y_send.at[k - 1] if k else y_keep)[m // S2, lax.rem(m, S2)] = summed(m, third(g, 0))

        each(PLANES * S2, first)
    for k in range(S2):
        a = lax.rem(s2 + k, S2)

        def second_part(i, k=k, a=a):
            p, g = i // groups, lax.rem(i, groups)
            (x_send.at[k - 1] if k else x_keep)[p, g] = summed(p * S2 + a, third(g, 1))

        each(PLANES * groups, second_part)
    z_parts = [z_keep, z_send_1, z_send_2, z_send_3]
    for k in range(PLANES):
        p = lax.rem(plane + k, PLANES)

        def third_part(i, k=k, p=p):
            a, g = i // groups, lax.rem(i, groups)
            z_parts[k][a, g] = summed(p * S2 + a, third(g, 2))

        each(S2 * groups, third_part)
    for copy in away:
        copy.wait()


def middle(n, groups, lowt, tokens, cotangent, gains, out_w, exp_w, con_w, joint_shard, con_got):
    bf, f32 = jnp.bfloat16, jnp.float32
    S2 = n // PLANES // 2
    T, D = tokens.shape
    ffn = con_w.shape[0] * groups
    used = (D + 2 * ffn + ffn) // n + 8
    height = -(-used // (groups * 48)) * 16
    any_, vm = pl.BlockSpec(memory_space=pl.ANY), pl.BlockSpec(memory_space=pltpu.VMEM)
    sems = lambda count: pltpu.SemaphoreType.DMA((2, count))
    shape = lambda *s: jax.ShapeDtypeStruct(s, bf)
    half = (n // 2, 3 * groups * height, D)
    return pl.pallas_call(
        functools.partial(middle_kernel, n, groups),
        out_shape=(
            shape(T, D),
            jax.ShapeDtypeStruct((T, D), f32),
            shape(PLANES, QW, T),
            shape(PLANES, S2, height, D),
            shape(groups - 1, PLANES, S2, height, D),
            shape(PLANES, groups, height, D),
            shape(S2 - 1, PLANES, groups, height, D),
            shape(S2, groups, height, D),
            *[shape(S2, groups, height, D)] * (PLANES - 1),
            shape(3 * QW, D),
        ),
        in_specs=[vm, vm, vm, vm, any_, any_, any_, any_] + [any_] * (groups - 1),
        out_specs=tuple([vm] * 12),
        scratch_shapes=[
            pltpu.VMEM(out_w.shape, bf),
            pltpu.VMEM(exp_w.shape, bf),
            pltpu.VMEM((ffn, D), bf),
            pltpu.SemaphoreType.DMA((4 + groups - 1,)),
            sems(groups - 1),
            pltpu.VMEM(joint_shard.shape, bf),
            pltpu.VMEM((2, 3 * QW // 2, D // groups), bf),
            pltpu.VMEM((groups, 2, 3 * QW // 2, D // groups), bf),
            sems(2 * (groups - 1)),
            pltpu.VMEM((D, 3 * QW), bf),
            pltpu.VMEM((PLANES, QW, T), bf),
            sems(PLANES - 1),
            pltpu.VMEM((PLANES, QW, T), bf),
            sems(PLANES - 1),
            pltpu.VMEM((T, D), f32),
            pltpu.VMEM((T, D), bf),
            pltpu.VMEM((T, D), bf),
            pltpu.VMEM((T, ffn), f32),
            pltpu.VMEM((T, ffn), bf),
            pltpu.VMEM((T, 2 * ffn), bf),
            pltpu.VMEM((ffn, D), f32),
            pltpu.VMEM(half, bf),
            pltpu.VMEM(half, bf),
            pltpu.VMEM(half, bf),
            sems(2 + 2 * ffn // D),
        ],
        compiler_params=pltpu.CompilerParams(collective_id=2, has_side_effects=True, vmem_limit_bytes=60 << 20),
    )(lowt, tokens, cotangent, gains, out_w, exp_w, con_w, joint_shard, *con_got)


def tail_kernel(
    n,
    groups,
    deal_ref,
    dq_hbm,
    dkv_hbm,
    turn_ref,
    gains_ref,
    joint_hbm,
    joint_t_hbm,
    joint_near_hbm,
    first_hbm,
    tokens_hbm,
    grad_hidden_hbm,
    y_keep_hbm,
    y_got_hbm,
    x_keep_hbm,
    x_got_hbm,
    z_keep_hbm,
    z_got_1,
    z_got_2,
    z_got_3,
    d_got,
    w_all,
    jq_all,
    jk_all,
    joint_rows,
    joint_t,
    joint_near,
    first,
    tokens,
    grad_hidden,
    y_keep,
    y_got,
    x_keep,
    x_got,
    z_keep,
    z_came,
    local_sems,
    dq_ref,
    kv_own,
    own_sems,
    kv_near,
    kv_send,
    kv_far,
    kv_sems,
    mixed,
    mixed_got,
    mixed_send_sems,
    mixed_recv_sems,
    part,
    part_got,
    part_send_sems,
    part_recv_sems,
    j_acc,
    jq,
    jq_core,
    jq_side,
    jq_plane,
    jk,
    jk_core,
    jk_side,
    jk_plane,
    j_sems,
    x1_got,
    y2_got,
    y3_got,
    z1_got,
    z1_sems,
    x3_got,
    w_plane,
    w_plane_got,
    w_sems,
    d_send,
    d_mid,
    d_back,
    d_sems,
    row_sems,
    row_local,
):
    bf, f32 = jnp.bfloat16, jnp.float32
    S = n // PLANES
    S2 = S // 2
    T, D = tokens.shape
    me, group = lax.axis_index("ctx"), lax.axis_index("fsdp")
    plane, side = me // S, lax.rem(me, S)
    s2, core = side // 2, lax.rem(side, 2)
    MESH = pl.DeviceIdType.MESH

    def at(p, a, c, g):
        return (p * S + a * 2 + c, g)

    def plane_peer(k):
        return at(lax.rem(plane + k, PLANES), s2, core, group)

    def side_peer(k):
        return at(plane, lax.rem(s2 + k, S2), core, group)

    def group_peer(k):
        return at(plane, s2, core, lax.rem(group + k, groups))

    core_peer = at(plane, s2, 1 - core, group)

    def send(source, target, send_sem, recv_sem, device):
        return pltpu.make_async_remote_copy(
            src_ref=source, dst_ref=target, send_sem=send_sem, recv_sem=recv_sem, device_id=device, device_id_type=MESH
        )

    def remote(source, target, sems, index, device):
        return send(source, target, sems.at[0, index], sems.at[1, index], device)

    def total_of(terms):
        total = terms[0].astype(f32)
        for term in terms[1:]:
            total = total + term.astype(f32)
        return total

    lower = plane < 2
    middle = (plane == 1) | (plane == 2)
    order = [
        jnp.where(lower, 3, 0),
        jnp.where(plane == 0, 2, jnp.where(plane == 1, 0, jnp.where(plane == 2, 3, 1))),
        jnp.where((plane == 0) | (plane == 2), 1, 2),
        plane,
    ]
    steps = range(PLANES)
    back = [lax.rem(plane + PLANES - p, PLANES) for p in order]
    main = jnp.where(lower, 0, 1)
    main_plane = plane + 1 - 2 * main

    own_kv = [
        pltpu.make_async_copy(dkv_hbm.at[order[t], :, core], kv_own.at[t], own_sems.at[t]) for t in steps
    ] + [pltpu.make_async_copy(dq_hbm, dq_ref, own_sems.at[PLANES])]
    for copy in own_kv:
        copy.start()
    local = [
        pltpu.make_async_copy(source, target, local_sems.at[i])
        for i, (source, target) in enumerate(
            [
                (first_hbm, first),
                (joint_t_hbm, joint_t),
                (y_keep_hbm, y_keep),
                (y_got_hbm, y_got),
                (x_keep_hbm, x_keep),
                (x_got_hbm, x_got),
                (z_keep_hbm, z_keep),
                (z_got_1, z_came.at[0]),
                (z_got_2, z_came.at[1]),
                (z_got_3, z_came.at[2]),
                (tokens_hbm, tokens),
                (grad_hidden_hbm, grad_hidden),
                (joint_near_hbm, joint_near),
            ]
        )
    ]
    for copy in local:
        copy.start()
    barrier = pltpu.get_barrier_semaphore()

    def greet(k, carry):
        pl.semaphore_signal(barrier, inc=1, device_id=(lax.rem(me + k, n), group), device_id_type=MESH)
        return carry

    lax.fori_loop(1, n, greet, 0)
    for k in range(1, groups):
        pl.semaphore_signal(barrier, inc=1, device_id=group_peer(k), device_id_type=MESH)
    pl.semaphore_wait(barrier, n - 1 + groups - 1)

    core_kv = [remote(dkv_hbm.at[order[t], :, 1 - core], kv_near.at[t], kv_sems, t, core_peer) for t in steps]
    for copy in core_kv:
        copy.start()

    per_group = joint_hbm.shape[0]
    index = me - group * per_group
    held_here = (index >= 0) & (index < per_group)
    row_own = pltpu.make_async_copy(joint_hbm.at[jnp.clip(index, 0, per_group - 1)], joint_rows, row_local.at[0])
    row_moves = [
        send(
            joint_hbm.at[jnp.clip(index, 0, per_group - 1)],
            joint_rows,
            row_sems.at[k - 1],
            row_sems.at[groups - 1],
            group_peer(k),
        )
        for k in range(1, groups)
    ]

    @pl.when(held_here)
    def _():
        row_own.start()
        for copy in row_moves:
            copy.start()

    w_moves = []

    def w_copy(source, target, device):
        copy = remote(source, target, w_sems, len(w_moves), device)
        w_moves.append(copy)
        copy.start()
        return copy

    local[2].wait()
    local[3].wait()
    for p in range(PLANES):
        for a in range(S2):
            y_keep[p, a] = total_of([y_keep[p, a]] + [y_got[k, p, a] for k in range(groups - 1)]).astype(bf)

    def z1_send(t, slot, target):
        return send(
            y_keep.at[order[t]], z1_got.at[slot], z1_sems.at[0, t], z1_sems.at[1, slot], at(target, s2, core, group)
        )

    def z1_add(t, slot):
        z1_send(0, slot, main_plane).wait_recv()
        for a in range(S2):
            y_keep[order[t], a] = total_of([y_keep[order[t], a], z1_got[slot, a]]).astype(bf)

    def z1_relay(t, slot, onward, target):
        @pl.when(middle)
        def _():
            z1_add(t, slot)
            z1_send(t, onward, target).start()

    @pl.when(jnp.logical_not(middle))
    def _():
        for t in range(PLANES - 1):
            z1_send(t, t, main_plane).start()


    def turned_back(x, t):
        cos, sin = turn_ref[back[t], :HALF], turn_ref[back[t], HALF:]
        rows = []
        for h in range(HP):
            upper, lower = x[h * HD : h * HD + HALF], x[h * HD + HALF : (h + 1) * HD]
            rows += [upper * cos + lower * sin, lower * cos - upper * sin]
        return jnp.concatenate(rows, axis=0)

    side_kv = {}
    for t in steps:
        own_kv[t].wait()
        core_kv[t].wait()
        for a in range(S2):
            kv_send[t, a] = total_of([kv_own[t, a], kv_near[t, a]]).astype(bf)
        for k in range(1, S2):
            side_kv[t, k] = remote(
                kv_send.at[t, lax.rem(s2 + S2 - k, S2)],
                kv_far.at[t, k - 1],
                kv_sems,
                PLANES + t * (S2 - 1) + k - 1,
                side_peer(S2 - k),
            )
            side_kv[t, k].start()
    own_kv[PLANES].wait()
    for t in steps:
        mixed[t, :QW] = turned_back(dq_ref[back[t]], t).astype(bf)

    local[4].wait()
    local[5].wait()
    for p in range(PLANES):
        for g in range(groups):
            x_keep[p, g] = total_of([x_keep[p, g]] + [x_got[k, p, g] for k in range(S2 - 1)]).astype(bf)
    y2 = [w_copy(x_keep.at[:, lax.rem(group + k, groups)], y2_got.at[k - 1], group_peer(k)) for k in range(1, groups)]
    for i in range(6, 10):
        local[i].wait()
    for a in range(S2):
        for g in range(groups):
            z_keep[a, g] = total_of([z_keep[a, g]] + [z_came[k, a, g] for k in range(PLANES - 1)]).astype(bf)
    y3 = [w_copy(z_keep.at[:, lax.rem(group + k, groups)], y3_got.at[k - 1], group_peer(k)) for k in range(1, groups)]

    j_moves = []

    def j_copy(source, target, device):
        copy = remote(source, target, j_sems, len(j_moves), device)
        j_moves.append(copy)
        copy.start()
        return copy

    def j_core_stage(begin, height, grads, near):
        j_acc[:height] = total_of(
            [
                jnp.dot(mixed[t, begin : begin + height], first[back[t]], preferred_element_type=f32)
                for t in steps
            ]
        )
        shard_rows = D // n
        for i in range(D // 128):
            block = j_acc[:height, i * 128 : (i + 1) * 128].T
            row = i * 128
            while row < (i + 1) * 128:
                shard, offset = divmod(row, shard_rows)
                count = min(shard_rows - offset, (i + 1) * 128 - row)
                source = row - i * 128
                grads[shard // S, shard % S // 2, shard % 2, offset : offset + count] = block[
                    source : source + count
                ].astype(bf)
                row += count
        return [j_copy(grads.at[:, :, 1 - core], near, core_peer)]

    def j_side_stage(moves, grads, near, far):
        for copy in moves:
            copy.wait()
        for p in range(PLANES):
            for a in range(S2):
                near[p, a] = total_of([grads[p, a, core], near[p, a]]).astype(bf)
        return [j_copy(near.at[:, lax.rem(s2 + k, S2)], far.at[k - 1], side_peer(k)) for k in range(1, S2)]

    def j_plane_stage(moves, near, far, gathered):
        for copy in moves:
            copy.wait()
        for p in range(PLANES):
            far[0, p] = total_of([near[p, s2]] + [far[k, p] for k in range(S2 - 1)]).astype(bf)
        gathered[plane] = far[0, plane]
        return [
            j_copy(far.at[0, lax.rem(plane + k, PLANES)], gathered.at[plane], plane_peer(k)) for k in range(1, PLANES)
        ]

    def j_group_stage(moves, gathered, every):
        for copy in moves:
            copy.wait()
        every[group] = gathered[...]
        return [j_copy(gathered, every.at[group], group_peer(k)) for k in range(1, groups)]

    local[0].wait()
    jq_moves = j_core_stage(0, QW, jq, jq_core)
    z1_relay(0, 0, 3, main_plane)

    local[1].wait()

    half = T // 2
    halves = range(2)

    def mixed_send(t, e):
        lanes = pl.ds(e * half, half)
        return send(
            mixed.at[t, :, lanes],
            mixed_got.at[t, :, lanes],
            mixed_send_sems.at[t, e],
            mixed_recv_sems.at[t, e],
            at(main_plane, s2, core, group),
        )

    def part_send(t, e, direction, target):
        rows = pl.ds(e * half, half)
        return send(
            part.at[t, rows],
            part_got.at[direction, order[t], rows],
            part_send_sems.at[t, e],
            part_recv_sems.at[direction * PLANES + order[t], e],
            at(target, s2, core, group),
        )

    def part_came(direction, p, e):
        rows = pl.ds(e * half, half)
        return send(
            part.at[0, rows],
            part_got.at[direction, p, rows],
            part_send_sems.at[0, e],
            part_recv_sems.at[direction * PLANES + p, e],
            core_peer,
        )

    other_plane = 2 * plane - main_plane

    def product(grads, columns):
        return jnp.dot(grads.T, columns, preferred_element_type=f32)

    def add_mixed(t, slot, e):
        mixed_send(slot, e).wait_recv()
        rows = slice(e * half, (e + 1) * half)
        near = product(mixed_got[slot, :, rows], joint_near[...])
        part[t, rows] = (part[t, rows].astype(f32) + near).astype(bf)

    def add_part(t, direction, p, e):
        part_came(direction, p, e).wait_recv()
        rows = slice(e * half, (e + 1) * half)
        part[t, rows] = total_of([part[t, rows], part_got[direction, p, rows]]).astype(bf)

    def relay(t, slot):
        @pl.when(middle)
        def _():
            for e in halves:
                if slot is None:
                    add_part(t, 1 - main, order[t], e)
                    part_send(t, e, 1 - main, other_plane).start()
                else:
                    add_mixed(t, slot, e)
                    part_send(t, e, main, main_plane).start()

    def key_step(t):
        for k in range(1, S2):
            side_kv[t, k].wait()
        dk = total_of([kv_send[t, s2]] + [kv_far[t, k] for k in range(S2 - 1)]).T
        mixed[t, QW : 2 * QW] = turned_back(dk[:QW], t).astype(bf)
        mixed[t, 2 * QW :] = dk[QW:].astype(bf)
        if t < PLANES - 1:

            @pl.when(jnp.logical_not(middle))
            def _():
                for e in halves:
                    mixed_send(t, e).start()

            @pl.when(middle)
            def _():
                part[t] = product(mixed[t], joint_t[: 3 * QW]).astype(bf)

        else:
            part[t] = product(mixed[t], joint_t[: 3 * QW]).astype(bf)

    local[12].wait()
    key_step(0)
    z1_relay(2, 1, 4, main_plane)
    jq_moves = j_side_stage(jq_moves, jq, jq_core, jq_side)
    key_step(1)
    z1_relay(1, 3, 5, 2 * plane - main_plane)
    for copy in y2:
        copy.wait()
    for p in range(PLANES):
        w_plane[p] = total_of([x_keep[p, group]] + [y2_got[k, p] for k in range(groups - 1)]).astype(bf)
    w_last = [
        w_copy(w_plane.at[lax.rem(plane + k, PLANES)], w_plane_got.at[k - 1], plane_peer(k)) for k in range(1, PLANES)
    ]
    key_step(2)
    relay(0, 0)
    jq_moves = j_plane_stage(jq_moves, jq_core, jq_side, jq_plane)
    key_step(3)
    relay(2, 1)
    jk_moves = j_core_stage(QW, 2 * QW, jk, jk_core)

    for copy in y3:
        copy.wait()
    for a in range(S2):
        z_keep[a, group] = total_of([z_keep[a, group]] + [y3_got[k, a] for k in range(groups - 1)]).astype(bf)
    x3 = [w_copy(z_keep.at[lax.rem(s2 + k, S2), group], x3_got.at[k - 1], side_peer(k)) for k in range(1, S2)]
    @pl.when(middle)
    def _():
        z1_add(PLANES - 1, 2)
        z1_add(PLANES - 1, 4)

    @pl.when(jnp.logical_not(middle))
    def _():
        z1_add(PLANES - 1, 5)

    x1 = [w_copy(y_keep.at[plane, lax.rem(s2 + k, S2)], x1_got.at[k - 1], side_peer(k)) for k in range(1, S2)]
    relay(1, None)
    jk_moves = j_side_stage(jk_moves, jk, jk_core, jk_side)
    jq_moves = j_group_stage(jq_moves, jq_plane, jq_all)

    local[10].wait()
    local[11].wait()
    @pl.when(middle)
    def _():
        for e in halves:
            add_mixed(PLANES - 1, 2, e)

    for e in halves:
        add_part(PLANES - 1, 1 - main, plane, e)

    strip = 64

    def norm_back(i, carry):
        rows = pl.ds(pl.multiple_of(i * strip, strip), strip)
        grad = part[PLANES - 1, rows].astype(f32)
        values = tokens[rows].astype(f32)
        centred = values - jnp.mean(values, axis=-1, keepdims=True)
        scale = lax.rsqrt(jnp.mean(centred * centred, axis=-1, keepdims=True) + norm_eps)
        normal = centred * scale
        grad = grad * gains_ref[0:1]
        grad = grad - jnp.mean(grad, axis=-1, keepdims=True) - normal * jnp.mean(grad * normal, axis=-1, keepdims=True)
        grad_hidden[rows] = grad_hidden[rows] + grad * scale
        return carry

    lax.fori_loop(0, T // strip, norm_back, 0)

    blocks = T // BLOCK
    piece = BLOCK // n

    def d_copy(source, target, base, k):
        return remote(source.at[lax.rem(me + k, n)], target.at[me], d_sems, base + k, (lax.rem(me + k, n), group))

    for i in range(n):
        d_send[i] = jnp.concatenate(
            [grad_hidden[b * BLOCK + i * piece : b * BLOCK + (i + 1) * piece] for b in range(blocks)], axis=0
        ).astype(bf)
    out_deal = [d_copy(d_send, d_mid, 0, k) for k in range(1, n)]
    for copy in out_deal:
        copy.start()
    d_mid[me] = d_send[me]

    for copy in x1 + w_last + x3:
        copy.wait()
    height = w_plane.shape[1]
    w_all[group, :height] = total_of([y_keep[plane, s2]] + [x1_got[k] for k in range(S2 - 1)]).astype(bf)
    w_all[group, height : 2 * height] = total_of(
        [w_plane[plane]] + [w_plane_got[k] for k in range(PLANES - 1)]
    ).astype(bf)
    w_all[group, 2 * height :] = total_of([z_keep[s2, group]] + [x3_got[k] for k in range(S2 - 1)]).astype(bf)
    w_gather = [w_copy(w_all.at[group], w_all.at[group], group_peer(k)) for k in range(1, groups)]
    jk_moves = j_plane_stage(jk_moves, jk_core, jk_side, jk_plane)

    for copy in out_deal:
        copy.wait()
    for i in range(n):
        chosen = []
        for b in range(blocks):
            wanted = deal_ref[i * blocks + b]
            held = d_mid[wanted // blocks].astype(f32)
            rows = held[:piece]
            for other in range(1, blocks):
                rows = jnp.where(lax.rem(wanted, blocks) == other, held[other * piece : (other + 1) * piece], rows)
            chosen.append(rows)
        d_back[i] = jnp.concatenate(chosen, axis=0).astype(bf)
    back_deal = [d_copy(d_back, d_got, n, k) for k in range(1, n)]
    for copy in back_deal:
        copy.start()
    d_got[me] = d_back[me]

    jk_moves = j_group_stage(jk_moves, jk_plane, jk_all)

    for copy in back_deal + w_gather + jq_moves + jk_moves:
        copy.wait()
    for t in range(PLANES - 1):
        z1_send(t, 0, main_plane).wait_send()
        for e in halves:

            @pl.when(middle)
            def _(t=t, e=e):
                part_send(t, e, main, main_plane).wait_send()

            @pl.when(jnp.logical_not(middle))
            def _(t=t, e=e):
                mixed_send(t, e).wait_send()

    @pl.when(held_here)
    def _():
        row_own.wait()
        for copy in row_moves:
            copy.wait_send()

    @pl.when(jnp.logical_not(held_here))
    def _():
        row_moves[0].wait_recv()


def tail(n, groups, deal, dqt, dkv, turn, gains, joint_shard, joint_t, joint_near, first, tokens, grad_hidden, pieces):
    bf, f32 = jnp.bfloat16, jnp.float32
    S2 = n // PLANES // 2
    T, D = tokens.shape
    rows = D // n
    height = pieces[0].shape[2]
    piece_rows = T // n
    joint_shard = joint_shard.reshape(-1, rows, joint_shard.shape[1])
    any_, vm, sm = (pl.BlockSpec(memory_space=m) for m in (pl.ANY, pltpu.VMEM, pltpu.SMEM))
    sems = lambda count: pltpu.SemaphoreType.DMA((2, count))
    small = lambda *s: pltpu.VMEM(s, bf)
    j_buffers = lambda w: [
        small(PLANES, S2, 2, rows, w),
        small(PLANES, S2, rows, w),
        small(S2 - 1, PLANES, rows, w),
        small(PLANES, rows, w),
    ]
    return pl.pallas_call(
        functools.partial(tail_kernel, n, groups),
        out_shape=(
            jax.ShapeDtypeStruct((n, piece_rows, D), bf),
            jax.ShapeDtypeStruct((groups, 3 * height, D), bf),
            jax.ShapeDtypeStruct((groups, PLANES, rows, QW), bf),
            jax.ShapeDtypeStruct((groups, PLANES, rows, 2 * QW), bf),
            jax.ShapeDtypeStruct(joint_shard.shape[1:], bf),
        ),
        in_specs=[sm, any_, any_, vm, vm] + [any_] * 14,
        out_specs=tuple([vm] * 4) + (any_,),
        scratch_shapes=[
            pltpu.VMEM(joint_t.shape, bf),
            pltpu.VMEM(joint_near.shape, bf),
            pltpu.VMEM((PLANES, T, D), bf),
            pltpu.VMEM((T, D), bf),
            pltpu.VMEM((T, D), f32),
            *[pltpu.VMEM(p.shape, bf) for p in pieces[:5]],
            pltpu.VMEM((PLANES - 1, *pieces[5].shape), bf),
            pltpu.SemaphoreType.DMA((13,)),
            pltpu.VMEM(dqt.shape, f32),
            small(PLANES, S2, T, 2 * QW),
            pltpu.SemaphoreType.DMA((PLANES + 1,)),
            small(PLANES, S2, T, 2 * QW),
            small(PLANES, S2, T, 2 * QW),
            small(PLANES, S2 - 1, T, 2 * QW),
            sems(PLANES * S2),
            small(PLANES, 3 * QW, T),
            small(PLANES - 1, 3 * QW, T),
            pltpu.SemaphoreType.DMA((PLANES - 1, 2)),
            pltpu.SemaphoreType.DMA((PLANES - 1, 2)),
            small(PLANES, T, D),
            small(2, PLANES, T, D),
            pltpu.SemaphoreType.DMA((PLANES - 1, 2)),
            pltpu.SemaphoreType.DMA((2 * PLANES, 2)),
            pltpu.VMEM((2 * QW, D), f32),
            *j_buffers(QW),
            *j_buffers(2 * QW),
            sems(2 * (1 + S2 - 1 + PLANES - 1 + groups - 1)),
            small(S2 - 1, height, D),
            small(groups - 1, PLANES, height, D),
            small(groups - 1, S2, height, D),
            small(6, S2, height, D),
            pltpu.SemaphoreType.DMA((2, 6)),
            small(S2 - 1, height, D),
            small(PLANES, height, D),
            small(PLANES - 1, height, D),
            sems(3 * (groups - 1) + 2 * (S2 - 1) + PLANES - 1),
            small(n, piece_rows, D),
            small(n, piece_rows, D),
            small(n, piece_rows, D),
            sems(2 * n),
            pltpu.SemaphoreType.DMA((groups,)),
            pltpu.SemaphoreType.DMA((1,)),
        ],
        compiler_params=pltpu.CompilerParams(collective_id=0, has_side_effects=True, vmem_limit_bytes=60 << 20),
    )(deal, dqt, dkv, turn, gains, joint_shard, joint_t, joint_near, first, tokens, grad_hidden, *pieces)


def finish_kernel(
    n,
    d_ref,
    w_ref,
    jq_ref,
    jk_ref,
    rows_ref,
    gains_ref,
    dealt_ref,
    joint_ref,
    output_ref,
    expand_ref,
    contract_ref,
    gain_one_ref,
    gain_two_ref,
):
    f32 = jnp.float32
    T, D = dealt_ref.shape
    blocks = T // BLOCK
    piece = BLOCK // n
    for b in range(blocks):
        for i in range(0, n, 2):
            rows = [d_ref[i + e].astype(f32)[b * piece : (b + 1) * piece] for e in range(2)]
            dealt_ref[b * BLOCK + i * piece : b * BLOCK + (i + 2) * piece] = jnp.concatenate(rows, axis=0).astype(
                dealt_ref.dtype
            )

    def summed(ref, p):
        total = ref[0, p].astype(f32)
        for g in range(1, ref.shape[0]):
            total = total + ref[g, p].astype(f32)
        return total.T

    for i in range(PLANES // 2):
        pair = [summed(jq_ref, 2 * i + e) for e in range(2)]
        joint_ref[:, i * 2 * QW : (i + 1) * 2 * QW] = jnp.concatenate(pair, axis=0).T
        pair = [summed(jk_ref, 2 * i + e) for e in range(2)]
        for part in range(2):
            cols = (part + 1) * D + i * 2 * QW
            rows = [x[part * QW : (part + 1) * QW] for x in pair]
            joint_ref[:, cols : cols + 2 * QW] = jnp.concatenate(rows, axis=0).T
    shift = D - lax.axis_index("ctx") * (D // n)

    def own_lanes(x):
        return pltpu.roll(jnp.broadcast_to(x, (8, D)), shift, 1)[0:1, : D // n]

    product = jnp.sum(joint_ref[...] * rows_ref[...].astype(f32), axis=1, keepdims=True)
    product = jnp.broadcast_to(product, (D // n, 128)).T[0:1]
    gain_one_ref[...] = product / own_lanes(gains_ref[0:1])
    height = w_ref.shape[1]
    rows = D // n
    targets = [(output_ref, 0, rows)]
    targets += [(expand_ref, i * D, rows) for i in range(expand_ref.shape[1] // D)]
    targets += [(contract_ref, 0, contract_ref.shape[0])]
    row = 0
    for target, column, count in targets:
        done = 0
        while done < count:
            g, offset = divmod(row, height)
            part = min(count - done, height - offset)
            target[done : done + part, column : column + D] = w_ref[g, offset : offset + part].astype(f32)
            done += part
            row += part
    g, offset = divmod(row, height)
    gain_two_ref[...] = own_lanes(w_ref[g, offset : offset + 1].astype(f32))


def finish(n, T, wide, contract_rows, d_got, w_all, jq_all, jk_all, joint_rows, gains):
    D = d_got.shape[-1]
    rows = D // n
    f32 = jnp.float32
    vm = pl.BlockSpec(memory_space=pltpu.VMEM)
    return pl.pallas_call(
        functools.partial(finish_kernel, n),
        out_shape=(
            jax.ShapeDtypeStruct((T, D), jnp.bfloat16),
            jax.ShapeDtypeStruct((rows, 3 * D), f32),
            jax.ShapeDtypeStruct((rows, D), f32),
            jax.ShapeDtypeStruct((rows, wide), f32),
            jax.ShapeDtypeStruct((contract_rows, D), f32),
            jax.ShapeDtypeStruct((1, rows), f32),
            jax.ShapeDtypeStruct((1, rows), f32),
        ),
        in_specs=[vm] * 6,
        out_specs=tuple([vm] * 7),
    )(d_got, w_all, jq_all, jk_all, joint_rows, gains)


def on_device(
    n,
    groups,
    tokens,
    cotangent,
    lengths,
    deal,
    joint_projection,
    output_projection,
    expand_weight,
    contract_weight,
    gain_first,
    gain_second,
):
    T, D = tokens.shape[1:]
    S = n // PLANES
    S2 = S // 2

    def over_planes(x, k):
        return lax.ppermute(x, "ctx", [(h * S + s, (h + k) % PLANES * S + s) for h in range(PLANES) for s in range(S)])

    def over_sides(x, k):
        pairs = [
            (h * S + a * 2 + c, h * S + (a + k) % S2 * 2 + c) for h in range(PLANES) for a in range(S2) for c in range(2)
        ]
        return lax.ppermute(x, "ctx", pairs)

    def over_groups(x, k):
        return lax.ppermute(x, "fsdp", [(f, (f + k) % groups) for f in range(groups)])

    def moved(x, over):
        if x.shape[0] == 1:
            return over(x, 1)
        return jnp.stack([over(x[k], k + 1) for k in range(x.shape[0])])

    first, qt, kv, joint_t, turn, gains, out_w, exp_w, con_half = front(
        n,
        groups,
        lengths,
        tokens[0],
        joint_projection,
        gain_first,
        gain_second,
        output_projection,
        expand_weight,
        contract_weight,
    )
    con_got = [over_groups(con_half, k) for k in range(1, groups)]
    out_w, exp_w = (w.reshape(-1, w.shape[-1]) for w in (out_w, exp_w))
    ot, lowt, lse = attn_fwd(n, lengths, qt, kv)
    output, grad_hidden, gt, y_keep, y_send, x_keep, x_send, z_keep, *z_send, joint_near = middle(
        n, groups, lowt, tokens[0], cotangent[0], gains, out_w, exp_w, contract_weight, joint_projection, con_got
    )
    y_got, x_got = moved(y_send, over_groups), moved(x_send, over_sides)
    z_got = [over_planes(part, k + 1) for k, part in enumerate(z_send)]
    dqt, dkv = attn_bwd(n, lengths, qt, kv, ot, lse, gt)
    d_got, w_all, jq_all, jk_all, joint_rows = tail(
        n,
        groups,
        deal[0],
        dqt,
        dkv.reshape(PLANES, S2, 2, T, 2 * QW),
        turn,
        gains,
        joint_projection,
        joint_t,
        joint_near,
        first,
        tokens[0],
        grad_hidden,
        [y_keep, y_got, x_keep, x_got, z_keep, *z_got],
    )
    dealt, shard_joint, shard_output, shard_expand, shard_contract, gain_one, gain_two = finish(
        n, T, exp_w.shape[1], contract_weight.shape[0] * groups // n, d_got, w_all, jq_all, jk_all, joint_rows, gains
    )
    return (
        output[None],
        dealt[None],
        shard_joint,
        shard_output,
        shard_expand,
        shard_contract,
        gain_one[0],
        gain_two[0],
    )


def solution(mesh):
    return jax.shard_map(
        functools.partial(on_device, mesh.shape["ctx"], mesh.shape["fsdp"]),
        mesh=mesh,
        in_specs=(
            P("fsdp", "ctx", None),
            P("fsdp", "ctx", None),
            P("fsdp", None),
            P("fsdp", None),
            P("fsdp", None),
            P("fsdp", None),
            P("fsdp", None),
            P("fsdp", None),
            P("fsdp"),
            P("fsdp"),
        ),
        out_specs=(
            P("fsdp", "ctx", None),
            P("fsdp", "ctx", None),
            P("ctx", None),
            P("ctx", None),
            P("ctx", None),
            P("ctx", None),
            P("ctx"),
            P("ctx"),
        ),
        check_vma=False,
    )
```

```python
import functools
import math

import jax
import jax.numpy as jnp
import numpy as np
from jax import lax
from jax.experimental import pallas as pl
from jax.experimental.pallas import tpu as pltpu
from jax.sharding import PartitionSpec as P

FF = 1152
HEADS = 12
HEAD_DIM = 64
BLOCK = 128
PLANES = 4
HD = HEAD_DIM
HALF = HEAD_DIM // 2
HP = HEADS // PLANES
QW = HP * HEAD_DIM
rope_base = 160000.0
norm_eps = 1e-05
MASKED = -1e30


def ends_of(lengths_ref, count):
    ends, total = [], 0
    for i in range(count):
        total = total + lengths_ref[0, i]
        ends.append(total)
    return ends


def span_of(index, ends):
    begin, end = jnp.zeros_like(index), jnp.full_like(index, ends[0])
    for before, after in zip(ends[:-1], ends[1:]):
        begin = jnp.where(index >= before, before, begin)
        end = jnp.where(index >= before, after, end)
    return begin, end


def head_rows(x, head):
    rows = lax.broadcasted_iota(jnp.int32, x.shape, 0)
    return jnp.where((rows >= head * HD) & (rows < (head + 1) * HD), x, jnp.zeros_like(x))


def query_block(n, b, T, ends):
    S = n // PLANES
    me = lax.axis_index("ctx")
    base = (lax.rem(me // S + PLANES - b, PLANES) * S + lax.rem(me, S)) * T
    low_begin, low_end = span_of(base, ends)
    high_begin, high_end = span_of(base + T - 1, ends)
    low, high = low_begin // T, (high_end + T - 1) // T
    full_low = jnp.clip((high_begin + T - 1) // T, low, high)
    full_high = jnp.clip(low_end // T, full_low, high)
    begin, end = span_of(base + lax.broadcasted_iota(jnp.int32, (8, T), 1), ends)
    return (low, full_low, full_high, high), begin[0:1], end[0:1]


def over_units(bounds, step, sizes):
    low, full_low, full_high, high = bounds

    def run(begin, end, masked):
        def body(u, carry):
            step(u, masked)
            return carry

        lax.fori_loop(begin, end, body, 0)

    run(low, full_low, True)
    in_groups(full_low, full_high, lambda u: step(u, False), sizes)
    run(full_high, high, True)


def in_groups(begin, end, step, sizes):
    for size in sizes:
        count = (end - begin) // size

        def some(i, carry, size=size, begin=begin):
            for e in range(size):
                step(begin + size * i + e)
            return carry

        lax.fori_loop(0, count, some, 0)
        begin = begin + size * count


def fwd_kernel(n, count, lengths_ref, qt_ref, kv_ref, ot_ref, lowt_ref, lse_ref, values, scores, top, total, acc):
    units, T, _ = kv_ref.shape
    ends = ends_of(lengths_ref, count)

    def flip(u, carry):
        values[u] = kv_ref[u, :, 128:].T
        return carry

    lax.fori_loop(0, units, flip, 0, unroll=4)

    def one_query_block(b, carry):
        qt = qt_ref[b]
        qheads = [head_rows(qt, h) for h in range(HP)]
        bounds, q_start, q_end = query_block(n, b, T, ends)
        top[...] = jnp.full_like(top, MASKED)
        total[...] = jnp.zeros_like(total)
        acc[...] = jnp.zeros_like(acc)

        def score(u, masked):
            k = kv_ref[u, :, :QW]
            st = [jnp.dot(k, qheads[h], preferred_element_type=jnp.float32) for h in range(HP)]
            if masked:
                at = u * T + lax.broadcasted_iota(jnp.int32, (T, T), 0)
                allowed = (at >= q_start) & (at < q_end)
                st = [jnp.where(allowed, s, MASKED) for s in st]
            for h in range(HP):
                scores[u, h] = st[h]
                top[h] = jnp.maximum(top[h], jnp.max(st[h].reshape(T // 8, 8, T), axis=0))

        over_units(bounds, score, (2, 1))
        m = [jnp.max(top[h], axis=0, keepdims=True) for h in range(HP)]

        def gather(u):
            p = [jnp.exp(scores[u, h] - m[h]) for h in range(HP)]
            for h in range(HP):
                total[h] += jnp.sum(p[h].reshape(T // 8, 8, T), axis=0)
                rows = pl.ds(h * HD, HD)
                acc[rows, :] += jnp.dot(
                    values[u, pl.ds(HD + h * HD, HD), :], p[h].astype(jnp.bfloat16), preferred_element_type=jnp.float32
                )

        in_groups(bounds[0], bounds[3], gather, (4, 2, 1))
        for h in range(HP):
            rows = pl.ds(h * HD, HD)
            l = jnp.sum(total[h], axis=0, keepdims=True)
            o = acc[rows, :] / l
            ot_ref[b, rows, :] = o
            lowt_ref[b, rows, :] = o.astype(jnp.bfloat16)
            lse_ref[b, h : h + 1, :] = m[h] + jnp.log(l)
        return carry

    lax.fori_loop(0, qt_ref.shape[0], one_query_block, 0)


def attn_fwd(n, lengths, qt, kv):
    B, _, T = qt.shape
    U = kv.shape[0]
    sm, vm = pl.BlockSpec(memory_space=pltpu.SMEM), pl.BlockSpec(memory_space=pltpu.VMEM)
    return pl.pallas_call(
        functools.partial(fwd_kernel, n, lengths.shape[1]),
        out_shape=(
            jax.ShapeDtypeStruct((B, QW, T), jnp.float32),
            jax.ShapeDtypeStruct((B, QW, T), jnp.bfloat16),
            jax.ShapeDtypeStruct((B, 8, T), jnp.float32),
        ),
        in_specs=[sm, vm, vm],
        out_specs=(vm, vm, vm),
        scratch_shapes=[
            pltpu.VMEM((U, 256, T), jnp.bfloat16),
            pltpu.VMEM((U, HP, T, T), jnp.float32),
            pltpu.VMEM((HP, 8, T), jnp.float32),
            pltpu.VMEM((HP, 8, T), jnp.float32),
            pltpu.VMEM((QW, T), jnp.float32),
        ],
        compiler_params=pltpu.CompilerParams(vmem_limit_bytes=60 << 20),
    )(lengths, qt, kv)


def bwd_kernel(n, count, lengths_ref, qt_ref, kv_ref, ot_ref, lse_ref, gt_ref, dqt_ref, dkv_ref, keys, dk, dv, dq):
    units, T, _ = kv_ref.shape
    ends = ends_of(lengths_ref, count)

    def flip(u, carry):
        keys[u] = kv_ref[u, :, :256].T
        dk[u] = jnp.zeros_like(dk[u])
        dv[u] = jnp.zeros_like(dv[u])
        return carry

    lax.fori_loop(0, units, flip, 0, unroll=4)

    def one_query_block(b, carry):
        qt, gt = qt_ref[b], gt_ref[b]
        zero = jnp.zeros((HD, T), jnp.bfloat16)
        qheads = [head_rows(qt, h) for h in range(HP)]
        gheads = [head_rows(gt, h) for h in range(HP)]
        gpad = [jnp.concatenate([zero, x], axis=0) for x in gheads]
        lanes = lax.broadcasted_iota(jnp.int32, (T, 256), 1) // HD
        q, g = jnp.concatenate([qt, zero], axis=0).T, jnp.concatenate([zero, gt], axis=0).T
        q = jnp.concatenate([jnp.where(lanes == h, q, jnp.zeros_like(q)) for h in range(HP)], axis=0)
        g = jnp.concatenate([jnp.where(lanes == h + 1, g, jnp.zeros_like(g)) for h in range(HP)], axis=0)
        bounds, q_start, q_end = query_block(n, b, T, ends)
        prod = gt.astype(jnp.float32) * ot_ref[b]
        delta = [jnp.sum(prod[h * HD : (h + 1) * HD], axis=0, keepdims=True) for h in range(HP)]
        lse = [lse_ref[b, h : h + 1, :] for h in range(HP)]
        dq[...] = jnp.zeros_like(dq)

        def one_unit(u, masked):
            k, v = kv_ref[u, :, :QW], kv_ref[u, :, 128:]
            st = [jnp.dot(k, qheads[h], preferred_element_type=jnp.float32) for h in range(HP)]
            dp = [jnp.dot(v, gpad[h], preferred_element_type=jnp.float32) for h in range(HP)]
            st = [st[h] - lse[h] for h in range(HP)]
            if masked:
                at = u * T + lax.broadcasted_iota(jnp.int32, (T, T), 0)
                allowed = (at >= q_start) & (at < q_end)
                st = [jnp.where(allowed, s, MASKED) for s in st]
            p = [jnp.exp(s) for s in st]
            ds = [(p[h] * (dp[h] - delta[h])).astype(jnp.bfloat16) for h in range(HP)]
            p = [x.astype(jnp.bfloat16) for x in p]
            dv[u] += jnp.dot(jnp.concatenate(p, axis=1), g, preferred_element_type=jnp.float32)
            dk[u] += jnp.dot(jnp.concatenate(ds, axis=1), q, preferred_element_type=jnp.float32)
            for h in range(HP):
                rows = pl.ds(h * HD, HD)
                dq[rows, :] += jnp.dot(keys[u, rows, :], ds[h], preferred_element_type=jnp.float32)

        over_units(bounds, one_unit, (4, 2, 1))
        dqt_ref[b] = dq[...] * (HD**-0.5)
        return carry

    lax.fori_loop(0, qt_ref.shape[0], one_query_block, 0)

    def out(u, carry):
        dkv_ref[u, :, :128] = dk[u, :, :128].astype(jnp.bfloat16)
        dkv_ref[u, :, 128:256] = (dk[u, :, 128:] + dv[u, :, :128]).astype(jnp.bfloat16)
        dkv_ref[u, :, 256:] = dv[u, :, 128:].astype(jnp.bfloat16)
        return carry

    lax.fori_loop(0, units, out, 0, unroll=2)


def attn_bwd(n, lengths, qt, kv, ot, lse, gt):
    B, _, T = qt.shape
    U = kv.shape[0]
    sm, vm = pl.BlockSpec(memory_space=pltpu.SMEM), pl.BlockSpec(memory_space=pltpu.VMEM)
    return pl.pallas_call(
        functools.partial(bwd_kernel, n, lengths.shape[1]),
        out_shape=(jax.ShapeDtypeStruct((B, QW, T), jnp.float32), jax.ShapeDtypeStruct((U, T, 2 * QW), jnp.bfloat16)),
        in_specs=[sm] + [vm] * 5,
        out_specs=(vm, vm),
        scratch_shapes=[
            pltpu.VMEM((U, 256, T), jnp.bfloat16),
            pltpu.VMEM((U, T, 256), jnp.float32),
            pltpu.VMEM((U, T, 256), jnp.float32),
            pltpu.VMEM((QW, T), jnp.float32),
        ],
        compiler_params=pltpu.CompilerParams(vmem_limit_bytes=60 << 20),
    )(lengths, qt, kv, ot, lse, gt)
def front_kernel(
    n,
    groups,
    count,
    lengths_ref,
    tokens_ref,
    joint_ref,
    gain_one_ref,
    gain_two_ref,
    out_hbm,
    exp_hbm,
    con_hbm,
    first_ref,
    qt_ref,
    kv_ref,
    joint_t_out,
    turn_ref,
    gains_ref,
    out_all,
    exp_all,
    con_ref,
    held,
    t_sems,
    cols,
    cols_all,
    gain_held,
    g_sems,
    kv_own,
    kv_sems,
    own_sems,
    w_sems,
    w_local,
    joint_rows,
    out_held,
    exp_held,
    con_held,
):
    bf, f32 = jnp.bfloat16, jnp.float32
    S = n // PLANES
    S2 = S // 2
    T, D = tokens_ref.shape
    me, group = lax.axis_index("ctx"), lax.axis_index("fsdp")
    plane, side = me // S, lax.rem(me, S)
    s2, core = side // 2, lax.rem(side, 2)

    def at(p, a, c, g):
        return (p * S + a * 2 + c, g)

    def side_peer(k):
        return at(plane, lax.rem(s2 + k, S2), core, group)

    def group_peer(k):
        return at(plane, s2, core, lax.rem(group + k, groups))

    core_peer = at(plane, s2, 1 - core, group)

    def remote(source, target, sems, index, device):
        return pltpu.make_async_remote_copy(
            src_ref=source,
            dst_ref=target,
            send_sem=sems.at[0, index],
            recv_sem=sems.at[1, index],
            device_id=device,
            device_id_type=pl.DeviceIdType.MESH,
        )

    barrier = pltpu.get_barrier_semaphore()

    def greet(device):
        pl.semaphore_signal(barrier, inc=1, device_id=device, device_id_type=pl.DeviceIdType.MESH)

    for k in range(1, PLANES):
        greet(at(lax.rem(plane + k, PLANES), s2, core, group))
    for k in range(1, S2):
        greet(side_peer(k))
    for k in range(1, groups):
        greet(group_peer(k))
    greet(core_peer)
    pl.semaphore_wait(barrier, PLANES - 1 + S2 - 1 + groups - 1 + 1)

    def up(p):
        return remote(held.at[p], held.at[p], t_sems, p, at(plane + 1, s2, core, group))

    def down(p):
        return remote(held.at[p], held.at[p], t_sems, PLANES + p, at(plane - 1, s2, core, group))

    held[plane] = tokens_ref[...]

    @pl.when(plane < PLANES - 1)
    def _():
        up(plane).start()

    @pl.when(plane > 0)
    def _():
        down(plane).start()

    pair = 2 * QW
    for part in range(3):
        window = joint_ref[:, pl.ds(pl.multiple_of(part * D + plane // 2 * pair, 128), pair)].T
        chosen = jnp.where(lax.rem(plane, 2) == 0, window[:QW].astype(f32), window[QW:].astype(f32))
        half = 3 * QW // 2
        low, high = part * QW, (part + 1) * QW
        for c in range(2):
            begin, end = max(low, c * half), min(high, (c + 1) * half)
            if begin < end:
                cols[c, begin - c * half : end - c * half] = chosen[begin - low : end - low].astype(bf)
    gain_held[group] = jnp.zeros_like(gain_held[group])
    gain_held[group, 0:1] = gain_one_ref[...].astype(f32).reshape(1, -1)
    gain_held[group, 1:2] = gain_two_ref[...].astype(f32).reshape(1, -1)
    col_moves = [
        remote(cols.at[core], cols_all.at[group, core], g_sems, k - 1, group_peer(k)) for k in range(1, groups)
    ]
    col_hands = []
    for k in range(1, groups):
        came = cols_all.at[lax.rem(group + groups - k, groups), core]
        col_hands.append(remote(came, came, g_sems, 2 * (groups - 1) + k - 1, core_peer))
    gain_moves = [
        remote(gain_held.at[group], gain_held.at[group], g_sems, groups - 1 + k - 1, group_peer(k))
        for k in range(1, groups)
    ]
    for copy in gain_moves + col_moves:
        copy.start()
    cols_all[group] = cols[...]

    weights = [(out_hbm, out_all, out_held), (exp_hbm, exp_all, exp_held)]
    part = core if con_hbm.shape[0] == 2 else 0
    w_in = [pltpu.make_async_copy(con_hbm.at[part], con_held, w_local.at[0, len(weights)])]
    w_own = [pltpu.make_async_copy(con_held, con_ref, w_local.at[1, len(weights)])]
    w_first, w_second = [], []
    for i, (source, target, bounce) in enumerate(weights):
        w_in.append(pltpu.make_async_copy(source, bounce, w_local.at[0, i]))
        w_own.append(pltpu.make_async_copy(bounce, target.at[group], w_local.at[1, i]))
        for k in range(1, groups):
            index = (i * (groups - 1) + k - 1) * 2
            w_first.append(remote(source.at[core], target.at[group, core], w_sems, index, group_peer(k)))
            came = lax.rem(group + groups - k, groups)
            w_second.append(remote(target.at[came, core], target.at[came, core], w_sems, index + 1, core_peer))
    for copy in w_in:
        copy.start()
    for copy in w_first:
        copy.start()

    ends = ends_of(lengths_ref, count)
    row = lax.broadcasted_iota(jnp.int32, (HALF, T), 0)
    frequencies = jnp.zeros((HALF, T), f32)
    for i in range(HALF):
        frequencies = jnp.where(row == i, float(np.float32(rope_base ** (-2.0 * i / HEAD_DIM))), frequencies)
    for j in range(PLANES):
        base = (lax.rem(plane + PLANES - j, PLANES) * S + side) * T
        index = base + lax.broadcasted_iota(jnp.int32, (8, T), 1)
        begin, _ = span_of(index, ends)
        angles = (index - begin)[0:1].astype(f32) * frequencies
        turn_ref[j, :HALF] = jnp.cos(angles)
        turn_ref[j, HALF:] = jnp.sin(angles)

    strip = 64

    def kv_unit(p, a, c):
        return p * S + a * 2 + c

    def side_kv(j, k):
        p = lax.rem(plane + PLANES - j, PLANES)
        return remote(kv_own.at[j], kv_ref.at[kv_unit(p, s2, core)], kv_sems, j * (2 * S2 - 1) + k - 1, side_peer(k))

    def core_kv(j, k):
        p = lax.rem(plane + PLANES - j, PLANES)
        unit = kv_unit(p, lax.rem(s2 + S2 - k, S2), core)
        source = kv_own.at[j] if k == 0 else kv_ref.at[unit]
        return remote(source, kv_ref.at[unit], kv_sems, j * (2 * S2 - 1) + S2 - 1 + k, core_peer)

    def own_kv(j):
        p = lax.rem(plane + PLANES - j, PLANES)
        return pltpu.make_async_copy(kv_own.at[j], kv_ref.at[kv_unit(p, s2, core)], own_sems.at[j])

    def process(p):
        j = lax.rem(plane + PLANES - p, PLANES)

        def norm(i, carry):
            rows = pl.ds(pl.multiple_of(i * strip, strip), strip)
            values = held[p, rows].astype(f32)
            centred = values - jnp.mean(values, axis=-1, keepdims=True)
            spread = jnp.mean(centred * centred, axis=-1, keepdims=True)
            first_ref[j, rows] = (centred * lax.rsqrt(spread + norm_eps) * gains_ref[0:1]).astype(bf)
            return carry

        lax.fori_loop(0, T // strip, norm, 0)
        mixed = lax.dot_general(
            joint_t_out[: 3 * QW], first_ref[j], (((1,), (1,)), ((), ())), preferred_element_type=f32
        )
        cos, sin = turn_ref[j, :HALF], turn_ref[j, HALF:]
        turned = []
        for h in range(2 * HP):
            upper, lower = mixed[h * HD : h * HD + HALF], mixed[h * HD + HALF : (h + 1) * HD]
            turned += [upper * cos - lower * sin, lower * cos + upper * sin]
        q = jnp.concatenate(turned[: 2 * HP], axis=0).astype(bf)
        qt_ref[j] = (q.astype(f32) * HEAD_DIM**-0.5).astype(bf)
        kv_own[j] = jnp.concatenate(turned[2 * HP :] + [mixed[2 * QW :]], axis=0).T.astype(bf)
        for k in range(1, S2):
            side_kv(j, k).start()
        core_kv(j, 0).start()
        own_kv(j).start()

    def hand_on(t):
        @pl.when(plane >= t)
        def _():
            up(plane - t).wait_recv()

            @pl.when(plane < PLANES - 1)
            def _():
                up(plane - t).start()

        @pl.when(plane + t < PLANES)
        def _():
            down(plane + t).wait_recv()

            @pl.when(plane > 0)
            def _():
                down(plane + t).start()

    def process_arrived(t):
        below = jnp.where(plane >= t, 1, 0)
        above = jnp.where(plane + t < PLANES, 1, 0)

        def arrived(i, carry):
            process(jnp.where(i < below, plane - t, plane + t))
            return carry

        lax.fori_loop(0, below + above, arrived, 0)

    hand_on(1)
    for copy in gain_moves:
        copy.wait()
    share = D // groups
    total = jnp.zeros((8, D), f32)
    for g in range(groups):
        rows = lax.broadcasted_iota(jnp.int32, (share, D), 0)
        lanes = lax.broadcasted_iota(jnp.int32, (share, D), 1)
        place = jnp.where(lanes == rows + g * share, 1.0, 0.0).astype(bf)
        total = total + jnp.dot(gain_held[g].astype(bf), place, preferred_element_type=f32)
    gains_ref[...] = total
    for copy, hand in zip(col_moves, col_hands):
        copy.wait()
        hand.start()
    for copy in w_in:
        copy.wait()
    for copy in w_own:
        copy.start()
    for copy in col_hands:
        copy.wait()
    width = joint_t_out.shape[0]
    for g in range(groups):
        whole = jnp.concatenate([cols_all[g, 0], cols_all[g, 1], jnp.zeros((width - 3 * QW, share), bf)], axis=0)
        if share % 128 == 0:
            joint_t_out[:, g * share : (g + 1) * share] = whole
        else:
            joint_rows[g * share : (g + 1) * share] = whole.T
    if share % 128:
        for i in range(D // 128):
            joint_t_out[:, i * 128 : (i + 1) * 128] = joint_rows[i * 128 : (i + 1) * 128].T

    process(plane)
    process_arrived(1)
    hand_on(2)
    process_arrived(2)
    hand_on(3)
    for first_move, second_move in zip(w_first[: groups - 1], w_second):
        first_move.wait_recv()
        second_move.start()
    process_arrived(3)

    for j in range(PLANES):
        for k in range(1, S2):
            side_kv(j, k).wait_recv()
            core_kv(j, k).start()
    for first_move, second_move in zip(w_first[groups - 1 :], w_second[groups - 1 :]):
        first_move.wait_recv()
        second_move.start()

    for j in range(PLANES):
        own_kv(j).wait()
        for k in range(1, S2):
            side_kv(j, k).wait_send()
        for k in range(S2):
            core_kv(j, k).wait()
    for p in range(PLANES):

        @pl.when((plane < PLANES - 1) & (plane >= p))
        def _(p=p):
            up(p).wait_send()

        @pl.when((plane > 0) & (plane <= p))
        def _(p=p):
            down(p).wait_send()

    for copy in w_own:
        copy.wait()
    for first_move, second_move in zip(w_first, w_second):
        first_move.wait_send()
        second_move.wait()


def front(n, groups, lengths, tokens, joint_shard, gain_first, gain_second, out_w, exp_w, con_w):
    bf, f32 = jnp.bfloat16, jnp.float32
    S2 = n // PLANES // 2
    T, D = tokens.shape
    width = 3 * QW + 64
    share = D // groups
    any_, vm, sm = (pl.BlockSpec(memory_space=m) for m in (pl.ANY, pltpu.VMEM, pltpu.SMEM))
    sems = lambda count: pltpu.SemaphoreType.DMA((2, count))
    halves = lambda w: w.reshape(2, w.shape[0] // 2, w.shape[1])
    weights = [halves(w) for w in (out_w, exp_w)]
    con_w = con_w.reshape(2 if con_w.shape[0] % 32 == 0 else 1, -1, D)
    return pl.pallas_call(
        functools.partial(front_kernel, n, groups, lengths.shape[1]),
        out_shape=(
            jax.ShapeDtypeStruct((PLANES, T, D), bf),
            jax.ShapeDtypeStruct((PLANES, QW, T), bf),
            jax.ShapeDtypeStruct((n, T, 2 * QW), bf),
            jax.ShapeDtypeStruct((width, D), bf),
            jax.ShapeDtypeStruct((PLANES, 2 * HALF, T), f32),
            jax.ShapeDtypeStruct((8, D), f32),
            *[jax.ShapeDtypeStruct((groups, *w.shape), bf) for w in weights],
            jax.ShapeDtypeStruct(con_w.shape[1:], bf),
        ),
        in_specs=[sm, vm, vm, vm, vm, any_, any_, any_],
        out_specs=(vm, vm, any_, vm, vm, vm, any_, any_, any_),
        scratch_shapes=[
            pltpu.VMEM((PLANES, T, D), bf),
            sems(2 * PLANES),
            pltpu.VMEM((2, 3 * QW // 2, share), bf),
            pltpu.VMEM((groups, 2, 3 * QW // 2, share), bf),
            pltpu.VMEM((groups, 8, share), f32),
            sems(3 * (groups - 1)),
            pltpu.VMEM((PLANES, T, 2 * QW), bf),
            sems(PLANES * (2 * S2 - 1)),
            pltpu.SemaphoreType.DMA((PLANES,)),
            sems(2 * len(weights) * (groups - 1)),
            pltpu.SemaphoreType.DMA((2, len(weights) + 1)),
            pltpu.VMEM((D, width), bf),
            *[pltpu.VMEM(w.shape, bf) for w in weights],
            pltpu.VMEM(con_w.shape[1:], bf),
        ],
        compiler_params=pltpu.CompilerParams(collective_id=1, has_side_effects=True, vmem_limit_bytes=60 << 20),
    )(
        lengths,
        tokens,
        joint_shard,
        gain_first,
        gain_second,
        *weights,
        con_w,
    )


def middle_kernel(
    n,
    groups,
    low_ref,
    tokens_ref,
    cot_ref,
    gains_ref,
    out_hbm,
    exp_hbm,
    con_hbm,
    joint_hbm,
    *refs,
):
    con_got, refs = refs[: groups - 1], refs[groups - 1 :]
    (
        output_ref,
        grad_hidden_ref,
        gt_ref,
        y_keep,
        y_send,
        x_keep,
        x_send,
        z_keep,
        z_send_1,
        z_send_2,
        z_send_3,
        joint_near,
        out_w,
        exp_w,
        con_w,
        local_sems,
        c_sems,
        joint_shard,
        cols,
        cols_all,
        col_sems,
        joint_rows,
        att,
        a_sems,
        g_send,
        g_sems,
        hidden,
        second,
        branch,
        ga,
        act,
        gexp,
        acc,
        w_own,
        w_other,
        w_got,
        w_sems,
    ) = refs
    bf, f32 = jnp.bfloat16, jnp.float32
    S = n // PLANES
    S2 = S // 2
    T, D = tokens_ref.shape
    FFN = act.shape[1]
    me, group = lax.axis_index("ctx"), lax.axis_index("fsdp")
    plane, side = me // S, lax.rem(me, S)
    s2, core = side // 2, lax.rem(side, 2)

    def plane_peer(k):
        return (lax.rem(plane + k, PLANES) * S + side, group)

    core_peer = (plane * S + s2 * 2 + 1 - core, group)

    def group_peer(k):
        return (me, lax.rem(group + k, groups))


    def remote(source, target, sems, index, device):
        return pltpu.make_async_remote_copy(
            src_ref=source,
            dst_ref=target,
            send_sem=sems.at[0, index],
            recv_sem=sems.at[1, index],
            device_id=device,
            device_id_type=pl.DeviceIdType.MESH,
        )

    ff_share = con_hbm.shape[0]
    split = ff_share % 32 == 0

    def rows_of(g):
        return pl.ds(pl.multiple_of(g * ff_share, 16), ff_share)

    def half_of(g):
        if not split:
            return rows_of(g)
        half = ff_share // 2
        return pl.ds(pl.multiple_of(g * ff_share + core * half, 16), half)

    came = [half_of(lax.rem(group + groups - k, groups)) for k in range(1, groups)]
    con_hands = [remote(con_got[k], con_w.at[came[k]], c_sems, k, core_peer) for k in range(groups - 1)]
    con_local = [
        pltpu.make_async_copy(con_got[k], con_w.at[came[k]], local_sems.at[3 + k]) for k in range(groups - 1)
    ]
    local = [
        pltpu.make_async_copy(source, target, local_sems.at[i])
        for i, (source, target) in enumerate([(con_hbm, con_w.at[rows_of(group)]), (out_hbm, out_w), (exp_hbm, exp_w)])
    ]
    joint_local = pltpu.make_async_copy(joint_hbm, joint_shard, local_sems.at[3 + groups - 1])
    for copy in [joint_local] + local + con_local:
        copy.start()
    barrier = pltpu.get_barrier_semaphore()
    for k in range(1, PLANES):
        pl.semaphore_signal(barrier, inc=1, device_id=plane_peer(k), device_id_type=pl.DeviceIdType.MESH)
    pl.semaphore_signal(barrier, inc=1, device_id=core_peer, device_id_type=pl.DeviceIdType.MESH)
    for k in range(1, groups):
        pl.semaphore_signal(barrier, inc=1, device_id=group_peer(k), device_id_type=pl.DeviceIdType.MESH)
    pl.semaphore_wait(barrier, PLANES + groups - 1)

    home = [remote(low_ref.at[j], att.at[plane], a_sems, j - 1, plane_peer(PLANES - j)) for j in range(1, PLANES)]
    for copy in home + (con_hands if split else []):
        copy.start()
    att[plane] = low_ref[0]

    joint_local.wait()
    pair = 2 * QW
    for part in range(3):
        window = joint_shard[:, pl.ds(pl.multiple_of(part * D + plane // 2 * pair, 128), pair)].T
        chosen = jnp.where(lax.rem(plane, 2) == 1, window[:QW].astype(f32), window[QW:].astype(f32))
        half = 3 * QW // 2
        low, high = part * QW, (part + 1) * QW
        for c in range(2):
            begin, end = max(low, c * half), min(high, (c + 1) * half)
            if begin < end:
                cols[c, begin - c * half : end - c * half] = chosen[begin - low : end - low].astype(bf)
    col_moves = [
        remote(cols.at[core], cols_all.at[group, core], col_sems, k - 1, group_peer(k)) for k in range(1, groups)
    ]
    col_hands = []
    for k in range(1, groups):
        col_came = cols_all.at[lax.rem(group + groups - k, groups), core]
        col_hands.append(remote(col_came, col_came, col_sems, groups - 1 + k - 1, core_peer))
    for copy in col_moves:
        copy.start()
    cols_all[group] = cols[...]

    def nt(a, b):
        return lax.dot_general(a, b, (((1,), (1,)), ((), ())), preferred_element_type=f32)

    chunk = 384
    cot = cot_ref[...]
    local[0].wait()
    for copy in con_local + (con_hands if split else []):
        copy.wait()
    for c in range(0, FFN, chunk):
        ga[:, c : c + chunk] = nt(cot, con_w[c : c + chunk])
    local[1].wait()
    for copy in home:
        copy.wait()
    attended = att[...].reshape(D, T)
    hidden[...] = tokens_ref[...].astype(f32) + jnp.dot(attended.T, out_w[...], preferred_element_type=f32)

    strip = 64

    for copy, hand in zip(col_moves, col_hands):
        copy.wait()
        hand.start()

    def norm(i, carry):
        rows = pl.ds(pl.multiple_of(i * strip, strip), strip)
        values = hidden[rows]
        centred = values - jnp.mean(values, axis=-1, keepdims=True)
        spread = jnp.mean(centred * centred, axis=-1, keepdims=True)
        second[rows] = (centred * lax.rsqrt(spread + norm_eps) * gains_ref[1:2]).astype(bf)
        return carry

    lax.fori_loop(0, T // strip, norm, 0)
    local[2].wait()
    for c in range(0, FFN, chunk):
        cols, gate_cols = slice(c, c + chunk), slice(FFN + c, FFN + c + chunk)
        inner = jnp.dot(second[...], exp_w[:, cols], preferred_element_type=f32)
        gate = jnp.dot(second[...], exp_w[:, gate_cols], preferred_element_type=f32)
        share = 0.5 * (1.0 + lax.erf(inner * (0.5**0.5)))
        bent = inner * share
        act[:, cols] = (bent * gate).astype(bf)
        grad = ga[:, cols]
        slope = share + inner * jnp.exp(-0.5 * inner * inner) * ((2.0 * math.pi) ** -0.5)
        gexp[:, cols] = (grad * gate * slope).astype(bf)
        gexp[:, gate_cols] = (grad * bent).astype(bf)
    output_ref[...] = (hidden[...] + jnp.dot(act[...], con_w[...], preferred_element_type=f32)).astype(bf)
    acc[:T] = nt(gexp[...], exp_w[...])

    def norm_back(i, total):
        rows = pl.ds(pl.multiple_of(i * strip, strip), strip)
        values = hidden[rows]
        centred = values - jnp.mean(values, axis=-1, keepdims=True)
        scale = lax.rsqrt(jnp.mean(centred * centred, axis=-1, keepdims=True) + norm_eps)
        normal = centred * scale
        grad = acc[rows]
        total = total + jnp.sum(grad * normal, axis=0, keepdims=True)
        grad = grad * gains_ref[1:2]
        grad = grad - jnp.mean(grad, axis=-1, keepdims=True) - normal * jnp.mean(grad * normal, axis=-1, keepdims=True)
        back = cot_ref[rows].astype(f32) + grad * scale
        grad_hidden_ref[rows] = back
        branch[rows] = back.astype(bf)
        return total

    total = lax.fori_loop(0, T // strip, norm_back, jnp.zeros((1, D), f32))
    gain_two = jnp.broadcast_to(total, (8, D))
    for p in range(PLANES):
        g_send[p] = nt(out_w[p * QW : (p + 1) * QW], branch[...]).astype(bf)
    away = [
        remote(g_send.at[lax.rem(plane + k, PLANES)], gt_ref.at[k], g_sems, k - 1, plane_peer(k))
        for k in range(1, PLANES)
    ]
    for copy in away:
        copy.start()
    gt_ref[0] = g_send[plane]

    for copy in col_hands:
        copy.wait()
    share = D // groups
    for g in range(groups):
        whole = jnp.concatenate([cols_all[g, 0], cols_all[g, 1]], axis=0)
        if share % 128 == 0:
            joint_near[:, g * share : (g + 1) * share] = whole
        else:
            joint_rows[g * share : (g + 1) * share] = whole.T
    if share % 128:
        for i in range(D // 128):
            joint_near[:, i * 128 : (i + 1) * 128] = joint_rows[i * 128 : (i + 1) * 128].T

    sent = []

    def place(rows, offset, height):
        for target, parity in ((w_other, 1 - core), (w_own, core)):

            def body(m, carry):
                if rows % 8:
                    pair = acc[pl.ds(pl.multiple_of(2 * m * rows, 8), 2 * rows)]
                    value = jnp.where(parity == 0, pair[:rows], pair[rows:])
                else:
                    value = acc[pl.ds(pl.multiple_of((2 * m + parity) * rows, 8), rows)]
                if height > rows:
                    rest = jnp.zeros((height - rows - 8, D), f32)
                    value = jnp.concatenate([value, gain_two, rest], axis=0)
                value = value.astype(bf)
                target[m, offset : offset + height] = value
                return carry

            lax.fori_loop(0, n // 2, body, 0)
        part = pl.ds(offset, height)
        sent.append(remote(w_other.at[:, part], w_got.at[:, part], w_sems, len(sent), core_peer))
        sent[-1].start()

    rows = D // n
    wide = 2 * FFN // D
    for c in range(0, FFN, chunk):
        acc[c : c + chunk] = jnp.dot(act[:, c : c + chunk].T, cot_ref[...], preferred_element_type=f32)
    used = (1 + wide) * rows
    place(FFN // n, used, w_own.shape[1] - used)
    second_t = second[...].T
    for i in range(wide):
        acc[:D] = jnp.dot(second_t, gexp[:, i * D : (i + 1) * D], preferred_element_type=f32)
        place(rows, (1 + i) * rows, rows)
    acc[:D] = jnp.dot(attended, branch[...], preferred_element_type=f32)
    place(rows, 0, rows)

    for copy in sent:
        copy.wait()
    height = y_keep.shape[2]
    third = lambda g, i: pl.ds(pl.multiple_of((3 * g + i) * height, 16), height)

    def summed(m, part):
        return (w_own[m, part].astype(f32) + w_got[m, part].astype(f32)).astype(bf)

    def each(count, body):
        def step(i, carry):
            body(i)
            return carry

        lax.fori_loop(0, count, step, 0)

    for k in range(groups):
        g = lax.rem(group + k, groups)

        def first(m, k=k, g=g):
            (y_send.at[k - 1] if k else y_keep)[m // S2, lax.rem(m, S2)] = summed(m, third(g, 0))

        each(PLANES * S2, first)
    for k in range(S2):
        a = lax.rem(s2 + k, S2)

        def second_part(i, k=k, a=a):
            p, g = i // groups, lax.rem(i, groups)
            (x_send.at[k - 1] if k else x_keep)[p, g] = summed(p * S2 + a, third(g, 1))

        each(PLANES * groups, second_part)
    z_parts = [z_keep, z_send_1, z_send_2, z_send_3]
    for k in range(PLANES):
        p = lax.rem(plane + k, PLANES)

        def third_part(i, k=k, p=p):
            a, g = i // groups, lax.rem(i, groups)
            z_parts[k][a, g] = summed(p * S2 + a, third(g, 2))

        each(S2 * groups, third_part)
    for copy in away:
        copy.wait()


def middle(n, groups, lowt, tokens, cotangent, gains, out_w, exp_w, con_w, joint_shard, con_got):
    bf, f32 = jnp.bfloat16, jnp.float32
    S2 = n // PLANES // 2
    T, D = tokens.shape
    ffn = con_w.shape[0] * groups
    used = (D + 2 * ffn + ffn) // n + 8
    height = -(-used // (groups * 48)) * 16
    any_, vm = pl.BlockSpec(memory_space=pl.ANY), pl.BlockSpec(memory_space=pltpu.VMEM)
    sems = lambda count: pltpu.SemaphoreType.DMA((2, count))
    shape = lambda *s: jax.ShapeDtypeStruct(s, bf)
    half = (n // 2, 3 * groups * height, D)
    return pl.pallas_call(
        functools.partial(middle_kernel, n, groups),
        out_shape=(
            shape(T, D),
            jax.ShapeDtypeStruct((T, D), f32),
            shape(PLANES, QW, T),
            shape(PLANES, S2, height, D),
            shape(groups - 1, PLANES, S2, height, D),
            shape(PLANES, groups, height, D),
            shape(S2 - 1, PLANES, groups, height, D),
            shape(S2, groups, height, D),
            *[shape(S2, groups, height, D)] * (PLANES - 1),
            shape(3 * QW, D),
        ),
        in_specs=[vm, vm, vm, vm, any_, any_, any_, any_] + [any_] * (groups - 1),
        out_specs=tuple([vm] * 12),
        scratch_shapes=[
            pltpu.VMEM(out_w.shape, bf),
            pltpu.VMEM(exp_w.shape, bf),
            pltpu.VMEM((ffn, D), bf),
            pltpu.SemaphoreType.DMA((4 + groups - 1,)),
            sems(groups - 1),
            pltpu.VMEM(joint_shard.shape, bf),
            pltpu.VMEM((2, 3 * QW // 2, D // groups), bf),
            pltpu.VMEM((groups, 2, 3 * QW // 2, D // groups), bf),
            sems(2 * (groups - 1)),
            pltpu.VMEM((D, 3 * QW), bf),
            pltpu.VMEM((PLANES, QW, T), bf),
            sems(PLANES - 1),
            pltpu.VMEM((PLANES, QW, T), bf),
            sems(PLANES - 1),
            pltpu.VMEM((T, D), f32),
            pltpu.VMEM((T, D), bf),
            pltpu.VMEM((T, D), bf),
            pltpu.VMEM((T, ffn), f32),
            pltpu.VMEM((T, ffn), bf),
            pltpu.VMEM((T, 2 * ffn), bf),
            pltpu.VMEM((ffn, D), f32),
            pltpu.VMEM(half, bf),
            pltpu.VMEM(half, bf),
            pltpu.VMEM(half, bf),
            sems(2 + 2 * ffn // D),
        ],
        compiler_params=pltpu.CompilerParams(collective_id=2, has_side_effects=True, vmem_limit_bytes=60 << 20),
    )(lowt, tokens, cotangent, gains, out_w, exp_w, con_w, joint_shard, *con_got)


def tail_kernel(
    n,
    groups,
    deal_ref,
    dq_hbm,
    dkv_hbm,
    turn_ref,
    gains_ref,
    joint_hbm,
    joint_t_hbm,
    joint_near_hbm,
    first_hbm,
    tokens_hbm,
    grad_hidden_hbm,
    y_keep_hbm,
    y_got_hbm,
    x_keep_hbm,
    x_got_hbm,
    z_keep_hbm,
    z_got_1,
    z_got_2,
    z_got_3,
    d_got,
    w_all,
    jq_all,
    jk_all,
    joint_rows,
    joint_t,
    joint_near,
    first,
    tokens,
    grad_hidden,
    y_keep,
    y_got,
    x_keep,
    x_got,
    z_keep,
    z_came,
    local_sems,
    dq_ref,
    kv_own,
    own_sems,
    kv_near,
    kv_send,
    kv_far,
    kv_sems,
    mixed,
    mixed_got,
    mixed_send_sems,
    mixed_recv_sems,
    part,
    part_got,
    part_send_sems,
    part_recv_sems,
    j_acc,
    jq,
    jq_core,
    jq_side,
    jq_plane,
    jk,
    jk_core,
    jk_side,
    jk_plane,
    j_sems,
    x1_got,
    y2_got,
    y3_got,
    z1_got,
    z1_sems,
    x3_got,
    w_plane,
    w_plane_got,
    w_sems,
    d_send,
    d_mid,
    d_back,
    d_sems,
    row_sems,
    row_local,
):
    bf, f32 = jnp.bfloat16, jnp.float32
    S = n // PLANES
    S2 = S // 2
    T, D = tokens.shape
    me, group = lax.axis_index("ctx"), lax.axis_index("fsdp")
    plane, side = me // S, lax.rem(me, S)
    s2, core = side // 2, lax.rem(side, 2)
    MESH = pl.DeviceIdType.MESH

    def at(p, a, c, g):
        return (p * S + a * 2 + c, g)

    def plane_peer(k):
        return at(lax.rem(plane + k, PLANES), s2, core, group)

    def side_peer(k):
        return at(plane, lax.rem(s2 + k, S2), core, group)

    def group_peer(k):
        return at(plane, s2, core, lax.rem(group + k, groups))

    core_peer = at(plane, s2, 1 - core, group)

    def send(source, target, send_sem, recv_sem, device):
        return pltpu.make_async_remote_copy(
            src_ref=source, dst_ref=target, send_sem=send_sem, recv_sem=recv_sem, device_id=device, device_id_type=MESH
        )

    def remote(source, target, sems, index, device):
        return send(source, target, sems.at[0, index], sems.at[1, index], device)

    def total_of(terms):
        total = terms[0].astype(f32)
        for term in terms[1:]:
            total = total + term.astype(f32)
        return total

    lower = plane < 2
    middle = (plane == 1) | (plane == 2)
    order = [
        jnp.where(lower, 3, 0),
        jnp.where(plane == 0, 2, jnp.where(plane == 1, 0, jnp.where(plane == 2, 3, 1))),
        jnp.where((plane == 0) | (plane == 2), 1, 2),
        plane,
    ]
    steps = range(PLANES)
    back = [lax.rem(plane + PLANES - p, PLANES) for p in order]
    main = jnp.where(lower, 0, 1)
    main_plane = plane + 1 - 2 * main

    own_kv = [
        pltpu.make_async_copy(dkv_hbm.at[order[t], :, core], kv_own.at[t], own_sems.at[t]) for t in steps
    ] + [pltpu.make_async_copy(dq_hbm, dq_ref, own_sems.at[PLANES])]
    for copy in own_kv:
        copy.start()
    local = [
        pltpu.make_async_copy(source, target, local_sems.at[i])
        for i, (source, target) in enumerate(
            [
                (first_hbm, first),
                (joint_t_hbm, joint_t),
                (y_keep_hbm, y_keep),
                (y_got_hbm, y_got),
                (x_keep_hbm, x_keep),
                (x_got_hbm, x_got),
                (z_keep_hbm, z_keep),
                (z_got_1, z_came.at[0]),
                (z_got_2, z_came.at[1]),
                (z_got_3, z_came.at[2]),
                (tokens_hbm, tokens),
                (grad_hidden_hbm, grad_hidden),
                (joint_near_hbm, joint_near),
            ]
        )
    ]
    for i in (2, 3, 4, 5, 6, 7, 8, 9, 0, 1, 12, 10, 11):
        local[i].start()
    barrier = pltpu.get_barrier_semaphore()

    def greet(k, carry):
        pl.semaphore_signal(barrier, inc=1, device_id=(lax.rem(me + k, n), group), device_id_type=MESH)
        return carry

    lax.fori_loop(1, n, greet, 0)
    for k in range(1, groups):
        pl.semaphore_signal(barrier, inc=1, device_id=group_peer(k), device_id_type=MESH)
    pl.semaphore_wait(barrier, n - 1 + groups - 1)

    core_kv = [remote(dkv_hbm.at[order[t], :, 1 - core], kv_near.at[t], kv_sems, t, core_peer) for t in steps]
    for copy in core_kv:
        copy.start()

    per_group = joint_hbm.shape[0]
    index = me - group * per_group
    held_here = (index >= 0) & (index < per_group)
    row_own = pltpu.make_async_copy(joint_hbm.at[jnp.clip(index, 0, per_group - 1)], joint_rows, row_local.at[0])
    row_moves = [
        send(
            joint_hbm.at[jnp.clip(index, 0, per_group - 1)],
            joint_rows,
            row_sems.at[k - 1],
            row_sems.at[groups - 1],
            group_peer(k),
        )
        for k in range(1, groups)
    ]

    @pl.when(held_here)
    def _():
        row_own.start()
        for copy in row_moves:
            copy.start()

    w_moves = []

    def w_copy(source, target, device):
        copy = remote(source, target, w_sems, len(w_moves), device)
        w_moves.append(copy)
        copy.start()
        return copy

    local[2].wait()
    local[3].wait()
    for p in range(PLANES):
        for a in range(S2):
            y_keep[p, a] = total_of([y_keep[p, a]] + [y_got[k, p, a] for k in range(groups - 1)]).astype(bf)

    def z1_send(t, slot, target):
        return send(
            y_keep.at[order[t]], z1_got.at[slot], z1_sems.at[0, t], z1_sems.at[1, slot], at(target, s2, core, group)
        )

    def z1_add(t, slot):
        z1_send(0, slot, main_plane).wait_recv()
        for a in range(S2):
            y_keep[order[t], a] = total_of([y_keep[order[t], a], z1_got[slot, a]]).astype(bf)

    def z1_relay(t, slot, onward, target):
        @pl.when(middle)
        def _():
            z1_add(t, slot)
            z1_send(t, onward, target).start()

    @pl.when(jnp.logical_not(middle))
    def _():
        for t in range(PLANES - 1):
            z1_send(t, t, main_plane).start()


    def turned_back(x, t):
        cos, sin = turn_ref[back[t], :HALF], turn_ref[back[t], HALF:]
        rows = []
        for h in range(HP):
            upper, lower = x[h * HD : h * HD + HALF], x[h * HD + HALF : (h + 1) * HD]
            rows += [upper * cos + lower * sin, lower * cos - upper * sin]
        return jnp.concatenate(rows, axis=0)

    side_kv = {}
    for t in steps:
        own_kv[t].wait()
        core_kv[t].wait()
        for a in range(S2):
            kv_send[t, a] = total_of([kv_own[t, a], kv_near[t, a]]).astype(bf)
        for k in range(1, S2):
            side_kv[t, k] = remote(
                kv_send.at[t, lax.rem(s2 + S2 - k, S2)],
                kv_far.at[t, k - 1],
                kv_sems,
                PLANES + t * (S2 - 1) + k - 1,
                side_peer(S2 - k),
            )
            side_kv[t, k].start()
    own_kv[PLANES].wait()
    for t in steps:
        mixed[t, :QW] = turned_back(dq_ref[back[t]], t).astype(bf)

    local[4].wait()
    local[5].wait()
    for p in range(PLANES):
        for g in range(groups):
            x_keep[p, g] = total_of([x_keep[p, g]] + [x_got[k, p, g] for k in range(S2 - 1)]).astype(bf)
    y2 = [w_copy(x_keep.at[:, lax.rem(group + k, groups)], y2_got.at[k - 1], group_peer(k)) for k in range(1, groups)]
    for i in range(6, 10):
        local[i].wait()
    for a in range(S2):
        for g in range(groups):
            z_keep[a, g] = total_of([z_keep[a, g]] + [z_came[k, a, g] for k in range(PLANES - 1)]).astype(bf)
    y3 = [w_copy(z_keep.at[:, lax.rem(group + k, groups)], y3_got.at[k - 1], group_peer(k)) for k in range(1, groups)]

    j_moves = []

    def j_copy(source, target, device):
        copy = remote(source, target, j_sems, len(j_moves), device)
        j_moves.append(copy)
        copy.start()
        return copy

    def j_core_stage(begin, height, grads, near):
        j_acc[:height] = total_of(
            [
                jnp.dot(mixed[t, begin : begin + height], first[back[t]], preferred_element_type=f32)
                for t in steps
            ]
        )
        shard_rows = D // n
        for i in range(D // 128):
            block = j_acc[:height, i * 128 : (i + 1) * 128].T
            row = i * 128
            while row < (i + 1) * 128:
                shard, offset = divmod(row, shard_rows)
                count = min(shard_rows - offset, (i + 1) * 128 - row)
                source = row - i * 128
                grads[shard // S, shard % S // 2, shard % 2, offset : offset + count] = block[
                    source : source + count
                ].astype(bf)
                row += count
        return [j_copy(grads.at[:, :, 1 - core], near, core_peer)]

    def j_side_stage(moves, grads, near, far):
        for copy in moves:
            copy.wait()
        for p in range(PLANES):
            for a in range(S2):
                near[p, a] = total_of([grads[p, a, core], near[p, a]]).astype(bf)
        return [j_copy(near.at[:, lax.rem(s2 + k, S2)], far.at[k - 1], side_peer(k)) for k in range(1, S2)]

    def j_plane_stage(moves, near, far, gathered):
        for copy in moves:
            copy.wait()
        for p in range(PLANES):
            far[0, p] = total_of([near[p, s2]] + [far[k, p] for k in range(S2 - 1)]).astype(bf)
        gathered[plane] = far[0, plane]
        return [
            j_copy(far.at[0, lax.rem(plane + k, PLANES)], gathered.at[plane], plane_peer(k)) for k in range(1, PLANES)
        ]

    def j_group_stage(moves, gathered, every):
        for copy in moves:
            copy.wait()
        every[group] = gathered[...]
        return [j_copy(gathered, every.at[group], group_peer(k)) for k in range(1, groups)]

    local[0].wait()
    jq_moves = j_core_stage(0, QW, jq, jq_core)
    z1_relay(0, 0, 3, main_plane)

    local[1].wait()

    half = T // 2
    halves = range(2)

    def mixed_send(t, e):
        lanes = pl.ds(e * half, half)
        return send(
            mixed.at[t, :, lanes],
            mixed_got.at[t, :, lanes],
            mixed_send_sems.at[t, e],
            mixed_recv_sems.at[t, e],
            at(main_plane, s2, core, group),
        )

    def part_send(t, e, direction, target):
        rows = pl.ds(e * half, half)
        return send(
            part.at[t, rows],
            part_got.at[direction, order[t], rows],
            part_send_sems.at[t, e],
            part_recv_sems.at[direction * PLANES + order[t], e],
            at(target, s2, core, group),
        )

    def part_came(direction, p, e):
        rows = pl.ds(e * half, half)
        return send(
            part.at[0, rows],
            part_got.at[direction, p, rows],
            part_send_sems.at[0, e],
            part_recv_sems.at[direction * PLANES + p, e],
            core_peer,
        )

    other_plane = 2 * plane - main_plane

    def product(grads, columns):
        return jnp.dot(grads.T, columns, preferred_element_type=f32)

    def add_mixed(t, slot, e):
        mixed_send(slot, e).wait_recv()
        rows = slice(e * half, (e + 1) * half)
        near = product(mixed_got[slot, :, rows], joint_near[...])
        part[t, rows] = (part[t, rows].astype(f32) + near).astype(bf)

    def add_part(t, direction, p, e):
        part_came(direction, p, e).wait_recv()
        rows = slice(e * half, (e + 1) * half)
        part[t, rows] = total_of([part[t, rows], part_got[direction, p, rows]]).astype(bf)

    def relay(t, slot):
        @pl.when(middle)
        def _():
            for e in halves:
                if slot is None:
                    add_part(t, 1 - main, order[t], e)
                    part_send(t, e, 1 - main, other_plane).start()
                else:
                    add_mixed(t, slot, e)
                    part_send(t, e, main, main_plane).start()

    def key_step(t):
        for k in range(1, S2):
            side_kv[t, k].wait()
        dk = total_of([kv_send[t, s2]] + [kv_far[t, k] for k in range(S2 - 1)]).T
        mixed[t, QW : 2 * QW] = turned_back(dk[:QW], t).astype(bf)
        mixed[t, 2 * QW :] = dk[QW:].astype(bf)
        if t < PLANES - 1:

            @pl.when(jnp.logical_not(middle))
            def _():
                for e in halves:
                    mixed_send(t, e).start()

            @pl.when(middle)
            def _():
                part[t] = product(mixed[t], joint_t[: 3 * QW]).astype(bf)

        else:
            part[t] = product(mixed[t], joint_t[: 3 * QW]).astype(bf)

    local[12].wait()
    key_step(0)
    z1_relay(2, 1, 4, main_plane)
    jq_moves = j_side_stage(jq_moves, jq, jq_core, jq_side)
    key_step(1)
    z1_relay(1, 3, 5, 2 * plane - main_plane)
    for copy in y2:
        copy.wait()
    for p in range(PLANES):
        w_plane[p] = total_of([x_keep[p, group]] + [y2_got[k, p] for k in range(groups - 1)]).astype(bf)
    w_last = [
        w_copy(w_plane.at[lax.rem(plane + k, PLANES)], w_plane_got.at[k - 1], plane_peer(k)) for k in range(1, PLANES)
    ]
    key_step(2)
    relay(0, 0)
    jq_moves = j_plane_stage(jq_moves, jq_core, jq_side, jq_plane)
    key_step(3)
    relay(2, 1)
    jk_moves = j_core_stage(QW, 2 * QW, jk, jk_core)

    for copy in y3:
        copy.wait()
    for a in range(S2):
        z_keep[a, group] = total_of([z_keep[a, group]] + [y3_got[k, a] for k in range(groups - 1)]).astype(bf)
    x3 = [w_copy(z_keep.at[lax.rem(s2 + k, S2), group], x3_got.at[k - 1], side_peer(k)) for k in range(1, S2)]
    @pl.when(middle)
    def _():
        z1_add(PLANES - 1, 2)
        z1_add(PLANES - 1, 4)

    @pl.when(jnp.logical_not(middle))
    def _():
        z1_add(PLANES - 1, 5)

    x1 = [w_copy(y_keep.at[plane, lax.rem(s2 + k, S2)], x1_got.at[k - 1], side_peer(k)) for k in range(1, S2)]
    relay(1, None)
    jk_moves = j_side_stage(jk_moves, jk, jk_core, jk_side)
    jq_moves = j_group_stage(jq_moves, jq_plane, jq_all)

    local[10].wait()
    local[11].wait()
    @pl.when(middle)
    def _():
        for e in halves:
            add_mixed(PLANES - 1, 2, e)

    for e in halves:
        add_part(PLANES - 1, 1 - main, plane, e)

    strip = 64

    def norm_back(i, carry):
        rows = pl.ds(pl.multiple_of(i * strip, strip), strip)
        grad = part[PLANES - 1, rows].astype(f32)
        values = tokens[rows].astype(f32)
        centred = values - jnp.mean(values, axis=-1, keepdims=True)
        scale = lax.rsqrt(jnp.mean(centred * centred, axis=-1, keepdims=True) + norm_eps)
        normal = centred * scale
        grad = grad * gains_ref[0:1]
        grad = grad - jnp.mean(grad, axis=-1, keepdims=True) - normal * jnp.mean(grad * normal, axis=-1, keepdims=True)
        grad_hidden[rows] = grad_hidden[rows] + grad * scale
        return carry

    lax.fori_loop(0, T // strip, norm_back, 0)

    blocks = T // BLOCK
    piece = BLOCK // n

    def d_copy(source, target, base, k):
        return remote(source.at[lax.rem(me + k, n)], target.at[me], d_sems, base + k, (lax.rem(me + k, n), group))

    for i in range(n):
        d_send[i] = jnp.concatenate(
            [grad_hidden[b * BLOCK + i * piece : b * BLOCK + (i + 1) * piece] for b in range(blocks)], axis=0
        ).astype(bf)
    out_deal = [d_copy(d_send, d_mid, 0, k) for k in range(1, n)]
    for copy in out_deal:
        copy.start()
    d_mid[me] = d_send[me]

    for copy in x1 + w_last + x3:
        copy.wait()
    height = w_plane.shape[1]
    w_all[group, :height] = total_of([y_keep[plane, s2]] + [x1_got[k] for k in range(S2 - 1)]).astype(bf)
    w_all[group, height : 2 * height] = total_of(
        [w_plane[plane]] + [w_plane_got[k] for k in range(PLANES - 1)]
    ).astype(bf)
    w_all[group, 2 * height :] = total_of([z_keep[s2, group]] + [x3_got[k] for k in range(S2 - 1)]).astype(bf)
    w_gather = [w_copy(w_all.at[group], w_all.at[group], group_peer(k)) for k in range(1, groups)]
    jk_moves = j_plane_stage(jk_moves, jk_core, jk_side, jk_plane)

    for copy in out_deal:
        copy.wait()
    for i in range(n):
        chosen = []
        for b in range(blocks):
            wanted = deal_ref[i * blocks + b]
            held = d_mid[wanted // blocks].astype(f32)
            rows = held[:piece]
            for other in range(1, blocks):
                rows = jnp.where(lax.rem(wanted, blocks) == other, held[other * piece : (other + 1) * piece], rows)
            chosen.append(rows)
        d_back[i] = jnp.concatenate(chosen, axis=0).astype(bf)
    back_deal = [d_copy(d_back, d_got, n, k) for k in range(1, n)]
    for copy in back_deal:
        copy.start()
    d_got[me] = d_back[me]

    jk_moves = j_group_stage(jk_moves, jk_plane, jk_all)

    for copy in back_deal + w_gather + jq_moves + jk_moves:
        copy.wait()
    for t in range(PLANES - 1):
        z1_send(t, 0, main_plane).wait_send()
        for e in halves:

            @pl.when(middle)
            def _(t=t, e=e):
                part_send(t, e, main, main_plane).wait_send()

            @pl.when(jnp.logical_not(middle))
            def _(t=t, e=e):
                mixed_send(t, e).wait_send()

    @pl.when(held_here)
    def _():
        row_own.wait()
        for copy in row_moves:
            copy.wait_send()

    @pl.when(jnp.logical_not(held_here))
    def _():
        row_moves[0].wait_recv()


def tail(n, groups, deal, dqt, dkv, turn, gains, joint_shard, joint_t, joint_near, first, tokens, grad_hidden, pieces):
    bf, f32 = jnp.bfloat16, jnp.float32
    S2 = n // PLANES // 2
    T, D = tokens.shape
    rows = D // n
    height = pieces[0].shape[2]
    piece_rows = T // n
    joint_shard = joint_shard.reshape(-1, rows, joint_shard.shape[1])
    any_, vm, sm = (pl.BlockSpec(memory_space=m) for m in (pl.ANY, pltpu.VMEM, pltpu.SMEM))
    sems = lambda count: pltpu.SemaphoreType.DMA((2, count))
    small = lambda *s: pltpu.VMEM(s, bf)
    j_buffers = lambda w: [
        small(PLANES, S2, 2, rows, w),
        small(PLANES, S2, rows, w),
        small(S2 - 1, PLANES, rows, w),
        small(PLANES, rows, w),
    ]
    return pl.pallas_call(
        functools.partial(tail_kernel, n, groups),
        out_shape=(
            jax.ShapeDtypeStruct((n, piece_rows, D), bf),
            jax.ShapeDtypeStruct((groups, 3 * height, D), bf),
            jax.ShapeDtypeStruct((groups, PLANES, rows, QW), bf),
            jax.ShapeDtypeStruct((groups, PLANES, rows, 2 * QW), bf),
            jax.ShapeDtypeStruct(joint_shard.shape[1:], bf),
        ),
        in_specs=[sm, any_, any_, vm, vm] + [any_] * 14,
        out_specs=tuple([vm] * 4) + (any_,),
        scratch_shapes=[
            pltpu.VMEM(joint_t.shape, bf),
            pltpu.VMEM(joint_near.shape, bf),
            pltpu.VMEM((PLANES, T, D), bf),
            pltpu.VMEM((T, D), bf),
            pltpu.VMEM((T, D), f32),
            *[pltpu.VMEM(p.shape, bf) for p in pieces[:5]],
            pltpu.VMEM((PLANES - 1, *pieces[5].shape), bf),
            pltpu.SemaphoreType.DMA((13,)),
            pltpu.VMEM(dqt.shape, f32),
            small(PLANES, S2, T, 2 * QW),
            pltpu.SemaphoreType.DMA((PLANES + 1,)),
            small(PLANES, S2, T, 2 * QW),
            small(PLANES, S2, T, 2 * QW),
            small(PLANES, S2 - 1, T, 2 * QW),
            sems(PLANES * S2),
            small(PLANES, 3 * QW, T),
            small(PLANES - 1, 3 * QW, T),
            pltpu.SemaphoreType.DMA((PLANES - 1, 2)),
            pltpu.SemaphoreType.DMA((PLANES - 1, 2)),
            small(PLANES, T, D),
            small(2, PLANES, T, D),
            pltpu.SemaphoreType.DMA((PLANES - 1, 2)),
            pltpu.SemaphoreType.DMA((2 * PLANES, 2)),
            pltpu.VMEM((2 * QW, D), f32),
            *j_buffers(QW),
            *j_buffers(2 * QW),
            sems(2 * (1 + S2 - 1 + PLANES - 1 + groups - 1)),
            small(S2 - 1, height, D),
            small(groups - 1, PLANES, height, D),
            small(groups - 1, S2, height, D),
            small(6, S2, height, D),
            pltpu.SemaphoreType.DMA((2, 6)),
            small(S2 - 1, height, D),
            small(PLANES, height, D),
            small(PLANES - 1, height, D),
            sems(3 * (groups - 1) + 2 * (S2 - 1) + PLANES - 1),
            small(n, piece_rows, D),
            small(n, piece_rows, D),
            small(n, piece_rows, D),
            sems(2 * n),
            pltpu.SemaphoreType.DMA((groups,)),
            pltpu.SemaphoreType.DMA((1,)),
        ],
        compiler_params=pltpu.CompilerParams(collective_id=0, has_side_effects=True, vmem_limit_bytes=60 << 20),
    )(deal, dqt, dkv, turn, gains, joint_shard, joint_t, joint_near, first, tokens, grad_hidden, *pieces)


def finish_kernel(
    n,
    d_ref,
    w_ref,
    jq_ref,
    jk_ref,
    rows_ref,
    gains_ref,
    dealt_ref,
    joint_ref,
    output_ref,
    expand_ref,
    contract_ref,
    gain_one_ref,
    gain_two_ref,
):
    f32 = jnp.float32
    T, D = dealt_ref.shape
    blocks = T // BLOCK
    piece = BLOCK // n
    for b in range(blocks):
        for i in range(0, n, 2):
            rows = [d_ref[i + e].astype(f32)[b * piece : (b + 1) * piece] for e in range(2)]
            dealt_ref[b * BLOCK + i * piece : b * BLOCK + (i + 2) * piece] = jnp.concatenate(rows, axis=0).astype(
                dealt_ref.dtype
            )

    def summed(ref, p):
        total = ref[0, p].astype(f32)
        for g in range(1, ref.shape[0]):
            total = total + ref[g, p].astype(f32)
        return total.T

    for i in range(PLANES // 2):
        pair = [summed(jq_ref, 2 * i + e) for e in range(2)]
        joint_ref[:, i * 2 * QW : (i + 1) * 2 * QW] = jnp.concatenate(pair, axis=0).T
        pair = [summed(jk_ref, 2 * i + e) for e in range(2)]
        for part in range(2):
            cols = (part + 1) * D + i * 2 * QW
            rows = [x[part * QW : (part + 1) * QW] for x in pair]
            joint_ref[:, cols : cols + 2 * QW] = jnp.concatenate(rows, axis=0).T
    shift = D - lax.axis_index("ctx") * (D // n)

    def own_lanes(x):
        return pltpu.roll(jnp.broadcast_to(x, (8, D)), shift, 1)[0:1, : D // n]

    product = jnp.sum(joint_ref[...] * rows_ref[...].astype(f32), axis=1, keepdims=True)
    product = jnp.broadcast_to(product, (D // n, 128)).T[0:1]
    gain_one_ref[...] = product / own_lanes(gains_ref[0:1])
    height = w_ref.shape[1]
    rows = D // n
    targets = [(output_ref, 0, rows)]
    targets += [(expand_ref, i * D, rows) for i in range(expand_ref.shape[1] // D)]
    targets += [(contract_ref, 0, contract_ref.shape[0])]
    row = 0
    for target, column, count in targets:
        done = 0
        while done < count:
            g, offset = divmod(row, height)
            part = min(count - done, height - offset)
            target[done : done + part, column : column + D] = w_ref[g, offset : offset + part].astype(f32)
            done += part
            row += part
    g, offset = divmod(row, height)
    gain_two_ref[...] = own_lanes(w_ref[g, offset : offset + 1].astype(f32))


def finish(n, T, wide, contract_rows, d_got, w_all, jq_all, jk_all, joint_rows, gains):
    D = d_got.shape[-1]
    rows = D // n
    f32 = jnp.float32
    vm = pl.BlockSpec(memory_space=pltpu.VMEM)
    return pl.pallas_call(
        functools.partial(finish_kernel, n),
        out_shape=(
            jax.ShapeDtypeStruct((T, D), jnp.bfloat16),
            jax.ShapeDtypeStruct((rows, 3 * D), f32),
            jax.ShapeDtypeStruct((rows, D), f32),
            jax.ShapeDtypeStruct((rows, wide), f32),
            jax.ShapeDtypeStruct((contract_rows, D), f32),
            jax.ShapeDtypeStruct((1, rows), f32),
            jax.ShapeDtypeStruct((1, rows), f32),
        ),
        in_specs=[vm] * 6,
        out_specs=tuple([vm] * 7),
    )(d_got, w_all, jq_all, jk_all, joint_rows, gains)


def on_device(
    n,
    groups,
    tokens,
    cotangent,
    lengths,
    deal,
    joint_projection,
    output_projection,
    expand_weight,
    contract_weight,
    gain_first,
    gain_second,
):
    T, D = tokens.shape[1:]
    S = n // PLANES
    S2 = S // 2

    def over_planes(x, k):
        return lax.ppermute(x, "ctx", [(h * S + s, (h + k) % PLANES * S + s) for h in range(PLANES) for s in range(S)])

    def over_sides(x, k):
        pairs = [
            (h * S + a * 2 + c, h * S + (a + k) % S2 * 2 + c) for h in range(PLANES) for a in range(S2) for c in range(2)
        ]
        return lax.ppermute(x, "ctx", pairs)

    def over_groups(x, k):
        return lax.ppermute(x, "fsdp", [(f, (f + k) % groups) for f in range(groups)])

    def moved(x, over):
        if x.shape[0] == 1:
            return over(x, 1)
        return jnp.stack([over(x[k], k + 1) for k in range(x.shape[0])])

    first, qt, kv, joint_t, turn, gains, out_w, exp_w, con_half = front(
        n,
        groups,
        lengths,
        tokens[0],
        joint_projection,
        gain_first,
        gain_second,
        output_projection,
        expand_weight,
        contract_weight,
    )
    con_got = [over_groups(con_half, k) for k in range(1, groups)]
    out_w, exp_w = (w.reshape(-1, w.shape[-1]) for w in (out_w, exp_w))
    ot, lowt, lse = attn_fwd(n, lengths, qt, kv)
    output, grad_hidden, gt, y_keep, y_send, x_keep, x_send, z_keep, *z_send, joint_near = middle(
        n, groups, lowt, tokens[0], cotangent[0], gains, out_w, exp_w, contract_weight, joint_projection, con_got
    )
    y_got, x_got = moved(y_send, over_groups), moved(x_send, over_sides)
    z_got = [over_planes(part, k + 1) for k, part in enumerate(z_send)]
    dqt, dkv = attn_bwd(n, lengths, qt, kv, ot, lse, gt)
    d_got, w_all, jq_all, jk_all, joint_rows = tail(
        n,
        groups,
        deal[0],
        dqt,
        dkv.reshape(PLANES, S2, 2, T, 2 * QW),
        turn,
        gains,
        joint_projection,
        joint_t,
        joint_near,
        first,
        tokens[0],
        grad_hidden,
        [y_keep, y_got, x_keep, x_got, z_keep, *z_got],
    )
    dealt, shard_joint, shard_output, shard_expand, shard_contract, gain_one, gain_two = finish(
        n, T, exp_w.shape[1], contract_weight.shape[0] * groups // n, d_got, w_all, jq_all, jk_all, joint_rows, gains
    )
    return (
        output[None],
        dealt[None],
        shard_joint,
        shard_output,
        shard_expand,
        shard_contract,
        gain_one[0],
        gain_two[0],
    )


def solution(mesh):
    return jax.shard_map(
        functools.partial(on_device, mesh.shape["ctx"], mesh.shape["fsdp"]),
        mesh=mesh,
        in_specs=(
            P("fsdp", "ctx", None),
            P("fsdp", "ctx", None),
            P("fsdp", None),
            P("fsdp", None),
            P("fsdp", None),
            P("fsdp", None),
            P("fsdp", None),
            P("fsdp", None),
            P("fsdp"),
            P("fsdp"),
        ),
        out_specs=(
            P("fsdp", "ctx", None),
            P("fsdp", "ctx", None),
            P("ctx", None),
            P("ctx", None),
            P("ctx", None),
            P("ctx", None),
            P("ctx"),
            P("ctx"),
        ),
        check_vma=False,
    )
```

```python
import functools
import math

import jax
import jax.numpy as jnp
import numpy as np
from jax import lax
from jax.experimental import pallas as pl
from jax.experimental.pallas import tpu as pltpu
from jax.sharding import PartitionSpec as P

FF = 1152
HEADS = 12
HEAD_DIM = 64
BLOCK = 128
PLANES = 4
HD = HEAD_DIM
HALF = HEAD_DIM // 2
HP = HEADS // PLANES
QW = HP * HEAD_DIM
rope_base = 160000.0
norm_eps = 1e-05
MASKED = -1e30


def ends_of(lengths_ref, count):
    ends, total = [], 0
    for i in range(count):
        total = total + lengths_ref[0, i]
        ends.append(total)
    return ends


def span_of(index, ends):
    begin, end = jnp.zeros_like(index), jnp.full_like(index, ends[0])
    for before, after in zip(ends[:-1], ends[1:]):
        begin = jnp.where(index >= before, before, begin)
        end = jnp.where(index >= before, after, end)
    return begin, end


def head_rows(x, head):
    rows = lax.broadcasted_iota(jnp.int32, x.shape, 0)
    return jnp.where((rows >= head * HD) & (rows < (head + 1) * HD), x, jnp.zeros_like(x))


def query_block(n, b, T, ends):
    S = n // PLANES
    me = lax.axis_index("ctx")
    base = (lax.rem(me // S + PLANES - b, PLANES) * S + lax.rem(me, S)) * T
    low_begin, low_end = span_of(base, ends)
    high_begin, high_end = span_of(base + T - 1, ends)
    low, high = low_begin // T, (high_end + T - 1) // T
    full_low = jnp.clip((high_begin + T - 1) // T, low, high)
    full_high = jnp.clip(low_end // T, full_low, high)
    begin, end = span_of(base + lax.broadcasted_iota(jnp.int32, (8, T), 1), ends)
    return (low, full_low, full_high, high), begin[0:1], end[0:1]


def over_units(bounds, step, sizes):
    low, full_low, full_high, high = bounds
    in_groups(low, full_low, lambda u: step(u, True), sizes[-2:])
    in_groups(full_low, full_high, lambda u: step(u, False), sizes)
    in_groups(full_high, high, lambda u: step(u, True), sizes[-2:])


def in_groups(begin, end, step, sizes):
    for size in sizes:
        count = (end - begin) // size

        def some(i, carry, size=size, begin=begin):
            for e in range(size):
                step(begin + size * i + e)
            return carry

        lax.fori_loop(0, count, some, 0)
        begin = begin + size * count


def fwd_kernel(n, count, lengths_ref, qt_ref, kv_ref, ot_ref, lowt_ref, lse_ref, values, scores, top, total, acc):
    units, T, _ = kv_ref.shape
    ends = ends_of(lengths_ref, count)

    def flip(u, carry):
        values[u] = kv_ref[u, :, 128:].T
        return carry

    lax.fori_loop(0, units, flip, 0, unroll=4)

    def one_query_block(b, carry):
        qt = qt_ref[b]
        qheads = [head_rows(qt, h) for h in range(HP)]
        bounds, q_start, q_end = query_block(n, b, T, ends)
        top[...] = jnp.full_like(top, MASKED)
        total[...] = jnp.zeros_like(total)
        acc[...] = jnp.zeros_like(acc)

        def score(u, masked):
            k = kv_ref[u, :, :QW]
            st = [jnp.dot(k, qheads[h], preferred_element_type=jnp.float32) for h in range(HP)]
            if masked:
                at = u * T + lax.broadcasted_iota(jnp.int32, (T, T), 0)
                allowed = (at >= q_start) & (at < q_end)
                st = [jnp.where(allowed, s, MASKED) for s in st]
            for h in range(HP):
                scores[u, h] = st[h]
                top[h] = jnp.maximum(top[h], jnp.max(st[h].reshape(T // 8, 8, T), axis=0))

        over_units(bounds, score, (2, 1))
        m = [jnp.max(top[h], axis=0, keepdims=True) for h in range(HP)]

        def gather(u):
            p = [jnp.exp(scores[u, h] - m[h]) for h in range(HP)]
            for h in range(HP):
                total[h] += jnp.sum(p[h].reshape(T // 8, 8, T), axis=0)
                rows = pl.ds(h * HD, HD)
                acc[rows, :] += jnp.dot(
                    values[u, pl.ds(HD + h * HD, HD), :], p[h].astype(jnp.bfloat16), preferred_element_type=jnp.float32
                )

        in_groups(bounds[0], bounds[3], gather, (4, 2, 1))
        for h in range(HP):
            rows = pl.ds(h * HD, HD)
            l = jnp.sum(total[h], axis=0, keepdims=True)
            o = acc[rows, :] / l
            ot_ref[b, rows, :] = o
            lowt_ref[b, rows, :] = o.astype(jnp.bfloat16)
            lse_ref[b, h : h + 1, :] = m[h] + jnp.log(l)
        return carry

    lax.fori_loop(0, qt_ref.shape[0], one_query_block, 0)


def attn_fwd(n, lengths, qt, kv):
    B, _, T = qt.shape
    U = kv.shape[0]
    sm, vm = pl.BlockSpec(memory_space=pltpu.SMEM), pl.BlockSpec(memory_space=pltpu.VMEM)
    return pl.pallas_call(
        functools.partial(fwd_kernel, n, lengths.shape[1]),
        out_shape=(
            jax.ShapeDtypeStruct((B, QW, T), jnp.float32),
            jax.ShapeDtypeStruct((B, QW, T), jnp.bfloat16),
            jax.ShapeDtypeStruct((B, 8, T), jnp.float32),
        ),
        in_specs=[sm, vm, vm],
        out_specs=(vm, vm, vm),
        scratch_shapes=[
            pltpu.VMEM((U, 256, T), jnp.bfloat16),
            pltpu.VMEM((U, HP, T, T), jnp.float32),
            pltpu.VMEM((HP, 8, T), jnp.float32),
            pltpu.VMEM((HP, 8, T), jnp.float32),
            pltpu.VMEM((QW, T), jnp.float32),
        ],
        compiler_params=pltpu.CompilerParams(vmem_limit_bytes=60 << 20),
    )(lengths, qt, kv)


def bwd_kernel(n, count, lengths_ref, qt_ref, kv_ref, ot_ref, lse_ref, gt_ref, dqt_ref, dkv_ref, keys, dk, dv, dq):
    units, T, _ = kv_ref.shape
    ends = ends_of(lengths_ref, count)

    def flip(u, carry):
        keys[u] = kv_ref[u, :, :256].T
        dk[u] = jnp.zeros_like(dk[u])
        dv[u] = jnp.zeros_like(dv[u])
        return carry

    lax.fori_loop(0, units, flip, 0, unroll=4)

    def one_query_block(b, carry):
        qt, gt = qt_ref[b], gt_ref[b]
        zero = jnp.zeros((HD, T), jnp.bfloat16)
        qheads = [head_rows(qt, h) for h in range(HP)]
        gheads = [head_rows(gt, h) for h in range(HP)]
        gpad = [jnp.concatenate([zero, x], axis=0) for x in gheads]
        lanes = lax.broadcasted_iota(jnp.int32, (T, 256), 1) // HD
        q, g = jnp.concatenate([qt, zero], axis=0).T, jnp.concatenate([zero, gt], axis=0).T
        q = jnp.concatenate([jnp.where(lanes == h, q, jnp.zeros_like(q)) for h in range(HP)], axis=0)
        g = jnp.concatenate([jnp.where(lanes == h + 1, g, jnp.zeros_like(g)) for h in range(HP)], axis=0)
        bounds, q_start, q_end = query_block(n, b, T, ends)
        prod = gt.astype(jnp.float32) * ot_ref[b]
        delta = [jnp.sum(prod[h * HD : (h + 1) * HD], axis=0, keepdims=True) for h in range(HP)]
        lse = [lse_ref[b, h : h + 1, :] for h in range(HP)]
        dq[...] = jnp.zeros_like(dq)

        def one_unit(u, masked):
            k, v = kv_ref[u, :, :QW], kv_ref[u, :, 128:]
            st = [jnp.dot(k, qheads[h], preferred_element_type=jnp.float32) for h in range(HP)]
            dp = [jnp.dot(v, gpad[h], preferred_element_type=jnp.float32) for h in range(HP)]
            st = [st[h] - lse[h] for h in range(HP)]
            if masked:
                at = u * T + lax.broadcasted_iota(jnp.int32, (T, T), 0)
                allowed = (at >= q_start) & (at < q_end)
                st = [jnp.where(allowed, s, MASKED) for s in st]
            p = [jnp.exp(s) for s in st]
            ds = [(p[h] * (dp[h] - delta[h])).astype(jnp.bfloat16) for h in range(HP)]
            p = [x.astype(jnp.bfloat16) for x in p]
            dv[u] += jnp.dot(jnp.concatenate(p, axis=1), g, preferred_element_type=jnp.float32)
            dk[u] += jnp.dot(jnp.concatenate(ds, axis=1), q, preferred_element_type=jnp.float32)
            for h in range(HP):
                rows = pl.ds(h * HD, HD)
                dq[rows, :] += jnp.dot(keys[u, rows, :], ds[h], preferred_element_type=jnp.float32)

        over_units(bounds, one_unit, (4, 2, 1))
        dqt_ref[b] = dq[...] * (HD**-0.5)
        return carry

    lax.fori_loop(0, qt_ref.shape[0], one_query_block, 0)

    def out(u, carry):
        dkv_ref[u, :, :128] = dk[u, :, :128].astype(jnp.bfloat16)
        dkv_ref[u, :, 128:256] = (dk[u, :, 128:] + dv[u, :, :128]).astype(jnp.bfloat16)
        dkv_ref[u, :, 256:] = dv[u, :, 128:].astype(jnp.bfloat16)
        return carry

    lax.fori_loop(0, units, out, 0, unroll=2)


def attn_bwd(n, lengths, qt, kv, ot, lse, gt):
    B, _, T = qt.shape
    U = kv.shape[0]
    sm, vm = pl.BlockSpec(memory_space=pltpu.SMEM), pl.BlockSpec(memory_space=pltpu.VMEM)
    return pl.pallas_call(
        functools.partial(bwd_kernel, n, lengths.shape[1]),
        out_shape=(jax.ShapeDtypeStruct((B, QW, T), jnp.float32), jax.ShapeDtypeStruct((U, T, 2 * QW), jnp.bfloat16)),
        in_specs=[sm] + [vm] * 5,
        out_specs=(vm, vm),
        scratch_shapes=[
            pltpu.VMEM((U, 256, T), jnp.bfloat16),
            pltpu.VMEM((U, T, 256), jnp.float32),
            pltpu.VMEM((U, T, 256), jnp.float32),
            pltpu.VMEM((QW, T), jnp.float32),
        ],
        compiler_params=pltpu.CompilerParams(vmem_limit_bytes=60 << 20),
    )(lengths, qt, kv, ot, lse, gt)
def front_kernel(
    n,
    groups,
    count,
    lengths_ref,
    tokens_ref,
    joint_ref,
    gain_one_ref,
    gain_two_ref,
    out_hbm,
    exp_hbm,
    con_hbm,
    first_ref,
    qt_ref,
    kv_ref,
    joint_t_out,
    turn_ref,
    gains_ref,
    out_all,
    exp_all,
    con_ref,
    held,
    t_sems,
    cols,
    cols_all,
    gain_held,
    g_sems,
    kv_own,
    kv_sems,
    own_sems,
    w_sems,
    w_local,
    joint_rows,
    out_held,
    exp_held,
    con_held,
):
    bf, f32 = jnp.bfloat16, jnp.float32
    S = n // PLANES
    S2 = S // 2
    T, D = tokens_ref.shape
    me, group = lax.axis_index("ctx"), lax.axis_index("fsdp")
    plane, side = me // S, lax.rem(me, S)
    s2, core = side // 2, lax.rem(side, 2)

    def at(p, a, c, g):
        return (p * S + a * 2 + c, g)

    def side_peer(k):
        return at(plane, lax.rem(s2 + k, S2), core, group)

    def group_peer(k):
        return at(plane, s2, core, lax.rem(group + k, groups))

    core_peer = at(plane, s2, 1 - core, group)

    def remote(source, target, sems, index, device):
        return pltpu.make_async_remote_copy(
            src_ref=source,
            dst_ref=target,
            send_sem=sems.at[0, index],
            recv_sem=sems.at[1, index],
            device_id=device,
            device_id_type=pl.DeviceIdType.MESH,
        )

    barrier = pltpu.get_barrier_semaphore()

    def greet(device):
        pl.semaphore_signal(barrier, inc=1, device_id=device, device_id_type=pl.DeviceIdType.MESH)

    for k in range(1, PLANES):
        greet(at(lax.rem(plane + k, PLANES), s2, core, group))
    for k in range(1, S2):
        greet(side_peer(k))
    for k in range(1, groups):
        greet(group_peer(k))
    greet(core_peer)
    pl.semaphore_wait(barrier, PLANES - 1 + S2 - 1 + groups - 1 + 1)

    def up(p):
        return remote(held.at[p], held.at[p], t_sems, p, at(plane + 1, s2, core, group))

    def down(p):
        return remote(held.at[p], held.at[p], t_sems, PLANES + p, at(plane - 1, s2, core, group))

    held[plane] = tokens_ref[...]

    @pl.when(plane < PLANES - 1)
    def _():
        up(plane).start()

    @pl.when(plane > 0)
    def _():
        down(plane).start()

    pair = 2 * QW
    for part in range(3):
        window = joint_ref[:, pl.ds(pl.multiple_of(part * D + plane // 2 * pair, 128), pair)].T
        chosen = jnp.where(lax.rem(plane, 2) == 0, window[:QW].astype(f32), window[QW:].astype(f32))
        half = 3 * QW // 2
        low, high = part * QW, (part + 1) * QW
        for c in range(2):
            begin, end = max(low, c * half), min(high, (c + 1) * half)
            if begin < end:
                cols[c, begin - c * half : end - c * half] = chosen[begin - low : end - low].astype(bf)
    gain_held[group] = jnp.zeros_like(gain_held[group])
    gain_held[group, 0:1] = gain_one_ref[...].astype(f32).reshape(1, -1)
    gain_held[group, 1:2] = gain_two_ref[...].astype(f32).reshape(1, -1)
    col_moves = [
        remote(cols.at[core], cols_all.at[group, core], g_sems, k - 1, group_peer(k)) for k in range(1, groups)
    ]
    col_hands = []
    for k in range(1, groups):
        came = cols_all.at[lax.rem(group + groups - k, groups), core]
        col_hands.append(remote(came, came, g_sems, 2 * (groups - 1) + k - 1, core_peer))
    gain_moves = [
        remote(gain_held.at[group], gain_held.at[group], g_sems, groups - 1 + k - 1, group_peer(k))
        for k in range(1, groups)
    ]
    for copy in gain_moves + col_moves:
        copy.start()
    cols_all[group] = cols[...]

    weights = [(out_hbm, out_all, out_held), (exp_hbm, exp_all, exp_held)]
    part = core if con_hbm.shape[0] == 2 else 0
    w_in = [pltpu.make_async_copy(con_hbm.at[part], con_held, w_local.at[0, len(weights)])]
    w_own = [pltpu.make_async_copy(con_held, con_ref, w_local.at[1, len(weights)])]
    w_first, w_second = [], []
    for i, (source, target, bounce) in enumerate(weights):
        w_in.append(pltpu.make_async_copy(source, bounce, w_local.at[0, i]))
        w_own.append(pltpu.make_async_copy(bounce, target.at[group], w_local.at[1, i]))
        for k in range(1, groups):
            index = (i * (groups - 1) + k - 1) * 2
            w_first.append(remote(source.at[core], target.at[group, core], w_sems, index, group_peer(k)))
            came = lax.rem(group + groups - k, groups)
            w_second.append(remote(target.at[came, core], target.at[came, core], w_sems, index + 1, core_peer))
    for copy in w_in:
        copy.start()
    for copy in w_first:
        copy.start()

    ends = ends_of(lengths_ref, count)
    row = lax.broadcasted_iota(jnp.int32, (HALF, T), 0)
    frequencies = jnp.zeros((HALF, T), f32)
    for i in range(HALF):
        frequencies = jnp.where(row == i, float(np.float32(rope_base ** (-2.0 * i / HEAD_DIM))), frequencies)
    for j in range(PLANES):
        base = (lax.rem(plane + PLANES - j, PLANES) * S + side) * T
        index = base + lax.broadcasted_iota(jnp.int32, (8, T), 1)
        begin, _ = span_of(index, ends)
        angles = (index - begin)[0:1].astype(f32) * frequencies
        turn_ref[j, :HALF] = jnp.cos(angles)
        turn_ref[j, HALF:] = jnp.sin(angles)

    strip = 64

    def kv_unit(p, a, c):
        return p * S + a * 2 + c

    def side_kv(j, k):
        p = lax.rem(plane + PLANES - j, PLANES)
        return remote(kv_own.at[j], kv_ref.at[kv_unit(p, s2, core)], kv_sems, j * (2 * S2 - 1) + k - 1, side_peer(k))

    def core_kv(j, k):
        p = lax.rem(plane + PLANES - j, PLANES)
        unit = kv_unit(p, lax.rem(s2 + S2 - k, S2), core)
        source = kv_own.at[j] if k == 0 else kv_ref.at[unit]
        return remote(source, kv_ref.at[unit], kv_sems, j * (2 * S2 - 1) + S2 - 1 + k, core_peer)

    def own_kv(j):
        p = lax.rem(plane + PLANES - j, PLANES)
        return pltpu.make_async_copy(kv_own.at[j], kv_ref.at[kv_unit(p, s2, core)], own_sems.at[j])

    def process(p):
        j = lax.rem(plane + PLANES - p, PLANES)

        def norm(i, carry):
            rows = pl.ds(pl.multiple_of(i * strip, strip), strip)
            values = held[p, rows].astype(f32)
            centred = values - jnp.mean(values, axis=-1, keepdims=True)
            spread = jnp.mean(centred * centred, axis=-1, keepdims=True)
            first_ref[j, rows] = (centred * lax.rsqrt(spread + norm_eps) * gains_ref[0:1]).astype(bf)
            return carry

        lax.fori_loop(0, T // strip, norm, 0)
        mixed = lax.dot_general(
            joint_t_out[: 3 * QW], first_ref[j], (((1,), (1,)), ((), ())), preferred_element_type=f32
        )
        cos, sin = turn_ref[j, :HALF], turn_ref[j, HALF:]
        turned = []
        for h in range(2 * HP):
            upper, lower = mixed[h * HD : h * HD + HALF], mixed[h * HD + HALF : (h + 1) * HD]
            turned += [upper * cos - lower * sin, lower * cos + upper * sin]
        q = jnp.concatenate(turned[: 2 * HP], axis=0).astype(bf)
        qt_ref[j] = (q.astype(f32) * HEAD_DIM**-0.5).astype(bf)
        kv_own[j] = jnp.concatenate(turned[2 * HP :] + [mixed[2 * QW :]], axis=0).T.astype(bf)
        for k in range(1, S2):
            side_kv(j, k).start()
        core_kv(j, 0).start()
        own_kv(j).start()

    def hand_on(t):
        @pl.when(plane >= t)
        def _():
            up(plane - t).wait_recv()

            @pl.when(plane < PLANES - 1)
            def _():
                up(plane - t).start()

        @pl.when(plane + t < PLANES)
        def _():
            down(plane + t).wait_recv()

            @pl.when(plane > 0)
            def _():
                down(plane + t).start()

    def process_arrived(t):
        below = jnp.where(plane >= t, 1, 0)
        above = jnp.where(plane + t < PLANES, 1, 0)

        def arrived(i, carry):
            process(jnp.where(i < below, plane - t, plane + t))
            return carry

        lax.fori_loop(0, below + above, arrived, 0)

    hand_on(1)
    for copy in gain_moves:
        copy.wait()
    share = D // groups
    total = jnp.zeros((8, D), f32)
    for g in range(groups):
        rows = lax.broadcasted_iota(jnp.int32, (share, D), 0)
        lanes = lax.broadcasted_iota(jnp.int32, (share, D), 1)
        place = jnp.where(lanes == rows + g * share, 1.0, 0.0).astype(bf)
        total = total + jnp.dot(gain_held[g].astype(bf), place, preferred_element_type=f32)
    gains_ref[...] = total
    for copy, hand in zip(col_moves, col_hands):
        copy.wait()
        hand.start()
    for copy in w_in:
        copy.wait()
    for copy in w_own:
        copy.start()
    for copy in col_hands:
        copy.wait()
    width = joint_t_out.shape[0]
    for g in range(groups):
        whole = jnp.concatenate([cols_all[g, 0], cols_all[g, 1], jnp.zeros((width - 3 * QW, share), bf)], axis=0)
        if share % 128 == 0:
            joint_t_out[:, g * share : (g + 1) * share] = whole
        else:
            joint_rows[g * share : (g + 1) * share] = whole.T
    if share % 128:
        for i in range(D // 128):
            joint_t_out[:, i * 128 : (i + 1) * 128] = joint_rows[i * 128 : (i + 1) * 128].T

    process(plane)
    process_arrived(1)
    hand_on(2)
    process_arrived(2)
    hand_on(3)
    for first_move, second_move in zip(w_first[: groups - 1], w_second):
        first_move.wait_recv()
        second_move.start()
    process_arrived(3)

    for j in range(PLANES):
        for k in range(1, S2):
            side_kv(j, k).wait_recv()
            core_kv(j, k).start()
    for first_move, second_move in zip(w_first[groups - 1 :], w_second[groups - 1 :]):
        first_move.wait_recv()
        second_move.start()

    for j in range(PLANES):
        own_kv(j).wait()
        for k in range(1, S2):
            side_kv(j, k).wait_send()
        for k in range(S2):
            core_kv(j, k).wait()
    for p in range(PLANES):

        @pl.when((plane < PLANES - 1) & (plane >= p))
        def _(p=p):
            up(p).wait_send()

        @pl.when((plane > 0) & (plane <= p))
        def _(p=p):
            down(p).wait_send()

    for copy in w_own:
        copy.wait()
    for first_move, second_move in zip(w_first, w_second):
        first_move.wait_send()
        second_move.wait()


def front(n, groups, lengths, tokens, joint_shard, gain_first, gain_second, out_w, exp_w, con_w):
    bf, f32 = jnp.bfloat16, jnp.float32
    S2 = n // PLANES // 2
    T, D = tokens.shape
    width = 3 * QW + 64
    share = D // groups
    any_, vm, sm = (pl.BlockSpec(memory_space=m) for m in (pl.ANY, pltpu.VMEM, pltpu.SMEM))
    sems = lambda count: pltpu.SemaphoreType.DMA((2, count))
    halves = lambda w: w.reshape(2, w.shape[0] // 2, w.shape[1])
    weights = [halves(w) for w in (out_w, exp_w)]
    con_w = con_w.reshape(2 if con_w.shape[0] % 32 == 0 else 1, -1, D)
    return pl.pallas_call(
        functools.partial(front_kernel, n, groups, lengths.shape[1]),
        out_shape=(
            jax.ShapeDtypeStruct((PLANES, T, D), bf),
            jax.ShapeDtypeStruct((PLANES, QW, T), bf),
            jax.ShapeDtypeStruct((n, T, 2 * QW), bf),
            jax.ShapeDtypeStruct((width, D), bf),
            jax.ShapeDtypeStruct((PLANES, 2 * HALF, T), f32),
            jax.ShapeDtypeStruct((8, D), f32),
            *[jax.ShapeDtypeStruct((groups, *w.shape), bf) for w in weights],
            jax.ShapeDtypeStruct(con_w.shape[1:], bf),
        ),
        in_specs=[sm, vm, vm, vm, vm, any_, any_, any_],
        out_specs=(vm, vm, any_, vm, vm, vm, any_, any_, any_),
        scratch_shapes=[
            pltpu.VMEM((PLANES, T, D), bf),
            sems(2 * PLANES),
            pltpu.VMEM((2, 3 * QW // 2, share), bf),
            pltpu.VMEM((groups, 2, 3 * QW // 2, share), bf),
            pltpu.VMEM((groups, 8, share), f32),
            sems(3 * (groups - 1)),
            pltpu.VMEM((PLANES, T, 2 * QW), bf),
            sems(PLANES * (2 * S2 - 1)),
            pltpu.SemaphoreType.DMA((PLANES,)),
            sems(2 * len(weights) * (groups - 1)),
            pltpu.SemaphoreType.DMA((2, len(weights) + 1)),
            pltpu.VMEM((D, width), bf),
            *[pltpu.VMEM(w.shape, bf) for w in weights],
            pltpu.VMEM(con_w.shape[1:], bf),
        ],
        compiler_params=pltpu.CompilerParams(collective_id=1, has_side_effects=True, vmem_limit_bytes=60 << 20),
    )(
        lengths,
        tokens,
        joint_shard,
        gain_first,
        gain_second,
        *weights,
        con_w,
    )


def middle_kernel(
    n,
    groups,
    low_ref,
    tokens_ref,
    cot_ref,
    gains_ref,
    out_hbm,
    exp_hbm,
    con_hbm,
    joint_hbm,
    *refs,
):
    con_got, refs = refs[: groups - 1], refs[groups - 1 :]
    (
        output_ref,
        grad_hidden_ref,
        gt_ref,
        y_keep,
        y_send,
        x_keep,
        x_send,
        z_keep,
        z_send_1,
        z_send_2,
        z_send_3,
        joint_near,
        out_w,
        exp_w,
        con_w,
        local_sems,
        c_sems,
        joint_shard,
        cols,
        cols_all,
        col_sems,
        joint_rows,
        att,
        a_sems,
        g_send,
        g_sems,
        hidden,
        second,
        branch,
        ga,
        act,
        gexp,
        acc,
        w_own,
        w_other,
        w_got,
        w_sems,
    ) = refs
    bf, f32 = jnp.bfloat16, jnp.float32
    S = n // PLANES
    S2 = S // 2
    T, D = tokens_ref.shape
    FFN = act.shape[1]
    me, group = lax.axis_index("ctx"), lax.axis_index("fsdp")
    plane, side = me // S, lax.rem(me, S)
    s2, core = side // 2, lax.rem(side, 2)

    def plane_peer(k):
        return (lax.rem(plane + k, PLANES) * S + side, group)

    core_peer = (plane * S + s2 * 2 + 1 - core, group)

    def group_peer(k):
        return (me, lax.rem(group + k, groups))


    def remote(source, target, sems, index, device):
        return pltpu.make_async_remote_copy(
            src_ref=source,
            dst_ref=target,
            send_sem=sems.at[0, index],
            recv_sem=sems.at[1, index],
            device_id=device,
            device_id_type=pl.DeviceIdType.MESH,
        )

    ff_share = con_hbm.shape[0]
    split = ff_share % 32 == 0

    def rows_of(g):
        return pl.ds(pl.multiple_of(g * ff_share, 16), ff_share)

    def half_of(g):
        if not split:
            return rows_of(g)
        half = ff_share // 2
        return pl.ds(pl.multiple_of(g * ff_share + core * half, 16), half)

    came = [half_of(lax.rem(group + groups - k, groups)) for k in range(1, groups)]
    con_hands = [remote(con_got[k], con_w.at[came[k]], c_sems, k, core_peer) for k in range(groups - 1)]
    con_local = [
        pltpu.make_async_copy(con_got[k], con_w.at[came[k]], local_sems.at[3 + k]) for k in range(groups - 1)
    ]
    local = [
        pltpu.make_async_copy(source, target, local_sems.at[i])
        for i, (source, target) in enumerate([(con_hbm, con_w.at[rows_of(group)]), (out_hbm, out_w), (exp_hbm, exp_w)])
    ]
    joint_local = pltpu.make_async_copy(joint_hbm, joint_shard, local_sems.at[3 + groups - 1])
    for copy in [joint_local] + local + con_local:
        copy.start()
    barrier = pltpu.get_barrier_semaphore()
    for k in range(1, PLANES):
        pl.semaphore_signal(barrier, inc=1, device_id=plane_peer(k), device_id_type=pl.DeviceIdType.MESH)
    pl.semaphore_signal(barrier, inc=1, device_id=core_peer, device_id_type=pl.DeviceIdType.MESH)
    for k in range(1, groups):
        pl.semaphore_signal(barrier, inc=1, device_id=group_peer(k), device_id_type=pl.DeviceIdType.MESH)
    pl.semaphore_wait(barrier, PLANES + groups - 1)

    home = [remote(low_ref.at[j], att.at[plane], a_sems, j - 1, plane_peer(PLANES - j)) for j in range(1, PLANES)]
    for copy in home + (con_hands if split else []):
        copy.start()
    att[plane] = low_ref[0]

    joint_local.wait()
    pair = 2 * QW
    for part in range(3):
        window = joint_shard[:, pl.ds(pl.multiple_of(part * D + plane // 2 * pair, 128), pair)].T
        chosen = jnp.where(lax.rem(plane, 2) == 1, window[:QW].astype(f32), window[QW:].astype(f32))
        half = 3 * QW // 2
        low, high = part * QW, (part + 1) * QW
        for c in range(2):
            begin, end = max(low, c * half), min(high, (c + 1) * half)
            if begin < end:
                cols[c, begin - c * half : end - c * half] = chosen[begin - low : end - low].astype(bf)
    col_moves = [
        remote(cols.at[core], cols_all.at[group, core], col_sems, k - 1, group_peer(k)) for k in range(1, groups)
    ]
    col_hands = []
    for k in range(1, groups):
        col_came = cols_all.at[lax.rem(group + groups - k, groups), core]
        col_hands.append(remote(col_came, col_came, col_sems, groups - 1 + k - 1, core_peer))
    for copy in col_moves:
        copy.start()
    cols_all[group] = cols[...]

    def nt(a, b):
        return lax.dot_general(a, b, (((1,), (1,)), ((), ())), preferred_element_type=f32)

    chunk = 384
    cot = cot_ref[...]
    local[0].wait()
    for copy in con_local + (con_hands if split else []):
        copy.wait()
    for c in range(0, FFN, chunk):
        ga[:, c : c + chunk] = nt(cot, con_w[c : c + chunk])
    local[1].wait()
    for copy in home:
        copy.wait()
    attended = att[...].reshape(D, T)
    hidden[...] = tokens_ref[...].astype(f32) + jnp.dot(attended.T, out_w[...], preferred_element_type=f32)

    strip = 64

    for copy, hand in zip(col_moves, col_hands):
        copy.wait()
        hand.start()

    def norm(i, carry):
        rows = pl.ds(pl.multiple_of(i * strip, strip), strip)
        values = hidden[rows]
        centred = values - jnp.mean(values, axis=-1, keepdims=True)
        spread = jnp.mean(centred * centred, axis=-1, keepdims=True)
        second[rows] = (centred * lax.rsqrt(spread + norm_eps) * gains_ref[1:2]).astype(bf)
        return carry

    lax.fori_loop(0, T // strip, norm, 0)
    local[2].wait()
    for c in range(0, FFN, chunk):
        cols, gate_cols = slice(c, c + chunk), slice(FFN + c, FFN + c + chunk)
        inner = jnp.dot(second[...], exp_w[:, cols], preferred_element_type=f32)
        gate = jnp.dot(second[...], exp_w[:, gate_cols], preferred_element_type=f32)
        share = 0.5 * (1.0 + lax.erf(inner * (0.5**0.5)))
        bent = inner * share
        act[:, cols] = (bent * gate).astype(bf)
        grad = ga[:, cols]
        slope = share + inner * jnp.exp(-0.5 * inner * inner) * ((2.0 * math.pi) ** -0.5)
        gexp[:, cols] = (grad * gate * slope).astype(bf)
        gexp[:, gate_cols] = (grad * bent).astype(bf)
    output_ref[...] = (hidden[...] + jnp.dot(act[...], con_w[...], preferred_element_type=f32)).astype(bf)
    acc[:T] = nt(gexp[...], exp_w[...])

    def norm_back(i, total):
        rows = pl.ds(pl.multiple_of(i * strip, strip), strip)
        values = hidden[rows]
        centred = values - jnp.mean(values, axis=-1, keepdims=True)
        scale = lax.rsqrt(jnp.mean(centred * centred, axis=-1, keepdims=True) + norm_eps)
        normal = centred * scale
        grad = acc[rows]
        total = total + jnp.sum(grad * normal, axis=0, keepdims=True)
        grad = grad * gains_ref[1:2]
        grad = grad - jnp.mean(grad, axis=-1, keepdims=True) - normal * jnp.mean(grad * normal, axis=-1, keepdims=True)
        back = cot_ref[rows].astype(f32) + grad * scale
        grad_hidden_ref[rows] = back
        branch[rows] = back.astype(bf)
        return total

    total = lax.fori_loop(0, T // strip, norm_back, jnp.zeros((1, D), f32))
    gain_two = jnp.broadcast_to(total, (8, D))
    for p in range(PLANES):
        g_send[p] = nt(out_w[p * QW : (p + 1) * QW], branch[...]).astype(bf)
    away = [
        remote(g_send.at[lax.rem(plane + k, PLANES)], gt_ref.at[k], g_sems, k - 1, plane_peer(k))
        for k in range(1, PLANES)
    ]
    for copy in away:
        copy.start()
    gt_ref[0] = g_send[plane]

    for copy in col_hands:
        copy.wait()
    share = D // groups
    for g in range(groups):
        whole = jnp.concatenate([cols_all[g, 0], cols_all[g, 1]], axis=0)
        if share % 128 == 0:
            joint_near[:, g * share : (g + 1) * share] = whole
        else:
            joint_rows[g * share : (g + 1) * share] = whole.T
    if share % 128:
        for i in range(D // 128):
            joint_near[:, i * 128 : (i + 1) * 128] = joint_rows[i * 128 : (i + 1) * 128].T

    sent = []

    def place(rows, offset, height):
        for target, parity in ((w_other, 1 - core), (w_own, core)):

            def body(m, carry):
                if rows % 8:
                    pair = acc[pl.ds(pl.multiple_of(2 * m * rows, 8), 2 * rows)]
                    value = jnp.where(parity == 0, pair[:rows], pair[rows:])
                else:
                    value = acc[pl.ds(pl.multiple_of((2 * m + parity) * rows, 8), rows)]
                if height > rows:
                    rest = jnp.zeros((height - rows - 8, D), f32)
                    value = jnp.concatenate([value, gain_two, rest], axis=0)
                value = value.astype(bf)
                target[m, offset : offset + height] = value
                return carry

            lax.fori_loop(0, n // 2, body, 0)
        part = pl.ds(offset, height)
        sent.append(remote(w_other.at[:, part], w_got.at[:, part], w_sems, len(sent), core_peer))
        sent[-1].start()

    rows = D // n
    wide = 2 * FFN // D
    for c in range(0, FFN, chunk):
        acc[c : c + chunk] = jnp.dot(act[:, c : c + chunk].T, cot_ref[...], preferred_element_type=f32)
    used = (1 + wide) * rows
    place(FFN // n, used, w_own.shape[1] - used)
    second_t = second[...].T
    for i in range(wide):
        acc[:D] = jnp.dot(second_t, gexp[:, i * D : (i + 1) * D], preferred_element_type=f32)
        place(rows, (1 + i) * rows, rows)
    acc[:D] = jnp.dot(attended, branch[...], preferred_element_type=f32)
    place(rows, 0, rows)

    for copy in sent:
        copy.wait()
    height = y_keep.shape[2]
    third = lambda g, i: pl.ds(pl.multiple_of((3 * g + i) * height, 16), height)

    def summed(m, part):
        return (w_own[m, part].astype(f32) + w_got[m, part].astype(f32)).astype(bf)

    def each(count, body):
        def step(i, carry):
            body(i)
            return carry

        lax.fori_loop(0, count, step, 0)

    for k in range(groups):
        g = lax.rem(group + k, groups)

        def first(m, k=k, g=g):
            (y_send.at[k - 1] if k else y_keep)[m // S2, lax.rem(m, S2)] = summed(m, third(g, 0))

        each(PLANES * S2, first)
    for k in range(S2):
        a = lax.rem(s2 + k, S2)

        def second_part(i, k=k, a=a):
            p, g = i // groups, lax.rem(i, groups)
            (x_send.at[k - 1] if k else x_keep)[p, g] = summed(p * S2 + a, third(g, 1))

        each(PLANES * groups, second_part)
    z_parts = [z_keep, z_send_1, z_send_2, z_send_3]
    for k in range(PLANES):
        p = lax.rem(plane + k, PLANES)

        def third_part(i, k=k, p=p):
            a, g = i // groups, lax.rem(i, groups)
            z_parts[k][a, g] = summed(p * S2 + a, third(g, 2))

        each(S2 * groups, third_part)
    for copy in away:
        copy.wait()


def middle(n, groups, lowt, tokens, cotangent, gains, out_w, exp_w, con_w, joint_shard, con_got):
    bf, f32 = jnp.bfloat16, jnp.float32
    S2 = n // PLANES // 2
    T, D = tokens.shape
    ffn = con_w.shape[0] * groups
    used = (D + 2 * ffn + ffn) // n + 8
    height = -(-used // (groups * 48)) * 16
    any_, vm = pl.BlockSpec(memory_space=pl.ANY), pl.BlockSpec(memory_space=pltpu.VMEM)
    sems = lambda count: pltpu.SemaphoreType.DMA((2, count))
    shape = lambda *s: jax.ShapeDtypeStruct(s, bf)
    half = (n // 2, 3 * groups * height, D)
    return pl.pallas_call(
        functools.partial(middle_kernel, n, groups),
        out_shape=(
            shape(T, D),
            jax.ShapeDtypeStruct((T, D), f32),
            shape(PLANES, QW, T),
            shape(PLANES, S2, height, D),
            shape(groups - 1, PLANES, S2, height, D),
            shape(PLANES, groups, height, D),
            shape(S2 - 1, PLANES, groups, height, D),
            shape(S2, groups, height, D),
            *[shape(S2, groups, height, D)] * (PLANES - 1),
            shape(3 * QW, D),
        ),
        in_specs=[vm, vm, vm, vm, any_, any_, any_, any_] + [any_] * (groups - 1),
        out_specs=tuple([vm] * 12),
        scratch_shapes=[
            pltpu.VMEM(out_w.shape, bf),
            pltpu.VMEM(exp_w.shape, bf),
            pltpu.VMEM((ffn, D), bf),
            pltpu.SemaphoreType.DMA((4 + groups - 1,)),
            sems(groups - 1),
            pltpu.VMEM(joint_shard.shape, bf),
            pltpu.VMEM((2, 3 * QW // 2, D // groups), bf),
            pltpu.VMEM((groups, 2, 3 * QW // 2, D // groups), bf),
            sems(2 * (groups - 1)),
            pltpu.VMEM((D, 3 * QW), bf),
            pltpu.VMEM((PLANES, QW, T), bf),
            sems(PLANES - 1),
            pltpu.VMEM((PLANES, QW, T), bf),
            sems(PLANES - 1),
            pltpu.VMEM((T, D), f32),
            pltpu.VMEM((T, D), bf),
            pltpu.VMEM((T, D), bf),
            pltpu.VMEM((T, ffn), f32),
            pltpu.VMEM((T, ffn), bf),
            pltpu.VMEM((T, 2 * ffn), bf),
            pltpu.VMEM((ffn, D), f32),
            pltpu.VMEM(half, bf),
            pltpu.VMEM(half, bf),
            pltpu.VMEM(half, bf),
            sems(2 + 2 * ffn // D),
        ],
        compiler_params=pltpu.CompilerParams(collective_id=2, has_side_effects=True, vmem_limit_bytes=60 << 20),
    )(lowt, tokens, cotangent, gains, out_w, exp_w, con_w, joint_shard, *con_got)


def tail_kernel(
    n,
    groups,
    deal_ref,
    dq_hbm,
    dkv_hbm,
    turn_ref,
    gains_ref,
    joint_hbm,
    joint_t_hbm,
    joint_near_hbm,
    first_hbm,
    tokens_hbm,
    grad_hidden_hbm,
    y_keep_hbm,
    y_got_hbm,
    x_keep_hbm,
    x_got_hbm,
    z_keep_hbm,
    z_got_1,
    z_got_2,
    z_got_3,
    d_got,
    w_all,
    jq_all,
    jk_all,
    joint_rows,
    joint_t,
    joint_near,
    first,
    tokens,
    grad_hidden,
    y_keep,
    y_got,
    x_keep,
    x_got,
    z_keep,
    z_came,
    local_sems,
    dq_ref,
    kv_own,
    own_sems,
    kv_near,
    kv_send,
    kv_far,
    kv_sems,
    mixed,
    mixed_got,
    mixed_send_sems,
    mixed_recv_sems,
    part,
    part_got,
    part_send_sems,
    part_recv_sems,
    j_acc,
    jq,
    jq_core,
    jq_side,
    jq_plane,
    jk,
    jk_core,
    jk_side,
    jk_plane,
    j_sems,
    x1_got,
    y2_got,
    y3_got,
    z1_got,
    z1_sems,
    x3_got,
    w_plane,
    w_plane_got,
    w_sems,
    d_send,
    d_mid,
    d_back,
    d_sems,
    row_sems,
    row_local,
):
    bf, f32 = jnp.bfloat16, jnp.float32
    S = n // PLANES
    S2 = S // 2
    T, D = tokens.shape
    me, group = lax.axis_index("ctx"), lax.axis_index("fsdp")
    plane, side = me // S, lax.rem(me, S)
    s2, core = side // 2, lax.rem(side, 2)
    MESH = pl.DeviceIdType.MESH

    def at(p, a, c, g):
        return (p * S + a * 2 + c, g)

    def plane_peer(k):
        return at(lax.rem(plane + k, PLANES), s2, core, group)

    def side_peer(k):
        return at(plane, lax.rem(s2 + k, S2), core, group)

    def group_peer(k):
        return at(plane, s2, core, lax.rem(group + k, groups))

    core_peer = at(plane, s2, 1 - core, group)

    def send(source, target, send_sem, recv_sem, device):
        return pltpu.make_async_remote_copy(
            src_ref=source, dst_ref=target, send_sem=send_sem, recv_sem=recv_sem, device_id=device, device_id_type=MESH
        )

    def remote(source, target, sems, index, device):
        return send(source, target, sems.at[0, index], sems.at[1, index], device)

    def total_of(terms):
        total = terms[0].astype(f32)
        for term in terms[1:]:
            total = total + term.astype(f32)
        return total

    lower = plane < 2
    middle = (plane == 1) | (plane == 2)
    order = [
        jnp.where(lower, 3, 0),
        jnp.where(plane == 0, 2, jnp.where(plane == 1, 0, jnp.where(plane == 2, 3, 1))),
        jnp.where((plane == 0) | (plane == 2), 1, 2),
        plane,
    ]
    steps = range(PLANES)
    back = [lax.rem(plane + PLANES - p, PLANES) for p in order]
    main = jnp.where(lower, 0, 1)
    main_plane = plane + 1 - 2 * main

    own_kv = [
        pltpu.make_async_copy(dkv_hbm.at[order[t], :, core], kv_own.at[t], own_sems.at[t]) for t in steps
    ] + [pltpu.make_async_copy(dq_hbm, dq_ref, own_sems.at[PLANES])]
    for copy in own_kv:
        copy.start()
    local = [
        pltpu.make_async_copy(source, target, local_sems.at[i])
        for i, (source, target) in enumerate(
            [
                (first_hbm, first),
                (joint_t_hbm, joint_t),
                (y_keep_hbm, y_keep),
                (y_got_hbm, y_got),
                (x_keep_hbm, x_keep),
                (x_got_hbm, x_got),
                (z_keep_hbm, z_keep),
                (z_got_1, z_came.at[0]),
                (z_got_2, z_came.at[1]),
                (z_got_3, z_came.at[2]),
                (tokens_hbm, tokens),
                (grad_hidden_hbm, grad_hidden),
                (joint_near_hbm, joint_near),
            ]
        )
    ]
    for i in (2, 3, 4, 5, 6, 7, 8, 9, 0, 1, 12, 10, 11):
        local[i].start()
    barrier = pltpu.get_barrier_semaphore()

    def greet(k, carry):
        pl.semaphore_signal(barrier, inc=1, device_id=(lax.rem(me + k, n), group), device_id_type=MESH)
        return carry

    lax.fori_loop(1, n, greet, 0)
    for k in range(1, groups):
        pl.semaphore_signal(barrier, inc=1, device_id=group_peer(k), device_id_type=MESH)
    pl.semaphore_wait(barrier, n - 1 + groups - 1)

    core_kv = [remote(dkv_hbm.at[order[t], :, 1 - core], kv_near.at[t], kv_sems, t, core_peer) for t in steps]
    for copy in core_kv:
        copy.start()

    per_group = joint_hbm.shape[0]
    index = me - group * per_group
    held_here = (index >= 0) & (index < per_group)
    row_own = pltpu.make_async_copy(joint_hbm.at[jnp.clip(index, 0, per_group - 1)], joint_rows, row_local.at[0])
    row_moves = [
        send(
            joint_hbm.at[jnp.clip(index, 0, per_group - 1)],
            joint_rows,
            row_sems.at[k - 1],
            row_sems.at[groups - 1],
            group_peer(k),
        )
        for k in range(1, groups)
    ]

    @pl.when(held_here)
    def _():
        row_own.start()
        for copy in row_moves:
            copy.start()

    w_moves = []

    def w_copy(source, target, device):
        copy = remote(source, target, w_sems, len(w_moves), device)
        w_moves.append(copy)
        copy.start()
        return copy

    local[2].wait()
    local[3].wait()
    for p in range(PLANES):
        for a in range(S2):
            y_keep[p, a] = total_of([y_keep[p, a]] + [y_got[k, p, a] for k in range(groups - 1)]).astype(bf)

    def z1_send(t, slot, target):
        return send(
            y_keep.at[order[t]], z1_got.at[slot], z1_sems.at[0, t], z1_sems.at[1, slot], at(target, s2, core, group)
        )

    def z1_add(t, slot):
        z1_send(0, slot, main_plane).wait_recv()
        for a in range(S2):
            y_keep[order[t], a] = total_of([y_keep[order[t], a], z1_got[slot, a]]).astype(bf)

    def z1_relay(t, slot, onward, target):
        @pl.when(middle)
        def _():
            z1_add(t, slot)
            z1_send(t, onward, target).start()

    @pl.when(jnp.logical_not(middle))
    def _():
        for t in range(PLANES - 1):
            z1_send(t, t, main_plane).start()


    def turned_back(x, t):
        cos, sin = turn_ref[back[t], :HALF], turn_ref[back[t], HALF:]
        rows = []
        for h in range(HP):
            upper, lower = x[h * HD : h * HD + HALF], x[h * HD + HALF : (h + 1) * HD]
            rows += [upper * cos + lower * sin, lower * cos - upper * sin]
        return jnp.concatenate(rows, axis=0)

    side_kv = {}
    for t in steps:
        own_kv[t].wait()
        core_kv[t].wait()
        for a in range(S2):
            kv_send[t, a] = total_of([kv_own[t, a], kv_near[t, a]]).astype(bf)
        for k in range(1, S2):
            side_kv[t, k] = remote(
                kv_send.at[t, lax.rem(s2 + S2 - k, S2)],
                kv_far.at[t, k - 1],
                kv_sems,
                PLANES + t * (S2 - 1) + k - 1,
                side_peer(S2 - k),
            )
            side_kv[t, k].start()
    own_kv[PLANES].wait()
    for t in steps:
        mixed[t, :QW] = turned_back(dq_ref[back[t]], t).astype(bf)

    local[4].wait()
    local[5].wait()
    for p in range(PLANES):
        for g in range(groups):
            x_keep[p, g] = total_of([x_keep[p, g]] + [x_got[k, p, g] for k in range(S2 - 1)]).astype(bf)
    y2 = [w_copy(x_keep.at[:, lax.rem(group + k, groups)], y2_got.at[k - 1], group_peer(k)) for k in range(1, groups)]
    for i in range(6, 10):
        local[i].wait()
    for a in range(S2):
        for g in range(groups):
            z_keep[a, g] = total_of([z_keep[a, g]] + [z_came[k, a, g] for k in range(PLANES - 1)]).astype(bf)
    y3 = [w_copy(z_keep.at[:, lax.rem(group + k, groups)], y3_got.at[k - 1], group_peer(k)) for k in range(1, groups)]

    j_moves = []

    def j_copy(source, target, device):
        copy = remote(source, target, j_sems, len(j_moves), device)
        j_moves.append(copy)
        copy.start()
        return copy

    def j_core_stage(begin, height, grads, near):
        j_acc[:height] = total_of(
            [
                jnp.dot(mixed[t, begin : begin + height], first[back[t]], preferred_element_type=f32)
                for t in steps
            ]
        )
        shard_rows = D // n
        for i in range(D // 128):
            block = j_acc[:height, i * 128 : (i + 1) * 128].T
            row = i * 128
            while row < (i + 1) * 128:
                shard, offset = divmod(row, shard_rows)
                count = min(shard_rows - offset, (i + 1) * 128 - row)
                source = row - i * 128
                grads[shard // S, shard % S // 2, shard % 2, offset : offset + count] = block[
                    source : source + count
                ].astype(bf)
                row += count
        return [j_copy(grads.at[:, :, 1 - core], near, core_peer)]

    def j_side_stage(moves, grads, near, far):
        for copy in moves:
            copy.wait()
        for p in range(PLANES):
            for a in range(S2):
                near[p, a] = total_of([grads[p, a, core], near[p, a]]).astype(bf)
        return [j_copy(near.at[:, lax.rem(s2 + k, S2)], far.at[k - 1], side_peer(k)) for k in range(1, S2)]

    def j_plane_stage(moves, near, far, gathered):
        for copy in moves:
            copy.wait()
        for p in range(PLANES):
            far[0, p] = total_of([near[p, s2]] + [far[k, p] for k in range(S2 - 1)]).astype(bf)
        gathered[plane] = far[0, plane]
        return [
            j_copy(far.at[0, lax.rem(plane + k, PLANES)], gathered.at[plane], plane_peer(k)) for k in range(1, PLANES)
        ]

    def j_group_stage(moves, gathered, every):
        for copy in moves:
            copy.wait()
        every[group] = gathered[...]
        return [j_copy(gathered, every.at[group], group_peer(k)) for k in range(1, groups)]

    local[0].wait()
    jq_moves = j_core_stage(0, QW, jq, jq_core)
    z1_relay(0, 0, 3, main_plane)

    local[1].wait()

    half = T // 2
    halves = range(2)

    def mixed_send(t, e):
        lanes = pl.ds(e * half, half)
        return send(
            mixed.at[t, :, lanes],
            mixed_got.at[t, :, lanes],
            mixed_send_sems.at[t, e],
            mixed_recv_sems.at[t, e],
            at(main_plane, s2, core, group),
        )

    def part_send(t, e, direction, target):
        rows = pl.ds(e * half, half)
        return send(
            part.at[t, rows],
            part_got.at[direction, order[t], rows],
            part_send_sems.at[t, e],
            part_recv_sems.at[direction * PLANES + order[t], e],
            at(target, s2, core, group),
        )

    def part_came(direction, p, e):
        rows = pl.ds(e * half, half)
        return send(
            part.at[0, rows],
            part_got.at[direction, p, rows],
            part_send_sems.at[0, e],
            part_recv_sems.at[direction * PLANES + p, e],
            core_peer,
        )

    other_plane = 2 * plane - main_plane

    def product(grads, columns):
        return jnp.dot(grads.T, columns, preferred_element_type=f32)

    def add_mixed(t, slot, e):
        mixed_send(slot, e).wait_recv()
        rows = slice(e * half, (e + 1) * half)
        near = product(mixed_got[slot, :, rows], joint_near[...])
        part[t, rows] = (part[t, rows].astype(f32) + near).astype(bf)

    def add_part(t, direction, p, e):
        part_came(direction, p, e).wait_recv()
        rows = slice(e * half, (e + 1) * half)
        part[t, rows] = total_of([part[t, rows], part_got[direction, p, rows]]).astype(bf)

    def relay(t, slot):
        @pl.when(middle)
        def _():
            for e in halves:
                if slot is None:
                    add_part(t, 1 - main, order[t], e)
                    part_send(t, e, 1 - main, other_plane).start()
                else:
                    add_mixed(t, slot, e)
                    part_send(t, e, main, main_plane).start()

    def key_step(t):
        for k in range(1, S2):
            side_kv[t, k].wait()
        dk = total_of([kv_send[t, s2]] + [kv_far[t, k] for k in range(S2 - 1)]).T
        mixed[t, QW : 2 * QW] = turned_back(dk[:QW], t).astype(bf)
        mixed[t, 2 * QW :] = dk[QW:].astype(bf)
        if t < PLANES - 1:

            @pl.when(jnp.logical_not(middle))
            def _():
                for e in halves:
                    mixed_send(t, e).start()

            @pl.when(middle)
            def _():
                part[t] = product(mixed[t], joint_t[: 3 * QW]).astype(bf)

        else:
            part[t] = product(mixed[t], joint_t[: 3 * QW]).astype(bf)

    local[12].wait()
    key_step(0)
    z1_relay(2, 1, 4, main_plane)
    jq_moves = j_side_stage(jq_moves, jq, jq_core, jq_side)
    key_step(1)
    z1_relay(1, 3, 5, 2 * plane - main_plane)
    for copy in y2:
        copy.wait()
    for p in range(PLANES):
        w_plane[p] = total_of([x_keep[p, group]] + [y2_got[k, p] for k in range(groups - 1)]).astype(bf)
    w_last = [
        w_copy(w_plane.at[lax.rem(plane + k, PLANES)], w_plane_got.at[k - 1], plane_peer(k)) for k in range(1, PLANES)
    ]
    key_step(2)
    relay(0, 0)
    jq_moves = j_plane_stage(jq_moves, jq_core, jq_side, jq_plane)
    key_step(3)
    relay(2, 1)
    jk_moves = j_core_stage(QW, 2 * QW, jk, jk_core)

    for copy in y3:
        copy.wait()
    for a in range(S2):
        z_keep[a, group] = total_of([z_keep[a, group]] + [y3_got[k, a] for k in range(groups - 1)]).astype(bf)
    x3 = [w_copy(z_keep.at[lax.rem(s2 + k, S2), group], x3_got.at[k - 1], side_peer(k)) for k in range(1, S2)]
    @pl.when(middle)
    def _():
        z1_add(PLANES - 1, 2)
        z1_add(PLANES - 1, 4)

    @pl.when(jnp.logical_not(middle))
    def _():
        z1_add(PLANES - 1, 5)

    x1 = [w_copy(y_keep.at[plane, lax.rem(s2 + k, S2)], x1_got.at[k - 1], side_peer(k)) for k in range(1, S2)]
    relay(1, None)
    jk_moves = j_side_stage(jk_moves, jk, jk_core, jk_side)
    jq_moves = j_group_stage(jq_moves, jq_plane, jq_all)

    local[10].wait()
    local[11].wait()
    @pl.when(middle)
    def _():
        for e in halves:
            add_mixed(PLANES - 1, 2, e)

    for e in halves:
        add_part(PLANES - 1, 1 - main, plane, e)

    strip = 64

    def norm_back(i, carry):
        rows = pl.ds(pl.multiple_of(i * strip, strip), strip)
        grad = part[PLANES - 1, rows].astype(f32)
        values = tokens[rows].astype(f32)
        centred = values - jnp.mean(values, axis=-1, keepdims=True)
        scale = lax.rsqrt(jnp.mean(centred * centred, axis=-1, keepdims=True) + norm_eps)
        normal = centred * scale
        grad = grad * gains_ref[0:1]
        grad = grad - jnp.mean(grad, axis=-1, keepdims=True) - normal * jnp.mean(grad * normal, axis=-1, keepdims=True)
        grad_hidden[rows] = grad_hidden[rows] + grad * scale
        return carry

    lax.fori_loop(0, T // strip, norm_back, 0)

    blocks = T // BLOCK
    piece = BLOCK // n

    def d_copy(source, target, base, k):
        return remote(source.at[lax.rem(me + k, n)], target.at[me], d_sems, base + k, (lax.rem(me + k, n), group))

    for i in range(n):
        d_send[i] = jnp.concatenate(
            [grad_hidden[b * BLOCK + i * piece : b * BLOCK + (i + 1) * piece] for b in range(blocks)], axis=0
        ).astype(bf)
    out_deal = [d_copy(d_send, d_mid, 0, k) for k in range(1, n)]
    for copy in out_deal:
        copy.start()
    d_mid[me] = d_send[me]

    for copy in x1 + w_last + x3:
        copy.wait()
    height = w_plane.shape[1]
    w_all[group, :height] = total_of([y_keep[plane, s2]] + [x1_got[k] for k in range(S2 - 1)]).astype(bf)
    w_all[group, height : 2 * height] = total_of(
        [w_plane[plane]] + [w_plane_got[k] for k in range(PLANES - 1)]
    ).astype(bf)
    w_all[group, 2 * height :] = total_of([z_keep[s2, group]] + [x3_got[k] for k in range(S2 - 1)]).astype(bf)
    w_gather = [w_copy(w_all.at[group], w_all.at[group], group_peer(k)) for k in range(1, groups)]
    jk_moves = j_plane_stage(jk_moves, jk_core, jk_side, jk_plane)

    for copy in out_deal:
        copy.wait()
    for i in range(n):
        chosen = []
        for b in range(blocks):
            wanted = deal_ref[i * blocks + b]
            held = d_mid[wanted // blocks].astype(f32)
            rows = held[:piece]
            for other in range(1, blocks):
                rows = jnp.where(lax.rem(wanted, blocks) == other, held[other * piece : (other + 1) * piece], rows)
            chosen.append(rows)
        d_back[i] = jnp.concatenate(chosen, axis=0).astype(bf)
    back_deal = [d_copy(d_back, d_got, n, k) for k in range(1, n)]
    for copy in back_deal:
        copy.start()
    d_got[me] = d_back[me]

    jk_moves = j_group_stage(jk_moves, jk_plane, jk_all)

    for copy in back_deal + w_gather + jq_moves + jk_moves:
        copy.wait()
    for t in range(PLANES - 1):
        z1_send(t, 0, main_plane).wait_send()
        for e in halves:

            @pl.when(middle)
            def _(t=t, e=e):
                part_send(t, e, main, main_plane).wait_send()

            @pl.when(jnp.logical_not(middle))
            def _(t=t, e=e):
                mixed_send(t, e).wait_send()

    @pl.when(held_here)
    def _():
        row_own.wait()
        for copy in row_moves:
            copy.wait_send()

    @pl.when(jnp.logical_not(held_here))
    def _():
        row_moves[0].wait_recv()


def tail(n, groups, deal, dqt, dkv, turn, gains, joint_shard, joint_t, joint_near, first, tokens, grad_hidden, pieces):
    bf, f32 = jnp.bfloat16, jnp.float32
    S2 = n // PLANES // 2
    T, D = tokens.shape
    rows = D // n
    height = pieces[0].shape[2]
    piece_rows = T // n
    joint_shard = joint_shard.reshape(-1, rows, joint_shard.shape[1])
    any_, vm, sm = (pl.BlockSpec(memory_space=m) for m in (pl.ANY, pltpu.VMEM, pltpu.SMEM))
    sems = lambda count: pltpu.SemaphoreType.DMA((2, count))
    small = lambda *s: pltpu.VMEM(s, bf)
    j_buffers = lambda w: [
        small(PLANES, S2, 2, rows, w),
        small(PLANES, S2, rows, w),
        small(S2 - 1, PLANES, rows, w),
        small(PLANES, rows, w),
    ]
    return pl.pallas_call(
        functools.partial(tail_kernel, n, groups),
        out_shape=(
            jax.ShapeDtypeStruct((n, piece_rows, D), bf),
            jax.ShapeDtypeStruct((groups, 3 * height, D), bf),
            jax.ShapeDtypeStruct((groups, PLANES, rows, QW), bf),
            jax.ShapeDtypeStruct((groups, PLANES, rows, 2 * QW), bf),
            jax.ShapeDtypeStruct(joint_shard.shape[1:], bf),
        ),
        in_specs=[sm, any_, any_, vm, vm] + [any_] * 14,
        out_specs=tuple([vm] * 4) + (any_,),
        scratch_shapes=[
            pltpu.VMEM(joint_t.shape, bf),
            pltpu.VMEM(joint_near.shape, bf),
            pltpu.VMEM((PLANES, T, D), bf),
            pltpu.VMEM((T, D), bf),
            pltpu.VMEM((T, D), f32),
            *[pltpu.VMEM(p.shape, bf) for p in pieces[:5]],
            pltpu.VMEM((PLANES - 1, *pieces[5].shape), bf),
            pltpu.SemaphoreType.DMA((13,)),
            pltpu.VMEM(dqt.shape, f32),
            small(PLANES, S2, T, 2 * QW),
            pltpu.SemaphoreType.DMA((PLANES + 1,)),
            small(PLANES, S2, T, 2 * QW),
            small(PLANES, S2, T, 2 * QW),
            small(PLANES, S2 - 1, T, 2 * QW),
            sems(PLANES * S2),
            small(PLANES, 3 * QW, T),
            small(PLANES - 1, 3 * QW, T),
            pltpu.SemaphoreType.DMA((PLANES - 1, 2)),
            pltpu.SemaphoreType.DMA((PLANES - 1, 2)),
            small(PLANES, T, D),
            small(2, PLANES, T, D),
            pltpu.SemaphoreType.DMA((PLANES - 1, 2)),
            pltpu.SemaphoreType.DMA((2 * PLANES, 2)),
            pltpu.VMEM((2 * QW, D), f32),
            *j_buffers(QW),
            *j_buffers(2 * QW),
            sems(2 * (1 + S2 - 1 + PLANES - 1 + groups - 1)),
            small(S2 - 1, height, D),
            small(groups - 1, PLANES, height, D),
            small(groups - 1, S2, height, D),
            small(6, S2, height, D),
            pltpu.SemaphoreType.DMA((2, 6)),
            small(S2 - 1, height, D),
            small(PLANES, height, D),
            small(PLANES - 1, height, D),
            sems(3 * (groups - 1) + 2 * (S2 - 1) + PLANES - 1),
            small(n, piece_rows, D),
            small(n, piece_rows, D),
            small(n, piece_rows, D),
            sems(2 * n),
            pltpu.SemaphoreType.DMA((groups,)),
            pltpu.SemaphoreType.DMA((1,)),
        ],
        compiler_params=pltpu.CompilerParams(collective_id=0, has_side_effects=True, vmem_limit_bytes=60 << 20),
    )(deal, dqt, dkv, turn, gains, joint_shard, joint_t, joint_near, first, tokens, grad_hidden, *pieces)


def finish_kernel(
    n,
    d_ref,
    w_ref,
    jq_ref,
    jk_ref,
    rows_ref,
    gains_ref,
    dealt_ref,
    joint_ref,
    output_ref,
    expand_ref,
    contract_ref,
    gain_one_ref,
    gain_two_ref,
):
    f32 = jnp.float32
    T, D = dealt_ref.shape
    blocks = T // BLOCK
    piece = BLOCK // n
    for b in range(blocks):
        for i in range(0, n, 2):
            rows = [d_ref[i + e].astype(f32)[b * piece : (b + 1) * piece] for e in range(2)]
            dealt_ref[b * BLOCK + i * piece : b * BLOCK + (i + 2) * piece] = jnp.concatenate(rows, axis=0).astype(
                dealt_ref.dtype
            )

    def summed(ref, p):
        total = ref[0, p].astype(f32)
        for g in range(1, ref.shape[0]):
            total = total + ref[g, p].astype(f32)
        return total.T

    for i in range(PLANES // 2):
        pair = [summed(jq_ref, 2 * i + e) for e in range(2)]
        joint_ref[:, i * 2 * QW : (i + 1) * 2 * QW] = jnp.concatenate(pair, axis=0).T
        pair = [summed(jk_ref, 2 * i + e) for e in range(2)]
        for part in range(2):
            cols = (part + 1) * D + i * 2 * QW
            rows = [x[part * QW : (part + 1) * QW] for x in pair]
            joint_ref[:, cols : cols + 2 * QW] = jnp.concatenate(rows, axis=0).T
    shift = D - lax.axis_index("ctx") * (D // n)

    def own_lanes(x):
        return pltpu.roll(jnp.broadcast_to(x, (8, D)), shift, 1)[0:1, : D // n]

    product = jnp.sum(joint_ref[...] * rows_ref[...].astype(f32), axis=1, keepdims=True)
    product = jnp.broadcast_to(product, (D // n, 128)).T[0:1]
    gain_one_ref[...] = product / own_lanes(gains_ref[0:1])
    height = w_ref.shape[1]
    rows = D // n
    targets = [(output_ref, 0, rows)]
    targets += [(expand_ref, i * D, rows) for i in range(expand_ref.shape[1] // D)]
    targets += [(contract_ref, 0, contract_ref.shape[0])]
    row = 0
    for target, column, count in targets:
        done = 0
        while done < count:
            g, offset = divmod(row, height)
            part = min(count - done, height - offset)
            target[done : done + part, column : column + D] = w_ref[g, offset : offset + part].astype(f32)
            done += part
            row += part
    g, offset = divmod(row, height)
    gain_two_ref[...] = own_lanes(w_ref[g, offset : offset + 1].astype(f32))


def finish(n, T, wide, contract_rows, d_got, w_all, jq_all, jk_all, joint_rows, gains):
    D = d_got.shape[-1]
    rows = D // n
    f32 = jnp.float32
    vm = pl.BlockSpec(memory_space=pltpu.VMEM)
    return pl.pallas_call(
        functools.partial(finish_kernel, n),
        out_shape=(
            jax.ShapeDtypeStruct((T, D), jnp.bfloat16),
            jax.ShapeDtypeStruct((rows, 3 * D), f32),
            jax.ShapeDtypeStruct((rows, D), f32),
            jax.ShapeDtypeStruct((rows, wide), f32),
            jax.ShapeDtypeStruct((contract_rows, D), f32),
            jax.ShapeDtypeStruct((1, rows), f32),
            jax.ShapeDtypeStruct((1, rows), f32),
        ),
        in_specs=[vm] * 6,
        out_specs=tuple([vm] * 7),
    )(d_got, w_all, jq_all, jk_all, joint_rows, gains)


def on_device(
    n,
    groups,
    tokens,
    cotangent,
    lengths,
    deal,
    joint_projection,
    output_projection,
    expand_weight,
    contract_weight,
    gain_first,
    gain_second,
):
    T, D = tokens.shape[1:]
    S = n // PLANES
    S2 = S // 2

    def over_planes(x, k):
        return lax.ppermute(x, "ctx", [(h * S + s, (h + k) % PLANES * S + s) for h in range(PLANES) for s in range(S)])

    def over_sides(x, k):
        pairs = [
            (h * S + a * 2 + c, h * S + (a + k) % S2 * 2 + c) for h in range(PLANES) for a in range(S2) for c in range(2)
        ]
        return lax.ppermute(x, "ctx", pairs)

    def over_groups(x, k):
        return lax.ppermute(x, "fsdp", [(f, (f + k) % groups) for f in range(groups)])

    def moved(x, over):
        if x.shape[0] == 1:
            return over(x, 1)
        return jnp.stack([over(x[k], k + 1) for k in range(x.shape[0])])

    first, qt, kv, joint_t, turn, gains, out_w, exp_w, con_half = front(
        n,
        groups,
        lengths,
        tokens[0],
        joint_projection,
        gain_first,
        gain_second,
        output_projection,
        expand_weight,
        contract_weight,
    )
    con_got = [over_groups(con_half, k) for k in range(1, groups)]
    out_w, exp_w = (w.reshape(-1, w.shape[-1]) for w in (out_w, exp_w))
    ot, lowt, lse = attn_fwd(n, lengths, qt, kv)
    output, grad_hidden, gt, y_keep, y_send, x_keep, x_send, z_keep, *z_send, joint_near = middle(
        n, groups, lowt, tokens[0], cotangent[0], gains, out_w, exp_w, contract_weight, joint_projection, con_got
    )
    y_got, x_got = moved(y_send, over_groups), moved(x_send, over_sides)
    z_got = [over_planes(part, k + 1) for k, part in enumerate(z_send)]
    dqt, dkv = attn_bwd(n, lengths, qt, kv, ot, lse, gt)
    d_got, w_all, jq_all, jk_all, joint_rows = tail(
        n,
        groups,
        deal[0],
        dqt,
        dkv.reshape(PLANES, S2, 2, T, 2 * QW),
        turn,
        gains,
        joint_projection,
        joint_t,
        joint_near,
        first,
        tokens[0],
        grad_hidden,
        [y_keep, y_got, x_keep, x_got, z_keep, *z_got],
    )
    dealt, shard_joint, shard_output, shard_expand, shard_contract, gain_one, gain_two = finish(
        n, T, exp_w.shape[1], contract_weight.shape[0] * groups // n, d_got, w_all, jq_all, jk_all, joint_rows, gains
    )
    return (
        output[None],
        dealt[None],
        shard_joint,
        shard_output,
        shard_expand,
        shard_contract,
        gain_one[0],
        gain_two[0],
    )


def solution(mesh):
    return jax.shard_map(
        functools.partial(on_device, mesh.shape["ctx"], mesh.shape["fsdp"]),
        mesh=mesh,
        in_specs=(
            P("fsdp", "ctx", None),
            P("fsdp", "ctx", None),
            P("fsdp", None),
            P("fsdp", None),
            P("fsdp", None),
            P("fsdp", None),
            P("fsdp", None),
            P("fsdp", None),
            P("fsdp"),
            P("fsdp"),
        ),
        out_specs=(
            P("fsdp", "ctx", None),
            P("fsdp", "ctx", None),
            P("ctx", None),
            P("ctx", None),
            P("ctx", None),
            P("ctx", None),
            P("ctx"),
            P("ctx"),
        ),
        check_vma=False,
    )
```

```python
import functools
import math

import jax
import jax.numpy as jnp
import numpy as np
from jax import lax
from jax.experimental import pallas as pl
from jax.experimental.pallas import tpu as pltpu
from jax.sharding import PartitionSpec as P

FF = 1152
HEADS = 12
HEAD_DIM = 64
BLOCK = 128
PLANES = 4
HD = HEAD_DIM
HALF = HEAD_DIM // 2
HP = HEADS // PLANES
QW = HP * HEAD_DIM
rope_base = 160000.0
norm_eps = 1e-05
MASKED = -1e30


def ends_of(lengths_ref, count):
    ends, total = [], 0
    for i in range(count):
        total = total + lengths_ref[0, i]
        ends.append(total)
    return ends


def span_of(index, ends):
    begin, end = jnp.zeros_like(index), jnp.full_like(index, ends[0])
    for before, after in zip(ends[:-1], ends[1:]):
        begin = jnp.where(index >= before, before, begin)
        end = jnp.where(index >= before, after, end)
    return begin, end


def head_rows(x, head):
    rows = lax.broadcasted_iota(jnp.int32, x.shape, 0)
    return jnp.where((rows >= head * HD) & (rows < (head + 1) * HD), x, jnp.zeros_like(x))


def query_block(n, b, T, ends):
    S = n // PLANES
    me = lax.axis_index("ctx")
    base = (lax.rem(me // S + PLANES - b, PLANES) * S + lax.rem(me, S)) * T
    low_begin, low_end = span_of(base, ends)
    high_begin, high_end = span_of(base + T - 1, ends)
    low, high = low_begin // T, (high_end + T - 1) // T
    full_low = jnp.clip((high_begin + T - 1) // T, low, high)
    full_high = jnp.clip(low_end // T, full_low, high)
    begin, end = span_of(base + lax.broadcasted_iota(jnp.int32, (8, T), 1), ends)
    return (low, full_low, full_high, high), begin[0:1], end[0:1]


def over_units(bounds, step, sizes):
    low, full_low, full_high, high = bounds
    in_groups(low, full_low, lambda u: step(u, True), sizes[-2:])
    in_groups(full_low, full_high, lambda u: step(u, False), sizes)
    in_groups(full_high, high, lambda u: step(u, True), sizes[-2:])


def in_groups(begin, end, step, sizes):
    for size in sizes:
        count = (end - begin) // size

        def some(i, carry, size=size, begin=begin):
            for e in range(size):
                step(begin + size * i + e)
            return carry

        lax.fori_loop(0, count, some, 0)
        begin = begin + size * count


def fwd_kernel(n, count, lengths_ref, qt_ref, kv_ref, ot_ref, lowt_ref, lse_ref, values, scores, top, total, acc):
    units, T, _ = kv_ref.shape
    ends = ends_of(lengths_ref, count)

    def flip(u, carry):
        values[u] = kv_ref[u, :, 128:].T
        return carry

    lax.fori_loop(0, units, flip, 0, unroll=4)

    def one_query_block(b, carry):
        qt = qt_ref[b]
        qheads = [head_rows(qt, h) for h in range(HP)]
        bounds, q_start, q_end = query_block(n, b, T, ends)
        top[...] = jnp.full_like(top, MASKED)
        total[...] = jnp.zeros_like(total)
        acc[...] = jnp.zeros_like(acc)

        def score(u, masked):
            k = kv_ref[u, :, :QW]
            st = [jnp.dot(k, qheads[h], preferred_element_type=jnp.float32) for h in range(HP)]
            if masked:
                at = u * T + lax.broadcasted_iota(jnp.int32, (T, T), 0)
                allowed = (at >= q_start) & (at < q_end)
                st = [jnp.where(allowed, s, MASKED) for s in st]
            for h in range(HP):
                scores[u, h] = st[h]
                top[h] = jnp.maximum(top[h], jnp.max(st[h].reshape(T // 8, 8, T), axis=0))

        over_units(bounds, score, (2, 1))
        m = [jnp.max(top[h], axis=0, keepdims=True) for h in range(HP)]

        def gather(u):
            p = [jnp.exp(scores[u, h] - m[h]) for h in range(HP)]
            for h in range(HP):
                total[h] += jnp.sum(p[h].reshape(T // 8, 8, T), axis=0)
                rows = pl.ds(h * HD, HD)
                acc[rows, :] += jnp.dot(
                    values[u, pl.ds(HD + h * HD, HD), :], p[h].astype(jnp.bfloat16), preferred_element_type=jnp.float32
                )

        in_groups(bounds[0], bounds[3], gather, (4, 2, 1))
        for h in range(HP):
            rows = pl.ds(h * HD, HD)
            l = jnp.sum(total[h], axis=0, keepdims=True)
            o = acc[rows, :] / l
            ot_ref[b, rows, :] = o
            lowt_ref[b, rows, :] = o.astype(jnp.bfloat16)
            lse_ref[b, h : h + 1, :] = m[h] + jnp.log(l)
        return carry

    lax.fori_loop(0, qt_ref.shape[0], one_query_block, 0)


def attn_fwd(n, lengths, qt, kv):
    B, _, T = qt.shape
    U = kv.shape[0]
    sm, vm = pl.BlockSpec(memory_space=pltpu.SMEM), pl.BlockSpec(memory_space=pltpu.VMEM)
    return pl.pallas_call(
        functools.partial(fwd_kernel, n, lengths.shape[1]),
        out_shape=(
            jax.ShapeDtypeStruct((B, QW, T), jnp.float32),
            jax.ShapeDtypeStruct((B, QW, T), jnp.bfloat16),
            jax.ShapeDtypeStruct((B, 8, T), jnp.float32),
        ),
        in_specs=[sm, vm, vm],
        out_specs=(vm, vm, vm),
        scratch_shapes=[
            pltpu.VMEM((U, 256, T), jnp.bfloat16),
            pltpu.VMEM((U, HP, T, T), jnp.float32),
            pltpu.VMEM((HP, 8, T), jnp.float32),
            pltpu.VMEM((HP, 8, T), jnp.float32),
            pltpu.VMEM((QW, T), jnp.float32),
        ],
        compiler_params=pltpu.CompilerParams(vmem_limit_bytes=60 << 20),
    )(lengths, qt, kv)


def bwd_kernel(n, count, lengths_ref, qt_ref, kv_ref, ot_ref, lse_ref, gt_ref, dqt_ref, dkv_ref, keys, dk, dv, dq):
    units, T, _ = kv_ref.shape
    ends = ends_of(lengths_ref, count)

    def flip(u, carry):
        keys[u] = kv_ref[u, :, :256].T
        dk[u] = jnp.zeros_like(dk[u])
        dv[u] = jnp.zeros_like(dv[u])
        return carry

    lax.fori_loop(0, units, flip, 0, unroll=4)

    def one_query_block(b, carry):
        qt, gt = qt_ref[b], gt_ref[b]
        zero = jnp.zeros((HD, T), jnp.bfloat16)
        qheads = [head_rows(qt, h) for h in range(HP)]
        gheads = [head_rows(gt, h) for h in range(HP)]
        gpad = [jnp.concatenate([zero, x], axis=0) for x in gheads]
        lanes = lax.broadcasted_iota(jnp.int32, (T, 256), 1) // HD
        q, g = jnp.concatenate([qt, zero], axis=0).T, jnp.concatenate([zero, gt], axis=0).T
        q = jnp.concatenate([jnp.where(lanes == h, q, jnp.zeros_like(q)) for h in range(HP)], axis=0)
        g = jnp.concatenate([jnp.where(lanes == h + 1, g, jnp.zeros_like(g)) for h in range(HP)], axis=0)
        bounds, q_start, q_end = query_block(n, b, T, ends)
        prod = gt.astype(jnp.float32) * ot_ref[b]
        delta = [jnp.sum(prod[h * HD : (h + 1) * HD], axis=0, keepdims=True) for h in range(HP)]
        lse = [lse_ref[b, h : h + 1, :] for h in range(HP)]
        dq[...] = jnp.zeros_like(dq)

        def one_unit(u, masked):
            k, v = kv_ref[u, :, :QW], kv_ref[u, :, 128:]
            st = [jnp.dot(k, qheads[h], preferred_element_type=jnp.float32) for h in range(HP)]
            dp = [jnp.dot(v, gpad[h], preferred_element_type=jnp.float32) for h in range(HP)]
            st = [st[h] - lse[h] for h in range(HP)]
            if masked:
                at = u * T + lax.broadcasted_iota(jnp.int32, (T, T), 0)
                allowed = (at >= q_start) & (at < q_end)
                st = [jnp.where(allowed, s, MASKED) for s in st]
            p = [jnp.exp(s) for s in st]
            ds = [(p[h] * (dp[h] - delta[h])).astype(jnp.bfloat16) for h in range(HP)]
            p = [x.astype(jnp.bfloat16) for x in p]
            dv[u] += jnp.dot(jnp.concatenate(p, axis=1), g, preferred_element_type=jnp.float32)
            dk[u] += jnp.dot(jnp.concatenate(ds, axis=1), q, preferred_element_type=jnp.float32)
            for h in range(HP):
                rows = pl.ds(h * HD, HD)
                dq[rows, :] += jnp.dot(keys[u, rows, :], ds[h], preferred_element_type=jnp.float32)

        over_units(bounds, one_unit, (4, 2, 1))
        dqt_ref[b] = dq[...] * (HD**-0.5)
        return carry

    lax.fori_loop(0, qt_ref.shape[0], one_query_block, 0)

    def out(u, carry):
        dkv_ref[u, :, :128] = dk[u, :, :128].astype(jnp.bfloat16)
        dkv_ref[u, :, 128:256] = (dk[u, :, 128:] + dv[u, :, :128]).astype(jnp.bfloat16)
        dkv_ref[u, :, 256:] = dv[u, :, 128:].astype(jnp.bfloat16)
        return carry

    lax.fori_loop(0, units, out, 0, unroll=2)


def attn_bwd(n, lengths, qt, kv, ot, lse, gt):
    B, _, T = qt.shape
    U = kv.shape[0]
    sm, vm = pl.BlockSpec(memory_space=pltpu.SMEM), pl.BlockSpec(memory_space=pltpu.VMEM)
    return pl.pallas_call(
        functools.partial(bwd_kernel, n, lengths.shape[1]),
        out_shape=(jax.ShapeDtypeStruct((B, QW, T), jnp.float32), jax.ShapeDtypeStruct((U, T, 2 * QW), jnp.bfloat16)),
        in_specs=[sm] + [vm] * 5,
        out_specs=(vm, vm),
        scratch_shapes=[
            pltpu.VMEM((U, 256, T), jnp.bfloat16),
            pltpu.VMEM((U, T, 256), jnp.float32),
            pltpu.VMEM((U, T, 256), jnp.float32),
            pltpu.VMEM((QW, T), jnp.float32),
        ],
        compiler_params=pltpu.CompilerParams(vmem_limit_bytes=60 << 20),
    )(lengths, qt, kv, ot, lse, gt)
def front_kernel(
    n,
    groups,
    count,
    lengths_ref,
    tokens_ref,
    joint_ref,
    gain_one_ref,
    gain_two_ref,
    out_hbm,
    exp_hbm,
    con_hbm,
    first_ref,
    qt_ref,
    kv_ref,
    joint_t_out,
    turn_ref,
    gains_ref,
    out_all,
    exp_all,
    con_ref,
    held,
    t_sems,
    cols,
    cols_all,
    gain_held,
    g_sems,
    kv_own,
    kv_sems,
    own_sems,
    w_sems,
    w_local,
    joint_rows,
    out_held,
    exp_held,
    con_held,
):
    bf, f32 = jnp.bfloat16, jnp.float32
    S = n // PLANES
    S2 = S // 2
    T, D = tokens_ref.shape
    me, group = lax.axis_index("ctx"), lax.axis_index("fsdp")
    plane, side = me // S, lax.rem(me, S)
    s2, core = side // 2, lax.rem(side, 2)

    def at(p, a, c, g):
        return (p * S + a * 2 + c, g)

    def side_peer(k):
        return at(plane, lax.rem(s2 + k, S2), core, group)

    def group_peer(k):
        return at(plane, s2, core, lax.rem(group + k, groups))

    core_peer = at(plane, s2, 1 - core, group)

    def remote(source, target, sems, index, device):
        return pltpu.make_async_remote_copy(
            src_ref=source,
            dst_ref=target,
            send_sem=sems.at[0, index],
            recv_sem=sems.at[1, index],
            device_id=device,
            device_id_type=pl.DeviceIdType.MESH,
        )

    barrier = pltpu.get_barrier_semaphore()

    def greet(device):
        pl.semaphore_signal(barrier, inc=1, device_id=device, device_id_type=pl.DeviceIdType.MESH)

    for k in range(1, PLANES):
        greet(at(lax.rem(plane + k, PLANES), s2, core, group))
    for k in range(1, S2):
        greet(side_peer(k))
    for k in range(1, groups):
        greet(group_peer(k))
    greet(core_peer)
    pl.semaphore_wait(barrier, PLANES - 1 + S2 - 1 + groups - 1 + 1)

    def up(p):
        return remote(held.at[p], held.at[p], t_sems, p, at(plane + 1, s2, core, group))

    def down(p):
        return remote(held.at[p], held.at[p], t_sems, PLANES + p, at(plane - 1, s2, core, group))

    held[plane] = tokens_ref[...]

    @pl.when(plane < PLANES - 1)
    def _():
        up(plane).start()

    @pl.when(plane > 0)
    def _():
        down(plane).start()

    pair = 2 * QW
    for part in range(3):
        window = joint_ref[:, pl.ds(pl.multiple_of(part * D + plane // 2 * pair, 128), pair)].T
        chosen = jnp.where(lax.rem(plane, 2) == 0, window[:QW].astype(f32), window[QW:].astype(f32))
        half = 3 * QW // 2
        low, high = part * QW, (part + 1) * QW
        for c in range(2):
            begin, end = max(low, c * half), min(high, (c + 1) * half)
            if begin < end:
                cols[c, begin - c * half : end - c * half] = chosen[begin - low : end - low].astype(bf)
    gain_held[group] = jnp.zeros_like(gain_held[group])
    gain_held[group, 0:1] = gain_one_ref[...].astype(f32).reshape(1, -1)
    gain_held[group, 1:2] = gain_two_ref[...].astype(f32).reshape(1, -1)
    col_moves = [
        remote(cols.at[core], cols_all.at[group, core], g_sems, k - 1, group_peer(k)) for k in range(1, groups)
    ]
    col_hands = []
    for k in range(1, groups):
        came = cols_all.at[lax.rem(group + groups - k, groups), core]
        col_hands.append(remote(came, came, g_sems, 2 * (groups - 1) + k - 1, core_peer))
    gain_moves = [
        remote(gain_held.at[group], gain_held.at[group], g_sems, groups - 1 + k - 1, group_peer(k))
        for k in range(1, groups)
    ]
    for copy in gain_moves + col_moves:
        copy.start()
    cols_all[group] = cols[...]

    weights = [(out_hbm, out_all, out_held), (exp_hbm, exp_all, exp_held)]
    part = core if con_hbm.shape[0] == 2 else 0
    w_in = [pltpu.make_async_copy(con_hbm.at[part], con_held, w_local.at[0, len(weights)])]
    w_own = [pltpu.make_async_copy(con_held, con_ref, w_local.at[1, len(weights)])]
    w_first, w_second = [], []
    for i, (source, target, bounce) in enumerate(weights):
        w_in.append(pltpu.make_async_copy(source, bounce, w_local.at[0, i]))
        w_own.append(pltpu.make_async_copy(bounce, target.at[group], w_local.at[1, i]))
        for k in range(1, groups):
            index = (i * (groups - 1) + k - 1) * 2
            w_first.append(remote(source.at[core], target.at[group, core], w_sems, index, group_peer(k)))
            came = lax.rem(group + groups - k, groups)
            w_second.append(remote(target.at[came, core], target.at[came, core], w_sems, index + 1, core_peer))
    for copy in w_in:
        copy.start()
    for copy in w_first:
        copy.start()

    ends = ends_of(lengths_ref, count)
    row = lax.broadcasted_iota(jnp.int32, (HALF, T), 0)
    frequencies = jnp.zeros((HALF, T), f32)
    for i in range(HALF):
        frequencies = jnp.where(row == i, float(np.float32(rope_base ** (-2.0 * i / HEAD_DIM))), frequencies)
    for j in range(PLANES):
        base = (lax.rem(plane + PLANES - j, PLANES) * S + side) * T
        index = base + lax.broadcasted_iota(jnp.int32, (8, T), 1)
        begin, _ = span_of(index, ends)
        angles = (index - begin)[0:1].astype(f32) * frequencies
        turn_ref[j, :HALF] = jnp.cos(angles)
        turn_ref[j, HALF:] = jnp.sin(angles)

    strip = 128

    def kv_unit(p, a, c):
        return p * S + a * 2 + c

    def side_kv(j, k):
        p = lax.rem(plane + PLANES - j, PLANES)
        return remote(kv_own.at[j], kv_ref.at[kv_unit(p, s2, core)], kv_sems, j * (2 * S2 - 1) + k - 1, side_peer(k))

    def core_kv(j, k):
        p = lax.rem(plane + PLANES - j, PLANES)
        unit = kv_unit(p, lax.rem(s2 + S2 - k, S2), core)
        source = kv_own.at[j] if k == 0 else kv_ref.at[unit]
        return remote(source, kv_ref.at[unit], kv_sems, j * (2 * S2 - 1) + S2 - 1 + k, core_peer)

    def own_kv(j):
        p = lax.rem(plane + PLANES - j, PLANES)
        return pltpu.make_async_copy(kv_own.at[j], kv_ref.at[kv_unit(p, s2, core)], own_sems.at[j])

    def process(p):
        j = lax.rem(plane + PLANES - p, PLANES)

        def norm(i, carry):
            rows = pl.ds(pl.multiple_of(i * strip, strip), strip)
            values = held[p, rows].astype(f32)
            centred = values - jnp.mean(values, axis=-1, keepdims=True)
            spread = jnp.mean(centred * centred, axis=-1, keepdims=True)
            first_ref[j, rows] = (centred * lax.rsqrt(spread + norm_eps) * gains_ref[0:1]).astype(bf)
            return carry

        lax.fori_loop(0, T // strip, norm, 0)
        mixed = lax.dot_general(
            joint_t_out[: 3 * QW], first_ref[j], (((1,), (1,)), ((), ())), preferred_element_type=f32
        )
        cos, sin = turn_ref[j, :HALF], turn_ref[j, HALF:]
        turned = []
        for h in range(2 * HP):
            upper, lower = mixed[h * HD : h * HD + HALF], mixed[h * HD + HALF : (h + 1) * HD]
            turned += [upper * cos - lower * sin, lower * cos + upper * sin]
        q = jnp.concatenate(turned[: 2 * HP], axis=0).astype(bf)
        qt_ref[j] = (q.astype(f32) * HEAD_DIM**-0.5).astype(bf)
        kv_own[j] = jnp.concatenate(turned[2 * HP :] + [mixed[2 * QW :]], axis=0).T.astype(bf)
        for k in range(1, S2):
            side_kv(j, k).start()
        core_kv(j, 0).start()
        own_kv(j).start()

    def hand_on(t):
        @pl.when(plane >= t)
        def _():
            up(plane - t).wait_recv()

            @pl.when(plane < PLANES - 1)
            def _():
                up(plane - t).start()

        @pl.when(plane + t < PLANES)
        def _():
            down(plane + t).wait_recv()

            @pl.when(plane > 0)
            def _():
                down(plane + t).start()

    def process_arrived(t):
        below = jnp.where(plane >= t, 1, 0)
        above = jnp.where(plane + t < PLANES, 1, 0)

        def arrived(i, carry):
            process(jnp.where(i < below, plane - t, plane + t))
            return carry

        lax.fori_loop(0, below + above, arrived, 0)

    hand_on(1)
    for copy in gain_moves:
        copy.wait()
    share = D // groups
    total = jnp.zeros((8, D), f32)
    for g in range(groups):
        rows = lax.broadcasted_iota(jnp.int32, (share, D), 0)
        lanes = lax.broadcasted_iota(jnp.int32, (share, D), 1)
        place = jnp.where(lanes == rows + g * share, 1.0, 0.0).astype(bf)
        total = total + jnp.dot(gain_held[g].astype(bf), place, preferred_element_type=f32)
    gains_ref[...] = total
    for copy, hand in zip(col_moves, col_hands):
        copy.wait()
        hand.start()
    for copy in w_in:
        copy.wait()
    for copy in w_own:
        copy.start()
    for copy in col_hands:
        copy.wait()
    width = joint_t_out.shape[0]
    for g in range(groups):
        whole = jnp.concatenate([cols_all[g, 0], cols_all[g, 1], jnp.zeros((width - 3 * QW, share), bf)], axis=0)
        if share % 128 == 0:
            joint_t_out[:, g * share : (g + 1) * share] = whole
        else:
            joint_rows[g * share : (g + 1) * share] = whole.T
    if share % 128:
        for i in range(D // 128):
            joint_t_out[:, i * 128 : (i + 1) * 128] = joint_rows[i * 128 : (i + 1) * 128].T

    process(plane)
    process_arrived(1)
    hand_on(2)
    process_arrived(2)
    hand_on(3)
    for first_move, second_move in zip(w_first[: groups - 1], w_second):
        first_move.wait_recv()
        second_move.start()
    process_arrived(3)

    for j in range(PLANES):
        for k in range(1, S2):
            side_kv(j, k).wait_recv()
            core_kv(j, k).start()
    for first_move, second_move in zip(w_first[groups - 1 :], w_second[groups - 1 :]):
        first_move.wait_recv()
        second_move.start()

    for j in range(PLANES):
        own_kv(j).wait()
        for k in range(1, S2):
            side_kv(j, k).wait_send()
        for k in range(S2):
            core_kv(j, k).wait()
    for p in range(PLANES):

        @pl.when((plane < PLANES - 1) & (plane >= p))
        def _(p=p):
            up(p).wait_send()

        @pl.when((plane > 0) & (plane <= p))
        def _(p=p):
            down(p).wait_send()

    for copy in w_own:
        copy.wait()
    for first_move, second_move in zip(w_first, w_second):
        first_move.wait_send()
        second_move.wait()


def front(n, groups, lengths, tokens, joint_shard, gain_first, gain_second, out_w, exp_w, con_w):
    bf, f32 = jnp.bfloat16, jnp.float32
    S2 = n // PLANES // 2
    T, D = tokens.shape
    width = 3 * QW + 64
    share = D // groups
    any_, vm, sm = (pl.BlockSpec(memory_space=m) for m in (pl.ANY, pltpu.VMEM, pltpu.SMEM))
    sems = lambda count: pltpu.SemaphoreType.DMA((2, count))
    halves = lambda w: w.reshape(2, w.shape[0] // 2, w.shape[1])
    weights = [halves(w) for w in (out_w, exp_w)]
    con_w = con_w.reshape(2 if con_w.shape[0] % 32 == 0 else 1, -1, D)
    return pl.pallas_call(
        functools.partial(front_kernel, n, groups, lengths.shape[1]),
        out_shape=(
            jax.ShapeDtypeStruct((PLANES, T, D), bf),
            jax.ShapeDtypeStruct((PLANES, QW, T), bf),
            jax.ShapeDtypeStruct((n, T, 2 * QW), bf),
            jax.ShapeDtypeStruct((width, D), bf),
            jax.ShapeDtypeStruct((PLANES, 2 * HALF, T), f32),
            jax.ShapeDtypeStruct((8, D), f32),
            *[jax.ShapeDtypeStruct((groups, *w.shape), bf) for w in weights],
            jax.ShapeDtypeStruct(con_w.shape[1:], bf),
        ),
        in_specs=[sm, vm, vm, vm, vm, any_, any_, any_],
        out_specs=(vm, vm, any_, vm, vm, vm, any_, any_, any_),
        scratch_shapes=[
            pltpu.VMEM((PLANES, T, D), bf),
            sems(2 * PLANES),
            pltpu.VMEM((2, 3 * QW // 2, share), bf),
            pltpu.VMEM((groups, 2, 3 * QW // 2, share), bf),
            pltpu.VMEM((groups, 8, share), f32),
            sems(3 * (groups - 1)),
            pltpu.VMEM((PLANES, T, 2 * QW), bf),
            sems(PLANES * (2 * S2 - 1)),
            pltpu.SemaphoreType.DMA((PLANES,)),
            sems(2 * len(weights) * (groups - 1)),
            pltpu.SemaphoreType.DMA((2, len(weights) + 1)),
            pltpu.VMEM((D, width), bf),
            *[pltpu.VMEM(w.shape, bf) for w in weights],
            pltpu.VMEM(con_w.shape[1:], bf),
        ],
        compiler_params=pltpu.CompilerParams(collective_id=1, has_side_effects=True, vmem_limit_bytes=60 << 20),
    )(
        lengths,
        tokens,
        joint_shard,
        gain_first,
        gain_second,
        *weights,
        con_w,
    )


def middle_kernel(
    n,
    groups,
    low_ref,
    tokens_ref,
    cot_ref,
    gains_ref,
    out_hbm,
    exp_hbm,
    con_hbm,
    joint_hbm,
    *refs,
):
    con_got, refs = refs[: groups - 1], refs[groups - 1 :]
    (
        output_ref,
        grad_hidden_ref,
        gt_ref,
        y_keep,
        y_send,
        x_keep,
        x_send,
        z_keep,
        z_send_1,
        z_send_2,
        z_send_3,
        joint_near,
        out_w,
        exp_w,
        con_w,
        local_sems,
        c_sems,
        joint_shard,
        cols,
        cols_all,
        col_sems,
        joint_rows,
        att,
        a_sems,
        g_send,
        g_sems,
        hidden,
        second,
        branch,
        ga,
        act,
        gexp,
        acc,
        w_own,
        w_other,
        w_got,
        w_sems,
    ) = refs
    bf, f32 = jnp.bfloat16, jnp.float32
    S = n // PLANES
    S2 = S // 2
    T, D = tokens_ref.shape
    FFN = act.shape[1]
    me, group = lax.axis_index("ctx"), lax.axis_index("fsdp")
    plane, side = me // S, lax.rem(me, S)
    s2, core = side // 2, lax.rem(side, 2)

    def plane_peer(k):
        return (lax.rem(plane + k, PLANES) * S + side, group)

    core_peer = (plane * S + s2 * 2 + 1 - core, group)

    def group_peer(k):
        return (me, lax.rem(group + k, groups))


    def remote(source, target, sems, index, device):
        return pltpu.make_async_remote_copy(
            src_ref=source,
            dst_ref=target,
            send_sem=sems.at[0, index],
            recv_sem=sems.at[1, index],
            device_id=device,
            device_id_type=pl.DeviceIdType.MESH,
        )

    ff_share = con_hbm.shape[0]
    split = ff_share % 32 == 0

    def rows_of(g):
        return pl.ds(pl.multiple_of(g * ff_share, 16), ff_share)

    def half_of(g):
        if not split:
            return rows_of(g)
        half = ff_share // 2
        return pl.ds(pl.multiple_of(g * ff_share + core * half, 16), half)

    came = [half_of(lax.rem(group + groups - k, groups)) for k in range(1, groups)]
    con_hands = [remote(con_got[k], con_w.at[came[k]], c_sems, k, core_peer) for k in range(groups - 1)]
    con_local = [
        pltpu.make_async_copy(con_got[k], con_w.at[came[k]], local_sems.at[3 + k]) for k in range(groups - 1)
    ]
    local = [
        pltpu.make_async_copy(source, target, local_sems.at[i])
        for i, (source, target) in enumerate([(con_hbm, con_w.at[rows_of(group)]), (out_hbm, out_w), (exp_hbm, exp_w)])
    ]
    joint_local = pltpu.make_async_copy(joint_hbm, joint_shard, local_sems.at[3 + groups - 1])
    for copy in [joint_local] + local + con_local:
        copy.start()
    barrier = pltpu.get_barrier_semaphore()
    for k in range(1, PLANES):
        pl.semaphore_signal(barrier, inc=1, device_id=plane_peer(k), device_id_type=pl.DeviceIdType.MESH)
    pl.semaphore_signal(barrier, inc=1, device_id=core_peer, device_id_type=pl.DeviceIdType.MESH)
    for k in range(1, groups):
        pl.semaphore_signal(barrier, inc=1, device_id=group_peer(k), device_id_type=pl.DeviceIdType.MESH)
    pl.semaphore_wait(barrier, PLANES + groups - 1)

    home = [remote(low_ref.at[j], att.at[plane], a_sems, j - 1, plane_peer(PLANES - j)) for j in range(1, PLANES)]
    for copy in home + (con_hands if split else []):
        copy.start()
    att[plane] = low_ref[0]

    joint_local.wait()
    pair = 2 * QW
    for part in range(3):
        window = joint_shard[:, pl.ds(pl.multiple_of(part * D + plane // 2 * pair, 128), pair)].T
        chosen = jnp.where(lax.rem(plane, 2) == 1, window[:QW].astype(f32), window[QW:].astype(f32))
        half = 3 * QW // 2
        low, high = part * QW, (part + 1) * QW
        for c in range(2):
            begin, end = max(low, c * half), min(high, (c + 1) * half)
            if begin < end:
                cols[c, begin - c * half : end - c * half] = chosen[begin - low : end - low].astype(bf)
    col_moves = [
        remote(cols.at[core], cols_all.at[group, core], col_sems, k - 1, group_peer(k)) for k in range(1, groups)
    ]
    col_hands = []
    for k in range(1, groups):
        col_came = cols_all.at[lax.rem(group + groups - k, groups), core]
        col_hands.append(remote(col_came, col_came, col_sems, groups - 1 + k - 1, core_peer))
    for copy in col_moves:
        copy.start()
    cols_all[group] = cols[...]

    def nt(a, b):
        return lax.dot_general(a, b, (((1,), (1,)), ((), ())), preferred_element_type=f32)

    chunk = 384
    cot = cot_ref[...]
    local[0].wait()
    for copy in con_local + (con_hands if split else []):
        copy.wait()
    for c in range(0, FFN, chunk):
        ga[:, c : c + chunk] = nt(cot, con_w[c : c + chunk])
    local[1].wait()
    for copy in home:
        copy.wait()
    attended = att[...].reshape(D, T)
    hidden[...] = tokens_ref[...].astype(f32) + jnp.dot(attended.T, out_w[...], preferred_element_type=f32)

    strip = 256

    for copy, hand in zip(col_moves, col_hands):
        copy.wait()
        hand.start()

    def norm(i, carry):
        rows = pl.ds(pl.multiple_of(i * strip, strip), strip)
        values = hidden[rows]
        centred = values - jnp.mean(values, axis=-1, keepdims=True)
        spread = jnp.mean(centred * centred, axis=-1, keepdims=True)
        second[rows] = (centred * lax.rsqrt(spread + norm_eps) * gains_ref[1:2]).astype(bf)
        return carry

    lax.fori_loop(0, T // strip, norm, 0)
    local[2].wait()
    for c in range(0, FFN, chunk):
        cols, gate_cols = slice(c, c + chunk), slice(FFN + c, FFN + c + chunk)
        inner = jnp.dot(second[...], exp_w[:, cols], preferred_element_type=f32)
        gate = jnp.dot(second[...], exp_w[:, gate_cols], preferred_element_type=f32)
        share = 0.5 * (1.0 + lax.erf(inner * (0.5**0.5)))
        bent = inner * share
        act[:, cols] = (bent * gate).astype(bf)
        grad = ga[:, cols]
        slope = share + inner * jnp.exp(-0.5 * inner * inner) * ((2.0 * math.pi) ** -0.5)
        gexp[:, cols] = (grad * gate * slope).astype(bf)
        gexp[:, gate_cols] = (grad * bent).astype(bf)
    output_ref[...] = (hidden[...] + jnp.dot(act[...], con_w[...], preferred_element_type=f32)).astype(bf)
    acc[:T] = nt(gexp[...], exp_w[...])

    def norm_back(i, total):
        rows = pl.ds(pl.multiple_of(i * strip, strip), strip)
        values = hidden[rows]
        centred = values - jnp.mean(values, axis=-1, keepdims=True)
        scale = lax.rsqrt(jnp.mean(centred * centred, axis=-1, keepdims=True) + norm_eps)
        normal = centred * scale
        grad = acc[rows]
        total = total + jnp.sum(grad * normal, axis=0, keepdims=True)
        grad = grad * gains_ref[1:2]
        grad = grad - jnp.mean(grad, axis=-1, keepdims=True) - normal * jnp.mean(grad * normal, axis=-1, keepdims=True)
        back = cot_ref[rows].astype(f32) + grad * scale
        grad_hidden_ref[rows] = back
        branch[rows] = back.astype(bf)
        return total

    total = lax.fori_loop(0, T // strip, norm_back, jnp.zeros((1, D), f32))
    gain_two = jnp.broadcast_to(total, (8, D))
    for p in range(PLANES):
        g_send[p] = nt(out_w[p * QW : (p + 1) * QW], branch[...]).astype(bf)
    away = [
        remote(g_send.at[lax.rem(plane + k, PLANES)], gt_ref.at[k], g_sems, k - 1, plane_peer(k))
        for k in range(1, PLANES)
    ]
    for copy in away:
        copy.start()
    gt_ref[0] = g_send[plane]

    for copy in col_hands:
        copy.wait()
    share = D // groups
    for g in range(groups):
        whole = jnp.concatenate([cols_all[g, 0], cols_all[g, 1]], axis=0)
        if share % 128 == 0:
            joint_near[:, g * share : (g + 1) * share] = whole
        else:
            joint_rows[g * share : (g + 1) * share] = whole.T
    if share % 128:
        for i in range(D // 128):
            joint_near[:, i * 128 : (i + 1) * 128] = joint_rows[i * 128 : (i + 1) * 128].T

    sent = []

    def place(rows, offset, height):
        for target, parity in ((w_other, 1 - core), (w_own, core)):

            def body(m, carry):
                if rows % 8:
                    pair = acc[pl.ds(pl.multiple_of(2 * m * rows, 8), 2 * rows)]
                    value = jnp.where(parity == 0, pair[:rows], pair[rows:])
                else:
                    value = acc[pl.ds(pl.multiple_of((2 * m + parity) * rows, 8), rows)]
                if height > rows:
                    rest = jnp.zeros((height - rows - 8, D), f32)
                    value = jnp.concatenate([value, gain_two, rest], axis=0)
                value = value.astype(bf)
                target[m, offset : offset + height] = value
                return carry

            lax.fori_loop(0, n // 2, body, 0)
        part = pl.ds(offset, height)
        sent.append(remote(w_other.at[:, part], w_got.at[:, part], w_sems, len(sent), core_peer))
        sent[-1].start()

    rows = D // n
    wide = 2 * FFN // D
    for c in range(0, FFN, chunk):
        acc[c : c + chunk] = jnp.dot(act[:, c : c + chunk].T, cot_ref[...], preferred_element_type=f32)
    used = (1 + wide) * rows
    place(FFN // n, used, w_own.shape[1] - used)
    second_t = second[...].T
    for i in range(wide):
        acc[:D] = jnp.dot(second_t, gexp[:, i * D : (i + 1) * D], preferred_element_type=f32)
        place(rows, (1 + i) * rows, rows)
    acc[:D] = jnp.dot(attended, branch[...], preferred_element_type=f32)
    place(rows, 0, rows)

    for copy in sent:
        copy.wait()
    height = y_keep.shape[2]
    third = lambda g, i: pl.ds(pl.multiple_of((3 * g + i) * height, 16), height)

    def summed(m, part):
        return (w_own[m, part].astype(f32) + w_got[m, part].astype(f32)).astype(bf)

    def each(count, body):
        def step(i, carry):
            body(i)
            return carry

        lax.fori_loop(0, count, step, 0)

    for k in range(groups):
        g = lax.rem(group + k, groups)

        def first(m, k=k, g=g):
            (y_send.at[k - 1] if k else y_keep)[m // S2, lax.rem(m, S2)] = summed(m, third(g, 0))

        each(PLANES * S2, first)
    for k in range(S2):
        a = lax.rem(s2 + k, S2)

        def second_part(i, k=k, a=a):
            p, g = i // groups, lax.rem(i, groups)
            (x_send.at[k - 1] if k else x_keep)[p, g] = summed(p * S2 + a, third(g, 1))

        each(PLANES * groups, second_part)
    z_parts = [z_keep, z_send_1, z_send_2, z_send_3]
    for k in range(PLANES):
        p = lax.rem(plane + k, PLANES)

        def third_part(i, k=k, p=p):
            a, g = i // groups, lax.rem(i, groups)
            z_parts[k][a, g] = summed(p * S2 + a, third(g, 2))

        each(S2 * groups, third_part)
    for copy in away:
        copy.wait()


def middle(n, groups, lowt, tokens, cotangent, gains, out_w, exp_w, con_w, joint_shard, con_got):
    bf, f32 = jnp.bfloat16, jnp.float32
    S2 = n // PLANES // 2
    T, D = tokens.shape
    ffn = con_w.shape[0] * groups
    used = (D + 2 * ffn + ffn) // n + 8
    height = -(-used // (groups * 48)) * 16
    any_, vm = pl.BlockSpec(memory_space=pl.ANY), pl.BlockSpec(memory_space=pltpu.VMEM)
    sems = lambda count: pltpu.SemaphoreType.DMA((2, count))
    shape = lambda *s: jax.ShapeDtypeStruct(s, bf)
    half = (n // 2, 3 * groups * height, D)
    return pl.pallas_call(
        functools.partial(middle_kernel, n, groups),
        out_shape=(
            shape(T, D),
            jax.ShapeDtypeStruct((T, D), f32),
            shape(PLANES, QW, T),
            shape(PLANES, S2, height, D),
            shape(groups - 1, PLANES, S2, height, D),
            shape(PLANES, groups, height, D),
            shape(S2 - 1, PLANES, groups, height, D),
            shape(S2, groups, height, D),
            *[shape(S2, groups, height, D)] * (PLANES - 1),
            shape(3 * QW, D),
        ),
        in_specs=[vm, vm, vm, vm, any_, any_, any_, any_] + [any_] * (groups - 1),
        out_specs=tuple([vm] * 12),
        scratch_shapes=[
            pltpu.VMEM(out_w.shape, bf),
            pltpu.VMEM(exp_w.shape, bf),
            pltpu.VMEM((ffn, D), bf),
            pltpu.SemaphoreType.DMA((4 + groups - 1,)),
            sems(groups - 1),
            pltpu.VMEM(joint_shard.shape, bf),
            pltpu.VMEM((2, 3 * QW // 2, D // groups), bf),
            pltpu.VMEM((groups, 2, 3 * QW // 2, D // groups), bf),
            sems(2 * (groups - 1)),
            pltpu.VMEM((D, 3 * QW), bf),
            pltpu.VMEM((PLANES, QW, T), bf),
            sems(PLANES - 1),
            pltpu.VMEM((PLANES, QW, T), bf),
            sems(PLANES - 1),
            pltpu.VMEM((T, D), f32),
            pltpu.VMEM((T, D), bf),
            pltpu.VMEM((T, D), bf),
            pltpu.VMEM((T, ffn), f32),
            pltpu.VMEM((T, ffn), bf),
            pltpu.VMEM((T, 2 * ffn), bf),
            pltpu.VMEM((ffn, D), f32),
            pltpu.VMEM(half, bf),
            pltpu.VMEM(half, bf),
            pltpu.VMEM(half, bf),
            sems(2 + 2 * ffn // D),
        ],
        compiler_params=pltpu.CompilerParams(collective_id=2, has_side_effects=True, vmem_limit_bytes=60 << 20),
    )(lowt, tokens, cotangent, gains, out_w, exp_w, con_w, joint_shard, *con_got)


def tail_kernel(
    n,
    groups,
    deal_ref,
    dq_hbm,
    dkv_hbm,
    turn_ref,
    gains_ref,
    joint_hbm,
    joint_t_hbm,
    joint_near_hbm,
    first_hbm,
    tokens_hbm,
    grad_hidden_hbm,
    y_keep_hbm,
    y_got_hbm,
    x_keep_hbm,
    x_got_hbm,
    z_keep_hbm,
    z_got_1,
    z_got_2,
    z_got_3,
    d_got,
    w_all,
    jq_all,
    jk_all,
    joint_rows,
    joint_t,
    joint_near,
    first,
    tokens,
    grad_hidden,
    y_keep,
    y_got,
    x_keep,
    x_got,
    z_keep,
    z_came,
    local_sems,
    dq_ref,
    kv_own,
    own_sems,
    kv_near,
    kv_send,
    kv_far,
    kv_sems,
    mixed,
    mixed_got,
    mixed_send_sems,
    mixed_recv_sems,
    part,
    part_got,
    part_send_sems,
    part_recv_sems,
    j_acc,
    jq,
    jq_core,
    jq_side,
    jq_plane,
    jk,
    jk_core,
    jk_side,
    jk_plane,
    j_sems,
    x1_got,
    y2_got,
    y3_got,
    z1_got,
    z1_sems,
    x3_got,
    w_plane,
    w_plane_got,
    w_sems,
    d_send,
    d_mid,
    d_back,
    d_sems,
    row_sems,
    row_local,
):
    bf, f32 = jnp.bfloat16, jnp.float32
    S = n // PLANES
    S2 = S // 2
    T, D = tokens.shape
    me, group = lax.axis_index("ctx"), lax.axis_index("fsdp")
    plane, side = me // S, lax.rem(me, S)
    s2, core = side // 2, lax.rem(side, 2)
    MESH = pl.DeviceIdType.MESH

    def at(p, a, c, g):
        return (p * S + a * 2 + c, g)

    def plane_peer(k):
        return at(lax.rem(plane + k, PLANES), s2, core, group)

    def side_peer(k):
        return at(plane, lax.rem(s2 + k, S2), core, group)

    def group_peer(k):
        return at(plane, s2, core, lax.rem(group + k, groups))

    core_peer = at(plane, s2, 1 - core, group)

    def send(source, target, send_sem, recv_sem, device):
        return pltpu.make_async_remote_copy(
            src_ref=source, dst_ref=target, send_sem=send_sem, recv_sem=recv_sem, device_id=device, device_id_type=MESH
        )

    def remote(source, target, sems, index, device):
        return send(source, target, sems.at[0, index], sems.at[1, index], device)

    def total_of(terms):
        total = terms[0].astype(f32)
        for term in terms[1:]:
            total = total + term.astype(f32)
        return total

    lower = plane < 2
    middle = (plane == 1) | (plane == 2)
    order = [
        jnp.where(lower, 3, 0),
        jnp.where(plane == 0, 2, jnp.where(plane == 1, 0, jnp.where(plane == 2, 3, 1))),
        jnp.where((plane == 0) | (plane == 2), 1, 2),
        plane,
    ]
    steps = range(PLANES)
    back = [lax.rem(plane + PLANES - p, PLANES) for p in order]
    main = jnp.where(lower, 0, 1)
    main_plane = plane + 1 - 2 * main

    own_kv = [
        pltpu.make_async_copy(dkv_hbm.at[order[t], :, core], kv_own.at[t], own_sems.at[t]) for t in steps
    ] + [pltpu.make_async_copy(dq_hbm, dq_ref, own_sems.at[PLANES])]
    for copy in own_kv:
        copy.start()
    local = [
        pltpu.make_async_copy(source, target, local_sems.at[i])
        for i, (source, target) in enumerate(
            [
                (first_hbm, first),
                (joint_t_hbm, joint_t),
                (y_keep_hbm, y_keep),
                (y_got_hbm, y_got),
                (x_keep_hbm, x_keep),
                (x_got_hbm, x_got),
                (z_keep_hbm, z_keep),
                (z_got_1, z_came.at[0]),
                (z_got_2, z_came.at[1]),
                (z_got_3, z_came.at[2]),
                (tokens_hbm, tokens),
                (grad_hidden_hbm, grad_hidden),
                (joint_near_hbm, joint_near),
            ]
        )
    ]
    for i in (2, 3, 4, 5, 6, 7, 8, 9, 0, 1, 12, 10, 11):
        local[i].start()
    barrier = pltpu.get_barrier_semaphore()

    def greet(k, carry):
        pl.semaphore_signal(barrier, inc=1, device_id=(lax.rem(me + k, n), group), device_id_type=MESH)
        return carry

    lax.fori_loop(1, n, greet, 0)
    for k in range(1, groups):
        pl.semaphore_signal(barrier, inc=1, device_id=group_peer(k), device_id_type=MESH)
    pl.semaphore_wait(barrier, n - 1 + groups - 1)

    core_kv = [remote(dkv_hbm.at[order[t], :, 1 - core], kv_near.at[t], kv_sems, t, core_peer) for t in steps]
    for copy in core_kv:
        copy.start()

    per_group = joint_hbm.shape[0]
    index = me - group * per_group
    held_here = (index >= 0) & (index < per_group)
    row_own = pltpu.make_async_copy(joint_hbm.at[jnp.clip(index, 0, per_group - 1)], joint_rows, row_local.at[0])
    row_moves = [
        send(
            joint_hbm.at[jnp.clip(index, 0, per_group - 1)],
            joint_rows,
            row_sems.at[k - 1],
            row_sems.at[groups - 1],
            group_peer(k),
        )
        for k in range(1, groups)
    ]

    @pl.when(held_here)
    def _():
        row_own.start()
        for copy in row_moves:
            copy.start()

    w_moves = []

    def w_copy(source, target, device):
        copy = remote(source, target, w_sems, len(w_moves), device)
        w_moves.append(copy)
        copy.start()
        return copy

    local[2].wait()
    local[3].wait()
    for p in range(PLANES):
        for a in range(S2):
            y_keep[p, a] = total_of([y_keep[p, a]] + [y_got[k, p, a] for k in range(groups - 1)]).astype(bf)

    def z1_send(t, slot, target):
        return send(
            y_keep.at[order[t]], z1_got.at[slot], z1_sems.at[0, t], z1_sems.at[1, slot], at(target, s2, core, group)
        )

    def z1_add(t, slot):
        z1_send(0, slot, main_plane).wait_recv()
        for a in range(S2):
            y_keep[order[t], a] = total_of([y_keep[order[t], a], z1_got[slot, a]]).astype(bf)

    def z1_relay(t, slot, onward, target):
        @pl.when(middle)
        def _():
            z1_add(t, slot)
            z1_send(t, onward, target).start()

    @pl.when(jnp.logical_not(middle))
    def _():
        for t in range(PLANES - 1):
            z1_send(t, t, main_plane).start()


    def turned_back(x, t):
        cos, sin = turn_ref[back[t], :HALF], turn_ref[back[t], HALF:]
        rows = []
        for h in range(HP):
            upper, lower = x[h * HD : h * HD + HALF], x[h * HD + HALF : (h + 1) * HD]
            rows += [upper * cos + lower * sin, lower * cos - upper * sin]
        return jnp.concatenate(rows, axis=0)

    side_kv = {}
    for t in steps:
        own_kv[t].wait()
        core_kv[t].wait()
        for a in range(S2):
            kv_send[t, a] = total_of([kv_own[t, a], kv_near[t, a]]).astype(bf)
        for k in range(1, S2):
            side_kv[t, k] = remote(
                kv_send.at[t, lax.rem(s2 + S2 - k, S2)],
                kv_far.at[t, k - 1],
                kv_sems,
                PLANES + t * (S2 - 1) + k - 1,
                side_peer(S2 - k),
            )
            side_kv[t, k].start()
    own_kv[PLANES].wait()
    for t in steps:
        mixed[t, :QW] = turned_back(dq_ref[back[t]], t).astype(bf)

    local[4].wait()
    local[5].wait()
    for p in range(PLANES):
        for g in range(groups):
            x_keep[p, g] = total_of([x_keep[p, g]] + [x_got[k, p, g] for k in range(S2 - 1)]).astype(bf)
    y2 = [w_copy(x_keep.at[:, lax.rem(group + k, groups)], y2_got.at[k - 1], group_peer(k)) for k in range(1, groups)]
    for i in range(6, 10):
        local[i].wait()
    for a in range(S2):
        for g in range(groups):
            z_keep[a, g] = total_of([z_keep[a, g]] + [z_came[k, a, g] for k in range(PLANES - 1)]).astype(bf)
    y3 = [w_copy(z_keep.at[:, lax.rem(group + k, groups)], y3_got.at[k - 1], group_peer(k)) for k in range(1, groups)]

    j_moves = []

    def j_copy(source, target, device):
        copy = remote(source, target, j_sems, len(j_moves), device)
        j_moves.append(copy)
        copy.start()
        return copy

    def j_core_stage(begin, height, grads, near):
        j_acc[:height] = total_of(
            [
                jnp.dot(mixed[t, begin : begin + height], first[back[t]], preferred_element_type=f32)
                for t in steps
            ]
        )
        shard_rows = D // n
        for i in range(D // 128):
            block = j_acc[:height, i * 128 : (i + 1) * 128].T
            row = i * 128
            while row < (i + 1) * 128:
                shard, offset = divmod(row, shard_rows)
                count = min(shard_rows - offset, (i + 1) * 128 - row)
                source = row - i * 128
                grads[shard // S, shard % S // 2, shard % 2, offset : offset + count] = block[
                    source : source + count
                ].astype(bf)
                row += count
        return [j_copy(grads.at[:, :, 1 - core], near, core_peer)]

    def j_side_stage(moves, grads, near, far):
        for copy in moves:
            copy.wait()
        for p in range(PLANES):
            for a in range(S2):
                near[p, a] = total_of([grads[p, a, core], near[p, a]]).astype(bf)
        return [j_copy(near.at[:, lax.rem(s2 + k, S2)], far.at[k - 1], side_peer(k)) for k in range(1, S2)]

    def j_plane_stage(moves, near, far, gathered):
        for copy in moves:
            copy.wait()
        for p in range(PLANES):
            far[0, p] = total_of([near[p, s2]] + [far[k, p] for k in range(S2 - 1)]).astype(bf)
        gathered[plane] = far[0, plane]
        return [
            j_copy(far.at[0, lax.rem(plane + k, PLANES)], gathered.at[plane], plane_peer(k)) for k in range(1, PLANES)
        ]

    def j_group_stage(moves, gathered, every):
        for copy in moves:
            copy.wait()
        every[group] = gathered[...]
        return [j_copy(gathered, every.at[group], group_peer(k)) for k in range(1, groups)]

    local[0].wait()
    jq_moves = j_core_stage(0, QW, jq, jq_core)
    z1_relay(0, 0, 3, main_plane)

    local[1].wait()

    half = T // 2
    halves = range(2)

    def mixed_send(t, e):
        lanes = pl.ds(e * half, half)
        return send(
            mixed.at[t, :, lanes],
            mixed_got.at[t, :, lanes],
            mixed_send_sems.at[t, e],
            mixed_recv_sems.at[t, e],
            at(main_plane, s2, core, group),
        )

    def part_send(t, e, direction, target):
        rows = pl.ds(e * half, half)
        return send(
            part.at[t, rows],
            part_got.at[direction, order[t], rows],
            part_send_sems.at[t, e],
            part_recv_sems.at[direction * PLANES + order[t], e],
            at(target, s2, core, group),
        )

    def part_came(direction, p, e):
        rows = pl.ds(e * half, half)
        return send(
            part.at[0, rows],
            part_got.at[direction, p, rows],
            part_send_sems.at[0, e],
            part_recv_sems.at[direction * PLANES + p, e],
            core_peer,
        )

    other_plane = 2 * plane - main_plane

    def product(grads, columns):
        return jnp.dot(grads.T, columns, preferred_element_type=f32)

    def add_mixed(t, slot, e):
        mixed_send(slot, e).wait_recv()
        rows = slice(e * half, (e + 1) * half)
        near = product(mixed_got[slot, :, rows], joint_near[...])
        part[t, rows] = (part[t, rows].astype(f32) + near).astype(bf)

    def add_part(t, direction, p, e):
        part_came(direction, p, e).wait_recv()
        rows = slice(e * half, (e + 1) * half)
        part[t, rows] = total_of([part[t, rows], part_got[direction, p, rows]]).astype(bf)

    def relay(t, slot):
        @pl.when(middle)
        def _():
            for e in halves:
                if slot is None:
                    add_part(t, 1 - main, order[t], e)
                    part_send(t, e, 1 - main, other_plane).start()
                else:
                    add_mixed(t, slot, e)
                    part_send(t, e, main, main_plane).start()

    def key_step(t):
        for k in range(1, S2):
            side_kv[t, k].wait()
        dk = total_of([kv_send[t, s2]] + [kv_far[t, k] for k in range(S2 - 1)]).T
        mixed[t, QW : 2 * QW] = turned_back(dk[:QW], t).astype(bf)
        mixed[t, 2 * QW :] = dk[QW:].astype(bf)
        if t < PLANES - 1:

            @pl.when(jnp.logical_not(middle))
            def _():
                for e in halves:
                    mixed_send(t, e).start()

            @pl.when(middle)
            def _():
                part[t] = product(mixed[t], joint_t[: 3 * QW]).astype(bf)

        else:
            part[t] = product(mixed[t], joint_t[: 3 * QW]).astype(bf)

    local[12].wait()
    key_step(0)
    z1_relay(2, 1, 4, main_plane)
    jq_moves = j_side_stage(jq_moves, jq, jq_core, jq_side)
    key_step(1)
    z1_relay(1, 3, 5, 2 * plane - main_plane)
    for copy in y2:
        copy.wait()
    for p in range(PLANES):
        w_plane[p] = total_of([x_keep[p, group]] + [y2_got[k, p] for k in range(groups - 1)]).astype(bf)
    w_last = [
        w_copy(w_plane.at[lax.rem(plane + k, PLANES)], w_plane_got.at[k - 1], plane_peer(k)) for k in range(1, PLANES)
    ]
    key_step(2)
    relay(0, 0)
    jq_moves = j_plane_stage(jq_moves, jq_core, jq_side, jq_plane)
    key_step(3)
    relay(2, 1)
    jk_moves = j_core_stage(QW, 2 * QW, jk, jk_core)

    for copy in y3:
        copy.wait()
    for a in range(S2):
        z_keep[a, group] = total_of([z_keep[a, group]] + [y3_got[k, a] for k in range(groups - 1)]).astype(bf)
    x3 = [w_copy(z_keep.at[lax.rem(s2 + k, S2), group], x3_got.at[k - 1], side_peer(k)) for k in range(1, S2)]
    @pl.when(middle)
    def _():
        z1_add(PLANES - 1, 2)
        z1_add(PLANES - 1, 4)

    @pl.when(jnp.logical_not(middle))
    def _():
        z1_add(PLANES - 1, 5)

    x1 = [w_copy(y_keep.at[plane, lax.rem(s2 + k, S2)], x1_got.at[k - 1], side_peer(k)) for k in range(1, S2)]
    relay(1, None)
    jk_moves = j_side_stage(jk_moves, jk, jk_core, jk_side)
    jq_moves = j_group_stage(jq_moves, jq_plane, jq_all)

    local[10].wait()
    local[11].wait()
    @pl.when(middle)
    def _():
        for e in halves:
            add_mixed(PLANES - 1, 2, e)

    for e in halves:
        add_part(PLANES - 1, 1 - main, plane, e)

    strip = 64

    def norm_back(i, carry):
        rows = pl.ds(pl.multiple_of(i * strip, strip), strip)
        grad = part[PLANES - 1, rows].astype(f32)
        values = tokens[rows].astype(f32)
        centred = values - jnp.mean(values, axis=-1, keepdims=True)
        scale = lax.rsqrt(jnp.mean(centred * centred, axis=-1, keepdims=True) + norm_eps)
        normal = centred * scale
        grad = grad * gains_ref[0:1]
        grad = grad - jnp.mean(grad, axis=-1, keepdims=True) - normal * jnp.mean(grad * normal, axis=-1, keepdims=True)
        grad_hidden[rows] = grad_hidden[rows] + grad * scale
        return carry

    lax.fori_loop(0, T // strip, norm_back, 0)

    blocks = T // BLOCK
    piece = BLOCK // n

    def d_copy(source, target, base, k):
        return remote(source.at[lax.rem(me + k, n)], target.at[me], d_sems, base + k, (lax.rem(me + k, n), group))

    for i in range(n):
        d_send[i] = jnp.concatenate(
            [grad_hidden[b * BLOCK + i * piece : b * BLOCK + (i + 1) * piece] for b in range(blocks)], axis=0
        ).astype(bf)
    out_deal = [d_copy(d_send, d_mid, 0, k) for k in range(1, n)]
    for copy in out_deal:
        copy.start()
    d_mid[me] = d_send[me]

    for copy in x1 + w_last + x3:
        copy.wait()
    height = w_plane.shape[1]
    w_all[group, :height] = total_of([y_keep[plane, s2]] + [x1_got[k] for k in range(S2 - 1)]).astype(bf)
    w_all[group, height : 2 * height] = total_of(
        [w_plane[plane]] + [w_plane_got[k] for k in range(PLANES - 1)]
    ).astype(bf)
    w_all[group, 2 * height :] = total_of([z_keep[s2, group]] + [x3_got[k] for k in range(S2 - 1)]).astype(bf)
    w_gather = [w_copy(w_all.at[group], w_all.at[group], group_peer(k)) for k in range(1, groups)]
    jk_moves = j_plane_stage(jk_moves, jk_core, jk_side, jk_plane)

    for copy in out_deal:
        copy.wait()
    for i in range(n):
        chosen = []
        for b in range(blocks):
            wanted = deal_ref[i * blocks + b]
            held = d_mid[wanted // blocks].astype(f32)
            rows = held[:piece]
            for other in range(1, blocks):
                rows = jnp.where(lax.rem(wanted, blocks) == other, held[other * piece : (other + 1) * piece], rows)
            chosen.append(rows)
        d_back[i] = jnp.concatenate(chosen, axis=0).astype(bf)
    back_deal = [d_copy(d_back, d_got, n, k) for k in range(1, n)]
    for copy in back_deal:
        copy.start()
    d_got[me] = d_back[me]

    jk_moves = j_group_stage(jk_moves, jk_plane, jk_all)

    for copy in back_deal + w_gather + jq_moves + jk_moves:
        copy.wait()
    for t in range(PLANES - 1):
        z1_send(t, 0, main_plane).wait_send()
        for e in halves:

            @pl.when(middle)
            def _(t=t, e=e):
                part_send(t, e, main, main_plane).wait_send()

            @pl.when(jnp.logical_not(middle))
            def _(t=t, e=e):
                mixed_send(t, e).wait_send()

    @pl.when(held_here)
    def _():
        row_own.wait()
        for copy in row_moves:
            copy.wait_send()

    @pl.when(jnp.logical_not(held_here))
    def _():
        row_moves[0].wait_recv()


def tail(n, groups, deal, dqt, dkv, turn, gains, joint_shard, joint_t, joint_near, first, tokens, grad_hidden, pieces):
    bf, f32 = jnp.bfloat16, jnp.float32
    S2 = n // PLANES // 2
    T, D = tokens.shape
    rows = D // n
    height = pieces[0].shape[2]
    piece_rows = T // n
    joint_shard = joint_shard.reshape(-1, rows, joint_shard.shape[1])
    any_, vm, sm = (pl.BlockSpec(memory_space=m) for m in (pl.ANY, pltpu.VMEM, pltpu.SMEM))
    sems = lambda count: pltpu.SemaphoreType.DMA((2, count))
    small = lambda *s: pltpu.VMEM(s, bf)
    j_buffers = lambda w: [
        small(PLANES, S2, 2, rows, w),
        small(PLANES, S2, rows, w),
        small(S2 - 1, PLANES, rows, w),
        small(PLANES, rows, w),
    ]
    return pl.pallas_call(
        functools.partial(tail_kernel, n, groups),
        out_shape=(
            jax.ShapeDtypeStruct((n, piece_rows, D), bf),
            jax.ShapeDtypeStruct((groups, 3 * height, D), bf),
            jax.ShapeDtypeStruct((groups, PLANES, rows, QW), bf),
            jax.ShapeDtypeStruct((groups, PLANES, rows, 2 * QW), bf),
            jax.ShapeDtypeStruct(joint_shard.shape[1:], bf),
        ),
        in_specs=[sm, any_, any_, vm, vm] + [any_] * 14,
        out_specs=tuple([vm] * 4) + (any_,),
        scratch_shapes=[
            pltpu.VMEM(joint_t.shape, bf),
            pltpu.VMEM(joint_near.shape, bf),
            pltpu.VMEM((PLANES, T, D), bf),
            pltpu.VMEM((T, D), bf),
            pltpu.VMEM((T, D), f32),
            *[pltpu.VMEM(p.shape, bf) for p in pieces[:5]],
            pltpu.VMEM((PLANES - 1, *pieces[5].shape), bf),
            pltpu.SemaphoreType.DMA((13,)),
            pltpu.VMEM(dqt.shape, f32),
            small(PLANES, S2, T, 2 * QW),
            pltpu.SemaphoreType.DMA((PLANES + 1,)),
            small(PLANES, S2, T, 2 * QW),
            small(PLANES, S2, T, 2 * QW),
            small(PLANES, S2 - 1, T, 2 * QW),
            sems(PLANES * S2),
            small(PLANES, 3 * QW, T),
            small(PLANES - 1, 3 * QW, T),
            pltpu.SemaphoreType.DMA((PLANES - 1, 2)),
            pltpu.SemaphoreType.DMA((PLANES - 1, 2)),
            small(PLANES, T, D),
            small(2, PLANES, T, D),
            pltpu.SemaphoreType.DMA((PLANES - 1, 2)),
            pltpu.SemaphoreType.DMA((2 * PLANES, 2)),
            pltpu.VMEM((2 * QW, D), f32),
            *j_buffers(QW),
            *j_buffers(2 * QW),
            sems(2 * (1 + S2 - 1 + PLANES - 1 + groups - 1)),
            small(S2 - 1, height, D),
            small(groups - 1, PLANES, height, D),
            small(groups - 1, S2, height, D),
            small(6, S2, height, D),
            pltpu.SemaphoreType.DMA((2, 6)),
            small(S2 - 1, height, D),
            small(PLANES, height, D),
            small(PLANES - 1, height, D),
            sems(3 * (groups - 1) + 2 * (S2 - 1) + PLANES - 1),
            small(n, piece_rows, D),
            small(n, piece_rows, D),
            small(n, piece_rows, D),
            sems(2 * n),
            pltpu.SemaphoreType.DMA((groups,)),
            pltpu.SemaphoreType.DMA((1,)),
        ],
        compiler_params=pltpu.CompilerParams(collective_id=0, has_side_effects=True, vmem_limit_bytes=60 << 20),
    )(deal, dqt, dkv, turn, gains, joint_shard, joint_t, joint_near, first, tokens, grad_hidden, *pieces)


def finish_kernel(
    n,
    d_ref,
    w_ref,
    jq_ref,
    jk_ref,
    rows_ref,
    gains_ref,
    dealt_ref,
    joint_ref,
    output_ref,
    expand_ref,
    contract_ref,
    gain_one_ref,
    gain_two_ref,
):
    f32 = jnp.float32
    T, D = dealt_ref.shape
    blocks = T // BLOCK
    piece = BLOCK // n
    for b in range(blocks):
        for i in range(0, n, 2):
            rows = [d_ref[i + e].astype(f32)[b * piece : (b + 1) * piece] for e in range(2)]
            dealt_ref[b * BLOCK + i * piece : b * BLOCK + (i + 2) * piece] = jnp.concatenate(rows, axis=0).astype(
                dealt_ref.dtype
            )

    def summed(ref, p):
        total = ref[0, p].astype(f32)
        for g in range(1, ref.shape[0]):
            total = total + ref[g, p].astype(f32)
        return total.T

    for i in range(PLANES // 2):
        pair = [summed(jq_ref, 2 * i + e) for e in range(2)]
        joint_ref[:, i * 2 * QW : (i + 1) * 2 * QW] = jnp.concatenate(pair, axis=0).T
        pair = [summed(jk_ref, 2 * i + e) for e in range(2)]
        for part in range(2):
            cols = (part + 1) * D + i * 2 * QW
            rows = [x[part * QW : (part + 1) * QW] for x in pair]
            joint_ref[:, cols : cols + 2 * QW] = jnp.concatenate(rows, axis=0).T
    shift = D - lax.axis_index("ctx") * (D // n)

    def own_lanes(x):
        return pltpu.roll(jnp.broadcast_to(x, (8, D)), shift, 1)[0:1, : D // n]

    product = jnp.sum(joint_ref[...] * rows_ref[...].astype(f32), axis=1, keepdims=True)
    product = jnp.broadcast_to(product, (D // n, 128)).T[0:1]
    gain_one_ref[...] = product / own_lanes(gains_ref[0:1])
    height = w_ref.shape[1]
    rows = D // n
    targets = [(output_ref, 0, rows)]
    targets += [(expand_ref, i * D, rows) for i in range(expand_ref.shape[1] // D)]
    targets += [(contract_ref, 0, contract_ref.shape[0])]
    row = 0
    for target, column, count in targets:
        done = 0
        while done < count:
            g, offset = divmod(row, height)
            part = min(count - done, height - offset)
            target[done : done + part, column : column + D] = w_ref[g, offset : offset + part].astype(f32)
            done += part
            row += part
    g, offset = divmod(row, height)
    gain_two_ref[...] = own_lanes(w_ref[g, offset : offset + 1].astype(f32))


def finish(n, T, wide, contract_rows, d_got, w_all, jq_all, jk_all, joint_rows, gains):
    D = d_got.shape[-1]
    rows = D // n
    f32 = jnp.float32
    vm = pl.BlockSpec(memory_space=pltpu.VMEM)
    return pl.pallas_call(
        functools.partial(finish_kernel, n),
        out_shape=(
            jax.ShapeDtypeStruct((T, D), jnp.bfloat16),
            jax.ShapeDtypeStruct((rows, 3 * D), f32),
            jax.ShapeDtypeStruct((rows, D), f32),
            jax.ShapeDtypeStruct((rows, wide), f32),
            jax.ShapeDtypeStruct((contract_rows, D), f32),
            jax.ShapeDtypeStruct((1, rows), f32),
            jax.ShapeDtypeStruct((1, rows), f32),
        ),
        in_specs=[vm] * 6,
        out_specs=tuple([vm] * 7),
    )(d_got, w_all, jq_all, jk_all, joint_rows, gains)


def on_device(
    n,
    groups,
    tokens,
    cotangent,
    lengths,
    deal,
    joint_projection,
    output_projection,
    expand_weight,
    contract_weight,
    gain_first,
    gain_second,
):
    T, D = tokens.shape[1:]
    S = n // PLANES
    S2 = S // 2

    def over_planes(x, k):
        return lax.ppermute(x, "ctx", [(h * S + s, (h + k) % PLANES * S + s) for h in range(PLANES) for s in range(S)])

    def over_sides(x, k):
        pairs = [
            (h * S + a * 2 + c, h * S + (a + k) % S2 * 2 + c) for h in range(PLANES) for a in range(S2) for c in range(2)
        ]
        return lax.ppermute(x, "ctx", pairs)

    def over_groups(x, k):
        return lax.ppermute(x, "fsdp", [(f, (f + k) % groups) for f in range(groups)])

    def moved(x, over):
        if x.shape[0] == 1:
            return over(x, 1)
        return jnp.stack([over(x[k], k + 1) for k in range(x.shape[0])])

    first, qt, kv, joint_t, turn, gains, out_w, exp_w, con_half = front(
        n,
        groups,
        lengths,
        tokens[0],
        joint_projection,
        gain_first,
        gain_second,
        output_projection,
        expand_weight,
        contract_weight,
    )
    con_got = [over_groups(con_half, k) for k in range(1, groups)]
    out_w, exp_w = (w.reshape(-1, w.shape[-1]) for w in (out_w, exp_w))
    ot, lowt, lse = attn_fwd(n, lengths, qt, kv)
    output, grad_hidden, gt, y_keep, y_send, x_keep, x_send, z_keep, *z_send, joint_near = middle(
        n, groups, lowt, tokens[0], cotangent[0], gains, out_w, exp_w, contract_weight, joint_projection, con_got
    )
    y_got, x_got = moved(y_send, over_groups), moved(x_send, over_sides)
    z_got = [over_planes(part, k + 1) for k, part in enumerate(z_send)]
    dqt, dkv = attn_bwd(n, lengths, qt, kv, ot, lse, gt)
    d_got, w_all, jq_all, jk_all, joint_rows = tail(
        n,
        groups,
        deal[0],
        dqt,
        dkv.reshape(PLANES, S2, 2, T, 2 * QW),
        turn,
        gains,
        joint_projection,
        joint_t,
        joint_near,
        first,
        tokens[0],
        grad_hidden,
        [y_keep, y_got, x_keep, x_got, z_keep, *z_got],
    )
    dealt, shard_joint, shard_output, shard_expand, shard_contract, gain_one, gain_two = finish(
        n, T, exp_w.shape[1], contract_weight.shape[0] * groups // n, d_got, w_all, jq_all, jk_all, joint_rows, gains
    )
    return (
        output[None],
        dealt[None],
        shard_joint,
        shard_output,
        shard_expand,
        shard_contract,
        gain_one[0],
        gain_two[0],
    )


def solution(mesh):
    return jax.shard_map(
        functools.partial(on_device, mesh.shape["ctx"], mesh.shape["fsdp"]),
        mesh=mesh,
        in_specs=(
            P("fsdp", "ctx", None),
            P("fsdp", "ctx", None),
            P("fsdp", None),
            P("fsdp", None),
            P("fsdp", None),
            P("fsdp", None),
            P("fsdp", None),
            P("fsdp", None),
            P("fsdp"),
            P("fsdp"),
        ),
        out_specs=(
            P("fsdp", "ctx", None),
            P("fsdp", "ctx", None),
            P("ctx", None),
            P("ctx", None),
            P("ctx", None),
            P("ctx", None),
            P("ctx"),
            P("ctx"),
        ),
        check_vma=False,
    )
```

```python
import functools
import math

import jax
import jax.numpy as jnp
import numpy as np
from jax import lax
from jax.experimental import pallas as pl
from jax.experimental.pallas import tpu as pltpu
from jax.sharding import PartitionSpec as P

FF = 1152
HEADS = 12
HEAD_DIM = 64
BLOCK = 128
PLANES = 4
HD = HEAD_DIM
HALF = HEAD_DIM // 2
HP = HEADS // PLANES
QW = HP * HEAD_DIM
rope_base = 160000.0
norm_eps = 1e-05
MASKED = -1e30


def ends_of(lengths_ref, count):
    ends, total = [], 0
    for i in range(count):
        total = total + lengths_ref[0, i]
        ends.append(total)
    return ends


def span_of(index, ends):
    begin, end = jnp.zeros_like(index), jnp.full_like(index, ends[0])
    for before, after in zip(ends[:-1], ends[1:]):
        begin = jnp.where(index >= before, before, begin)
        end = jnp.where(index >= before, after, end)
    return begin, end


def head_rows(x, head):
    rows = lax.broadcasted_iota(jnp.int32, x.shape, 0)
    return jnp.where((rows >= head * HD) & (rows < (head + 1) * HD), x, jnp.zeros_like(x))


def query_block(n, b, T, ends):
    S = n // PLANES
    me = lax.axis_index("ctx")
    base = (lax.rem(me // S + PLANES - b, PLANES) * S + lax.rem(me, S)) * T
    low_begin, low_end = span_of(base, ends)
    high_begin, high_end = span_of(base + T - 1, ends)
    low, high = low_begin // T, (high_end + T - 1) // T
    full_low = jnp.clip((high_begin + T - 1) // T, low, high)
    full_high = jnp.clip(low_end // T, full_low, high)
    begin, end = span_of(base + lax.broadcasted_iota(jnp.int32, (8, T), 1), ends)
    return (low, full_low, full_high, high), begin[0:1], end[0:1]


def over_units(bounds, step, sizes, masked_sizes):
    low, full_low, full_high, high = bounds
    in_groups(low, full_low, lambda u: step(u, True), masked_sizes)
    in_groups(full_low, full_high, lambda u: step(u, False), sizes)
    in_groups(full_high, high, lambda u: step(u, True), masked_sizes)


def in_groups(begin, end, step, sizes):
    for size in sizes:
        count = (end - begin) // size

        def some(i, carry, size=size, begin=begin):
            for e in range(size):
                step(begin + size * i + e)
            return carry

        lax.fori_loop(0, count, some, 0)
        begin = begin + size * count


def fwd_kernel(n, count, lengths_ref, qt_ref, kv_ref, ot_ref, lowt_ref, lse_ref, values, scores, top, total, acc):
    units, T, _ = kv_ref.shape
    ends = ends_of(lengths_ref, count)

    def flip(u, carry):
        values[u] = kv_ref[u, :, 128:].T
        return carry

    lax.fori_loop(0, units, flip, 0, unroll=4)

    def one_query_block(b, carry):
        qt = qt_ref[b]
        qheads = [head_rows(qt, h) for h in range(HP)]
        bounds, q_start, q_end = query_block(n, b, T, ends)
        top[...] = jnp.full_like(top, MASKED)
        total[...] = jnp.zeros_like(total)
        acc[...] = jnp.zeros_like(acc)

        def score(u, masked):
            k = kv_ref[u, :, :QW]
            st = [jnp.dot(k, qheads[h], preferred_element_type=jnp.float32) for h in range(HP)]
            if masked:
                at = u * T + lax.broadcasted_iota(jnp.int32, (T, T), 0)
                allowed = (at >= q_start) & (at < q_end)
                st = [jnp.where(allowed, s, MASKED) for s in st]
            for h in range(HP):
                scores[u, h] = st[h]
                top[h] = jnp.maximum(top[h], jnp.max(st[h].reshape(T // 8, 8, T), axis=0))

        over_units(bounds, score, (2, 1), (2, 1))
        m = [jnp.max(top[h], axis=0, keepdims=True) for h in range(HP)]

        def gather(u):
            p = [jnp.exp(scores[u, h] - m[h]) for h in range(HP)]
            for h in range(HP):
                total[h] += jnp.sum(p[h].reshape(T // 8, 8, T), axis=0)
                rows = pl.ds(h * HD, HD)
                acc[rows, :] += jnp.dot(
                    values[u, pl.ds(HD + h * HD, HD), :], p[h].astype(jnp.bfloat16), preferred_element_type=jnp.float32
                )

        in_groups(bounds[0], bounds[3], gather, (4, 2, 1))
        for h in range(HP):
            rows = pl.ds(h * HD, HD)
            l = jnp.sum(total[h], axis=0, keepdims=True)
            o = acc[rows, :] / l
            ot_ref[b, rows, :] = o
            lowt_ref[b, rows, :] = o.astype(jnp.bfloat16)
            lse_ref[b, h : h + 1, :] = m[h] + jnp.log(l)
        return carry

    lax.fori_loop(0, qt_ref.shape[0], one_query_block, 0)


def attn_fwd(n, lengths, qt, kv):
    B, _, T = qt.shape
    U = kv.shape[0]
    sm, vm = pl.BlockSpec(memory_space=pltpu.SMEM), pl.BlockSpec(memory_space=pltpu.VMEM)
    return pl.pallas_call(
        functools.partial(fwd_kernel, n, lengths.shape[1]),
        out_shape=(
            jax.ShapeDtypeStruct((B, QW, T), jnp.float32),
            jax.ShapeDtypeStruct((B, QW, T), jnp.bfloat16),
            jax.ShapeDtypeStruct((B, 8, T), jnp.float32),
        ),
        in_specs=[sm, vm, vm],
        out_specs=(vm, vm, vm),
        scratch_shapes=[
            pltpu.VMEM((U, 256, T), jnp.bfloat16),
            pltpu.VMEM((U, HP, T, T), jnp.float32),
            pltpu.VMEM((HP, 8, T), jnp.float32),
            pltpu.VMEM((HP, 8, T), jnp.float32),
            pltpu.VMEM((QW, T), jnp.float32),
        ],
        compiler_params=pltpu.CompilerParams(vmem_limit_bytes=60 << 20),
    )(lengths, qt, kv)


def bwd_kernel(n, count, lengths_ref, qt_ref, kv_ref, ot_ref, lse_ref, gt_ref, dqt_ref, dkv_ref, keys, dk, dv, dq):
    units, T, _ = kv_ref.shape
    ends = ends_of(lengths_ref, count)

    def flip(u, carry):
        keys[u] = kv_ref[u, :, :256].T
        dk[u] = jnp.zeros_like(dk[u])
        dv[u] = jnp.zeros_like(dv[u])
        return carry

    lax.fori_loop(0, units, flip, 0, unroll=4)

    def one_query_block(b, carry):
        qt, gt = qt_ref[b], gt_ref[b]
        zero = jnp.zeros((HD, T), jnp.bfloat16)
        qheads = [head_rows(qt, h) for h in range(HP)]
        gheads = [head_rows(gt, h) for h in range(HP)]
        gpad = [jnp.concatenate([zero, x], axis=0) for x in gheads]
        lanes = lax.broadcasted_iota(jnp.int32, (T, 256), 1) // HD
        q, g = jnp.concatenate([qt, zero], axis=0).T, jnp.concatenate([zero, gt], axis=0).T
        q = jnp.concatenate([jnp.where(lanes == h, q, jnp.zeros_like(q)) for h in range(HP)], axis=0)
        g = jnp.concatenate([jnp.where(lanes == h + 1, g, jnp.zeros_like(g)) for h in range(HP)], axis=0)
        bounds, q_start, q_end = query_block(n, b, T, ends)
        prod = gt.astype(jnp.float32) * ot_ref[b]
        delta = [jnp.sum(prod[h * HD : (h + 1) * HD], axis=0, keepdims=True) for h in range(HP)]
        lse = [lse_ref[b, h : h + 1, :] for h in range(HP)]
        dq[...] = jnp.zeros_like(dq)

        def one_unit(u, masked):
            k, v = kv_ref[u, :, :QW], kv_ref[u, :, 128:]
            st = [jnp.dot(k, qheads[h], preferred_element_type=jnp.float32) for h in range(HP)]
            dp = [jnp.dot(v, gpad[h], preferred_element_type=jnp.float32) for h in range(HP)]
            st = [st[h] - lse[h] for h in range(HP)]
            if masked:
                at = u * T + lax.broadcasted_iota(jnp.int32, (T, T), 0)
                allowed = (at >= q_start) & (at < q_end)
                st = [jnp.where(allowed, s, MASKED) for s in st]
            p = [jnp.exp(s) for s in st]
            ds = [(p[h] * (dp[h] - delta[h])).astype(jnp.bfloat16) for h in range(HP)]
            p = [x.astype(jnp.bfloat16) for x in p]
            dv[u] += jnp.dot(jnp.concatenate(p, axis=1), g, preferred_element_type=jnp.float32)
            dk[u] += jnp.dot(jnp.concatenate(ds, axis=1), q, preferred_element_type=jnp.float32)
            for h in range(HP):
                rows = pl.ds(h * HD, HD)
                dq[rows, :] += jnp.dot(keys[u, rows, :], ds[h], preferred_element_type=jnp.float32)

        over_units(bounds, one_unit, (4, 2, 1), (4, 2, 1))
        dqt_ref[b] = dq[...] * (HD**-0.5)
        return carry

    lax.fori_loop(0, qt_ref.shape[0], one_query_block, 0)

    def out(u, carry):
        dkv_ref[u, :, :128] = dk[u, :, :128].astype(jnp.bfloat16)
        dkv_ref[u, :, 128:256] = (dk[u, :, 128:] + dv[u, :, :128]).astype(jnp.bfloat16)
        dkv_ref[u, :, 256:] = dv[u, :, 128:].astype(jnp.bfloat16)
        return carry

    lax.fori_loop(0, units, out, 0, unroll=2)


def attn_bwd(n, lengths, qt, kv, ot, lse, gt):
    B, _, T = qt.shape
    U = kv.shape[0]
    sm, vm = pl.BlockSpec(memory_space=pltpu.SMEM), pl.BlockSpec(memory_space=pltpu.VMEM)
    return pl.pallas_call(
        functools.partial(bwd_kernel, n, lengths.shape[1]),
        out_shape=(jax.ShapeDtypeStruct((B, QW, T), jnp.float32), jax.ShapeDtypeStruct((U, T, 2 * QW), jnp.bfloat16)),
        in_specs=[sm] + [vm] * 5,
        out_specs=(vm, vm),
        scratch_shapes=[
            pltpu.VMEM((U, 256, T), jnp.bfloat16),
            pltpu.VMEM((U, T, 256), jnp.float32),
            pltpu.VMEM((U, T, 256), jnp.float32),
            pltpu.VMEM((QW, T), jnp.float32),
        ],
        compiler_params=pltpu.CompilerParams(vmem_limit_bytes=60 << 20),
    )(lengths, qt, kv, ot, lse, gt)
def front_kernel(
    n,
    groups,
    count,
    lengths_ref,
    tokens_ref,
    joint_ref,
    gain_one_ref,
    gain_two_ref,
    out_hbm,
    exp_hbm,
    con_hbm,
    first_ref,
    qt_ref,
    kv_ref,
    joint_t_out,
    turn_ref,
    gains_ref,
    out_all,
    exp_all,
    con_ref,
    held,
    t_sems,
    cols,
    cols_all,
    gain_held,
    g_sems,
    kv_own,
    kv_sems,
    own_sems,
    w_sems,
    w_local,
    joint_rows,
    out_held,
    exp_held,
    con_held,
):
    bf, f32 = jnp.bfloat16, jnp.float32
    S = n // PLANES
    S2 = S // 2
    T, D = tokens_ref.shape
    me, group = lax.axis_index("ctx"), lax.axis_index("fsdp")
    plane, side = me // S, lax.rem(me, S)
    s2, core = side // 2, lax.rem(side, 2)

    def at(p, a, c, g):
        return (p * S + a * 2 + c, g)

    def side_peer(k):
        return at(plane, lax.rem(s2 + k, S2), core, group)

    def group_peer(k):
        return at(plane, s2, core, lax.rem(group + k, groups))

    core_peer = at(plane, s2, 1 - core, group)

    def remote(source, target, sems, index, device):
        return pltpu.make_async_remote_copy(
            src_ref=source,
            dst_ref=target,
            send_sem=sems.at[0, index],
            recv_sem=sems.at[1, index],
            device_id=device,
            device_id_type=pl.DeviceIdType.MESH,
        )

    barrier = pltpu.get_barrier_semaphore()

    def greet(device):
        pl.semaphore_signal(barrier, inc=1, device_id=device, device_id_type=pl.DeviceIdType.MESH)

    for k in range(1, PLANES):
        greet(at(lax.rem(plane + k, PLANES), s2, core, group))
    for k in range(1, S2):
        greet(side_peer(k))
    for k in range(1, groups):
        greet(group_peer(k))
    greet(core_peer)
    pl.semaphore_wait(barrier, PLANES - 1 + S2 - 1 + groups - 1 + 1)

    def up(p):
        return remote(held.at[p], held.at[p], t_sems, p, at(plane + 1, s2, core, group))

    def down(p):
        return remote(held.at[p], held.at[p], t_sems, PLANES + p, at(plane - 1, s2, core, group))

    held[plane] = tokens_ref[...]

    @pl.when(plane < PLANES - 1)
    def _():
        up(plane).start()

    @pl.when(plane > 0)
    def _():
        down(plane).start()

    pair = 2 * QW
    for part in range(3):
        window = joint_ref[:, pl.ds(pl.multiple_of(part * D + plane // 2 * pair, 128), pair)].T
        chosen = jnp.where(lax.rem(plane, 2) == 0, window[:QW].astype(f32), window[QW:].astype(f32))
        half = 3 * QW // 2
        low, high = part * QW, (part + 1) * QW
        for c in range(2):
            begin, end = max(low, c * half), min(high, (c + 1) * half)
            if begin < end:
                cols[c, begin - c * half : end - c * half] = chosen[begin - low : end - low].astype(bf)
    gain_held[group] = jnp.zeros_like(gain_held[group])
    gain_held[group, 0:1] = gain_one_ref[...].astype(f32).reshape(1, -1)
    gain_held[group, 1:2] = gain_two_ref[...].astype(f32).reshape(1, -1)
    col_moves = [
        remote(cols.at[core], cols_all.at[group, core], g_sems, k - 1, group_peer(k)) for k in range(1, groups)
    ]
    col_hands = []
    for k in range(1, groups):
        came = cols_all.at[lax.rem(group + groups - k, groups), core]
        col_hands.append(remote(came, came, g_sems, 2 * (groups - 1) + k - 1, core_peer))
    gain_moves = [
        remote(gain_held.at[group], gain_held.at[group], g_sems, groups - 1 + k - 1, group_peer(k))
        for k in range(1, groups)
    ]
    for copy in gain_moves + col_moves:
        copy.start()
    cols_all[group] = cols[...]

    weights = [(out_hbm, out_all, out_held), (exp_hbm, exp_all, exp_held)]
    part = core if con_hbm.shape[0] == 2 else 0
    w_in = [pltpu.make_async_copy(con_hbm.at[part], con_held, w_local.at[0, len(weights)])]
    w_own = [pltpu.make_async_copy(con_held, con_ref, w_local.at[1, len(weights)])]
    w_first, w_second = [], []
    for i, (source, target, bounce) in enumerate(weights):
        w_in.append(pltpu.make_async_copy(source, bounce, w_local.at[0, i]))
        w_own.append(pltpu.make_async_copy(bounce, target.at[group], w_local.at[1, i]))
        for k in range(1, groups):
            index = (i * (groups - 1) + k - 1) * 2
            w_first.append(remote(source.at[core], target.at[group, core], w_sems, index, group_peer(k)))
            came = lax.rem(group + groups - k, groups)
            w_second.append(remote(target.at[came, core], target.at[came, core], w_sems, index + 1, core_peer))
    for copy in w_in:
        copy.start()
    for copy in w_first:
        copy.start()

    ends = ends_of(lengths_ref, count)
    row = lax.broadcasted_iota(jnp.int32, (HALF, T), 0)
    frequencies = jnp.zeros((HALF, T), f32)
    for i in range(HALF):
        frequencies = jnp.where(row == i, float(np.float32(rope_base ** (-2.0 * i / HEAD_DIM))), frequencies)
    for j in range(PLANES):
        base = (lax.rem(plane + PLANES - j, PLANES) * S + side) * T
        index = base + lax.broadcasted_iota(jnp.int32, (8, T), 1)
        begin, _ = span_of(index, ends)
        angles = (index - begin)[0:1].astype(f32) * frequencies
        turn_ref[j, :HALF] = jnp.cos(angles)
        turn_ref[j, HALF:] = jnp.sin(angles)

    strip = 256

    def kv_unit(p, a, c):
        return p * S + a * 2 + c

    def side_kv(j, k):
        p = lax.rem(plane + PLANES - j, PLANES)
        return remote(kv_own.at[j], kv_ref.at[kv_unit(p, s2, core)], kv_sems, j * (2 * S2 - 1) + k - 1, side_peer(k))

    def core_kv(j, k):
        p = lax.rem(plane + PLANES - j, PLANES)
        unit = kv_unit(p, lax.rem(s2 + S2 - k, S2), core)
        source = kv_own.at[j] if k == 0 else kv_ref.at[unit]
        return remote(source, kv_ref.at[unit], kv_sems, j * (2 * S2 - 1) + S2 - 1 + k, core_peer)

    def own_kv(j):
        p = lax.rem(plane + PLANES - j, PLANES)
        return pltpu.make_async_copy(kv_own.at[j], kv_ref.at[kv_unit(p, s2, core)], own_sems.at[j])

    def process(p):
        j = lax.rem(plane + PLANES - p, PLANES)

        def norm(i, carry):
            rows = pl.ds(pl.multiple_of(i * strip, strip), strip)
            values = held[p, rows].astype(f32)
            centred = values - jnp.mean(values, axis=-1, keepdims=True)
            spread = jnp.mean(centred * centred, axis=-1, keepdims=True)
            first_ref[j, rows] = (centred * lax.rsqrt(spread + norm_eps) * gains_ref[0:1]).astype(bf)
            return carry

        lax.fori_loop(0, T // strip, norm, 0)
        mixed = lax.dot_general(
            joint_t_out[: 3 * QW], first_ref[j], (((1,), (1,)), ((), ())), preferred_element_type=f32
        )
        cos, sin = turn_ref[j, :HALF], turn_ref[j, HALF:]
        turned = []
        for h in range(2 * HP):
            upper, lower = mixed[h * HD : h * HD + HALF], mixed[h * HD + HALF : (h + 1) * HD]
            turned += [upper * cos - lower * sin, lower * cos + upper * sin]
        q = jnp.concatenate(turned[: 2 * HP], axis=0).astype(bf)
        qt_ref[j] = (q.astype(f32) * HEAD_DIM**-0.5).astype(bf)
        kv_own[j] = jnp.concatenate(turned[2 * HP :] + [mixed[2 * QW :]], axis=0).T.astype(bf)
        for k in range(1, S2):
            side_kv(j, k).start()
        core_kv(j, 0).start()
        own_kv(j).start()

    def hand_on(t):
        @pl.when(plane >= t)
        def _():
            up(plane - t).wait_recv()

            @pl.when(plane < PLANES - 1)
            def _():
                up(plane - t).start()

        @pl.when(plane + t < PLANES)
        def _():
            down(plane + t).wait_recv()

            @pl.when(plane > 0)
            def _():
                down(plane + t).start()

    def process_arrived(t):
        below = jnp.where(plane >= t, 1, 0)
        above = jnp.where(plane + t < PLANES, 1, 0)

        def arrived(i, carry):
            process(jnp.where(i < below, plane - t, plane + t))
            return carry

        lax.fori_loop(0, below + above, arrived, 0)

    hand_on(1)
    for copy in gain_moves:
        copy.wait()
    share = D // groups
    total = jnp.zeros((8, D), f32)
    for g in range(groups):
        rows = lax.broadcasted_iota(jnp.int32, (share, D), 0)
        lanes = lax.broadcasted_iota(jnp.int32, (share, D), 1)
        place = jnp.where(lanes == rows + g * share, 1.0, 0.0).astype(bf)
        total = total + jnp.dot(gain_held[g].astype(bf), place, preferred_element_type=f32)
    gains_ref[...] = total
    for copy, hand in zip(col_moves, col_hands):
        copy.wait()
        hand.start()
    for copy in w_in:
        copy.wait()
    for copy in w_own:
        copy.start()
    for copy in col_hands:
        copy.wait()
    width = joint_t_out.shape[0]
    for g in range(groups):
        whole = jnp.concatenate([cols_all[g, 0], cols_all[g, 1], jnp.zeros((width - 3 * QW, share), bf)], axis=0)
        if share % 128 == 0:
            joint_t_out[:, g * share : (g + 1) * share] = whole
        else:
            joint_rows[g * share : (g + 1) * share] = whole.T
    if share % 128:
        for i in range(D // 128):
            joint_t_out[:, i * 128 : (i + 1) * 128] = joint_rows[i * 128 : (i + 1) * 128].T

    process(plane)
    process_arrived(1)
    hand_on(2)
    process_arrived(2)
    hand_on(3)
    for first_move, second_move in zip(w_first[: groups - 1], w_second):
        first_move.wait_recv()
        second_move.start()
    process_arrived(3)

    for j in range(PLANES):
        for k in range(1, S2):
            side_kv(j, k).wait_recv()
            core_kv(j, k).start()
    for first_move, second_move in zip(w_first[groups - 1 :], w_second[groups - 1 :]):
        first_move.wait_recv()
        second_move.start()

    for j in range(PLANES):
        own_kv(j).wait()
        for k in range(1, S2):
            side_kv(j, k).wait_send()
        for k in range(S2):
            core_kv(j, k).wait()
    for p in range(PLANES):

        @pl.when((plane < PLANES - 1) & (plane >= p))
        def _(p=p):
            up(p).wait_send()

        @pl.when((plane > 0) & (plane <= p))
        def _(p=p):
            down(p).wait_send()

    for copy in w_own:
        copy.wait()
    for first_move, second_move in zip(w_first, w_second):
        first_move.wait_send()
        second_move.wait()


def front(n, groups, lengths, tokens, joint_shard, gain_first, gain_second, out_w, exp_w, con_w):
    bf, f32 = jnp.bfloat16, jnp.float32
    S2 = n // PLANES // 2
    T, D = tokens.shape
    width = 3 * QW + 64
    share = D // groups
    any_, vm, sm = (pl.BlockSpec(memory_space=m) for m in (pl.ANY, pltpu.VMEM, pltpu.SMEM))
    sems = lambda count: pltpu.SemaphoreType.DMA((2, count))
    halves = lambda w: w.reshape(2, w.shape[0] // 2, w.shape[1])
    weights = [halves(w) for w in (out_w, exp_w)]
    con_w = con_w.reshape(2 if con_w.shape[0] % 32 == 0 else 1, -1, D)
    return pl.pallas_call(
        functools.partial(front_kernel, n, groups, lengths.shape[1]),
        out_shape=(
            jax.ShapeDtypeStruct((PLANES, T, D), bf),
            jax.ShapeDtypeStruct((PLANES, QW, T), bf),
            jax.ShapeDtypeStruct((n, T, 2 * QW), bf),
            jax.ShapeDtypeStruct((width, D), bf),
            jax.ShapeDtypeStruct((PLANES, 2 * HALF, T), f32),
            jax.ShapeDtypeStruct((8, D), f32),
            *[jax.ShapeDtypeStruct((groups, *w.shape), bf) for w in weights],
            jax.ShapeDtypeStruct(con_w.shape[1:], bf),
        ),
        in_specs=[sm, vm, vm, vm, vm, any_, any_, any_],
        out_specs=(vm, vm, any_, vm, vm, vm, any_, any_, any_),
        scratch_shapes=[
            pltpu.VMEM((PLANES, T, D), bf),
            sems(2 * PLANES),
            pltpu.VMEM((2, 3 * QW // 2, share), bf),
            pltpu.VMEM((groups, 2, 3 * QW // 2, share), bf),
            pltpu.VMEM((groups, 8, share), f32),
            sems(3 * (groups - 1)),
            pltpu.VMEM((PLANES, T, 2 * QW), bf),
            sems(PLANES * (2 * S2 - 1)),
            pltpu.SemaphoreType.DMA((PLANES,)),
            sems(2 * len(weights) * (groups - 1)),
            pltpu.SemaphoreType.DMA((2, len(weights) + 1)),
            pltpu.VMEM((D, width), bf),
            *[pltpu.VMEM(w.shape, bf) for w in weights],
            pltpu.VMEM(con_w.shape[1:], bf),
        ],
        compiler_params=pltpu.CompilerParams(collective_id=1, has_side_effects=True, vmem_limit_bytes=60 << 20),
    )(
        lengths,
        tokens,
        joint_shard,
        gain_first,
        gain_second,
        *weights,
        con_w,
    )


def middle_kernel(
    n,
    groups,
    low_ref,
    tokens_ref,
    cot_ref,
    gains_ref,
    out_hbm,
    exp_hbm,
    con_hbm,
    joint_hbm,
    *refs,
):
    con_got, refs = refs[: groups - 1], refs[groups - 1 :]
    (
        output_ref,
        grad_hidden_ref,
        gt_ref,
        y_keep,
        y_send,
        x_keep,
        x_send,
        z_keep,
        z_send_1,
        z_send_2,
        z_send_3,
        joint_near,
        out_w,
        exp_w,
        con_w,
        local_sems,
        c_sems,
        joint_shard,
        cols,
        cols_all,
        col_sems,
        joint_rows,
        att,
        a_sems,
        g_send,
        g_sems,
        hidden,
        second,
        branch,
        ga,
        act,
        gexp,
        acc,
        w_own,
        w_other,
        w_got,
        w_sems,
    ) = refs
    bf, f32 = jnp.bfloat16, jnp.float32
    S = n // PLANES
    S2 = S // 2
    T, D = tokens_ref.shape
    FFN = act.shape[1]
    me, group = lax.axis_index("ctx"), lax.axis_index("fsdp")
    plane, side = me // S, lax.rem(me, S)
    s2, core = side // 2, lax.rem(side, 2)

    def plane_peer(k):
        return (lax.rem(plane + k, PLANES) * S + side, group)

    core_peer = (plane * S + s2 * 2 + 1 - core, group)

    def group_peer(k):
        return (me, lax.rem(group + k, groups))


    def remote(source, target, sems, index, device):
        return pltpu.make_async_remote_copy(
            src_ref=source,
            dst_ref=target,
            send_sem=sems.at[0, index],
            recv_sem=sems.at[1, index],
            device_id=device,
            device_id_type=pl.DeviceIdType.MESH,
        )

    ff_share = con_hbm.shape[0]
    split = ff_share % 32 == 0

    def rows_of(g):
        return pl.ds(pl.multiple_of(g * ff_share, 16), ff_share)

    def half_of(g):
        if not split:
            return rows_of(g)
        half = ff_share // 2
        return pl.ds(pl.multiple_of(g * ff_share + core * half, 16), half)

    came = [half_of(lax.rem(group + groups - k, groups)) for k in range(1, groups)]
    con_hands = [remote(con_got[k], con_w.at[came[k]], c_sems, k, core_peer) for k in range(groups - 1)]
    con_local = [
        pltpu.make_async_copy(con_got[k], con_w.at[came[k]], local_sems.at[3 + k]) for k in range(groups - 1)
    ]
    local = [
        pltpu.make_async_copy(source, target, local_sems.at[i])
        for i, (source, target) in enumerate([(con_hbm, con_w.at[rows_of(group)]), (out_hbm, out_w), (exp_hbm, exp_w)])
    ]
    joint_local = pltpu.make_async_copy(joint_hbm, joint_shard, local_sems.at[3 + groups - 1])
    for copy in [joint_local] + local + con_local:
        copy.start()
    barrier = pltpu.get_barrier_semaphore()
    for k in range(1, PLANES):
        pl.semaphore_signal(barrier, inc=1, device_id=plane_peer(k), device_id_type=pl.DeviceIdType.MESH)
    pl.semaphore_signal(barrier, inc=1, device_id=core_peer, device_id_type=pl.DeviceIdType.MESH)
    for k in range(1, groups):
        pl.semaphore_signal(barrier, inc=1, device_id=group_peer(k), device_id_type=pl.DeviceIdType.MESH)
    pl.semaphore_wait(barrier, PLANES + groups - 1)

    home = [remote(low_ref.at[j], att.at[plane], a_sems, j - 1, plane_peer(PLANES - j)) for j in range(1, PLANES)]
    for copy in home + (con_hands if split else []):
        copy.start()
    att[plane] = low_ref[0]

    joint_local.wait()
    pair = 2 * QW
    for part in range(3):
        window = joint_shard[:, pl.ds(pl.multiple_of(part * D + plane // 2 * pair, 128), pair)].T
        chosen = jnp.where(lax.rem(plane, 2) == 1, window[:QW].astype(f32), window[QW:].astype(f32))
        half = 3 * QW // 2
        low, high = part * QW, (part + 1) * QW
        for c in range(2):
            begin, end = max(low, c * half), min(high, (c + 1) * half)
            if begin < end:
                cols[c, begin - c * half : end - c * half] = chosen[begin - low : end - low].astype(bf)
    col_moves = [
        remote(cols.at[core], cols_all.at[group, core], col_sems, k - 1, group_peer(k)) for k in range(1, groups)
    ]
    col_hands = []
    for k in range(1, groups):
        col_came = cols_all.at[lax.rem(group + groups - k, groups), core]
        col_hands.append(remote(col_came, col_came, col_sems, groups - 1 + k - 1, core_peer))
    for copy in col_moves:
        copy.start()
    cols_all[group] = cols[...]

    def nt(a, b):
        return lax.dot_general(a, b, (((1,), (1,)), ((), ())), preferred_element_type=f32)

    chunk = 384
    cot = cot_ref[...]
    local[0].wait()
    for copy in con_local + (con_hands if split else []):
        copy.wait()
    for c in range(0, FFN, chunk):
        ga[:, c : c + chunk] = nt(cot, con_w[c : c + chunk])
    local[1].wait()
    for copy in home:
        copy.wait()
    attended = att[...].reshape(D, T)
    hidden[...] = tokens_ref[...].astype(f32) + jnp.dot(attended.T, out_w[...], preferred_element_type=f32)

    strip = 256

    for copy, hand in zip(col_moves, col_hands):
        copy.wait()
        hand.start()

    def norm(i, carry):
        rows = pl.ds(pl.multiple_of(i * strip, strip), strip)
        values = hidden[rows]
        centred = values - jnp.mean(values, axis=-1, keepdims=True)
        spread = jnp.mean(centred * centred, axis=-1, keepdims=True)
        second[rows] = (centred * lax.rsqrt(spread + norm_eps) * gains_ref[1:2]).astype(bf)
        return carry

    lax.fori_loop(0, T // strip, norm, 0)
    local[2].wait()
    for c in range(0, FFN, chunk):
        cols, gate_cols = slice(c, c + chunk), slice(FFN + c, FFN + c + chunk)
        inner = jnp.dot(second[...], exp_w[:, cols], preferred_element_type=f32)
        gate = jnp.dot(second[...], exp_w[:, gate_cols], preferred_element_type=f32)
        share = 0.5 * (1.0 + lax.erf(inner * (0.5**0.5)))
        bent = inner * share
        act[:, cols] = (bent * gate).astype(bf)
        grad = ga[:, cols]
        slope = share + inner * jnp.exp(-0.5 * inner * inner) * ((2.0 * math.pi) ** -0.5)
        gexp[:, cols] = (grad * gate * slope).astype(bf)
        gexp[:, gate_cols] = (grad * bent).astype(bf)
    output_ref[...] = (hidden[...] + jnp.dot(act[...], con_w[...], preferred_element_type=f32)).astype(bf)
    acc[:T] = nt(gexp[...], exp_w[...])

    def norm_back(i, total):
        rows = pl.ds(pl.multiple_of(i * strip, strip), strip)
        values = hidden[rows]
        centred = values - jnp.mean(values, axis=-1, keepdims=True)
        scale = lax.rsqrt(jnp.mean(centred * centred, axis=-1, keepdims=True) + norm_eps)
        normal = centred * scale
        grad = acc[rows]
        total = total + jnp.sum(grad * normal, axis=0, keepdims=True)
        grad = grad * gains_ref[1:2]
        grad = grad - jnp.mean(grad, axis=-1, keepdims=True) - normal * jnp.mean(grad * normal, axis=-1, keepdims=True)
        back = cot_ref[rows].astype(f32) + grad * scale
        grad_hidden_ref[rows] = back
        branch[rows] = back.astype(bf)
        return total

    total = lax.fori_loop(0, T // strip, norm_back, jnp.zeros((1, D), f32))
    gain_two = jnp.broadcast_to(total, (8, D))
    for p in range(PLANES):
        g_send[p] = nt(out_w[p * QW : (p + 1) * QW], branch[...]).astype(bf)
    away = [
        remote(g_send.at[lax.rem(plane + k, PLANES)], gt_ref.at[k], g_sems, k - 1, plane_peer(k))
        for k in range(1, PLANES)
    ]
    for copy in away:
        copy.start()
    gt_ref[0] = g_send[plane]

    for copy in col_hands:
        copy.wait()
    share = D // groups
    for g in range(groups):
        whole = jnp.concatenate([cols_all[g, 0], cols_all[g, 1]], axis=0)
        if share % 128 == 0:
            joint_near[:, g * share : (g + 1) * share] = whole
        else:
            joint_rows[g * share : (g + 1) * share] = whole.T
    if share % 128:
        for i in range(D // 128):
            joint_near[:, i * 128 : (i + 1) * 128] = joint_rows[i * 128 : (i + 1) * 128].T

    sent = []

    def place(rows, offset, height):
        for target, parity in ((w_other, 1 - core), (w_own, core)):

            def body(m, carry):
                if rows % 8:
                    pair = acc[pl.ds(pl.multiple_of(2 * m * rows, 8), 2 * rows)]
                    value = jnp.where(parity == 0, pair[:rows], pair[rows:])
                else:
                    value = acc[pl.ds(pl.multiple_of((2 * m + parity) * rows, 8), rows)]
                if height > rows:
                    rest = jnp.zeros((height - rows - 8, D), f32)
                    value = jnp.concatenate([value, gain_two, rest], axis=0)
                value = value.astype(bf)
                target[m, offset : offset + height] = value
                return carry

            lax.fori_loop(0, n // 2, body, 0)
        part = pl.ds(offset, height)
        sent.append(remote(w_other.at[:, part], w_got.at[:, part], w_sems, len(sent), core_peer))
        sent[-1].start()

    rows = D // n
    wide = 2 * FFN // D
    for c in range(0, FFN, chunk):
        acc[c : c + chunk] = jnp.dot(act[:, c : c + chunk].T, cot_ref[...], preferred_element_type=f32)
    used = (1 + wide) * rows
    place(FFN // n, used, w_own.shape[1] - used)
    second_t = second[...].T
    for i in range(wide):
        acc[:D] = jnp.dot(second_t, gexp[:, i * D : (i + 1) * D], preferred_element_type=f32)
        place(rows, (1 + i) * rows, rows)
    acc[:D] = jnp.dot(attended, branch[...], preferred_element_type=f32)
    place(rows, 0, rows)

    for copy in sent:
        copy.wait()
    height = y_keep.shape[2]
    third = lambda g, i: pl.ds(pl.multiple_of((3 * g + i) * height, 16), height)

    def summed(m, part):
        return (w_own[m, part].astype(f32) + w_got[m, part].astype(f32)).astype(bf)

    def each(count, body):
        def step(i, carry):
            body(i)
            return carry

        lax.fori_loop(0, count, step, 0)

    for k in range(groups):
        g = lax.rem(group + k, groups)

        def first(m, k=k, g=g):
            (y_send.at[k - 1] if k else y_keep)[m // S2, lax.rem(m, S2)] = summed(m, third(g, 0))

        each(PLANES * S2, first)
    for k in range(S2):
        a = lax.rem(s2 + k, S2)

        def second_part(i, k=k, a=a):
            p, g = i // groups, lax.rem(i, groups)
            (x_send.at[k - 1] if k else x_keep)[p, g] = summed(p * S2 + a, third(g, 1))

        each(PLANES * groups, second_part)
    z_parts = [z_keep, z_send_1, z_send_2, z_send_3]
    for k in range(PLANES):
        p = lax.rem(plane + k, PLANES)

        def third_part(i, k=k, p=p):
            a, g = i // groups, lax.rem(i, groups)
            z_parts[k][a, g] = summed(p * S2 + a, third(g, 2))

        each(S2 * groups, third_part)
    for copy in away:
        copy.wait()


def middle(n, groups, lowt, tokens, cotangent, gains, out_w, exp_w, con_w, joint_shard, con_got):
    bf, f32 = jnp.bfloat16, jnp.float32
    S2 = n // PLANES // 2
    T, D = tokens.shape
    ffn = con_w.shape[0] * groups
    used = (D + 2 * ffn + ffn) // n + 8
    height = -(-used // (groups * 48)) * 16
    any_, vm = pl.BlockSpec(memory_space=pl.ANY), pl.BlockSpec(memory_space=pltpu.VMEM)
    sems = lambda count: pltpu.SemaphoreType.DMA((2, count))
    shape = lambda *s: jax.ShapeDtypeStruct(s, bf)
    half = (n // 2, 3 * groups * height, D)
    return pl.pallas_call(
        functools.partial(middle_kernel, n, groups),
        out_shape=(
            shape(T, D),
            jax.ShapeDtypeStruct((T, D), f32),
            shape(PLANES, QW, T),
            shape(PLANES, S2, height, D),
            shape(groups - 1, PLANES, S2, height, D),
            shape(PLANES, groups, height, D),
            shape(S2 - 1, PLANES, groups, height, D),
            shape(S2, groups, height, D),
            *[shape(S2, groups, height, D)] * (PLANES - 1),
            shape(3 * QW, D),
        ),
        in_specs=[vm, vm, vm, vm, any_, any_, any_, any_] + [any_] * (groups - 1),
        out_specs=tuple([vm] * 12),
        scratch_shapes=[
            pltpu.VMEM(out_w.shape, bf),
            pltpu.VMEM(exp_w.shape, bf),
            pltpu.VMEM((ffn, D), bf),
            pltpu.SemaphoreType.DMA((4 + groups - 1,)),
            sems(groups - 1),
            pltpu.VMEM(joint_shard.shape, bf),
            pltpu.VMEM((2, 3 * QW // 2, D // groups), bf),
            pltpu.VMEM((groups, 2, 3 * QW // 2, D // groups), bf),
            sems(2 * (groups - 1)),
            pltpu.VMEM((D, 3 * QW), bf),
            pltpu.VMEM((PLANES, QW, T), bf),
            sems(PLANES - 1),
            pltpu.VMEM((PLANES, QW, T), bf),
            sems(PLANES - 1),
            pltpu.VMEM((T, D), f32),
            pltpu.VMEM((T, D), bf),
            pltpu.VMEM((T, D), bf),
            pltpu.VMEM((T, ffn), f32),
            pltpu.VMEM((T, ffn), bf),
            pltpu.VMEM((T, 2 * ffn), bf),
            pltpu.VMEM((ffn, D), f32),
            pltpu.VMEM(half, bf),
            pltpu.VMEM(half, bf),
            pltpu.VMEM(half, bf),
            sems(2 + 2 * ffn // D),
        ],
        compiler_params=pltpu.CompilerParams(collective_id=2, has_side_effects=True, vmem_limit_bytes=60 << 20),
    )(lowt, tokens, cotangent, gains, out_w, exp_w, con_w, joint_shard, *con_got)


def tail_kernel(
    n,
    groups,
    deal_ref,
    dq_hbm,
    dkv_hbm,
    turn_ref,
    gains_ref,
    joint_hbm,
    joint_t_hbm,
    joint_near_hbm,
    first_hbm,
    tokens_hbm,
    grad_hidden_hbm,
    y_keep_hbm,
    y_got_hbm,
    x_keep_hbm,
    x_got_hbm,
    z_keep_hbm,
    z_got_1,
    z_got_2,
    z_got_3,
    d_got,
    w_all,
    jq_all,
    jk_all,
    joint_rows,
    joint_t,
    joint_near,
    first,
    tokens,
    grad_hidden,
    y_keep,
    y_got,
    x_keep,
    x_got,
    z_keep,
    z_came,
    local_sems,
    dq_ref,
    kv_own,
    own_sems,
    kv_near,
    kv_send,
    kv_far,
    kv_sems,
    mixed,
    mixed_got,
    mixed_send_sems,
    mixed_recv_sems,
    part,
    part_got,
    part_send_sems,
    part_recv_sems,
    j_acc,
    jq,
    jq_core,
    jq_side,
    jq_plane,
    jk,
    jk_core,
    jk_side,
    jk_plane,
    j_sems,
    x1_got,
    y2_got,
    y3_got,
    z1_got,
    z1_sems,
    x3_got,
    w_plane,
    w_plane_got,
    w_sems,
    d_send,
    d_mid,
    d_back,
    d_sems,
    row_sems,
    row_local,
):
    bf, f32 = jnp.bfloat16, jnp.float32
    S = n // PLANES
    S2 = S // 2
    T, D = tokens.shape
    me, group = lax.axis_index("ctx"), lax.axis_index("fsdp")
    plane, side = me // S, lax.rem(me, S)
    s2, core = side // 2, lax.rem(side, 2)
    MESH = pl.DeviceIdType.MESH

    def at(p, a, c, g):
        return (p * S + a * 2 + c, g)

    def plane_peer(k):
        return at(lax.rem(plane + k, PLANES), s2, core, group)

    def side_peer(k):
        return at(plane, lax.rem(s2 + k, S2), core, group)

    def group_peer(k):
        return at(plane, s2, core, lax.rem(group + k, groups))

    core_peer = at(plane, s2, 1 - core, group)

    def send(source, target, send_sem, recv_sem, device):
        return pltpu.make_async_remote_copy(
            src_ref=source, dst_ref=target, send_sem=send_sem, recv_sem=recv_sem, device_id=device, device_id_type=MESH
        )

    def remote(source, target, sems, index, device):
        return send(source, target, sems.at[0, index], sems.at[1, index], device)

    def total_of(terms):
        total = terms[0].astype(f32)
        for term in terms[1:]:
            total = total + term.astype(f32)
        return total

    lower = plane < 2
    middle = (plane == 1) | (plane == 2)
    order = [
        jnp.where(lower, 3, 0),
        jnp.where(plane == 0, 2, jnp.where(plane == 1, 0, jnp.where(plane == 2, 3, 1))),
        jnp.where((plane == 0) | (plane == 2), 1, 2),
        plane,
    ]
    steps = range(PLANES)
    back = [lax.rem(plane + PLANES - p, PLANES) for p in order]
    main = jnp.where(lower, 0, 1)
    main_plane = plane + 1 - 2 * main

    own_kv = [
        pltpu.make_async_copy(dkv_hbm.at[order[t], :, core], kv_own.at[t], own_sems.at[t]) for t in steps
    ] + [pltpu.make_async_copy(dq_hbm, dq_ref, own_sems.at[PLANES])]
    for copy in own_kv:
        copy.start()
    local = [
        pltpu.make_async_copy(source, target, local_sems.at[i])
        for i, (source, target) in enumerate(
            [
                (first_hbm, first),
                (joint_t_hbm, joint_t),
                (y_keep_hbm, y_keep),
                (y_got_hbm, y_got),
                (x_keep_hbm, x_keep),
                (x_got_hbm, x_got),
                (z_keep_hbm, z_keep),
                (z_got_1, z_came.at[0]),
                (z_got_2, z_came.at[1]),
                (z_got_3, z_came.at[2]),
                (tokens_hbm, tokens),
                (grad_hidden_hbm, grad_hidden),
                (joint_near_hbm, joint_near),
            ]
        )
    ]
    for i in (2, 3, 4, 5, 6, 7, 8, 9, 0, 1, 12, 10, 11):
        local[i].start()
    barrier = pltpu.get_barrier_semaphore()

    def greet(k, carry):
        pl.semaphore_signal(barrier, inc=1, device_id=(lax.rem(me + k, n), group), device_id_type=MESH)
        return carry

    lax.fori_loop(1, n, greet, 0)
    for k in range(1, groups):
        pl.semaphore_signal(barrier, inc=1, device_id=group_peer(k), device_id_type=MESH)
    pl.semaphore_wait(barrier, n - 1 + groups - 1)

    core_kv = [remote(dkv_hbm.at[order[t], :, 1 - core], kv_near.at[t], kv_sems, t, core_peer) for t in steps]
    for copy in core_kv:
        copy.start()

    per_group = joint_hbm.shape[0]
    index = me - group * per_group
    held_here = (index >= 0) & (index < per_group)
    row_own = pltpu.make_async_copy(joint_hbm.at[jnp.clip(index, 0, per_group - 1)], joint_rows, row_local.at[0])
    row_moves = [
        send(
            joint_hbm.at[jnp.clip(index, 0, per_group - 1)],
            joint_rows,
            row_sems.at[k - 1],
            row_sems.at[groups - 1],
            group_peer(k),
        )
        for k in range(1, groups)
    ]

    @pl.when(held_here)
    def _():
        row_own.start()
        for copy in row_moves:
            copy.start()

    w_moves = []

    def w_copy(source, target, device):
        copy = remote(source, target, w_sems, len(w_moves), device)
        w_moves.append(copy)
        copy.start()
        return copy

    local[2].wait()
    local[3].wait()
    for p in range(PLANES):
        for a in range(S2):
            y_keep[p, a] = total_of([y_keep[p, a]] + [y_got[k, p, a] for k in range(groups - 1)]).astype(bf)

    def z1_send(t, slot, target):
        return send(
            y_keep.at[order[t]], z1_got.at[slot], z1_sems.at[0, t], z1_sems.at[1, slot], at(target, s2, core, group)
        )

    def z1_add(t, slot):
        z1_send(0, slot, main_plane).wait_recv()
        for a in range(S2):
            y_keep[order[t], a] = total_of([y_keep[order[t], a], z1_got[slot, a]]).astype(bf)

    def z1_relay(t, slot, onward, target):
        @pl.when(middle)
        def _():
            z1_add(t, slot)
            z1_send(t, onward, target).start()

    @pl.when(jnp.logical_not(middle))
    def _():
        for t in range(PLANES - 1):
            z1_send(t, t, main_plane).start()


    def turned_back(x, t):
        cos, sin = turn_ref[back[t], :HALF], turn_ref[back[t], HALF:]
        rows = []
        for h in range(HP):
            upper, lower = x[h * HD : h * HD + HALF], x[h * HD + HALF : (h + 1) * HD]
            rows += [upper * cos + lower * sin, lower * cos - upper * sin]
        return jnp.concatenate(rows, axis=0)

    side_kv = {}
    for t in steps:
        own_kv[t].wait()
        core_kv[t].wait()
        for a in range(S2):
            kv_send[t, a] = total_of([kv_own[t, a], kv_near[t, a]]).astype(bf)
        for k in range(1, S2):
            side_kv[t, k] = remote(
                kv_send.at[t, lax.rem(s2 + S2 - k, S2)],
                kv_far.at[t, k - 1],
                kv_sems,
                PLANES + t * (S2 - 1) + k - 1,
                side_peer(S2 - k),
            )
            side_kv[t, k].start()
    own_kv[PLANES].wait()
    for t in steps:
        mixed[t, :QW] = turned_back(dq_ref[back[t]], t).astype(bf)

    local[4].wait()
    local[5].wait()
    for p in range(PLANES):
        for g in range(groups):
            x_keep[p, g] = total_of([x_keep[p, g]] + [x_got[k, p, g] for k in range(S2 - 1)]).astype(bf)
    y2 = [w_copy(x_keep.at[:, lax.rem(group + k, groups)], y2_got.at[k - 1], group_peer(k)) for k in range(1, groups)]
    for i in range(6, 10):
        local[i].wait()
    for a in range(S2):
        for g in range(groups):
            z_keep[a, g] = total_of([z_keep[a, g]] + [z_came[k, a, g] for k in range(PLANES - 1)]).astype(bf)
    y3 = [w_copy(z_keep.at[:, lax.rem(group + k, groups)], y3_got.at[k - 1], group_peer(k)) for k in range(1, groups)]

    j_moves = []

    def j_copy(source, target, device):
        copy = remote(source, target, j_sems, len(j_moves), device)
        j_moves.append(copy)
        copy.start()
        return copy

    def j_core_stage(begin, height, grads, near):
        j_acc[:height] = total_of(
            [
                jnp.dot(mixed[t, begin : begin + height], first[back[t]], preferred_element_type=f32)
                for t in steps
            ]
        )
        shard_rows = D // n
        for i in range(D // 128):
            block = j_acc[:height, i * 128 : (i + 1) * 128].T
            row = i * 128
            while row < (i + 1) * 128:
                shard, offset = divmod(row, shard_rows)
                count = min(shard_rows - offset, (i + 1) * 128 - row)
                source = row - i * 128
                grads[shard // S, shard % S // 2, shard % 2, offset : offset + count] = block[
                    source : source + count
                ].astype(bf)
                row += count
        return [j_copy(grads.at[:, :, 1 - core], near, core_peer)]

    def j_side_stage(moves, grads, near, far):
        for copy in moves:
            copy.wait()
        for p in range(PLANES):
            for a in range(S2):
                near[p, a] = total_of([grads[p, a, core], near[p, a]]).astype(bf)
        return [j_copy(near.at[:, lax.rem(s2 + k, S2)], far.at[k - 1], side_peer(k)) for k in range(1, S2)]

    def j_plane_stage(moves, near, far, gathered):
        for copy in moves:
            copy.wait()
        for p in range(PLANES):
            far[0, p] = total_of([near[p, s2]] + [far[k, p] for k in range(S2 - 1)]).astype(bf)
        gathered[plane] = far[0, plane]
        return [
            j_copy(far.at[0, lax.rem(plane + k, PLANES)], gathered.at[plane], plane_peer(k)) for k in range(1, PLANES)
        ]

    def j_group_stage(moves, gathered, every):
        for copy in moves:
            copy.wait()
        every[group] = gathered[...]
        return [j_copy(gathered, every.at[group], group_peer(k)) for k in range(1, groups)]

    local[0].wait()
    jq_moves = j_core_stage(0, QW, jq, jq_core)
    z1_relay(0, 0, 3, main_plane)

    local[1].wait()

    half = T // 2
    halves = range(2)

    def mixed_send(t, e):
        lanes = pl.ds(e * half, half)
        return send(
            mixed.at[t, :, lanes],
            mixed_got.at[t, :, lanes],
            mixed_send_sems.at[t, e],
            mixed_recv_sems.at[t, e],
            at(main_plane, s2, core, group),
        )

    def part_send(t, e, direction, target):
        rows = pl.ds(e * half, half)
        return send(
            part.at[t, rows],
            part_got.at[direction, order[t], rows],
            part_send_sems.at[t, e],
            part_recv_sems.at[direction * PLANES + order[t], e],
            at(target, s2, core, group),
        )

    def part_came(direction, p, e):
        rows = pl.ds(e * half, half)
        return send(
            part.at[0, rows],
            part_got.at[direction, p, rows],
            part_send_sems.at[0, e],
            part_recv_sems.at[direction * PLANES + p, e],
            core_peer,
        )

    other_plane = 2 * plane - main_plane

    def product(grads, columns):
        return jnp.dot(grads.T, columns, preferred_element_type=f32)

    def add_mixed(t, slot, e):
        mixed_send(slot, e).wait_recv()
        rows = slice(e * half, (e + 1) * half)
        near = product(mixed_got[slot, :, rows], joint_near[...])
        part[t, rows] = (part[t, rows].astype(f32) + near).astype(bf)

    def add_part(t, direction, p, e):
        part_came(direction, p, e).wait_recv()
        rows = slice(e * half, (e + 1) * half)
        part[t, rows] = total_of([part[t, rows], part_got[direction, p, rows]]).astype(bf)

    def relay(t, slot):
        @pl.when(middle)
        def _():
            for e in halves:
                if slot is None:
                    add_part(t, 1 - main, order[t], e)
                    part_send(t, e, 1 - main, other_plane).start()
                else:
                    add_mixed(t, slot, e)
                    part_send(t, e, main, main_plane).start()

    def key_step(t):
        for k in range(1, S2):
            side_kv[t, k].wait()
        dk = total_of([kv_send[t, s2]] + [kv_far[t, k] for k in range(S2 - 1)]).T
        mixed[t, QW : 2 * QW] = turned_back(dk[:QW], t).astype(bf)
        mixed[t, 2 * QW :] = dk[QW:].astype(bf)
        if t < PLANES - 1:

            @pl.when(jnp.logical_not(middle))
            def _():
                for e in halves:
                    mixed_send(t, e).start()

            @pl.when(middle)
            def _():
                part[t] = product(mixed[t], joint_t[: 3 * QW]).astype(bf)

        else:
            part[t] = product(mixed[t], joint_t[: 3 * QW]).astype(bf)

    local[12].wait()
    key_step(0)
    z1_relay(2, 1, 4, main_plane)
    jq_moves = j_side_stage(jq_moves, jq, jq_core, jq_side)
    key_step(1)
    z1_relay(1, 3, 5, 2 * plane - main_plane)
    for copy in y2:
        copy.wait()
    for p in range(PLANES):
        w_plane[p] = total_of([x_keep[p, group]] + [y2_got[k, p] for k in range(groups - 1)]).astype(bf)
    w_last = [
        w_copy(w_plane.at[lax.rem(plane + k, PLANES)], w_plane_got.at[k - 1], plane_peer(k)) for k in range(1, PLANES)
    ]
    key_step(2)
    relay(0, 0)
    jq_moves = j_plane_stage(jq_moves, jq_core, jq_side, jq_plane)
    key_step(3)
    relay(2, 1)
    jk_moves = j_core_stage(QW, 2 * QW, jk, jk_core)

    for copy in y3:
        copy.wait()
    for a in range(S2):
        z_keep[a, group] = total_of([z_keep[a, group]] + [y3_got[k, a] for k in range(groups - 1)]).astype(bf)
    x3 = [w_copy(z_keep.at[lax.rem(s2 + k, S2), group], x3_got.at[k - 1], side_peer(k)) for k in range(1, S2)]
    @pl.when(middle)
    def _():
        z1_add(PLANES - 1, 2)
        z1_add(PLANES - 1, 4)

    @pl.when(jnp.logical_not(middle))
    def _():
        z1_add(PLANES - 1, 5)

    x1 = [w_copy(y_keep.at[plane, lax.rem(s2 + k, S2)], x1_got.at[k - 1], side_peer(k)) for k in range(1, S2)]
    relay(1, None)
    jk_moves = j_side_stage(jk_moves, jk, jk_core, jk_side)
    jq_moves = j_group_stage(jq_moves, jq_plane, jq_all)

    local[10].wait()
    local[11].wait()
    @pl.when(middle)
    def _():
        for e in halves:
            add_mixed(PLANES - 1, 2, e)

    for e in halves:
        add_part(PLANES - 1, 1 - main, plane, e)

    strip = 64

    def norm_back(i, carry):
        rows = pl.ds(pl.multiple_of(i * strip, strip), strip)
        grad = part[PLANES - 1, rows].astype(f32)
        values = tokens[rows].astype(f32)
        centred = values - jnp.mean(values, axis=-1, keepdims=True)
        scale = lax.rsqrt(jnp.mean(centred * centred, axis=-1, keepdims=True) + norm_eps)
        normal = centred * scale
        grad = grad * gains_ref[0:1]
        grad = grad - jnp.mean(grad, axis=-1, keepdims=True) - normal * jnp.mean(grad * normal, axis=-1, keepdims=True)
        grad_hidden[rows] = grad_hidden[rows] + grad * scale
        return carry

    lax.fori_loop(0, T // strip, norm_back, 0)

    blocks = T // BLOCK
    piece = BLOCK // n

    def d_copy(source, target, base, k):
        return remote(source.at[lax.rem(me + k, n)], target.at[me], d_sems, base + k, (lax.rem(me + k, n), group))

    for i in range(n):
        d_send[i] = jnp.concatenate(
            [grad_hidden[b * BLOCK + i * piece : b * BLOCK + (i + 1) * piece] for b in range(blocks)], axis=0
        ).astype(bf)
    out_deal = [d_copy(d_send, d_mid, 0, k) for k in range(1, n)]
    for copy in out_deal:
        copy.start()
    d_mid[me] = d_send[me]

    for copy in x1 + w_last + x3:
        copy.wait()
    height = w_plane.shape[1]
    w_all[group, :height] = total_of([y_keep[plane, s2]] + [x1_got[k] for k in range(S2 - 1)]).astype(bf)
    w_all[group, height : 2 * height] = total_of(
        [w_plane[plane]] + [w_plane_got[k] for k in range(PLANES - 1)]
    ).astype(bf)
    w_all[group, 2 * height :] = total_of([z_keep[s2, group]] + [x3_got[k] for k in range(S2 - 1)]).astype(bf)
    w_gather = [w_copy(w_all.at[group], w_all.at[group], group_peer(k)) for k in range(1, groups)]
    jk_moves = j_plane_stage(jk_moves, jk_core, jk_side, jk_plane)

    for copy in out_deal:
        copy.wait()
    for i in range(n):
        chosen = []
        for b in range(blocks):
            wanted = deal_ref[i * blocks + b]
            held = d_mid[wanted // blocks].astype(f32)
            rows = held[:piece]
            for other in range(1, blocks):
                rows = jnp.where(lax.rem(wanted, blocks) == other, held[other * piece : (other + 1) * piece], rows)
            chosen.append(rows)
        d_back[i] = jnp.concatenate(chosen, axis=0).astype(bf)
    back_deal = [d_copy(d_back, d_got, n, k) for k in range(1, n)]
    for copy in back_deal:
        copy.start()
    d_got[me] = d_back[me]

    jk_moves = j_group_stage(jk_moves, jk_plane, jk_all)

    for copy in back_deal + w_gather + jq_moves + jk_moves:
        copy.wait()
    for t in range(PLANES - 1):
        z1_send(t, 0, main_plane).wait_send()
        for e in halves:

            @pl.when(middle)
            def _(t=t, e=e):
                part_send(t, e, main, main_plane).wait_send()

            @pl.when(jnp.logical_not(middle))
            def _(t=t, e=e):
                mixed_send(t, e).wait_send()

    @pl.when(held_here)
    def _():
        row_own.wait()
        for copy in row_moves:
            copy.wait_send()

    @pl.when(jnp.logical_not(held_here))
    def _():
        row_moves[0].wait_recv()


def tail(n, groups, deal, dqt, dkv, turn, gains, joint_shard, joint_t, joint_near, first, tokens, grad_hidden, pieces):
    bf, f32 = jnp.bfloat16, jnp.float32
    S2 = n // PLANES // 2
    T, D = tokens.shape
    rows = D // n
    height = pieces[0].shape[2]
    piece_rows = T // n
    joint_shard = joint_shard.reshape(-1, rows, joint_shard.shape[1])
    any_, vm, sm = (pl.BlockSpec(memory_space=m) for m in (pl.ANY, pltpu.VMEM, pltpu.SMEM))
    sems = lambda count: pltpu.SemaphoreType.DMA((2, count))
    small = lambda *s: pltpu.VMEM(s, bf)
    j_buffers = lambda w: [
        small(PLANES, S2, 2, rows, w),
        small(PLANES, S2, rows, w),
        small(S2 - 1, PLANES, rows, w),
        small(PLANES, rows, w),
    ]
    return pl.pallas_call(
        functools.partial(tail_kernel, n, groups),
        out_shape=(
            jax.ShapeDtypeStruct((n, piece_rows, D), bf),
            jax.ShapeDtypeStruct((groups, 3 * height, D), bf),
            jax.ShapeDtypeStruct((groups, PLANES, rows, QW), bf),
            jax.ShapeDtypeStruct((groups, PLANES, rows, 2 * QW), bf),
            jax.ShapeDtypeStruct(joint_shard.shape[1:], bf),
        ),
        in_specs=[sm, any_, any_, vm, vm] + [any_] * 14,
        out_specs=tuple([vm] * 4) + (any_,),
        scratch_shapes=[
            pltpu.VMEM(joint_t.shape, bf),
            pltpu.VMEM(joint_near.shape, bf),
            pltpu.VMEM((PLANES, T, D), bf),
            pltpu.VMEM((T, D), bf),
            pltpu.VMEM((T, D), f32),
            *[pltpu.VMEM(p.shape, bf) for p in pieces[:5]],
            pltpu.VMEM((PLANES - 1, *pieces[5].shape), bf),
            pltpu.SemaphoreType.DMA((13,)),
            pltpu.VMEM(dqt.shape, f32),
            small(PLANES, S2, T, 2 * QW),
            pltpu.SemaphoreType.DMA((PLANES + 1,)),
            small(PLANES, S2, T, 2 * QW),
            small(PLANES, S2, T, 2 * QW),
            small(PLANES, S2 - 1, T, 2 * QW),
            sems(PLANES * S2),
            small(PLANES, 3 * QW, T),
            small(PLANES - 1, 3 * QW, T),
            pltpu.SemaphoreType.DMA((PLANES - 1, 2)),
            pltpu.SemaphoreType.DMA((PLANES - 1, 2)),
            small(PLANES, T, D),
            small(2, PLANES, T, D),
            pltpu.SemaphoreType.DMA((PLANES - 1, 2)),
            pltpu.SemaphoreType.DMA((2 * PLANES, 2)),
            pltpu.VMEM((2 * QW, D), f32),
            *j_buffers(QW),
            *j_buffers(2 * QW),
            sems(2 * (1 + S2 - 1 + PLANES - 1 + groups - 1)),
            small(S2 - 1, height, D),
            small(groups - 1, PLANES, height, D),
            small(groups - 1, S2, height, D),
            small(6, S2, height, D),
            pltpu.SemaphoreType.DMA((2, 6)),
            small(S2 - 1, height, D),
            small(PLANES, height, D),
            small(PLANES - 1, height, D),
            sems(3 * (groups - 1) + 2 * (S2 - 1) + PLANES - 1),
            small(n, piece_rows, D),
            small(n, piece_rows, D),
            small(n, piece_rows, D),
            sems(2 * n),
            pltpu.SemaphoreType.DMA((groups,)),
            pltpu.SemaphoreType.DMA((1,)),
        ],
        compiler_params=pltpu.CompilerParams(collective_id=0, has_side_effects=True, vmem_limit_bytes=60 << 20),
    )(deal, dqt, dkv, turn, gains, joint_shard, joint_t, joint_near, first, tokens, grad_hidden, *pieces)


def finish_kernel(
    n,
    d_ref,
    w_ref,
    jq_ref,
    jk_ref,
    rows_ref,
    gains_ref,
    dealt_ref,
    joint_ref,
    output_ref,
    expand_ref,
    contract_ref,
    gain_one_ref,
    gain_two_ref,
):
    f32 = jnp.float32
    T, D = dealt_ref.shape
    blocks = T // BLOCK
    piece = BLOCK // n
    for b in range(blocks):
        for i in range(0, n, 2):
            rows = [d_ref[i + e].astype(f32)[b * piece : (b + 1) * piece] for e in range(2)]
            dealt_ref[b * BLOCK + i * piece : b * BLOCK + (i + 2) * piece] = jnp.concatenate(rows, axis=0).astype(
                dealt_ref.dtype
            )

    def summed(ref, p):
        total = ref[0, p].astype(f32)
        for g in range(1, ref.shape[0]):
            total = total + ref[g, p].astype(f32)
        return total.T

    for i in range(PLANES // 2):
        pair = [summed(jq_ref, 2 * i + e) for e in range(2)]
        joint_ref[:, i * 2 * QW : (i + 1) * 2 * QW] = jnp.concatenate(pair, axis=0).T
        pair = [summed(jk_ref, 2 * i + e) for e in range(2)]
        for part in range(2):
            cols = (part + 1) * D + i * 2 * QW
            rows = [x[part * QW : (part + 1) * QW] for x in pair]
            joint_ref[:, cols : cols + 2 * QW] = jnp.concatenate(rows, axis=0).T
    shift = D - lax.axis_index("ctx") * (D // n)

    def own_lanes(x):
        return pltpu.roll(jnp.broadcast_to(x, (8, D)), shift, 1)[0:1, : D // n]

    product = jnp.sum(joint_ref[...] * rows_ref[...].astype(f32), axis=1, keepdims=True)
    product = jnp.broadcast_to(product, (D // n, 128)).T[0:1]
    gain_one_ref[...] = product / own_lanes(gains_ref[0:1])
    height = w_ref.shape[1]
    rows = D // n
    targets = [(output_ref, 0, rows)]
    targets += [(expand_ref, i * D, rows) for i in range(expand_ref.shape[1] // D)]
    targets += [(contract_ref, 0, contract_ref.shape[0])]
    row = 0
    for target, column, count in targets:
        done = 0
        while done < count:
            g, offset = divmod(row, height)
            part = min(count - done, height - offset)
            target[done : done + part, column : column + D] = w_ref[g, offset : offset + part].astype(f32)
            done += part
            row += part
    g, offset = divmod(row, height)
    gain_two_ref[...] = own_lanes(w_ref[g, offset : offset + 1].astype(f32))


def finish(n, T, wide, contract_rows, d_got, w_all, jq_all, jk_all, joint_rows, gains):
    D = d_got.shape[-1]
    rows = D // n
    f32 = jnp.float32
    vm = pl.BlockSpec(memory_space=pltpu.VMEM)
    return pl.pallas_call(
        functools.partial(finish_kernel, n),
        out_shape=(
            jax.ShapeDtypeStruct((T, D), jnp.bfloat16),
            jax.ShapeDtypeStruct((rows, 3 * D), f32),
            jax.ShapeDtypeStruct((rows, D), f32),
            jax.ShapeDtypeStruct((rows, wide), f32),
            jax.ShapeDtypeStruct((contract_rows, D), f32),
            jax.ShapeDtypeStruct((1, rows), f32),
            jax.ShapeDtypeStruct((1, rows), f32),
        ),
        in_specs=[vm] * 6,
        out_specs=tuple([vm] * 7),
    )(d_got, w_all, jq_all, jk_all, joint_rows, gains)


def on_device(
    n,
    groups,
    tokens,
    cotangent,
    lengths,
    deal,
    joint_projection,
    output_projection,
    expand_weight,
    contract_weight,
    gain_first,
    gain_second,
):
    T, D = tokens.shape[1:]
    S = n // PLANES
    S2 = S // 2

    def over_planes(x, k):
        return lax.ppermute(x, "ctx", [(h * S + s, (h + k) % PLANES * S + s) for h in range(PLANES) for s in range(S)])

    def over_sides(x, k):
        pairs = [
            (h * S + a * 2 + c, h * S + (a + k) % S2 * 2 + c) for h in range(PLANES) for a in range(S2) for c in range(2)
        ]
        return lax.ppermute(x, "ctx", pairs)

    def over_groups(x, k):
        return lax.ppermute(x, "fsdp", [(f, (f + k) % groups) for f in range(groups)])

    def moved(x, over):
        if x.shape[0] == 1:
            return over(x, 1)
        return jnp.stack([over(x[k], k + 1) for k in range(x.shape[0])])

    first, qt, kv, joint_t, turn, gains, out_w, exp_w, con_half = front(
        n,
        groups,
        lengths,
        tokens[0],
        joint_projection,
        gain_first,
        gain_second,
        output_projection,
        expand_weight,
        contract_weight,
    )
    con_got = [over_groups(con_half, k) for k in range(1, groups)]
    out_w, exp_w = (w.reshape(-1, w.shape[-1]) for w in (out_w, exp_w))
    ot, lowt, lse = attn_fwd(n, lengths, qt, kv)
    output, grad_hidden, gt, y_keep, y_send, x_keep, x_send, z_keep, *z_send, joint_near = middle(
        n, groups, lowt, tokens[0], cotangent[0], gains, out_w, exp_w, contract_weight, joint_projection, con_got
    )
    y_got, x_got = moved(y_send, over_groups), moved(x_send, over_sides)
    z_got = [over_planes(part, k + 1) for k, part in enumerate(z_send)]
    dqt, dkv = attn_bwd(n, lengths, qt, kv, ot, lse, gt)
    d_got, w_all, jq_all, jk_all, joint_rows = tail(
        n,
        groups,
        deal[0],
        dqt,
        dkv.reshape(PLANES, S2, 2, T, 2 * QW),
        turn,
        gains,
        joint_projection,
        joint_t,
        joint_near,
        first,
        tokens[0],
        grad_hidden,
        [y_keep, y_got, x_keep, x_got, z_keep, *z_got],
    )
    dealt, shard_joint, shard_output, shard_expand, shard_contract, gain_one, gain_two = finish(
        n, T, exp_w.shape[1], contract_weight.shape[0] * groups // n, d_got, w_all, jq_all, jk_all, joint_rows, gains
    )
    return (
        output[None],
        dealt[None],
        shard_joint,
        shard_output,
        shard_expand,
        shard_contract,
        gain_one[0],
        gain_two[0],
    )


def solution(mesh):
    return jax.shard_map(
        functools.partial(on_device, mesh.shape["ctx"], mesh.shape["fsdp"]),
        mesh=mesh,
        in_specs=(
            P("fsdp", "ctx", None),
            P("fsdp", "ctx", None),
            P("fsdp", None),
            P("fsdp", None),
            P("fsdp", None),
            P("fsdp", None),
            P("fsdp", None),
            P("fsdp", None),
            P("fsdp"),
            P("fsdp"),
        ),
        out_specs=(
            P("fsdp", "ctx", None),
            P("fsdp", "ctx", None),
            P("ctx", None),
            P("ctx", None),
            P("ctx", None),
            P("ctx", None),
            P("ctx"),
            P("ctx"),
        ),
        check_vma=False,
    )
```
